128 devices in a mesh: dp: 64 (over y, x, z), tensor: 2 (over core).
Axes of the slice: x: 4, y: 4, z: 4, core: 2. Of those that a mesh axis runs over, the one named last changes fastest.
Arguments:
- tokens: bfloat16 [16384, 1536], P('dp'), may hold values from -6 to 6
- out_grad: bfloat16 [16384, 1536], P('dp'), may hold values from -6 to 6
- norm1_gain: float32 [1536], replicated, may hold values from 0.5 to 1.5
- norm2_gain: float32 [1536], replicated, may hold values from 0.5 to 1.5
- w_query: bfloat16 [1536, 1536], P(None, 'tensor'), may hold values from -0.15625 to 0.15625
- w_key: bfloat16 [1536, 512], P(None, 'tensor'), may hold values from -0.15625 to 0.15625
- w_value: bfloat16 [1536, 512], P(None, 'tensor'), may hold values from -0.15625 to 0.15625
- w_out: bfloat16 [1536, 1536], P('tensor'), may hold values from -1.25 to 1.25
- w_gate: bfloat16 [64, 1536, 512], P('dp', None, 'tensor'), may hold values from -0.15625 to 0.15625
- w_up: bfloat16 [64, 1536, 512], P('dp', None, 'tensor'), may hold values from -0.15625 to 0.15625
- w_down: bfloat16 [64, 512, 1536], P('dp', 'tensor'), may hold values from -1 to 1
- route_ids: int32 [16384, 8], P('dp'), may hold values from 0 to 39, all different within a row; in each aligned block of 256 rows (0 to 255, 256 to 511, ...) at most 64 rows name the same one
- route_logits: float32 [16384, 8], P('dp'), may hold values from -3 to 3
- seq_ids: int32 [16384], P('dp'), may hold values from 0 to 31, never falling along the last dimension, each value on 1 to 1024 neighbouring positions
- piece_ids: int32 [16384], P('dp'), may hold values from 0 to 64, as said below
- clip_limit: float32 [24], P('tensor'), may hold values from 3 to 9
Outputs:
- output: bfloat16 [16384, 1536], P('dp')
- input_grad: float32 [16384, 1536], P('dp')
- grad_query: float32 [1536, 1536], P(None, 'tensor')
- grad_key: float32 [1536, 512], P(None, 'tensor')
- grad_value: float32 [1536, 512], P(None, 'tensor')
- grad_out: float32 [1536, 1536], P('tensor')
- grad_norm1: float32 [1536], replicated
- grad_norm2: float32 [1536], replicated
- grad_gate: float32 [64, 1536, 512], P('dp', None, 'tensor')
- grad_up: float32 [64, 1536, 512], P('dp', None, 'tensor')
- grad_down: float32 [64, 512, 1536], P('dp', 'tensor')
- clipped_query: bfloat16 [1536, 1536], P(None, 'tensor')
- clipped_key: bfloat16 [1536, 512], P(None, 'tensor')
- head_peaks: float32 [24], P('tensor')
The draws below stay inside these ranges and needn't reach their ends.
Inputs may be any that keep to these rules, and one draw needn't show every extreme that they name: `route_ids`: each row names 8 different experts; in the rows of one index of dp no expert is named more than 64 times, a bound that some block reaches. `seq_ids`: never falling; each sequence is 1 to 1024 consecutive tokens, the longest exactly 1024. `piece_ids`: A nonzero number k + 1 marks exactly the tokens k * 256 to (k + 1) * 256 - 1; the last 256 tokens are always marked.
All inputs are finite; a program needn't handle non-finite values.
Results may differ from the reference program's by a relative error of at most 0.018.
Values may be sent and summed in bfloat16 or wider, within the bound.
No kernel may reach another device: no remote copies, remote signals or barrier semaphores. Data moves between devices by JAX's collectives and lax.ppermute only.
A program may use at most 320 MiB of HBM per device.

```python
import math
import jax
import jax.numpy as jnp
import numpy as np
from jax import lax

D = 1536
H = 24
KVH = 8
HD = 64
EXPERTS = 40
TOP = 8
FF_E = 512
TOK_DEV = 256
LEN = 1024
PIECE = 256
TOKENS = 16384
SEQS = 32
CAP = 64
EXP_SLOTS = 64
N_DP = 64


def draw_piece_ids(key, part):
    slot_total = TOKENS // PIECE
    marks = jax.random.randint(key, (slot_total,), 0, 2, dtype=jnp.int32)
    marks = marks.at[slot_total - 1].set(1)
    numbers = marks * (jnp.arange(slot_total, dtype=jnp.int32) + 1)
    return jnp.repeat(numbers, PIECE).astype(jnp.int32)


def shard_levels(stream_key, dims, split, low, high):
    def one(position, parts):
        steps = jax.random.uniform(jax.random.fold_in(jax.random.fold_in(stream_key, 6), position), (parts,), jnp.float32, low / len(split), high / len(split))
        return jnp.repeat(jnp.exp(steps), dims[position] // parts).reshape((-1,) + (1,) * (len(dims) - position - 1))

    loudness = one(*split[0])
    for cut in split[1:]:
        loudness = loudness * one(*cut)
    return loudness


def profile(number_of, total, limit, skew):
    weights = [(1 << 20) // math.isqrt(grade ** skew) + 1 for grade in range(2, number_of + 1)]
    surplus, given = total - limit - (number_of - 1), [1] * (number_of - 1)
    while surplus > 0:
        candidates = [i for i in range(number_of - 1) if given[i] < limit]
        pool, left = sum([weights[i] for i in candidates]), surplus
        for i in candidates:
            extra = min(limit - given[i], max(1, left * weights[i] // pool), surplus)
            given[i] = given[i] + extra
            surplus = surplus - extra
    return np.array([limit] + given)


def ragged(rng, count, total, most, slope):
    if count == 2:
        one = jax.random.randint(rng, (), max(1, total - most), min(most, total - 1) + 1)
        return jnp.stack([one, total - one])
    lengths = jnp.asarray(profile(count, total, most, slope), jnp.int32)
    twos = (count - 1) // 2
    donor, sink = lengths[1:1 + 2 * twos:2], lengths[2:2 + 2 * twos:2]
    slack = jnp.minimum(donor - 1, most - sink)
    passed = jax.random.randint(jax.random.fold_in(rng, 1), (twos,), 0, 1 << 20) % (slack + 1)
    lengths = lengths.at[1:1 + 2 * twos:2].set(donor - passed).at[2:2 + 2 * twos:2].set(sink + passed)
    return lengths[jax.random.permutation(jax.random.fold_in(rng, 2), count)]


def assign_block(own_key, own, number, rows, amount, top, reach, skew):
    sequence = jax.random.permutation(own_key, amount)
    packed, usual = load_shares(amount, rows * top, reach, skew, True), load_shares(amount, rows * top, reach, skew, False)
    places = jnp.arange(amount)

    def named(lengths, rotation):
        used = int((lengths > 0).sum())
        fixed = max(1, used // 4)
        passed = fixed + (places - fixed + rotation * (used - fixed)) % max(1, amount - fixed)
        return jnp.zeros((amount,), jnp.int32).at[sequence[jnp.where(places < fixed, places, passed)]].set(jnp.asarray(lengths, jnp.int32))

    lengths = jnp.where(number % 4 == 0, named(packed, number // 4), named(usual, number - number // 4 - 1))
    mixed = jax.random.permutation(jax.random.fold_in(own, 3), amount)
    source_of, receiver = mixed[0:amount // 2 * 2:2], mixed[1:amount // 2 * 2:2]
    room = jnp.minimum(lengths[source_of] - 1, reach - lengths[receiver]) // 2
    room = jnp.where((source_of == sequence[0]) | (receiver == sequence[0]) | (lengths[receiver] == 0), 0, jnp.maximum(room, 0))
    passed = jax.random.randint(jax.random.fold_in(own, 4), (amount // 2,), 0, 1 << 20) % (room + 1)
    lengths = lengths.at[source_of].add(-passed).at[receiver].add(passed)
    labels = jnp.searchsorted(jnp.cumsum(lengths), jnp.arange(rows * top), side="right").astype(jnp.int32)
    listing = labels.reshape(top, rows).T
    listing = listing[jax.random.permutation(jax.random.fold_in(own, 1), rows)]
    rotation = jax.random.randint(jax.random.fold_in(own, 2), (rows, 1), 0, top)
    return jnp.take_along_axis(listing, (jnp.arange(top)[None, :] + rotation) % top, axis=1)


def load_shares(count, total, reach, skew, full):
    portions = [(1 << 20) // math.isqrt(grade ** skew) + 1 for grade in range(1, count + 1)]
    largest = reach if full else min(reach, max(-(-total // count), total * portions[0] // sum(portions)))
    least = 1 if total - largest >= count - 1 else 0
    holding, rest = [largest] + [least] * (count - 1), total - largest - least * (count - 1)
    while rest > 0:
        movable = [i for i in range(1, count) if holding[i] < largest] or [i for i in range(1, count) if holding[i] < reach]
        pool, remaining = sum([portions[i] for i in movable]), rest
        for i in movable:
            extra = min(reach - holding[i], max(1, remaining * portions[i] // pool), rest)
            holding[i] = holding[i] + extra
            rest = rest - extra
    return np.array(holding)


def gaussian(key, dims, deviation, bound, split=(), kind=jnp.bfloat16):
    drawn = jax.random.normal(key, dims, jnp.float32) * deviation
    if len(split) > 0:
        drawn = shard_levels(key, dims, split, -0.22, 0.18) * drawn
    return jnp.clip(drawn, min=-bound, max=bound).astype(kind)


def setup_inputs(seed: int = 0) -> dict:
    seeds = jax.random.split(jax.random.key(seed), 17)
    tokens = gaussian(seeds[0], (TOKENS, D), 1.0, 6.0, ((0, 64),))
    out_grad = gaussian(seeds[1], (TOKENS, D), 1.0, 6.0, ((0, 64),))
    norm1_gain = jnp.clip(1.0 + 0.1 * jax.random.normal(seeds[2], (D,), jnp.float32), 0.5, 1.5)
    norm2_gain = jnp.clip(1.0 + 0.1 * jax.random.normal(seeds[3], (D,), jnp.float32), 0.5, 1.5)
    w_query = gaussian(seeds[4], (D, H * HD), D ** -0.5, 0.15625, ((1, 2),))
    w_key = gaussian(seeds[5], (D, KVH * HD), D ** -0.5, 0.15625, ((1, 2),))
    w_value = gaussian(seeds[6], (D, KVH * HD), D ** -0.5, 0.15625, ((1, 2),))
    w_out = gaussian(seeds[7], (H * HD, D), (max(H * HD // 64, 1)) ** -0.5, 1.25, ((0, 2),))
    w_gate = gaussian(seeds[8], (EXP_SLOTS, D, FF_E), D ** -0.5, 0.15625, ((0, 64), (2, 2)))
    w_up = gaussian(seeds[9], (EXP_SLOTS, D, FF_E), D ** -0.5, 0.15625, ((0, 64), (2, 2)))
    w_down = gaussian(seeds[10], (EXP_SLOTS, FF_E, D), (FF_E // 16) ** -0.5, 1.0, ((0, 64), (1, 2)))
    route_ids_keys = jax.random.split(jax.random.fold_in(seeds[11], 1), TOKENS // TOK_DEV)
    route_ids_turns = jax.random.permutation(jax.random.fold_in(seeds[11], 3), TOKENS // TOK_DEV)
    route_ids = jax.vmap(lambda own, number: assign_block(jax.random.fold_in(seeds[11], 2), own, number, TOK_DEV, EXPERTS, TOP, CAP, 0))(route_ids_keys, route_ids_turns).reshape((TOKENS, TOP))
    route_logits = gaussian(seeds[12], (TOKENS, TOP), 0.5, 3.0, ((0, 64),), jnp.float32)
    seq_ids = jnp.searchsorted(jnp.cumsum(ragged(seeds[13], SEQS, TOKENS, LEN, 0)), jnp.arange(TOKENS), side="right").astype(jnp.int32)
    piece_ids = draw_piece_ids(jax.random.fold_in(seeds[16], 71), 0)
    clip_limit = jnp.clip(jnp.exp(math.log(9.0) - 1.0986123 * jax.random.uniform(seeds[15], (H,), jnp.float32) ** shard_levels(seeds[15], (H,), ((0, 2),), -0.2, 0.2)), 3.0, 9.0)
    return {"tokens": tokens, "out_grad": out_grad, "norm1_gain": norm1_gain, "norm2_gain": norm2_gain, "w_query": w_query, "w_key": w_key, "w_value": w_value, "w_out": w_out, "w_gate": w_gate, "w_up": w_up, "w_down": w_down, "route_ids": route_ids, "route_logits": route_logits, "seq_ids": seq_ids, "piece_ids": piece_ids, "clip_limit": clip_limit}


EPS = 1e-06
ROPE_BASE = 10000.0
NEG_FILL = -1e+30
HIGHEST = lax.Precision.HIGHEST

@jax.custom_vjp
def low(v):
    return lax.optimization_barrier(v.astype(jnp.bfloat16)).astype(jnp.float32)

@jax.custom_vjp
def low_back(v):
    return v

def low_keep(v):
    return (low(v), None)

def low_pass(kept, grad):
    return (grad,)

def back_keep(v):
    return (v, None)

def back_low(kept, grad):
    return (low(grad),)
low.defvjp(low_keep, low_pass)
low_back.defvjp(back_keep, back_low)

def matmul(left, right):
    return jnp.dot(left, right, precision=HIGHEST, preferred_element_type=jnp.float32)

def rope_tables(positions, head_width):
    half_width = head_width // 2
    frequency = jnp.exp(jnp.arange(half_width, dtype=jnp.float32) * (-2.0 * math.log(ROPE_BASE) / head_width))
    angles = positions.astype(jnp.float32)[:, None] * frequency[None, :]
    return (jnp.cos(angles), jnp.sin(angles))

def rotate(values, cosine, sine_tab):
    half_width = values.shape[-1] // 2
    first_half = values[..., :half_width]
    second = values[..., half_width:]
    cos_wide = cosine[:, None, :]
    sin_wide = sine_tab[:, None, :]
    return jnp.concatenate([first_half * cos_wide - second * sin_wide, second * cos_wide + first_half * sin_wide], axis=-1)

def rms_scale(values):
    return lax.rsqrt(lax.optimization_barrier(jnp.mean(values * values, axis=-1, keepdims=True)) + EPS)

def reference(tokens, out_grad, norm1_gain, norm2_gain, w_query, w_key, w_value, w_out, w_gate, w_up, w_down, route_ids, route_logits, seq_ids, piece_ids, clip_limit):
    group_size = H // KVH
    score_scale = float(HD) ** (-0.5)
    index_all = jnp.arange(TOKENS, dtype=jnp.int32)
    previous_ids = jnp.concatenate([seq_ids[:1] - 1, seq_ids[:-1]])
    seq_start = lax.cummax(jnp.where(seq_ids != previous_ids, index_all, 0), axis=0)
    cosine, sine_tab = rope_tables(index_all - seq_start, HD)
    seq_pad = jnp.concatenate([jnp.full((LEN,), -1, jnp.int32), seq_ids])
    piece_pad = jnp.concatenate([jnp.zeros((LEN,), jnp.int32), piece_ids])
    gate_exp = jnp.exp(route_logits - lax.optimization_barrier(jnp.max(route_logits, axis=-1, keepdims=True)))
    gates = gate_exp / lax.optimization_barrier(jnp.sum(gate_exp, axis=-1, keepdims=True))
    flat_expert = route_ids.reshape(-1)
    flat_token = jnp.arange(TOKENS * TOP, dtype=jnp.int32) // TOP
    onehot = (flat_expert[:, None] == jnp.arange(EXPERTS, dtype=jnp.int32)[None, :]).astype(jnp.int32)
    onehot = onehot.reshape(N_DP, TOK_DEV * TOP, EXPERTS)
    slot_rank = (lax.optimization_barrier(jnp.sum(jnp.cumsum(onehot, axis=1) * onehot, axis=2)) - 1).reshape(-1)
    slot_index = flat_token // TOK_DEV * CAP + slot_rank
    table_token = jnp.full((EXPERTS, N_DP * CAP), TOKENS, jnp.int32).at[flat_expert, slot_index].set(flat_token)
    table_gate = jnp.zeros((EXPERTS, N_DP * CAP), jnp.float32).at[flat_expert, slot_index].set(gates.reshape(-1))

    def forward(x_in, wq_in, wk_in, wv_in, wo_in, gain_one, gain_two, wg_in, wu_in, wd_in):
        normed1 = low(x_in * rms_scale(x_in) * gain_one)
        query_pre = low_back(matmul(normed1, wq_in)).reshape(TOKENS, H, HD)
        key_pre = low_back(matmul(normed1, wk_in)).reshape(TOKENS, KVH, HD)
        value_rows = low(low_back(matmul(normed1, wv_in))).reshape(TOKENS, KVH, HD)
        query_rot = low(rotate(query_pre, cosine, sine_tab))
        key_rot = low(rotate(key_pre, cosine, sine_tab))
        key_pad = jnp.concatenate([jnp.zeros((LEN, KVH, HD), jnp.float32), key_rot])
        value_pad = jnp.concatenate([jnp.zeros((LEN, KVH, HD), jnp.float32), value_rows])

        def attend_block(block_id):
            first_row = block_id * LEN
            query_block = lax.dynamic_slice_in_dim(query_rot, first_row, LEN, 0).reshape(LEN, KVH, group_size, HD)
            key_block = lax.dynamic_slice_in_dim(key_pad, first_row, 2 * LEN, 0)
            value_block = lax.dynamic_slice_in_dim(value_pad, first_row, 2 * LEN, 0)
            query_index = first_row + jnp.arange(LEN, dtype=jnp.int32)
            key_index = first_row - LEN + jnp.arange(2 * LEN, dtype=jnp.int32)
            start_block = lax.dynamic_slice_in_dim(seq_start, first_row, LEN, 0)
            seq_query = lax.dynamic_slice_in_dim(seq_ids, first_row, LEN, 0)
            piece_query = lax.dynamic_slice_in_dim(piece_ids, first_row, LEN, 0)
            seq_key = lax.dynamic_slice_in_dim(seq_pad, first_row, 2 * LEN, 0)
            piece_key = lax.dynamic_slice_in_dim(piece_pad, first_row, 2 * LEN, 0)
            same_piece = (piece_query[:, None] == piece_key[None, :]) & (piece_query[:, None] > 0) & (seq_query[:, None] == seq_key[None, :])
            allowed = (key_index[None, :] >= start_block[:, None]) & ((key_index[None, :] <= query_index[:, None]) | same_piece)
            raw_scores = jnp.einsum('qkgd,skd->kgqs', query_block, key_block, precision=HIGHEST) * score_scale
            scores = jnp.where(allowed[None, None], low_back(raw_scores), NEG_FILL)
            row_max = lax.optimization_barrier(jnp.max(scores, axis=-1, keepdims=True))
            exp_scores = jnp.exp(scores - row_max)
            probs = exp_scores / lax.optimization_barrier(jnp.sum(exp_scores, axis=-1, keepdims=True))
            attended = jnp.einsum('kgqs,skd->qkgd', low(probs), value_block, precision=HIGHEST).reshape(LEN, H * HD)
            return (attended, lax.optimization_barrier(jnp.max(row_max[..., 0], axis=-1)).reshape(H))
        block_out, block_peaks = lax.map(jax.checkpoint(attend_block), jnp.arange(TOKENS // LEN, dtype=jnp.int32))
        attended_low = low_back(low(block_out.reshape(TOKENS, H * HD)))
        hidden1 = x_in + low_back(matmul(attended_low, wo_in))
        normed2 = low(hidden1 * rms_scale(hidden1) * gain_two)
        norm_pad = jnp.concatenate([normed2, jnp.zeros((1, D), jnp.float32)])

        def expert_term(pieces):
            gate_w, up_w, down_w, token_idx, gate_val = pieces
            row_values = norm_pad[token_idx]
            gate_act = low_back(matmul(row_values, gate_w))
            up_act = low_back(matmul(row_values, up_w))
            inner_act = low(gate_act * jax.nn.sigmoid(gate_act) * up_act)
            expert_out = low_back(matmul(inner_act, down_w))
            return jnp.zeros((TOKENS + 1, D), jnp.float32).at[token_idx].add(expert_out * gate_val[:, None])

        def expert_step(accum, pieces):
            return (accum + jax.checkpoint(expert_term)(pieces), None)
        mixed, unused = lax.scan(expert_step, jnp.zeros((TOKENS + 1, D), jnp.float32), (wg_in, wu_in, wd_in, table_token, table_gate))
        return (hidden1 + mixed[:TOKENS], lax.optimization_barrier(jnp.max(block_peaks, axis=0)))
    primals = (tokens.astype(jnp.float32), w_query.astype(jnp.float32), w_key.astype(jnp.float32), w_value.astype(jnp.float32), w_out.astype(jnp.float32), norm1_gain.astype(jnp.float32), norm2_gain.astype(jnp.float32), w_gate[:EXPERTS].astype(jnp.float32), w_up[:EXPERTS].astype(jnp.float32), w_down[:EXPERTS].astype(jnp.float32))
    out_value, backward, head_peaks = jax.vjp(forward, *primals, has_aux=True)
    grads = backward(out_grad.astype(jnp.float32))
    spare = EXP_SLOTS - EXPERTS
    grad_gate = jnp.concatenate([grads[7], jnp.zeros((spare, D, FF_E), jnp.float32)])
    grad_up = jnp.concatenate([grads[8], jnp.zeros((spare, D, FF_E), jnp.float32)])
    grad_down = jnp.concatenate([grads[9], jnp.zeros((spare, FF_E, D), jnp.float32)])
    factor = clip_limit / jnp.maximum(head_peaks, clip_limit)
    key_factor = lax.optimization_barrier(jnp.min(factor.reshape(KVH, group_size), axis=1))
    clipped_query = (w_query.astype(jnp.float32) * jnp.repeat(jnp.sqrt(factor), HD)[None, :]).astype(jnp.bfloat16)
    clipped_key = (w_key.astype(jnp.float32) * jnp.repeat(jnp.sqrt(key_factor), HD)[None, :]).astype(jnp.bfloat16)
    return (out_value.astype(jnp.bfloat16), grads[0], grads[1], grads[2], grads[3], grads[4], grads[5], grads[6], grad_gate, grad_up, grad_down, clipped_query, clipped_key, head_peaks)
```

```python
import functools
import math

import jax
import jax.numpy as jnp
import numpy as np
from jax import lax
from jax.experimental import pallas as pl
from jax.experimental.pallas import tpu as pltpu
from jax.sharding import PartitionSpec as P

HD = 64
TOP = 8
CAP = 64
HOPS = 4
SLOTS = 64
AUX = 16

EPS = 1e-06
ROPE_BASE = 10000.0
NEG_FILL = -1e30
BF16 = jnp.bfloat16
F32 = jnp.float32


def contract(left, right, dims):
    return lax.dot_general(left, right, (dims, ((), ())), preferred_element_type=F32)


NN = ((1,), (0,))
NT = ((1,), (1,))
TN = ((0,), (0,))


def swapped(array):
    return lax.ppermute(array, "tensor", [(0, 1), (1, 0)])


def passed_along(value, steps):
    count = lax.axis_size("dp")
    first, last = (max(0, -steps), min(count, count - steps))
    return lax.ppermute(value, "dp", [(s, s + steps) for s in range(first, last)])


def to_all(array):
    return lax.all_to_all(array, "dp", 0, 0, tiled=True)


def rope_tables(count, dp_size):
    freq = np.exp(np.arange(HD // 2) * (-2.0 * math.log(ROPE_BASE) / HD))
    base = np.arange(dp_size)[:, None] * count * freq[None, :]
    local = freq[:, None] * np.arange(count)[None, :]
    index = lax.axis_index("dp")
    cos_base = jnp.asarray(np.cos(base), F32)[index][:, None]
    sin_base = jnp.asarray(np.sin(base), F32)[index][:, None]
    cos_local, sin_local = (jnp.asarray(np.cos(local), F32), jnp.asarray(np.sin(local), F32))
    return (
        cos_base * cos_local - sin_base * sin_local,
        sin_base * cos_local + cos_base * sin_local,
    )


def rotate(values, cosine, sine):
    half = HD // 2
    heads = values.reshape(-1, HD, values.shape[-1])
    first, second = (heads[:, :half], heads[:, half:])
    turned = jnp.concatenate(
        [first * cosine - second * sine, second * cosine + first * sine], axis=1
    )
    return turned.reshape(values.shape)


def fill_bias(blocks, bias):
    tok = bias.shape[1]
    rows = blocks[-1].shape[0] - AUX
    own = blocks[-1][rows:, :].astype(F32)
    seq_q, piece_q = (own[0:1, :], own[1:2, :])
    for number, block in enumerate(blocks):
        side = jnp.transpose(block[rows:, :].astype(F32))
        keep = side[:, 0:1] == seq_q
        if number == len(blocks) - 1:
            at_key = lax.broadcasted_iota(jnp.int32, (tok, tok), 0)
            at_query = lax.broadcasted_iota(jnp.int32, (tok, tok), 1)
            piece = (side[:, 1:2] == piece_q) & (piece_q > 0.0)
            keep = keep & ((at_key <= at_query) | piece)
        bias[number * tok : (number + 1) * tok, :] = jnp.where(keep, 0.0, NEG_FILL)


def all_keys(blocks, start):
    return jnp.concatenate([block[pl.ds(start, HD), :] for block in blocks], axis=1)


def attend_kernel(group, q_ref, k4, k3, k2, k1, k0, out_ref, log_ref, peak_ref, bias):
    blocks = (k4, k3, k2, k1, k0)
    fill_bias(blocks, bias)
    kv_rows = (k0.shape[0] - AUX) // 2

    def one_group(g, _):
        at = pl.multiple_of(g * HD, HD)
        keys = all_keys(blocks, at)
        values = all_keys(blocks, kv_rows + at)
        for j in range(group):
            head = g * group + j
            here = pl.ds(pl.multiple_of(head * HD, HD), HD)
            scores = contract(keys, q_ref[here, :], TN) + bias[...]
            peak = jnp.max(scores, axis=0, keepdims=True)
            weight = jnp.exp(scores - peak)
            total = jnp.sum(weight, axis=0, keepdims=True)
            mixed = contract(values, weight.astype(BF16), NN) * (1.0 / total)
            out_ref[here, :] = mixed.astype(BF16)
            log_ref[pl.ds(head, 1), :] = peak + jnp.log(total)
            peak_ref[pl.ds(head, 1), :] = peak
        return 0

    lax.fori_loop(0, kv_rows // HD, one_group, 0)


def attend(q, blocks, group):
    rows, tok = q.shape
    heads = rows // HD
    return pl.pallas_call(
        functools.partial(attend_kernel, group),
        out_shape=(
            jax.ShapeDtypeStruct((rows, tok), BF16),
            jax.ShapeDtypeStruct((heads, tok), F32),
            jax.ShapeDtypeStruct((heads, tok), F32),
        ),
        scratch_shapes=[pltpu.VMEM((len(blocks) * tok, tok), F32)],
        compiler_params=pltpu.CompilerParams(vmem_limit_bytes=48 << 20),
        cost_estimate=pl.CostEstimate(
            flops=4 * rows * tok * tok * len(blocks),
            bytes_accessed=4 * rows * tok + 2 * len(blocks) * 528 * tok,
            transcendentals=heads * tok * tok * len(blocks),
        ),
    )(q, *blocks)


def attend_back_kernel(
    group, q_ref, g_ref, log_ref, cos_ref, sin_ref, k4, k3, k2, k1, k0,
    dq_ref, d4, d3, d2, d1, d0, bias,
):
    blocks = (k4, k3, k2, k1, k0)
    grads = (d4, d3, d2, d1, d0)
    fill_bias(blocks, bias)
    kv_rows = (k0.shape[0] - AUX) // 2
    tok = bias.shape[1]
    half = HD // 2

    def one_group(g, _):
        at = pl.multiple_of(g * HD, HD)
        keys = all_keys(blocks, at)
        values = all_keys(blocks, kv_rows + at)
        key_sum = value_sum = None
        for j in range(group):
            head = g * group + j
            start = pl.multiple_of(head * HD, HD)
            query, grad = (q_ref[pl.ds(start, HD), :], g_ref[pl.ds(start, HD), :])
            scores = contract(keys, query, TN) + bias[...]
            probs = jnp.exp(scores - log_ref[pl.ds(head, 1), :])
            grad_probs = contract(values, grad, TN)
            delta = jnp.sum(probs * grad_probs, axis=0, keepdims=True)
            grad_scores = (probs * (grad_probs - delta)).astype(BF16)
            key_part = contract(query, grad_scores, NT)
            value_part = contract(grad, probs.astype(BF16), NT)
            key_sum = key_part if key_sum is None else key_sum + key_part
            value_sum = value_part if value_sum is None else value_sum + value_part
            turned = contract(keys, grad_scores, NN) * (HD**-0.5)
            first, second = (turned[:half], turned[half:])
            cosine, sine = (cos_ref[...], sin_ref[...])
            dq_ref[pl.ds(start, half), :] = (first * cosine + second * sine).astype(BF16)
            dq_ref[pl.ds(start + half, half), :] = (second * cosine - first * sine).astype(BF16)
        for number, grad_ref in enumerate(grads):
            piece = slice(number * tok, (number + 1) * tok)
            grad_ref[pl.ds(at, HD), :] = key_sum[:, piece].astype(grad_ref.dtype)
            grad_ref[pl.ds(kv_rows + at, HD), :] = value_sum[:, piece].astype(grad_ref.dtype)
        return 0

    lax.fori_loop(0, kv_rows // HD, one_group, 0)


def attend_back(q, grad, log_total, cosine, sine, blocks, group):
    rows, tok = q.shape
    kv = blocks[0].shape[0] - AUX
    return pl.pallas_call(
        functools.partial(attend_back_kernel, group),
        out_shape=(
            jax.ShapeDtypeStruct((rows, tok), BF16),
            *(jax.ShapeDtypeStruct((kv, tok), BF16) for _ in blocks[1:]),
            jax.ShapeDtypeStruct((kv, tok), F32),
        ),
        scratch_shapes=[pltpu.VMEM((len(blocks) * tok, tok), F32)],
        compiler_params=pltpu.CompilerParams(vmem_limit_bytes=48 << 20),
        cost_estimate=pl.CostEstimate(
            flops=10 * rows * tok * tok * len(blocks),
            bytes_accessed=6 * rows * tok + 4 * len(blocks) * 528 * tok,
            transcendentals=rows // HD * tok * tok * len(blocks),
        ),
    )(q, grad, log_total, cosine, sine, *blocks)


def expert_kernel(x_ref, g_ref, go, gp, uo, up, do, dp, dx_ref, *outs):
    rows, grads = (x_ref[...], g_ref[...])
    back = None
    for side, (gate_w, up_w, down_w) in enumerate(((go, uo, do), (gp, up, dp))):
        inner_ref, dgate_ref, dup_ref = outs[3 * side : 3 * side + 3]
        gate_act = contract(rows, gate_w[...], NN)
        up_act = contract(rows, up_w[...], NN)
        grad_inner = contract(grads, down_w[...], NT)
        sigmoid = 1.0 / (1.0 + jnp.exp(-gate_act))
        silu = gate_act * sigmoid
        inner_ref[...] = (silu * up_act).astype(BF16)
        dgate = (grad_inner * up_act * (sigmoid * (1.0 + gate_act * (1.0 - sigmoid)))).astype(BF16)
        dup = (grad_inner * silu).astype(BF16)
        dgate_ref[...] = dgate
        dup_ref[...] = dup
        part = contract(dgate, gate_w[...], NT) + contract(dup, up_w[...], NT)
        back = part if back is None else back + part
    dx_ref[...] = back.astype(BF16)


def experts(rows, grads, own, peer):
    count, width = rows.shape
    hidden = own[0].shape[1]
    tile = 256
    wide = pl.BlockSpec((tile, width), lambda i: (i, 0))
    thin = pl.BlockSpec((tile, hidden), lambda i: (i, 0))
    into = pl.BlockSpec((width, hidden), lambda i: (0, 0))
    out_of = pl.BlockSpec((hidden, width), lambda i: (0, 0))
    return pl.pallas_call(
        expert_kernel,
        grid=(count // tile,),
        in_specs=[wide, wide, into, into, into, into, out_of, out_of],
        out_specs=[wide] + [thin] * 6,
        out_shape=[jax.ShapeDtypeStruct((count, width), BF16)]
        + [jax.ShapeDtypeStruct((count, hidden), BF16)] * 6,
        compiler_params=pltpu.CompilerParams(vmem_limit_bytes=48 << 20),
        cost_estimate=pl.CostEstimate(
            flops=20 * count * width * hidden,
            bytes_accessed=6 * count * width + 12 * count * hidden + 12 * width * hidden,
            transcendentals=2 * count * hidden,
        ),
    )(rows, grads, own[0], peer[0], own[1], peer[1], own[2], peer[2])


def rms_scale(values):
    return lax.rsqrt(jnp.mean(values * values, axis=-1, keepdims=True) + EPS)


def norm_back(grad_normed, hidden, inverse, gain):
    weighted = grad_normed * gain
    grad_gain = jnp.sum(grad_normed * hidden * inverse, axis=0)
    grad_hidden = inverse * weighted - hidden * inverse**3 * jnp.mean(
        weighted * hidden, axis=-1, keepdims=True
    )
    return (grad_hidden, grad_gain)


def shards(
    tokens,
    out_grad,
    norm1_gain,
    norm2_gain,
    w_query,
    w_key,
    w_value,
    w_out,
    w_gate,
    w_up,
    w_down,
    route_ids,
    route_logits,
    seq_ids,
    piece_ids,
    clip_limit,
):
    tok_dev, model_width = tokens.shape
    dp_size = lax.axis_size("dp")
    tensor_size = lax.axis_size("tensor")
    core = lax.axis_index("tensor")
    local_heads = w_query.shape[1] // HD
    local_kv = w_key.shape[1] // HD
    group = local_heads // local_kv
    rank_rows = CAP // tensor_size
    own = (w_gate[0], w_up[0], w_down[0])
    peer = tuple(swapped(w) for w in own)

    picks = route_ids.T
    logits = route_logits.T
    gate_exp = jnp.exp(logits - jnp.max(logits, axis=0, keepdims=True))
    gates = gate_exp / jnp.sum(gate_exp, axis=0, keepdims=True)
    same = picks[None] == jnp.arange(SLOTS, dtype=jnp.int32)[:, None, None]
    member = jnp.any(same, axis=1)
    gate_of = jnp.sum(jnp.where(same, gates[None], 0.0), axis=1)
    place = jnp.arange(tok_dev, dtype=jnp.int32)
    before = (place[:, None] < place[None, :]).astype(BF16)
    rank = contract(member.astype(BF16), before, NN)
    rank = jnp.where(member, rank, -1.0)
    wanted = (tensor_size * jnp.arange(rank_rows, dtype=jnp.int32) + core).astype(F32)
    chosen = rank[:, None, :] == wanted[None, :, None]
    pick = chosen.astype(BF16).reshape(-1, tok_dev)
    gated = jnp.where(chosen, gate_of[:, None, :], 0.0)
    slot_gate = jnp.sum(gated, axis=2).reshape(-1, 1)
    gated = gated.astype(BF16).reshape(-1, tok_dev)

    def to_owners(rows):
        return to_all(rows.reshape(dp_size, rank_rows, model_width)).reshape(-1, model_width)

    grad_rows = to_owners((contract(pick, out_grad, NN) * slot_gate).astype(BF16))

    cosine, sine = rope_tables(tok_dev, dp_size)
    x_float = tokens.astype(F32)
    inverse1 = rms_scale(x_float)
    normed1 = (x_float * inverse1 * norm1_gain).astype(BF16)
    query = rotate(contract(w_query, normed1, ((0,), (1,))), cosine, sine)
    query = (query * (HD**-0.5)).astype(BF16)
    key = rotate(contract(w_key, normed1, ((0,), (1,))), cosine, sine).astype(BF16)
    value = contract(w_value, normed1, ((0,), (1,))).astype(BF16)
    side = jnp.concatenate(
        [(seq_ids + 1)[None], piece_ids[None], jnp.zeros((AUX - 2, tok_dev), jnp.int32)]
    ).astype(BF16)
    block = jnp.concatenate([key, value, side])
    blocks = tuple(passed_along(block, hop) for hop in range(HOPS, 0, -1)) + (block,)
    attended, log_total, peaks = attend(query, blocks, group)
    attn_part = contract(attended, w_out, TN)
    hidden1 = x_float + (attn_part + swapped(attn_part))
    inverse2 = rms_scale(hidden1)
    normed2 = (hidden1 * inverse2 * norm2_gain).astype(BF16)

    rows_in = to_owners(contract(pick, normed2, NN).astype(BF16))
    back, *acts = experts(rows_in, grad_rows, own, peer)

    def from_owners(rows):
        return to_all(rows.reshape(dp_size, rank_rows, model_width)).reshape(-1, model_width)

    def combined(weights, rows):
        part = contract(weights, from_owners(rows), TN).astype(BF16)
        return part.astype(F32) + swapped(part).astype(F32)

    grad_normed2 = combined(pick, back)
    inner, dgate, dup, inner_peer, dgate_peer, dup_peer = acts
    expert_out = (contract(inner, own[2], NN) + contract(inner_peer, peer[2], NN)).astype(BF16)
    grad_gate = contract(rows_in, dgate, TN) + swapped(
        contract(rows_in, dgate_peer, TN).astype(BF16)
    ).astype(F32)
    grad_up = contract(rows_in, dup, TN) + swapped(
        contract(rows_in, dup_peer, TN).astype(BF16)
    ).astype(F32)
    grad_down = contract(inner, grad_rows, TN) + swapped(
        contract(inner_peer, grad_rows, TN).astype(BF16)
    ).astype(F32)

    grad_top = out_grad.astype(F32)
    grad_from_norm2, grad_gain2 = norm_back(grad_normed2, hidden1, inverse2, norm2_gain)
    grad_hidden1 = grad_top + grad_from_norm2
    grad_branch = grad_hidden1.astype(BF16)
    grad_attended = contract(w_out, grad_branch, NT).astype(BF16)
    grad_query_pre, *grad_blocks = attend_back(
        query, grad_attended, log_total, cosine, sine, blocks, group
    )
    kv_total = grad_blocks[-1]
    for number, hop in enumerate(range(HOPS, 0, -1)):
        kv_total = kv_total + passed_along(grad_blocks[number], -hop).astype(F32)
    output = (hidden1 + combined(gated, expert_out)).astype(BF16)
    kv_rows = local_kv * HD
    grad_key_pre = rotate(kv_total[:kv_rows], cosine, -sine).astype(BF16)
    grad_value = kv_total[kv_rows:].astype(BF16)

    half = model_width // 2
    grad_wo = jnp.concatenate(
        [contract(attended, grad_branch[:, :half], NN), contract(attended, grad_branch[:, half:], NN)]
    )
    grad_wq = contract(normed1, grad_query_pre, ((0,), (1,)))
    grad_wk = contract(normed1, grad_key_pre, ((0,), (1,)))
    grad_wv = contract(normed1, grad_value, ((0,), (1,)))
    grad_norm1_part = (
        contract(grad_query_pre, w_query, ((0,), (1,)))
        + contract(grad_key_pre, w_key, ((0,), (1,)))
        + contract(grad_value, w_value, ((0,), (1,)))
    ).astype(BF16)

    def share(part):
        return jnp.sum(to_all(part.astype(BF16).reshape(dp_size, -1, part.shape[1])).astype(F32), axis=0)

    share_wo = share(grad_wo)
    share_wq = share(grad_wq)
    share_wkv = share(jnp.concatenate([grad_wk, grad_wv], axis=1))
    grad_normed1 = grad_norm1_part.astype(F32) + swapped(grad_norm1_part).astype(F32)
    grad_from_norm1, grad_gain1 = norm_back(grad_normed1, x_float, inverse1, norm1_gain)
    input_grad = grad_hidden1 + grad_from_norm1
    width = w_query.shape[1]
    peak = jnp.max(peaks, axis=1)
    peak_high = peak.astype(BF16)
    peak_low = (peak - peak_high.astype(F32)).astype(BF16)
    peak_row = jnp.pad(jnp.concatenate([peak_high, peak_low]), (0, width - 2 * local_heads))
    lines = [
        share_wo.astype(BF16),
        share_wq.astype(BF16),
        share_wkv.astype(BF16).reshape(-1, width),
        grad_gain1.astype(BF16).reshape(-1, width),
        grad_gain2.astype(BF16).reshape(-1, width),
        peak_row[None],
    ]
    counts = [len(line) for line in lines]
    packed = jnp.concatenate(lines)
    packed = jnp.pad(packed, ((0, -len(packed) % 8), (0, 0)))
    gathered = lax.all_gather(packed, "dp", axis=0)
    pieces, at = [], 0
    for count in counts:
        pieces.append(gathered[:, at : at + count].astype(F32))
        at += count
    grad_wo = pieces[0].reshape(-1, width)
    grad_wo = jnp.concatenate([grad_wo[: len(grad_wo) // 2], grad_wo[len(grad_wo) // 2 :]], axis=1)
    grad_wq = pieces[1].reshape(-1, width)
    grad_wkv = pieces[2].reshape(model_width, -1)
    grad_gain1 = jnp.sum(pieces[3], axis=0).reshape(-1)
    grad_gain2 = jnp.sum(pieces[4], axis=0).reshape(-1)
    all_peaks = pieces[5][:, 0]
    head_peaks = jnp.max(
        all_peaks[:, :local_heads] + all_peaks[:, local_heads : 2 * local_heads], axis=0
    )
    factor = clip_limit / jnp.maximum(head_peaks, clip_limit)
    key_factor = jnp.min(factor.reshape(local_kv, group), axis=1)
    clipped_query = (w_query.astype(F32) * jnp.repeat(jnp.sqrt(factor), HD)[None, :]).astype(BF16)
    clipped_key = (w_key.astype(F32) * jnp.repeat(jnp.sqrt(key_factor), HD)[None, :]).astype(BF16)
    return (
        output,
        input_grad,
        grad_wq,
        grad_wkv[:, :kv_rows],
        grad_wkv[:, kv_rows:],
        grad_wo,
        grad_gain1,
        grad_gain2,
        grad_gate[None],
        grad_up[None],
        grad_down[None],
        clipped_query,
        clipped_key,
        head_peaks,
    )


def solution(mesh):
    in_specs = (
        P("dp", None),
        P("dp", None),
        P(),
        P(),
        P(None, "tensor"),
        P(None, "tensor"),
        P(None, "tensor"),
        P("tensor", None),
        P("dp", None, "tensor"),
        P("dp", None, "tensor"),
        P("dp", "tensor", None),
        P("dp", None),
        P("dp", None),
        P("dp"),
        P("dp"),
        P("tensor"),
    )
    out_specs = (
        P("dp", None),
        P("dp", None),
        P(None, "tensor"),
        P(None, "tensor"),
        P(None, "tensor"),
        P("tensor", None),
        P(),
        P(),
        P("dp", None, "tensor"),
        P("dp", None, "tensor"),
        P("dp", "tensor", None),
        P(None, "tensor"),
        P(None, "tensor"),
        P("tensor"),
    )
    return jax.shard_map(shards, mesh=mesh, in_specs=in_specs, out_specs=out_specs, check_vma=False)
```

```python
import functools
import math

import jax
import jax.numpy as jnp
import numpy as np
from jax import lax
from jax.experimental import pallas as pl
from jax.experimental.pallas import tpu as pltpu
from jax.sharding import PartitionSpec as P

HD = 64
TOP = 8
CAP = 64
HOPS = 4
RANK_ROWS = 32
PLANE = 16
SEGMENTS = 3
AUX = 16

EPS = 1e-06
ROPE_BASE = 10000.0
NEG_FILL = -1e30
BF16 = jnp.bfloat16
F32 = jnp.float32


def contract(left, right, dims):
    return lax.dot_general(left, right, (dims, ((), ())), preferred_element_type=F32)


NN = ((1,), (0,))
NT = ((1,), (1,))
TN = ((0,), (0,))


def swapped(array):
    return lax.ppermute(array, "tensor", [(0, 1), (1, 0)])


def after(array, other):
    return lax.optimization_barrier((array, other))[0]


def passed_along(value, steps):
    count = lax.axis_size("dp")
    first, last = (max(0, -steps), min(count, count - steps))
    return lax.ppermute(value, "dp", [(s, s + steps) for s in range(first, last)])


def to_all(array):
    return lax.all_to_all(array, "dp", 0, 0, tiled=True)


def rope_tables(count, dp_size):
    freq = np.exp(np.arange(HD // 2) * (-2.0 * math.log(ROPE_BASE) / HD))
    base = np.arange(dp_size)[:, None] * count * freq[None, :]
    local = freq[:, None] * np.arange(count)[None, :]
    index = lax.axis_index("dp")
    cos_base = jnp.asarray(np.cos(base), F32)[index][:, None]
    sin_base = jnp.asarray(np.sin(base), F32)[index][:, None]
    cos_local, sin_local = (jnp.asarray(np.cos(local), F32), jnp.asarray(np.sin(local), F32))
    return (
        cos_base * cos_local - sin_base * sin_local,
        sin_base * cos_local + cos_base * sin_local,
    )


def rotate(values, cosine, sine):
    half = HD // 2
    heads = values.reshape(-1, HD, values.shape[-1])
    first, second = (heads[:, :half], heads[:, half:])
    turned = jnp.concatenate(
        [first * cosine - second * sine, second * cosine + first * sine], axis=1
    )
    return turned.reshape(values.shape)


def fill_bias(blocks, bias):
    tok = bias.shape[1]
    rows = blocks[-1].shape[0] - AUX
    own = blocks[-1][rows:, :].astype(F32)
    seq_q, piece_q = (own[0:1, :], own[1:2, :])
    for number, block in enumerate(blocks):
        side = jnp.transpose(block[rows:, :].astype(F32))
        keep = side[:, 0:1] == seq_q
        if number == len(blocks) - 1:
            at_key = lax.broadcasted_iota(jnp.int32, (tok, tok), 0)
            at_query = lax.broadcasted_iota(jnp.int32, (tok, tok), 1)
            piece = (side[:, 1:2] == piece_q) & (piece_q > 0.0)
            keep = keep & ((at_key <= at_query) | piece)
        bias[number * tok : (number + 1) * tok, :] = jnp.where(keep, 0.0, NEG_FILL)


def all_keys(blocks, start):
    return jnp.concatenate([block[pl.ds(start, HD), :] for block in blocks], axis=1)


def attend_kernel(group, q_ref, k4, k3, k2, k1, k0, out_ref, log_ref, peak_ref, bias):
    blocks = (k4, k3, k2, k1, k0)
    fill_bias(blocks, bias)
    kv_rows = (k0.shape[0] - AUX) // 2

    def one_group(g, _):
        at = pl.multiple_of(g * HD, HD)
        keys = all_keys(blocks, at)
        values = all_keys(blocks, kv_rows + at)
        for j in range(group):
            head = g * group + j
            here = pl.ds(pl.multiple_of(head * HD, HD), HD)
            scores = contract(keys, q_ref[here, :], TN) + bias[...]
            peak = jnp.max(scores, axis=0, keepdims=True)
            weight = jnp.exp(scores - peak)
            total = jnp.sum(weight, axis=0, keepdims=True)
            mixed = contract(values, weight.astype(BF16), NN) * (1.0 / total)
            out_ref[here, :] = mixed.astype(BF16)
            log_ref[pl.ds(head, 1), :] = peak + jnp.log(total)
            peak_ref[pl.ds(head, 1), :] = peak
        return 0

    lax.fori_loop(0, kv_rows // HD, one_group, 0)


def attend(q, blocks, group):
    rows, tok = q.shape
    heads = rows // HD
    return pl.pallas_call(
        functools.partial(attend_kernel, group),
        out_shape=(
            jax.ShapeDtypeStruct((rows, tok), BF16),
            jax.ShapeDtypeStruct((heads, tok), F32),
            jax.ShapeDtypeStruct((heads, tok), F32),
        ),
        scratch_shapes=[pltpu.VMEM((len(blocks) * tok, tok), F32)],
        compiler_params=pltpu.CompilerParams(vmem_limit_bytes=48 << 20),
        cost_estimate=pl.CostEstimate(
            flops=4 * rows * tok * tok * len(blocks),
            bytes_accessed=4 * rows * tok + 2 * len(blocks) * 528 * tok,
            transcendentals=heads * tok * tok * len(blocks),
        ),
    )(q, *blocks)


def attend_back_kernel(
    group, q_ref, g_ref, log_ref, cos_ref, sin_ref, k4, k3, k2, k1, k0,
    dq_ref, d4, d3, d2, d1, d0, bias,
):
    blocks = (k4, k3, k2, k1, k0)
    grads = (d4, d3, d2, d1, d0)
    fill_bias(blocks, bias)
    kv_rows = (k0.shape[0] - AUX) // 2
    tok = bias.shape[1]
    half = HD // 2

    def one_group(g, _):
        at = pl.multiple_of(g * HD, HD)
        keys = all_keys(blocks, at)
        values = all_keys(blocks, kv_rows + at)
        key_sum = value_sum = None
        for j in range(group):
            head = g * group + j
            start = pl.multiple_of(head * HD, HD)
            query, grad = (q_ref[pl.ds(start, HD), :], g_ref[pl.ds(start, HD), :])
            scores = contract(keys, query, TN) + bias[...]
            probs = jnp.exp(scores - log_ref[pl.ds(head, 1), :])
            grad_probs = contract(values, grad, TN)
            delta = jnp.sum(probs * grad_probs, axis=0, keepdims=True)
            grad_scores = (probs * (grad_probs - delta)).astype(BF16)
            key_part = contract(query, grad_scores, NT)
            value_part = contract(grad, probs.astype(BF16), NT)
            key_sum = key_part if key_sum is None else key_sum + key_part
            value_sum = value_part if value_sum is None else value_sum + value_part
            turned = contract(keys, grad_scores, NN) * (HD**-0.5)
            first, second = (turned[:half], turned[half:])
            cosine, sine = (cos_ref[...], sin_ref[...])
            dq_ref[pl.ds(start, half), :] = (first * cosine + second * sine).astype(BF16)
            dq_ref[pl.ds(start + half, half), :] = (second * cosine - first * sine).astype(BF16)
        for number, grad_ref in enumerate(grads):
            piece = slice(number * tok, (number + 1) * tok)
            grad_ref[pl.ds(at, HD), :] = key_sum[:, piece].astype(grad_ref.dtype)
            grad_ref[pl.ds(kv_rows + at, HD), :] = value_sum[:, piece].astype(grad_ref.dtype)
        return 0

    lax.fori_loop(0, kv_rows // HD, one_group, 0)


def attend_back(q, grad, log_total, cosine, sine, blocks, group):
    rows, tok = q.shape
    kv = blocks[0].shape[0] - AUX
    return pl.pallas_call(
        functools.partial(attend_back_kernel, group),
        out_shape=(
            jax.ShapeDtypeStruct((rows, tok), BF16),
            *(jax.ShapeDtypeStruct((kv, tok), BF16) for _ in blocks[1:]),
            jax.ShapeDtypeStruct((kv, tok), F32),
        ),
        scratch_shapes=[pltpu.VMEM((len(blocks) * tok, tok), F32)],
        compiler_params=pltpu.CompilerParams(vmem_limit_bytes=48 << 20),
        cost_estimate=pl.CostEstimate(
            flops=1000 * rows * tok * tok * len(blocks),
            bytes_accessed=6 * rows * tok + 4 * len(blocks) * 528 * tok,
            transcendentals=rows // HD * tok * tok * len(blocks),
        ),
    )(q, grad, log_total, cosine, sine, *blocks)


def expert_kernel(x_ref, g_ref, own_ref, peer_ref, dx_ref, inner_ref, acts_ref):
    width = x_ref.shape[-1]
    rows, grads = (x_ref[...].reshape(-1, width), g_ref[...].reshape(-1, width))
    hidden = own_ref.shape[-1]
    back = None
    for side, weights in enumerate((own_ref, peer_ref)):
        gate_w, up_w, down_w = (weights[0, 0], weights[0, 1], weights[0, 2])
        gate_act = contract(rows, gate_w, NN)
        up_act = contract(rows, up_w, NN)
        grad_inner = contract(grads, down_w, NN)
        sigmoid = 1.0 / (1.0 + jnp.exp(-gate_act))
        silu = gate_act * sigmoid
        dgate = (grad_inner * up_act * (sigmoid * (1.0 + gate_act * (1.0 - sigmoid)))).astype(BF16)
        dup = (grad_inner * silu).astype(BF16)
        at = side * hidden
        inner_ref[0, :, at : at + hidden] = (silu * up_act).astype(BF16)
        acts_ref[0, :, at : at + hidden] = dgate
        acts_ref[0, :, (2 * hidden + at) : (3 * hidden + at)] = dup
        part = contract(dgate, gate_w, NT) + contract(dup, up_w, NT)
        back = part if back is None else back + part
    dx_ref[...] = back.astype(BF16).reshape(dx_ref.shape)


def expert_back(rows, grads, own, peer):
    sources, lines, width = rows.shape
    segments, hidden = (lines // RANK_ROWS, own.shape[-1])
    count = sources * RANK_ROWS
    wide = pl.BlockSpec((sources, RANK_ROWS, width), lambda s: (0, s, 0))
    weight = pl.BlockSpec((1, 3, width, hidden), lambda s: (s, 0, 0, 0))
    flops = 20 * sources * lines * width * hidden
    return pl.pallas_call(
        expert_kernel,
        grid=(segments,),
        in_specs=[wide, wide, weight, weight],
        out_specs=[
            wide,
            pl.BlockSpec((1, count, 2 * hidden), lambda s: (s, 0, 0)),
            pl.BlockSpec((1, count, 4 * hidden), lambda s: (s, 0, 0)),
        ],
        out_shape=[
            jax.ShapeDtypeStruct(rows.shape, BF16),
            jax.ShapeDtypeStruct((segments, count, 2 * hidden), BF16),
            jax.ShapeDtypeStruct((segments, count, 4 * hidden), BF16),
        ],
        compiler_params=pltpu.CompilerParams(vmem_limit_bytes=56 << 20),
        cost_estimate=pl.CostEstimate(
            flops=flops,
            bytes_accessed=6 * sources * lines * width + 12 * segments * width * hidden,
            transcendentals=2 * sources * lines * hidden,
        ),
    )(rows, grads, own, peer)


def expert_sums_kernel(x_ref, g_ref, inner_ref, acts_ref, own_ref, peer_ref, sum_own, sum_peer, out_ref):
    width = x_ref.shape[-1]
    rows, grads = (x_ref[...].reshape(-1, width), g_ref[...].reshape(-1, width))
    hidden = own_ref.shape[-1]
    inner = inner_ref[0]
    sums = contract(rows, acts_ref[0], TN).astype(BF16)
    down = contract(grads, inner, TN).astype(BF16)
    for side, target in enumerate((sum_own, sum_peer)):
        at = side * hidden
        target[0, 0] = sums[:, at : at + hidden]
        target[0, 1] = sums[:, (2 * hidden + at) : (3 * hidden + at)]
        target[0, 2] = down[:, at : at + hidden]
    out = contract(inner[:, :hidden], own_ref[0, 0], NT)
    out = out + contract(inner[:, hidden:], peer_ref[0, 0], NT)
    out_ref[...] = out.astype(BF16).reshape(out_ref.shape)


def expert_sums(rows, grads, inner, acts, own, peer):
    sources, lines, width = rows.shape
    segments, hidden = (lines // RANK_ROWS, own.shape[-1])
    count = sources * RANK_ROWS
    wide = pl.BlockSpec((sources, RANK_ROWS, width), lambda s: (0, s, 0))
    down = pl.BlockSpec((1, 1, width, hidden), lambda s: (s, 2, 0, 0))
    total = pl.BlockSpec((1, 3, width, hidden), lambda s: (s, 0, 0, 0))
    return pl.pallas_call(
        expert_sums_kernel,
        grid=(segments,),
        in_specs=[
            wide,
            wide,
            pl.BlockSpec((1, count, 2 * hidden), lambda s: (s, 0, 0)),
            pl.BlockSpec((1, count, 4 * hidden), lambda s: (s, 0, 0)),
            down,
            down,
        ],
        out_specs=[total, total, wide],
        out_shape=[
            jax.ShapeDtypeStruct((segments, 3, width, hidden), BF16),
            jax.ShapeDtypeStruct((segments, 3, width, hidden), BF16),
            jax.ShapeDtypeStruct(rows.shape, BF16),
        ],
        compiler_params=pltpu.CompilerParams(vmem_limit_bytes=60 << 20),
        cost_estimate=pl.CostEstimate(
            flops=16 * sources * lines * width * hidden,
            bytes_accessed=6 * sources * lines * width + 16 * segments * width * hidden,
            transcendentals=0,
        ),
    )(rows, grads, inner, acts, own, peer)


def both_cores_kernel(own_ref, peer_ref, out_ref):
    @pl.when(pl.program_id(0) < SEGMENTS)
    def _():
        out_ref[...] = (own_ref[...].astype(F32) + peer_ref[...].astype(F32)).astype(BF16)

    @pl.when(pl.program_id(0) >= SEGMENTS)
    def _():
        out_ref[...] = jnp.zeros_like(out_ref)


def both_cores(own, peer, slots):
    segments, kinds, width, hidden = own.shape
    shape = (1, 1, width, hidden)
    part = pl.BlockSpec(shape, lambda s, k: (jnp.minimum(s, segments - 1), k, 0, 0))
    return pl.pallas_call(
        both_cores_kernel,
        grid=(slots, kinds),
        in_specs=[part, part],
        out_specs=pl.BlockSpec(shape, lambda s, k: (s, k, 0, 0)),
        out_shape=jax.ShapeDtypeStruct((slots, kinds, width, hidden), BF16),
        cost_estimate=pl.CostEstimate(
            flops=slots * kinds * width * hidden,
            bytes_accessed=6 * slots * kinds * width * hidden,
            transcendentals=0,
        ),
    )(own, peer)


def unpack_kernel(in_ref, wo_ref, wq_ref, wk_ref, wv_ref, sum_ref):
    step = pl.program_id(0)
    chunks, lines, width = in_ref.shape
    third = lines // 3
    narrow = wk_ref.shape[1]
    for c in range(chunks):
        here = slice(c * third, (c + 1) * third)
        wo_ref[here, :] = in_ref[c, :third, :].astype(F32)
        wq_ref[here, :] = in_ref[c, third : 2 * third, :].astype(F32)
        wk_ref[here, :] = in_ref[c, 2 * third :, :narrow].astype(F32)
        wv_ref[here, :] = in_ref[c, 2 * third :, narrow : 2 * narrow].astype(F32)
    more = in_ref[:, 2 * third :, 2 * narrow :].astype(F32)
    total = jnp.sum(more, axis=0)

    @pl.when(step == 0)
    def _():
        sum_ref[...] = total

    @pl.when(step > 0)
    def _():
        sum_ref[...] = sum_ref[...] + total


def unpack(gathered, narrow):
    parts, lines, width = gathered.shape
    steps = 16
    per, third = (parts // steps, lines // 3)
    rows = per * third
    total = parts * third
    extra = (third, width - 2 * narrow)
    return pl.pallas_call(
        unpack_kernel,
        grid=(steps,),
        in_specs=[pl.BlockSpec((per, lines, width), lambda i: (i, 0, 0))],
        out_specs=[
            pl.BlockSpec((rows, width), lambda i: (i % (steps // 2), i // (steps // 2))),
            pl.BlockSpec((rows, width), lambda i: (i, 0)),
            pl.BlockSpec((rows, narrow), lambda i: (i, 0)),
            pl.BlockSpec((rows, narrow), lambda i: (i, 0)),
            pl.BlockSpec(extra, lambda i: (0, 0)),
        ],
        out_shape=[
            jax.ShapeDtypeStruct((total // 2, 2 * width), F32),
            jax.ShapeDtypeStruct((total, width), F32),
            jax.ShapeDtypeStruct((total, narrow), F32),
            jax.ShapeDtypeStruct((total, narrow), F32),
            jax.ShapeDtypeStruct(extra, F32),
        ],
        compiler_params=pltpu.CompilerParams(vmem_limit_bytes=32 << 20),
        cost_estimate=pl.CostEstimate(
            flops=parts * lines * width, bytes_accessed=6 * parts * lines * width, transcendentals=0
        ),
    )(gathered)


def rms_scale(values):
    return lax.rsqrt(jnp.mean(values * values, axis=-1, keepdims=True) + EPS)


def norm_back(grad_normed, hidden, inverse, gain):
    weighted = grad_normed * gain
    grad_gain = jnp.sum(grad_normed * hidden * inverse, axis=0)
    grad_hidden = inverse * weighted - hidden * inverse**3 * jnp.mean(
        weighted * hidden, axis=-1, keepdims=True
    )
    return (grad_hidden, grad_gain)


def shards(
    tokens,
    out_grad,
    norm1_gain,
    norm2_gain,
    w_query,
    w_key,
    w_value,
    w_out,
    w_gate,
    w_up,
    w_down,
    route_ids,
    route_logits,
    seq_ids,
    piece_ids,
    clip_limit,
):
    tok_dev, model_width = tokens.shape
    dp_size = lax.axis_size("dp")
    tensor_size = lax.axis_size("tensor")
    core = lax.axis_index("tensor")
    local_heads = w_query.shape[1] // HD
    local_kv = w_key.shape[1] // HD
    group = local_heads // local_kv
    plane_groups = [list(range(at, at + PLANE)) for at in range(0, dp_size, PLANE)]
    column_groups = [list(range(at, dp_size, PLANE)) for at in range(PLANE)]

    packed_w = jnp.stack([w_gate[0], w_up[0], w_down[0].T])
    own = lax.all_gather(packed_w, "dp", axis=0, axis_index_groups=column_groups)

    picks = route_ids.T
    logits = route_logits.T
    gate_exp = jnp.exp(logits - jnp.max(logits, axis=0, keepdims=True))
    gates = gate_exp / jnp.sum(gate_exp, axis=0, keepdims=True)
    number = jnp.arange(PLANE * SEGMENTS, dtype=jnp.int32)
    number = number % SEGMENTS * PLANE + number // SEGMENTS
    same = picks[None] == number[:, None, None]
    member = jnp.any(same, axis=1)
    gate_of = jnp.sum(jnp.where(same, gates[None], 0.0), axis=1)
    place = jnp.arange(tok_dev, dtype=jnp.int32)
    before = (place[:, None] < place[None, :]).astype(BF16)
    rank = contract(member.astype(BF16), before, NN)
    rank = jnp.where(member, rank, -1.0)
    wanted = (tensor_size * jnp.arange(RANK_ROWS, dtype=jnp.int32) + core).astype(F32)
    chosen = rank[:, None, :] == wanted[None, :, None]
    pick = chosen.astype(BF16).reshape(-1, tok_dev)
    gated = jnp.where(chosen, gate_of[:, None, :], 0.0)
    slot_gate = jnp.sum(gated, axis=2).reshape(-1, 1)
    gated = gated.astype(BF16).reshape(-1, tok_dev)

    def in_plane(rows):
        rows = rows.reshape(PLANE, -1, model_width)
        return lax.all_to_all(rows, "dp", 0, 0, tiled=True, axis_index_groups=plane_groups)

    grad_rows = (contract(pick, out_grad, NN) * slot_gate).astype(BF16)

    cosine, sine = rope_tables(tok_dev, dp_size)
    x_float = tokens.astype(F32)
    inverse1 = rms_scale(x_float)
    normed1 = (x_float * inverse1 * norm1_gain).astype(BF16)
    query = rotate(contract(w_query, normed1, ((0,), (1,))), cosine, sine)
    query = (query * (HD**-0.5)).astype(BF16)
    key = rotate(contract(w_key, normed1, ((0,), (1,))), cosine, sine).astype(BF16)
    value = contract(w_value, normed1, ((0,), (1,))).astype(BF16)
    side = jnp.concatenate(
        [(seq_ids + 1)[None], piece_ids[None], jnp.zeros((AUX - 2, tok_dev), jnp.int32)]
    ).astype(BF16)
    block = jnp.concatenate([key, value, side])
    blocks = tuple(passed_along(block, hop) for hop in range(HOPS, 0, -1)) + (block,)
    blocks, grad_rows = lax.optimization_barrier((blocks, grad_rows))
    grad_rows = in_plane(grad_rows)
    attended, log_total, peaks = attend(query, blocks, group)
    attn_part = contract(attended, w_out, TN)
    hidden1 = x_float + (attn_part + swapped(attn_part))
    inverse2 = rms_scale(hidden1)
    normed2 = (hidden1 * inverse2 * norm2_gain).astype(BF16)

    rows_out = contract(pick, normed2, NN).astype(BF16)
    rows_out = after(rows_out, grad_rows)
    own = after(own, rows_out)
    peer = swapped(own)
    rows_in = in_plane(rows_out)
    back, inner, acts = expert_back(rows_in, grad_rows, own, peer)

    def combined(weights, rows):
        part = contract(weights, rows.reshape(-1, model_width), TN).astype(BF16)
        return part.astype(F32) + swapped(part).astype(F32)

    sum_own, sum_peer, expert_out = expert_sums(rows_in, grad_rows, inner, acts, own, peer)
    sums = both_cores(sum_own, swapped(sum_peer), dp_size // PLANE)
    grad_normed2 = combined(pick, after(in_plane(back), sum_own))
    sums = lax.psum_scatter(
        sums, "dp", scatter_dimension=0, tiled=True, axis_index_groups=column_groups
    )

    grad_top = out_grad.astype(F32)
    grad_from_norm2, grad_gain2 = norm_back(grad_normed2, hidden1, inverse2, norm2_gain)
    grad_hidden1 = grad_top + grad_from_norm2
    grad_branch = grad_hidden1.astype(BF16)
    grad_attended = contract(w_out, grad_branch, NT).astype(BF16)
    grad_query_pre, *grad_blocks = attend_back(
        query, grad_attended, log_total, cosine, sine, blocks, group
    )
    half = model_width // 2
    grad_wo = jnp.concatenate(
        [contract(attended, grad_branch[:, :half], NN), contract(attended, grad_branch[:, half:], NN)]
    ).astype(BF16)

    def spread(part):
        return to_all(part.reshape(dp_size, -1, part.shape[1]))

    def share(parts):
        return jnp.sum(parts.astype(F32), axis=0).astype(BF16)

    share_wo = share(spread(grad_wo))
    returned = [
        passed_along(grad_blocks[number], -hop) for number, hop in enumerate(range(HOPS, 0, -1))
    ]
    returned = after(returned, share_wo)
    kv_total = grad_blocks[-1]
    for part in returned:
        kv_total = kv_total + part.astype(F32)
    kv_rows = local_kv * HD
    grad_key_pre = rotate(kv_total[:kv_rows], cosine, -sine).astype(BF16)
    grad_value = kv_total[kv_rows:].astype(BF16)

    grad_wqkv = jnp.concatenate(
        [
            contract(normed1, part, ((0,), (1,))).astype(BF16)
            for part in (grad_query_pre, grad_key_pre, grad_value)
        ],
        axis=1,
    )
    share_wqkv = share(spread(grad_wqkv))
    grad_norm1_part = (
        contract(grad_query_pre, w_query, ((0,), (1,)))
        + contract(grad_key_pre, w_key, ((0,), (1,)))
        + contract(grad_value, w_value, ((0,), (1,)))
    ).astype(BF16)

    grad_normed1 = grad_norm1_part.astype(F32) + swapped(grad_norm1_part).astype(F32)
    grad_from_norm1, grad_gain1 = norm_back(grad_normed1, x_float, inverse1, norm1_gain)
    input_grad = grad_hidden1 + grad_from_norm1
    width = w_query.shape[1]
    peak = jnp.max(peaks, axis=1)
    peak_high = peak.astype(BF16)
    peak_low = (peak - peak_high.astype(F32)).astype(BF16)
    third = model_width // dp_size
    more = width - 2 * kv_rows
    extra = jnp.concatenate(
        [
            grad_gain1.astype(BF16).reshape(-1, more),
            grad_gain2.astype(BF16).reshape(-1, more),
            jnp.pad(jnp.stack([peak_high, peak_low]), ((0, 0), (0, more - local_heads))),
        ]
    )
    gain_rows = model_width // more
    extra = jnp.pad(extra, ((0, third - len(extra)), (0, 0)))
    packed = jnp.concatenate(
        [
            share_wo,
            share_wqkv[:, :width],
            jnp.concatenate([share_wqkv[:, width:], extra], axis=1),
        ]
    )
    packed, sums, expert_out = lax.optimization_barrier((packed, sums, expert_out))
    gathered = lax.all_gather(packed, "dp", axis=0)
    output = (hidden1 + combined(gated, in_plane(expert_out))).astype(BF16)
    sums = sums[0].astype(F32)
    grad_gate, grad_up, grad_down = (sums[0], sums[1], sums[2].T)
    grad_wo, grad_wq, grad_wk, grad_wv, totals = unpack(gathered, kv_rows)
    grad_gain1 = totals[:gain_rows].reshape(-1)
    grad_gain2 = totals[gain_rows : 2 * gain_rows].reshape(-1)
    head_peaks = jnp.max(
        gathered[:, 2 * third + 2 * gain_rows, 2 * kv_rows : 2 * kv_rows + local_heads].astype(F32)
        + gathered[:, 2 * third + 2 * gain_rows + 1, 2 * kv_rows : 2 * kv_rows + local_heads].astype(F32),
        axis=0,
    )
    factor = clip_limit / jnp.maximum(head_peaks, clip_limit)
    key_factor = jnp.min(factor.reshape(local_kv, group), axis=1)
    clipped_query = (w_query.astype(F32) * jnp.repeat(jnp.sqrt(factor), HD)[None, :]).astype(BF16)
    clipped_key = (w_key.astype(F32) * jnp.repeat(jnp.sqrt(key_factor), HD)[None, :]).astype(BF16)
    return (
        output,
        input_grad,
        grad_wq,
        grad_wk,
        grad_wv,
        grad_wo,
        grad_gain1,
        grad_gain2,
        grad_gate[None],
        grad_up[None],
        grad_down[None],
        clipped_query,
        clipped_key,
        head_peaks,
    )


def solution(mesh):
    in_specs = (
        P("dp", None),
        P("dp", None),
        P(),
        P(),
        P(None, "tensor"),
        P(None, "tensor"),
        P(None, "tensor"),
        P("tensor", None),
        P("dp", None, "tensor"),
        P("dp", None, "tensor"),
        P("dp", "tensor", None),
        P("dp", None),
        P("dp", None),
        P("dp"),
        P("dp"),
        P("tensor"),
    )
    out_specs = (
        P("dp", None),
        P("dp", None),
        P(None, "tensor"),
        P(None, "tensor"),
        P(None, "tensor"),
        P("tensor", None),
        P(),
        P(),
        P("dp", None, "tensor"),
        P("dp", None, "tensor"),
        P("dp", "tensor", None),
        P(None, "tensor"),
        P(None, "tensor"),
        P("tensor"),
    )
    return jax.shard_map(shards, mesh=mesh, in_specs=in_specs, out_specs=out_specs, check_vma=False)
```

```python
import functools
import math

import jax
import jax.numpy as jnp
import numpy as np
from jax import lax
from jax.experimental import pallas as pl
from jax.experimental.pallas import tpu as pltpu
from jax.sharding import PartitionSpec as P

HD = 64
TOP = 8
CAP = 64
HOPS = 4
RANK_ROWS = 32
PLANE = 16
SEGMENTS = 3
AUX = 16

EPS = 1e-06
ROPE_BASE = 10000.0
NEG_FILL = -1e30
BF16 = jnp.bfloat16
F32 = jnp.float32


def contract(left, right, dims):
    return lax.dot_general(left, right, (dims, ((), ())), preferred_element_type=F32)


NN = ((1,), (0,))
NT = ((1,), (1,))
TN = ((0,), (0,))


def swapped(array):
    return lax.ppermute(array, "tensor", [(0, 1), (1, 0)])


def after(array, other):
    return lax.optimization_barrier((array, other))[0]


def passed_along(value, steps):
    count = lax.axis_size("dp")
    first, last = (max(0, -steps), min(count, count - steps))
    return lax.ppermute(value, "dp", [(s, s + steps) for s in range(first, last)])


def to_all(array):
    return lax.all_to_all(array, "dp", 0, 0, tiled=True)


def rope_tables(count, dp_size):
    freq = np.exp(np.arange(HD // 2) * (-2.0 * math.log(ROPE_BASE) / HD))
    base = np.arange(dp_size)[:, None] * count * freq[None, :]
    local = freq[:, None] * np.arange(count)[None, :]
    index = lax.axis_index("dp")
    cos_base = jnp.asarray(np.cos(base), F32)[index][:, None]
    sin_base = jnp.asarray(np.sin(base), F32)[index][:, None]
    cos_local, sin_local = (jnp.asarray(np.cos(local), F32), jnp.asarray(np.sin(local), F32))
    return (
        cos_base * cos_local - sin_base * sin_local,
        sin_base * cos_local + cos_base * sin_local,
    )


def rotate(values, cosine, sine):
    half = HD // 2
    heads = values.reshape(-1, HD, values.shape[-1])
    first, second = (heads[:, :half], heads[:, half:])
    turned = jnp.concatenate(
        [first * cosine - second * sine, second * cosine + first * sine], axis=1
    )
    return turned.reshape(values.shape)


def fill_bias(blocks, bias):
    tok = bias.shape[1]
    rows = blocks[-1].shape[0] - AUX
    own = blocks[-1][rows:, :].astype(F32)
    seq_q, piece_q = (own[0:1, :], own[1:2, :])
    for number, block in enumerate(blocks):
        side = jnp.transpose(block[rows:, :].astype(F32))
        keep = side[:, 0:1] == seq_q
        if number == len(blocks) - 1:
            at_key = lax.broadcasted_iota(jnp.int32, (tok, tok), 0)
            at_query = lax.broadcasted_iota(jnp.int32, (tok, tok), 1)
            piece = (side[:, 1:2] == piece_q) & (piece_q > 0.0)
            keep = keep & ((at_key <= at_query) | piece)
        bias[number * tok : (number + 1) * tok, :] = jnp.where(keep, 0.0, NEG_FILL)


def all_keys(blocks, start):
    return jnp.concatenate([block[pl.ds(start, HD), :] for block in blocks], axis=1)


def attend_kernel(group, q_ref, k4, k3, k2, k1, k0, out_ref, log_ref, peak_ref, bias):
    blocks = (k4, k3, k2, k1, k0)
    fill_bias(blocks, bias)
    kv_rows = (k0.shape[0] - AUX) // 2

    def one_group(g, _):
        at = pl.multiple_of(g * HD, HD)
        keys = all_keys(blocks, at)
        values = all_keys(blocks, kv_rows + at)
        for j in range(group):
            head = g * group + j
            here = pl.ds(pl.multiple_of(head * HD, HD), HD)
            scores = contract(keys, q_ref[here, :], TN) + bias[...]
            peak = jnp.max(scores, axis=0, keepdims=True)
            weight = jnp.exp(scores - peak)
            total = jnp.sum(weight, axis=0, keepdims=True)
            mixed = contract(values, weight.astype(BF16), NN) * (1.0 / total)
            out_ref[here, :] = mixed.astype(BF16)
            log_ref[pl.ds(head, 1), :] = peak + jnp.log(total)
            peak_ref[pl.ds(head, 1), :] = peak
        return 0

    lax.fori_loop(0, kv_rows // HD, one_group, 0)


def attend(q, blocks, group):
    rows, tok = q.shape
    heads = rows // HD
    return pl.pallas_call(
        functools.partial(attend_kernel, group),
        out_shape=(
            jax.ShapeDtypeStruct((rows, tok), BF16),
            jax.ShapeDtypeStruct((heads, tok), F32),
            jax.ShapeDtypeStruct((heads, tok), F32),
        ),
        scratch_shapes=[pltpu.VMEM((len(blocks) * tok, tok), F32)],
        compiler_params=pltpu.CompilerParams(vmem_limit_bytes=48 << 20),
        cost_estimate=pl.CostEstimate(
            flops=4 * rows * tok * tok * len(blocks),
            bytes_accessed=4 * rows * tok + 2 * len(blocks) * 528 * tok,
            transcendentals=heads * tok * tok * len(blocks),
        ),
    )(q, *blocks)


def attend_back_kernel(
    group, q_ref, g_ref, log_ref, cos_ref, sin_ref, k4, k3, k2, k1, k0,
    dq_ref, d4, d3, d2, d1, d0, bias,
):
    blocks = (k4, k3, k2, k1, k0)
    grads = (d4, d3, d2, d1, d0)
    fill_bias(blocks, bias)
    kv_rows = (k0.shape[0] - AUX) // 2
    tok = bias.shape[1]
    half = HD // 2

    def one_group(g, _):
        at = pl.multiple_of(g * HD, HD)
        keys = all_keys(blocks, at)
        values = all_keys(blocks, kv_rows + at)
        key_sum = value_sum = None
        for j in range(group):
            head = g * group + j
            start = pl.multiple_of(head * HD, HD)
            query, grad = (q_ref[pl.ds(start, HD), :], g_ref[pl.ds(start, HD), :])
            scores = contract(keys, query, TN) + bias[...]
            probs = jnp.exp(scores - log_ref[pl.ds(head, 1), :])
            grad_probs = contract(values, grad, TN)
            delta = jnp.sum(probs * grad_probs, axis=0, keepdims=True)
            grad_scores = (probs * (grad_probs - delta)).astype(BF16)
            key_part = contract(query, grad_scores, NT)
            value_part = contract(grad, probs.astype(BF16), NT)
            key_sum = key_part if key_sum is None else key_sum + key_part
            value_sum = value_part if value_sum is None else value_sum + value_part
            turned = contract(keys, grad_scores, NN) * (HD**-0.5)
            first, second = (turned[:half], turned[half:])
            cosine, sine = (cos_ref[...], sin_ref[...])
            dq_ref[pl.ds(start, half), :] = (first * cosine + second * sine).astype(BF16)
            dq_ref[pl.ds(start + half, half), :] = (second * cosine - first * sine).astype(BF16)
        for number, grad_ref in enumerate(grads):
            piece = slice(number * tok, (number + 1) * tok)
            grad_ref[pl.ds(at, HD), :] = key_sum[:, piece].astype(grad_ref.dtype)
            grad_ref[pl.ds(kv_rows + at, HD), :] = value_sum[:, piece].astype(grad_ref.dtype)
        return 0

    lax.fori_loop(0, kv_rows // HD, one_group, 0)


def attend_back(q, grad, log_total, cosine, sine, blocks, group):
    rows, tok = q.shape
    kv = blocks[0].shape[0] - AUX
    return pl.pallas_call(
        functools.partial(attend_back_kernel, group),
        out_shape=(
            jax.ShapeDtypeStruct((rows, tok), BF16),
            *(jax.ShapeDtypeStruct((kv, tok), BF16) for _ in blocks[1:]),
            jax.ShapeDtypeStruct((kv, tok), F32),
        ),
        scratch_shapes=[pltpu.VMEM((len(blocks) * tok, tok), F32)],
        compiler_params=pltpu.CompilerParams(vmem_limit_bytes=48 << 20),
        cost_estimate=pl.CostEstimate(
            flops=1000 * rows * tok * tok * len(blocks),
            bytes_accessed=6 * rows * tok + 4 * len(blocks) * 528 * tok,
            transcendentals=rows // HD * tok * tok * len(blocks),
        ),
    )(q, grad, log_total, cosine, sine, *blocks)


def expert_kernel(x_ref, g_ref, own_ref, peer_ref, dx_ref, own_acts, peer_acts):
    width = x_ref.shape[-1]
    rows, grads = (x_ref[...].reshape(-1, width), g_ref[...].reshape(-1, width))
    hidden = own_ref.shape[-1] // 3
    back = None
    for weights, acts in ((own_ref, own_acts), (peer_ref, peer_acts)):
        both = contract(rows, weights[0, :, : 2 * hidden], NN)
        grad_inner = contract(grads, weights[0, :, 2 * hidden :], NN)
        gate_act, up_act = (both[:, :hidden], both[:, hidden:])
        sigmoid = 1.0 / (1.0 + jnp.exp(-gate_act))
        silu = gate_act * sigmoid
        dgate = grad_inner * up_act * (sigmoid * (1.0 + gate_act * (1.0 - sigmoid)))
        acts[0, :, :hidden] = dgate.astype(BF16)
        acts[0, :, hidden : 2 * hidden] = (grad_inner * silu).astype(BF16)
        acts[0, :, 2 * hidden :] = (silu * up_act).astype(BF16)
        part = contract(acts[0, :, : 2 * hidden], weights[0, :, : 2 * hidden], NT)
        back = part if back is None else back + part
    dx_ref[...] = back.astype(BF16).reshape(dx_ref.shape)


def expert_back(rows, grads, own, peer):
    sources, lines, width = rows.shape
    segments, triple = (lines // RANK_ROWS, own.shape[-1])
    count = sources * RANK_ROWS
    wide = pl.BlockSpec((sources, RANK_ROWS, width), lambda s: (0, s, 0))
    weight = pl.BlockSpec((1, width, triple), lambda s: (s, 0, 0))
    act = pl.BlockSpec((1, count, triple), lambda s: (s, 0, 0))
    return pl.pallas_call(
        expert_kernel,
        grid=(segments,),
        in_specs=[wide, wide, weight, weight],
        out_specs=[wide, act, act],
        out_shape=[
            jax.ShapeDtypeStruct(rows.shape, BF16),
            jax.ShapeDtypeStruct((segments, count, triple), BF16),
            jax.ShapeDtypeStruct((segments, count, triple), BF16),
        ],
        compiler_params=pltpu.CompilerParams(vmem_limit_bytes=56 << 20),
        cost_estimate=pl.CostEstimate(
            flops=7 * sources * lines * width * triple,
            bytes_accessed=6 * sources * lines * width + 4 * segments * width * triple,
            transcendentals=2 * sources * lines * triple // 3,
        ),
    )(rows, grads, own, peer)


def expert_sums_kernel(x_ref, g_ref, own_acts, peer_acts, own_ref, peer_ref, sum_own, *outs):
    width = x_ref.shape[-1]
    rows, grads = (x_ref[...].reshape(-1, width), g_ref[...].reshape(-1, width))
    hidden = own_ref.shape[-1]
    out_ref = outs[-1]
    out = None
    for side, (acts, weights) in enumerate(((own_acts, own_ref), (peer_acts, peer_ref))):
        first = contract(rows, acts[0, :, : 2 * hidden], TN).astype(BF16)
        second = contract(grads, acts[0, :, 2 * hidden :], TN).astype(BF16)
        if side == 0:
            sum_own[0, :, : 2 * hidden] = first
            sum_own[0, :, 2 * hidden :] = second
        else:
            outs[0][0] = first[:, :hidden]
            outs[1][0] = first[:, hidden:]
            outs[2][0] = second
        part = contract(acts[0, :, 2 * hidden :], weights[0], NT)
        out = part if out is None else out + part
    out_ref[...] = out.astype(BF16).reshape(out_ref.shape)


def expert_sums(rows, grads, own_acts, peer_acts, own, peer):
    sources, lines, width = rows.shape
    segments, triple = (lines // RANK_ROWS, own.shape[-1])
    hidden = triple // 3
    count = sources * RANK_ROWS
    wide = pl.BlockSpec((sources, RANK_ROWS, width), lambda s: (0, s, 0))
    down = pl.BlockSpec((1, width, hidden), lambda s: (s, 0, 2))
    act = pl.BlockSpec((1, count, triple), lambda s: (s, 0, 0))
    return pl.pallas_call(
        expert_sums_kernel,
        grid=(segments,),
        in_specs=[wide, wide, act, act, down, down],
        out_specs=[pl.BlockSpec((1, width, triple), lambda s: (s, 0, 0))]
        + [pl.BlockSpec((1, width, hidden), lambda s: (s, 0, 0))] * 3
        + [wide],
        out_shape=[jax.ShapeDtypeStruct((segments, width, triple), BF16)]
        + [jax.ShapeDtypeStruct((segments, width, hidden), BF16)] * 3
        + [jax.ShapeDtypeStruct(rows.shape, BF16)],
        compiler_params=pltpu.CompilerParams(vmem_limit_bytes=60 << 20),
        cost_estimate=pl.CostEstimate(
            flops=6 * sources * lines * width * triple,
            bytes_accessed=6 * sources * lines * width + 5 * segments * width * triple,
            transcendentals=0,
        ),
    )(rows, grads, own_acts, peer_acts, own, peer)


def both_cores_kernel(own_ref, *refs):
    out_ref = refs[-1]
    hidden = refs[0].shape[-1]

    @pl.when(pl.program_id(0) < SEGMENTS)
    def _():
        for kind, peer_ref in enumerate(refs[:-1]):
            here = slice(kind * hidden, (kind + 1) * hidden)
            total = own_ref[0, :, here].astype(F32) + peer_ref[0].astype(F32)
            out_ref[0, :, here] = total.astype(BF16)

    @pl.when(pl.program_id(0) >= SEGMENTS)
    def _():
        out_ref[...] = jnp.zeros_like(out_ref)


def both_cores(own, peers, slots):
    segments, width, triple = own.shape
    rows = width // 2
    last = segments - 1
    part = pl.BlockSpec((1, rows, triple), lambda s, r: (jnp.minimum(s, last), r, 0))
    thin = pl.BlockSpec((1, rows, triple // 3), lambda s, r: (jnp.minimum(s, last), r, 0))
    return pl.pallas_call(
        both_cores_kernel,
        grid=(slots, 2),
        in_specs=[part] + [thin] * 3,
        out_specs=pl.BlockSpec((1, rows, triple), lambda s, r: (s, r, 0)),
        out_shape=jax.ShapeDtypeStruct((slots, width, triple), BF16),
        cost_estimate=pl.CostEstimate(
            flops=slots * width * triple, bytes_accessed=6 * slots * width * triple, transcendentals=0
        ),
    )(own, *peers)


def weight_grads_kernel(normed_ref, qkv_ref, attended_ref, branch_ref, out_ref):
    width = branch_ref.shape[1]
    out_ref[:, :width] = contract(attended_ref[...], branch_ref[...], NN).astype(BF16)
    out_ref[:, width:] = contract(normed_ref[...], qkv_ref[...], ((0,), (1,))).astype(BF16)


def weight_grads(normed, grad_qkv, attended, branch):
    tok, model = normed.shape
    width, columns = (attended.shape[0], grad_qkv.shape[0])
    half = width // 256
    return pl.pallas_call(
        weight_grads_kernel,
        grid=(model // 256,),
        in_specs=[
            pl.BlockSpec((tok, 256), lambda i: (0, i)),
            pl.BlockSpec((columns, tok), lambda i: (0, 0)),
            pl.BlockSpec((256, tok), lambda i: (i % half, 0)),
            pl.BlockSpec((tok, width), lambda i: (0, i // half)),
        ],
        out_specs=pl.BlockSpec((256, width + columns), lambda i: (i, 0)),
        out_shape=jax.ShapeDtypeStruct((model, width + columns), BF16),
        cost_estimate=pl.CostEstimate(
            flops=2 * tok * model * (width + columns),
            bytes_accessed=2 * model * (width + columns) + 4 * tok * model,
            transcendentals=0,
        ),
    )(normed, grad_qkv, attended, branch)


def unpack_kernel(
    in_ref, query_ref, key_ref, sq_ref, sk_ref,
    wo_ref, wq_ref, wk_ref, wv_ref, sum_ref, cq_ref, ck_ref,
):
    step = pl.program_id(0)
    chunks, lines, _ = in_ref.shape
    for c in range(chunks):
        here, at = (slice(c * lines, (c + 1) * lines), 0)
        for target in (wo_ref, wq_ref, wk_ref, wv_ref):
            size = target.shape[1]
            target[here, :] = in_ref[c, :, at : at + size].astype(F32)
            at += size
    total = jnp.sum(in_ref[:, :, at:].astype(F32), axis=0)
    cq_ref[...] = (query_ref[...].astype(F32) * sq_ref[...]).astype(BF16)
    ck_ref[...] = (key_ref[...].astype(F32) * sk_ref[...]).astype(BF16)

    @pl.when(step == 0)
    def _():
        sum_ref[...] = total

    @pl.when(step > 0)
    def _():
        sum_ref[...] = sum_ref[...] + total


def unpack(gathered, w_query, w_key, scale_query, scale_key):
    parts, lines, every = gathered.shape
    width, narrow = (w_query.shape[1], w_key.shape[1])
    steps = 16
    per = parts // steps
    rows = per * lines
    total = parts * lines
    extra = (lines, every - 2 * width - 2 * narrow)
    wide = pl.BlockSpec((rows, width), lambda i: (i, 0))
    thin = pl.BlockSpec((rows, narrow), lambda i: (i, 0))
    return pl.pallas_call(
        unpack_kernel,
        grid=(steps,),
        in_specs=[
            pl.BlockSpec((per, lines, every), lambda i: (i, 0, 0)),
            wide,
            thin,
            pl.BlockSpec((1, width), lambda i: (0, 0)),
            pl.BlockSpec((1, narrow), lambda i: (0, 0)),
        ],
        out_specs=[
            pl.BlockSpec((rows, width), lambda i: (i % (steps // 2), i // (steps // 2))),
            wide,
            thin,
            thin,
            pl.BlockSpec(extra, lambda i: (0, 0)),
            wide,
            thin,
        ],
        out_shape=[
            jax.ShapeDtypeStruct((total // 2, 2 * width), F32),
            jax.ShapeDtypeStruct((total, width), F32),
            jax.ShapeDtypeStruct((total, narrow), F32),
            jax.ShapeDtypeStruct((total, narrow), F32),
            jax.ShapeDtypeStruct(extra, F32),
            jax.ShapeDtypeStruct((total, width), BF16),
            jax.ShapeDtypeStruct((total, narrow), BF16),
        ],
        compiler_params=pltpu.CompilerParams(vmem_limit_bytes=32 << 20),
        cost_estimate=pl.CostEstimate(
            flops=total * every, bytes_accessed=8 * total * every, transcendentals=0
        ),
    )(gathered, w_query, w_key, scale_query, scale_key)


def rms_scale(values):
    return lax.rsqrt(jnp.mean(values * values, axis=-1, keepdims=True) + EPS)


def norm_back(grad_normed, hidden, inverse, gain):
    weighted = grad_normed * gain
    grad_gain = jnp.sum(grad_normed * hidden * inverse, axis=0)
    grad_hidden = inverse * weighted - hidden * inverse**3 * jnp.mean(
        weighted * hidden, axis=-1, keepdims=True
    )
    return (grad_hidden, grad_gain)


def shards(
    tokens,
    out_grad,
    norm1_gain,
    norm2_gain,
    w_query,
    w_key,
    w_value,
    w_out,
    w_gate,
    w_up,
    w_down,
    route_ids,
    route_logits,
    seq_ids,
    piece_ids,
    clip_limit,
):
    tok_dev, model_width = tokens.shape
    dp_size = lax.axis_size("dp")
    tensor_size = lax.axis_size("tensor")
    core = lax.axis_index("tensor")
    local_heads = w_query.shape[1] // HD
    local_kv = w_key.shape[1] // HD
    group = local_heads // local_kv
    plane_groups = [list(range(at, at + PLANE)) for at in range(0, dp_size, PLANE)]
    column_groups = [list(range(at, dp_size, PLANE)) for at in range(PLANE)]

    packed_w = jnp.concatenate([w_gate[0], w_up[0], w_down[0].T], axis=1)
    own = lax.all_gather(packed_w, "dp", axis=0, axis_index_groups=column_groups)

    picks = route_ids.T
    logits = route_logits.T
    gate_exp = jnp.exp(logits - jnp.max(logits, axis=0, keepdims=True))
    gates = gate_exp / jnp.sum(gate_exp, axis=0, keepdims=True)
    number = jnp.arange(PLANE * SEGMENTS, dtype=jnp.int32)
    number = number % SEGMENTS * PLANE + number // SEGMENTS
    same = picks[None] == number[:, None, None]
    member = jnp.any(same, axis=1)
    gate_of = jnp.sum(jnp.where(same, gates[None], 0.0), axis=1)
    place = jnp.arange(tok_dev, dtype=jnp.int32)
    before = (place[:, None] < place[None, :]).astype(BF16)
    rank = contract(member.astype(BF16), before, NN)
    rank = jnp.where(member, rank, -1.0)
    wanted = (tensor_size * jnp.arange(RANK_ROWS, dtype=jnp.int32) + core).astype(F32)
    chosen = rank[:, None, :] == wanted[None, :, None]
    pick = chosen.astype(BF16).reshape(-1, tok_dev)
    gated = jnp.where(chosen, gate_of[:, None, :], 0.0)
    slot_gate = jnp.sum(gated, axis=2).reshape(-1, 1)
    gated = gated.astype(BF16).reshape(-1, tok_dev)

    def in_plane(rows):
        rows = rows.reshape(PLANE, -1, model_width)
        return lax.all_to_all(rows, "dp", 0, 0, tiled=True, axis_index_groups=plane_groups)

    grad_rows = (contract(pick, out_grad, NN) * slot_gate).astype(BF16)

    cosine, sine = rope_tables(tok_dev, dp_size)
    x_float = tokens.astype(F32)
    inverse1 = rms_scale(x_float)
    normed1 = (x_float * inverse1 * norm1_gain).astype(BF16)
    query = rotate(contract(w_query, normed1, ((0,), (1,))), cosine, sine)
    query = (query * (HD**-0.5)).astype(BF16)
    key = rotate(contract(w_key, normed1, ((0,), (1,))), cosine, sine).astype(BF16)
    value = contract(w_value, normed1, ((0,), (1,))).astype(BF16)
    side = jnp.concatenate(
        [(seq_ids + 1)[None], piece_ids[None], jnp.zeros((AUX - 2, tok_dev), jnp.int32)]
    ).astype(BF16)
    block = jnp.concatenate([key, value, side])
    blocks = tuple(passed_along(block, hop) for hop in range(HOPS, 0, -1)) + (block,)
    blocks, grad_rows = lax.optimization_barrier((blocks, grad_rows))
    grad_rows = in_plane(grad_rows)
    attended, log_total, peaks = attend(query, blocks, group)
    attn_part = contract(attended, w_out, TN)
    hidden1 = x_float + (attn_part + swapped(attn_part))
    inverse2 = rms_scale(hidden1)
    normed2 = (hidden1 * inverse2 * norm2_gain).astype(BF16)

    rows_out = contract(pick, normed2, NN).astype(BF16)
    rows_out = after(rows_out, grad_rows)
    own = after(own, rows_out)
    peer = swapped(own)
    rows_in = in_plane(rows_out)
    back, own_acts, peer_acts = expert_back(rows_in, grad_rows, own, peer)

    def combined(weights, rows):
        part = contract(weights, rows.reshape(-1, model_width), TN).astype(BF16)
        return part.astype(F32) + swapped(part).astype(F32)

    sum_own, *sum_peer, expert_out = expert_sums(rows_in, grad_rows, own_acts, peer_acts, own, peer)
    sums = both_cores(sum_own, [swapped(part) for part in sum_peer], dp_size // PLANE)
    back = in_plane(back)
    expert_out = in_plane(after(expert_out, back))
    grad_normed2 = combined(pick, after(back, sums))
    sums = lax.psum_scatter(
        sums, "dp", scatter_dimension=0, tiled=True, axis_index_groups=column_groups
    )

    grad_top = out_grad.astype(F32)
    grad_from_norm2, grad_gain2 = norm_back(grad_normed2, hidden1, inverse2, norm2_gain)
    grad_hidden1 = grad_top + grad_from_norm2
    grad_branch = grad_hidden1.astype(BF16)
    grad_attended = contract(w_out, grad_branch, NT).astype(BF16)
    grad_query_pre, *grad_blocks = attend_back(
        query, grad_attended, log_total, cosine, sine, blocks, group
    )
    returned = [
        passed_along(grad_blocks[number], -hop) for number, hop in enumerate(range(HOPS, 0, -1))
    ]
    kv_total = grad_blocks[-1]
    for part in returned:
        kv_total = kv_total + part.astype(F32)
    kv_rows = local_kv * HD
    grad_key_pre = rotate(kv_total[:kv_rows], cosine, -sine).astype(BF16)
    grad_value = kv_total[kv_rows:].astype(BF16)

    grad_qkv = jnp.concatenate([grad_query_pre, grad_key_pre, grad_value])
    parts = weight_grads(normed1, grad_qkv, attended, grad_branch)
    parts = to_all(after(parts, expert_out).reshape(dp_size, -1, parts.shape[1]))
    summed = jnp.sum(parts.astype(F32), axis=0).astype(BF16)
    grad_norm1_part = (
        contract(grad_query_pre, w_query, ((0,), (1,)))
        + contract(grad_key_pre, w_key, ((0,), (1,)))
        + contract(grad_value, w_value, ((0,), (1,)))
    ).astype(BF16)

    grad_normed1 = grad_norm1_part.astype(F32) + swapped(grad_norm1_part).astype(F32)
    grad_from_norm1, grad_gain1 = norm_back(grad_normed1, x_float, inverse1, norm1_gain)
    input_grad = grad_hidden1 + grad_from_norm1
    width = w_query.shape[1]
    peak = jnp.max(peaks, axis=1)
    peak_high = peak.astype(BF16)
    peak_low = (peak - peak_high.astype(F32)).astype(BF16)
    third = model_width // dp_size
    more = width - 2 * kv_rows
    extra = jnp.concatenate(
        [
            grad_gain1.astype(BF16).reshape(-1, more),
            grad_gain2.astype(BF16).reshape(-1, more),
            jnp.pad(jnp.stack([peak_high, peak_low]), ((0, 0), (0, more - local_heads))),
        ]
    )
    gain_rows = model_width // more
    extra = jnp.pad(extra, ((0, third - len(extra)), (0, 0)))
    packed = jnp.concatenate([summed, extra], axis=1)
    packed, sums, expert_out = lax.optimization_barrier((packed, sums, expert_out))
    gathered = lax.all_gather(packed, "dp", axis=0)
    output = (hidden1 + combined(gated, expert_out)).astype(BF16)
    grad_gate, grad_up, grad_down = jnp.split(sums[0].astype(F32), 3, axis=1)
    grad_down = grad_down.T
    high = gathered[:, 2 * gain_rows, -more : local_heads - more].astype(F32)
    low = gathered[:, 2 * gain_rows + 1, -more : local_heads - more].astype(F32)
    head_peaks = jnp.max(high + low, axis=0)
    factor = clip_limit / jnp.maximum(head_peaks, clip_limit)
    key_factor = jnp.min(factor.reshape(local_kv, group), axis=1)
    scale_query = jnp.repeat(jnp.sqrt(factor), HD)[None, :]
    scale_key = jnp.repeat(jnp.sqrt(key_factor), HD)[None, :]
    grad_wo, grad_wq, grad_wk, grad_wv, totals, clipped_query, clipped_key = unpack(
        gathered, w_query, w_key, scale_query, scale_key
    )
    grad_gain1 = totals[:gain_rows].reshape(-1)
    grad_gain2 = totals[gain_rows : 2 * gain_rows].reshape(-1)
    return (
        output,
        input_grad,
        grad_wq,
        grad_wk,
        grad_wv,
        grad_wo,
        grad_gain1,
        grad_gain2,
        grad_gate[None],
        grad_up[None],
        grad_down[None],
        clipped_query,
        clipped_key,
        head_peaks,
    )


def solution(mesh):
    in_specs = (
        P("dp", None),
        P("dp", None),
        P(),
        P(),
        P(None, "tensor"),
        P(None, "tensor"),
        P(None, "tensor"),
        P("tensor", None),
        P("dp", None, "tensor"),
        P("dp", None, "tensor"),
        P("dp", "tensor", None),
        P("dp", None),
        P("dp", None),
        P("dp"),
        P("dp"),
        P("tensor"),
    )
    out_specs = (
        P("dp", None),
        P("dp", None),
        P(None, "tensor"),
        P(None, "tensor"),
        P(None, "tensor"),
        P("tensor", None),
        P(),
        P(),
        P("dp", None, "tensor"),
        P("dp", None, "tensor"),
        P("dp", "tensor", None),
        P(None, "tensor"),
        P(None, "tensor"),
        P("tensor"),
    )
    return jax.shard_map(shards, mesh=mesh, in_specs=in_specs, out_specs=out_specs, check_vma=False)
```

```python
import functools
import math

import jax
import jax.numpy as jnp
import numpy as np
from jax import lax
from jax.experimental import pallas as pl
from jax.experimental.pallas import tpu as pltpu
from jax.sharding import PartitionSpec as P

HD = 64
TOP = 8
CAP = 64
HOPS = 4
RANK_ROWS = 32
PLANE = 16
SEGMENTS = 3
AUX = 16
LANES = 256
MORE = 128

EPS = 1e-06
ROPE_BASE = 10000.0
NEG_FILL = -1e30
BF16 = jnp.bfloat16
F32 = jnp.float32


def contract(left, right, dims):
    return lax.dot_general(left, right, (dims, ((), ())), preferred_element_type=F32)


NN = ((1,), (0,))
NT = ((1,), (1,))
TN = ((0,), (0,))


def swapped(array):
    return lax.ppermute(array, "tensor", [(0, 1), (1, 0)])


def after(array, other):
    return lax.optimization_barrier((array, other))[0]


def passed_along(value, steps):
    count = lax.axis_size("dp")
    first, last = (max(0, -steps), min(count, count - steps))
    return lax.ppermute(value, "dp", [(s, s + steps) for s in range(first, last)])


def rope_tables(count, dp_size):
    freq = np.exp(np.arange(HD // 2) * (-2.0 * math.log(ROPE_BASE) / HD))
    base = np.arange(dp_size)[:, None] * count * freq[None, :]
    local = freq[:, None] * np.arange(count)[None, :]
    index = lax.axis_index("dp")
    cos_base = jnp.asarray(np.cos(base), F32)[index][:, None]
    sin_base = jnp.asarray(np.sin(base), F32)[index][:, None]
    cos_local, sin_local = (jnp.asarray(np.cos(local), F32), jnp.asarray(np.sin(local), F32))
    return (
        cos_base * cos_local - sin_base * sin_local,
        sin_base * cos_local + cos_base * sin_local,
    )


def rotate(values, cosine, sine):
    half = HD // 2
    heads = values.reshape(-1, HD, values.shape[-1])
    first, second = (heads[:, :half], heads[:, half:])
    turned = jnp.concatenate(
        [first * cosine - second * sine, second * cosine + first * sine], axis=1
    )
    return turned.reshape(values.shape)


def fill_bias(blocks, bias):
    tok = bias.shape[1]
    rows = blocks[-1].shape[0] - AUX
    own = blocks[-1][rows:, :].astype(F32)
    seq_q, piece_q = (own[0:1, :], own[1:2, :])
    for number, block in enumerate(blocks):
        side = jnp.transpose(block[rows:, :].astype(F32))
        keep = side[:, 0:1] == seq_q
        if number == len(blocks) - 1:
            at_key = lax.broadcasted_iota(jnp.int32, (tok, tok), 0)
            at_query = lax.broadcasted_iota(jnp.int32, (tok, tok), 1)
            piece = (side[:, 1:2] == piece_q) & (piece_q > 0.0)
            keep = keep & ((at_key <= at_query) | piece)
        bias[number * tok : (number + 1) * tok, :] = jnp.where(keep, 0.0, NEG_FILL)


def all_keys(blocks, start):
    return jnp.concatenate([block[pl.ds(start, HD), :] for block in blocks], axis=1)


def attend_kernel(group, q_ref, k4, k3, k2, k1, k0, out_ref, log_ref, peak_ref, bias):
    blocks = (k4, k3, k2, k1, k0)
    fill_bias(blocks, bias)
    kv_rows = (k0.shape[0] - AUX) // 2

    def one_group(g, _):
        at = pl.multiple_of(g * HD, HD)
        keys = all_keys(blocks, at)
        values = all_keys(blocks, kv_rows + at)
        for j in range(group):
            head = g * group + j
            here = pl.ds(pl.multiple_of(head * HD, HD), HD)
            scores = contract(keys, q_ref[here, :], TN) + bias[...]
            peak = jnp.max(scores, axis=0, keepdims=True)
            weight = jnp.exp(scores - peak)
            total = jnp.sum(weight, axis=0, keepdims=True)
            mixed = contract(values, weight.astype(BF16), NN) * (1.0 / total)
            out_ref[here, :] = mixed.astype(BF16)
            log_ref[pl.ds(head, 1), :] = peak + jnp.log(total)
            peak_ref[pl.ds(head, 1), :] = peak
        return 0

    lax.fori_loop(0, kv_rows // HD, one_group, 0)


def attend(q, blocks, group):
    rows, tok = q.shape
    heads = rows // HD
    return pl.pallas_call(
        functools.partial(attend_kernel, group),
        out_shape=(
            jax.ShapeDtypeStruct((rows, tok), BF16),
            jax.ShapeDtypeStruct((heads, tok), F32),
            jax.ShapeDtypeStruct((heads, tok), F32),
        ),
        scratch_shapes=[pltpu.VMEM((len(blocks) * tok, tok), F32)],
        compiler_params=pltpu.CompilerParams(vmem_limit_bytes=48 << 20),
        cost_estimate=pl.CostEstimate(
            flops=4 * rows * tok * tok * len(blocks),
            bytes_accessed=4 * rows * tok + 2 * len(blocks) * 528 * tok,
            transcendentals=heads * tok * tok * len(blocks),
        ),
    )(q, *blocks)


def attend_back_kernel(
    group, q_ref, g_ref, log_ref, cos_ref, sin_ref, k4, k3, k2, k1, k0,
    dq_ref, d4, d3, d2, d1, d0, bias,
):
    blocks = (k4, k3, k2, k1, k0)
    grads = (d4, d3, d2, d1, d0)
    fill_bias(blocks, bias)
    kv_rows = (k0.shape[0] - AUX) // 2
    tok = bias.shape[1]
    half = HD // 2

    def one_group(g, _):
        at = pl.multiple_of(g * HD, HD)
        keys = all_keys(blocks, at)
        values = all_keys(blocks, kv_rows + at)
        key_sum = value_sum = None
        for j in range(group):
            head = g * group + j
            start = pl.multiple_of(head * HD, HD)
            query, grad = (q_ref[pl.ds(start, HD), :], g_ref[pl.ds(start, HD), :])
            scores = contract(keys, query, TN) + bias[...]
            probs = jnp.exp(scores - log_ref[pl.ds(head, 1), :])
            grad_probs = contract(values, grad, TN)
            delta = jnp.sum(probs * grad_probs, axis=0, keepdims=True)
            grad_scores = (probs * (grad_probs - delta)).astype(BF16)
            key_part = contract(query, grad_scores, NT)
            value_part = contract(grad, probs.astype(BF16), NT)
            key_sum = key_part if key_sum is None else key_sum + key_part
            value_sum = value_part if value_sum is None else value_sum + value_part
            turned = contract(keys, grad_scores, NN) * (HD**-0.5)
            first, second = (turned[:half], turned[half:])
            cosine, sine = (cos_ref[...], sin_ref[...])
            dq_ref[pl.ds(start, half), :] = (first * cosine + second * sine).astype(BF16)
            dq_ref[pl.ds(start + half, half), :] = (second * cosine - first * sine).astype(BF16)
        for number, grad_ref in enumerate(grads):
            piece = slice(number * tok, (number + 1) * tok)
            grad_ref[pl.ds(at, HD), :] = key_sum[:, piece].astype(grad_ref.dtype)
            grad_ref[pl.ds(kv_rows + at, HD), :] = value_sum[:, piece].astype(grad_ref.dtype)
        return 0

    lax.fori_loop(0, kv_rows // HD, one_group, 0)


def attend_back(q, grad, log_total, cosine, sine, blocks, group):
    rows, tok = q.shape
    kv = blocks[0].shape[0] - AUX
    return pl.pallas_call(
        functools.partial(attend_back_kernel, group),
        out_shape=(
            jax.ShapeDtypeStruct((rows, tok), BF16),
            *(jax.ShapeDtypeStruct((kv, tok), BF16) for _ in blocks[1:]),
            jax.ShapeDtypeStruct((kv, tok), F32),
        ),
        scratch_shapes=[pltpu.VMEM((len(blocks) * tok, tok), F32)],
        compiler_params=pltpu.CompilerParams(vmem_limit_bytes=48 << 20),
        cost_estimate=pl.CostEstimate(
            flops=1000 * rows * tok * tok * len(blocks),
            bytes_accessed=6 * rows * tok + 4 * len(blocks) * 528 * tok,
            transcendentals=rows // HD * tok * tok * len(blocks),
        ),
    )(q, grad, log_total, cosine, sine, *blocks)


def pack_weights_kernel(gate_ref, up_ref, down_ref, out_ref):
    hidden = gate_ref.shape[1]
    out_ref[:, :hidden] = gate_ref[...]
    out_ref[:, hidden : 2 * hidden] = up_ref[...]
    out_ref[:, 2 * hidden :] = jnp.transpose(down_ref[...].astype(F32)).astype(BF16)


def pack_weights(gate, up, down):
    width, hidden = gate.shape
    thin = pl.BlockSpec((LANES, hidden), lambda i: (i, 0))
    return pl.pallas_call(
        pack_weights_kernel,
        grid=(width // LANES,),
        in_specs=[thin, thin, pl.BlockSpec((hidden, LANES), lambda i: (0, i))],
        out_specs=pl.BlockSpec((LANES, 3 * hidden), lambda i: (i, 0)),
        out_shape=jax.ShapeDtypeStruct((width, 3 * hidden), BF16),
        cost_estimate=pl.CostEstimate(
            flops=width * hidden, bytes_accessed=12 * width * hidden, transcendentals=0
        ),
    )(gate, up, down)


def expert_kernel(x_ref, g_ref, own_ref, peer_ref, dx_ref, own_acts, peer_acts):
    width = x_ref.shape[-1]
    rows, grads = (x_ref[...].reshape(-1, width), g_ref[...].reshape(-1, width))
    hidden = own_ref.shape[-1] // 3
    back = None
    for weights, acts in ((own_ref, own_acts), (peer_ref, peer_acts)):
        both = contract(rows, weights[0, :, : 2 * hidden], NN)
        grad_inner = contract(grads, weights[0, :, 2 * hidden :], NN)
        gate_act, up_act = (both[:, :hidden], both[:, hidden:])
        sigmoid = 1.0 / (1.0 + jnp.exp(-gate_act))
        silu = gate_act * sigmoid
        dgate = grad_inner * up_act * (sigmoid * (1.0 + gate_act * (1.0 - sigmoid)))
        acts[0, :, :hidden] = dgate.astype(BF16)
        acts[0, :, hidden : 2 * hidden] = (grad_inner * silu).astype(BF16)
        acts[0, :, 2 * hidden :] = (silu * up_act).astype(BF16)
        part = contract(acts[0, :, : 2 * hidden], weights[0, :, : 2 * hidden], NT)
        back = part if back is None else back + part
    dx_ref[...] = back.astype(BF16).reshape(dx_ref.shape)


def expert_back(rows, grads, own, peer):
    sources, lines, width = rows.shape
    segments, triple = (lines // RANK_ROWS, own.shape[-1])
    count = sources * RANK_ROWS
    wide = pl.BlockSpec((sources, RANK_ROWS, width), lambda s: (0, s, 0))
    weight = pl.BlockSpec((1, width, triple), lambda s: (s, 0, 0))
    act = pl.BlockSpec((1, count, triple), lambda s: (s, 0, 0))
    return pl.pallas_call(
        expert_kernel,
        grid=(segments,),
        in_specs=[wide, wide, weight, weight],
        out_specs=[wide, act, act],
        out_shape=[
            jax.ShapeDtypeStruct(rows.shape, BF16),
            jax.ShapeDtypeStruct((segments, count, triple), BF16),
            jax.ShapeDtypeStruct((segments, count, triple), BF16),
        ],
        compiler_params=pltpu.CompilerParams(vmem_limit_bytes=56 << 20),
        cost_estimate=pl.CostEstimate(
            flops=7 * sources * lines * width * triple,
            bytes_accessed=6 * sources * lines * width + 4 * segments * width * triple,
            transcendentals=2 * sources * lines * triple // 3,
        ),
    )(rows, grads, own, peer)


def expert_sums_kernel(x_ref, g_ref, own_acts, peer_acts, own_ref, peer_ref, sum_own, *outs):
    width = x_ref.shape[-1]
    rows, grads = (x_ref[...].reshape(-1, width), g_ref[...].reshape(-1, width))
    hidden = own_ref.shape[-1]
    out_ref = outs[-1]
    out = None
    for side, (acts, weights) in enumerate(((own_acts, own_ref), (peer_acts, peer_ref))):
        first = contract(rows, acts[0, :, : 2 * hidden], TN).astype(BF16)
        second = contract(grads, acts[0, :, 2 * hidden :], TN).astype(BF16)
        if side == 0:
            sum_own[0, :, : 2 * hidden] = first
            sum_own[0, :, 2 * hidden :] = second
        else:
            outs[0][0] = first[:, :hidden]
            outs[1][0] = first[:, hidden:]
            outs[2][0] = second
        part = contract(acts[0, :, 2 * hidden :], weights[0], NT)
        out = part if out is None else out + part
    out_ref[...] = out.astype(BF16).reshape(out_ref.shape)


def expert_sums(rows, grads, own_acts, peer_acts, own, peer):
    sources, lines, width = rows.shape
    segments, triple = (lines // RANK_ROWS, own.shape[-1])
    hidden = triple // 3
    count = sources * RANK_ROWS
    wide = pl.BlockSpec((sources, RANK_ROWS, width), lambda s: (0, s, 0))
    down = pl.BlockSpec((1, width, hidden), lambda s: (s, 0, 2))
    act = pl.BlockSpec((1, count, triple), lambda s: (s, 0, 0))
    return pl.pallas_call(
        expert_sums_kernel,
        grid=(segments,),
        in_specs=[wide, wide, act, act, down, down],
        out_specs=[pl.BlockSpec((1, width, triple), lambda s: (s, 0, 0))]
        + [pl.BlockSpec((1, width, hidden), lambda s: (s, 0, 0))] * 3
        + [wide],
        out_shape=[jax.ShapeDtypeStruct((segments, width, triple), BF16)]
        + [jax.ShapeDtypeStruct((segments, width, hidden), BF16)] * 3
        + [jax.ShapeDtypeStruct(rows.shape, BF16)],
        compiler_params=pltpu.CompilerParams(vmem_limit_bytes=60 << 20),
        cost_estimate=pl.CostEstimate(
            flops=6 * sources * lines * width * triple,
            bytes_accessed=6 * sources * lines * width + 5 * segments * width * triple,
            transcendentals=0,
        ),
    )(rows, grads, own_acts, peer_acts, own, peer)


def both_cores_kernel(own_ref, *refs):
    out_ref = refs[-1]
    hidden = refs[0].shape[-1]

    @pl.when(pl.program_id(0) < SEGMENTS)
    def _():
        for kind, peer_ref in enumerate(refs[:-1]):
            here = slice(kind * hidden, (kind + 1) * hidden)
            total = own_ref[0, :, here].astype(F32) + peer_ref[0].astype(F32)
            out_ref[0, :, here] = total.astype(BF16)

    @pl.when(pl.program_id(0) >= SEGMENTS)
    def _():
        out_ref[...] = jnp.zeros_like(out_ref)


def both_cores(own, peers, slots):
    segments, width, triple = own.shape
    rows = width // 2
    last = segments - 1
    part = pl.BlockSpec((1, rows, triple), lambda s, r: (jnp.minimum(s, last), r, 0))
    thin = pl.BlockSpec((1, rows, triple // 3), lambda s, r: (jnp.minimum(s, last), r, 0))
    return pl.pallas_call(
        both_cores_kernel,
        grid=(slots, 2),
        in_specs=[part] + [thin] * 3,
        out_specs=pl.BlockSpec((1, rows, triple), lambda s, r: (s, r, 0)),
        out_shape=jax.ShapeDtypeStruct((slots, width, triple), BF16),
        cost_estimate=pl.CostEstimate(
            flops=slots * width * triple, bytes_accessed=6 * slots * width * triple, transcendentals=0
        ),
    )(own, *peers)


def weight_grads_kernel(normed_ref, qkv_ref, attended_ref, branch_ref, extra_ref, out_ref):
    width = branch_ref.shape[1]
    columns = width + qkv_ref.shape[0]
    out_ref[:, :width] = contract(attended_ref[...], branch_ref[...], NN).astype(BF16)
    out_ref[:, width:columns] = contract(normed_ref[...], qkv_ref[...], ((0,), (1,))).astype(BF16)
    out_ref[:, columns:] = jnp.transpose(extra_ref[...]).astype(BF16)


def weight_grads(normed, grad_qkv, attended, branch, extra):
    tok, model = normed.shape
    width, columns = (attended.shape[0], grad_qkv.shape[0])
    half = width // LANES
    every = width + columns + MORE
    return pl.pallas_call(
        weight_grads_kernel,
        grid=(model // LANES,),
        in_specs=[
            pl.BlockSpec((tok, LANES), lambda i: (0, i)),
            pl.BlockSpec((columns, tok), lambda i: (0, 0)),
            pl.BlockSpec((LANES, tok), lambda i: (i % half, 0)),
            pl.BlockSpec((tok, width), lambda i: (0, i // half)),
            pl.BlockSpec((MORE, LANES), lambda i: (0, i)),
        ],
        out_specs=pl.BlockSpec((LANES, every), lambda i: (i, 0)),
        out_shape=jax.ShapeDtypeStruct((model, every), BF16),
        cost_estimate=pl.CostEstimate(
            flops=2 * tok * model * every,
            bytes_accessed=2 * model * every + 4 * tok * model,
            transcendentals=0,
        ),
    )(normed, grad_qkv, attended, branch, extra)


def unpack_kernel(
    in_ref, query_ref, key_ref, sq_ref, sk_ref,
    wo_ref, wq_ref, wk_ref, wv_ref, sum_ref, cq_ref, ck_ref,
):
    at = 0
    for target in (wo_ref, wq_ref, wk_ref, wv_ref):
        size = target.shape[1]
        target[...] = in_ref[:, at : at + size].astype(F32)
        at += size
    sum_ref[...] = jnp.transpose(in_ref[:, at:].astype(F32))[: sum_ref.shape[0]]
    cq_ref[...] = (query_ref[...].astype(F32) * sq_ref[...]).astype(BF16)
    ck_ref[...] = (key_ref[...].astype(F32) * sk_ref[...]).astype(BF16)


def unpack(summed, w_query, w_key, scale_query, scale_key):
    total, every = summed.shape
    width, narrow = (w_query.shape[1], w_key.shape[1])
    steps = total // LANES
    wide = pl.BlockSpec((LANES, width), lambda i: (i, 0))
    thin = pl.BlockSpec((LANES, narrow), lambda i: (i, 0))
    return pl.pallas_call(
        unpack_kernel,
        grid=(steps,),
        in_specs=[
            pl.BlockSpec((LANES, every), lambda i: (i, 0)),
            wide,
            thin,
            pl.BlockSpec((1, width), lambda i: (0, 0)),
            pl.BlockSpec((1, narrow), lambda i: (0, 0)),
        ],
        out_specs=[
            pl.BlockSpec((LANES, width), lambda i: (i % (steps // 2), i // (steps // 2))),
            wide,
            thin,
            thin,
            pl.BlockSpec((8, LANES), lambda i: (0, i)),
            wide,
            thin,
        ],
        out_shape=[
            jax.ShapeDtypeStruct((total // 2, 2 * width), F32),
            jax.ShapeDtypeStruct((total, width), F32),
            jax.ShapeDtypeStruct((total, narrow), F32),
            jax.ShapeDtypeStruct((total, narrow), F32),
            jax.ShapeDtypeStruct((8, total), F32),
            jax.ShapeDtypeStruct((total, width), BF16),
            jax.ShapeDtypeStruct((total, narrow), BF16),
        ],
        compiler_params=pltpu.CompilerParams(vmem_limit_bytes=32 << 20),
        cost_estimate=pl.CostEstimate(
            flops=total * every, bytes_accessed=8 * total * every, transcendentals=0
        ),
    )(summed, w_query, w_key, scale_query, scale_key)


def rms_scale(values):
    return lax.rsqrt(jnp.mean(values * values, axis=-1, keepdims=True) + EPS)


def norm_back(grad_normed, hidden, inverse, gain):
    weighted = grad_normed * gain
    grad_gain = jnp.sum(grad_normed * hidden * inverse, axis=0)
    grad_hidden = inverse * weighted - hidden * inverse**3 * jnp.mean(
        weighted * hidden, axis=-1, keepdims=True
    )
    return (grad_hidden, grad_gain)


def shards(
    tokens,
    out_grad,
    norm1_gain,
    norm2_gain,
    w_query,
    w_key,
    w_value,
    w_out,
    w_gate,
    w_up,
    w_down,
    route_ids,
    route_logits,
    seq_ids,
    piece_ids,
    clip_limit,
):
    tok_dev, model_width = tokens.shape
    dp_size = lax.axis_size("dp")
    tensor_size = lax.axis_size("tensor")
    core = lax.axis_index("tensor")
    local_heads = w_query.shape[1] // HD
    local_kv = w_key.shape[1] // HD
    group = local_heads // local_kv
    plane_groups = [list(range(at, at + PLANE)) for at in range(0, dp_size, PLANE)]
    column_groups = [list(range(at, dp_size, PLANE)) for at in range(PLANE)]

    packed_w = pack_weights(w_gate[0], w_up[0], w_down[0])
    own = lax.all_gather(packed_w, "dp", axis=0, axis_index_groups=column_groups)

    picks = route_ids.T
    logits = route_logits.T
    gate_exp = jnp.exp(logits - jnp.max(logits, axis=0, keepdims=True))
    gates = gate_exp / jnp.sum(gate_exp, axis=0, keepdims=True)
    number = jnp.arange(PLANE * SEGMENTS, dtype=jnp.int32)
    number = number % SEGMENTS * PLANE + number // SEGMENTS
    same = picks[None] == number[:, None, None]
    member = jnp.any(same, axis=1)
    gate_of = jnp.sum(jnp.where(same, gates[None], 0.0), axis=1)
    place = jnp.arange(tok_dev, dtype=jnp.int32)
    before = (place[:, None] < place[None, :]).astype(BF16)
    rank = contract(member.astype(BF16), before, NN)
    rank = jnp.where(member, rank, -1.0)
    wanted = (tensor_size * jnp.arange(RANK_ROWS, dtype=jnp.int32) + core).astype(F32)
    chosen = rank[:, None, :] == wanted[None, :, None]
    pick = chosen.astype(BF16).reshape(-1, tok_dev)
    gated = jnp.where(chosen, gate_of[:, None, :], 0.0)
    slot_gate = jnp.sum(gated, axis=2).reshape(-1, 1)
    gated = gated.astype(BF16).reshape(-1, tok_dev)

    def in_plane(rows):
        rows = rows.reshape(PLANE, -1, model_width)
        return lax.all_to_all(rows, "dp", 0, 0, tiled=True, axis_index_groups=plane_groups)

    grad_rows = (contract(pick, out_grad, NN) * slot_gate).astype(BF16)

    cosine, sine = rope_tables(tok_dev, dp_size)
    x_float = tokens.astype(F32)
    inverse1 = rms_scale(x_float)
    normed1 = (x_float * inverse1 * norm1_gain).astype(BF16)
    query = rotate(contract(w_query, normed1, ((0,), (1,))), cosine, sine)
    query = (query * (HD**-0.5)).astype(BF16)
    key = rotate(contract(w_key, normed1, ((0,), (1,))), cosine, sine).astype(BF16)
    value = contract(w_value, normed1, ((0,), (1,))).astype(BF16)
    side = jnp.concatenate(
        [(seq_ids + 1)[None], piece_ids[None], jnp.zeros((AUX - 2, tok_dev), jnp.int32)]
    ).astype(BF16)
    block = jnp.concatenate([key, value, side])
    blocks = tuple(passed_along(block, hop) for hop in range(HOPS, 0, -1)) + (block,)
    blocks, grad_rows = lax.optimization_barrier((blocks, grad_rows))
    grad_rows = in_plane(grad_rows)
    attended, log_total, peaks = attend(query, blocks, group)
    attn_part = contract(attended, w_out, TN)
    hidden1 = x_float + (attn_part + swapped(attn_part))
    inverse2 = rms_scale(hidden1)
    normed2 = (hidden1 * inverse2 * norm2_gain).astype(BF16)

    rows_out = contract(pick, normed2, NN).astype(BF16)
    rows_out = after(rows_out, grad_rows)
    own = after(own, rows_out)
    peer = swapped(own)
    rows_in = in_plane(rows_out)
    back, own_acts, peer_acts = expert_back(rows_in, grad_rows, own, peer)

    def combined(weights, rows):
        part = contract(weights, rows.reshape(-1, model_width), TN).astype(BF16)
        return part.astype(F32) + swapped(part).astype(F32)

    sum_own, *sum_peer, expert_out = expert_sums(rows_in, grad_rows, own_acts, peer_acts, own, peer)
    sums = both_cores(sum_own, [swapped(part) for part in sum_peer], dp_size // PLANE)
    back = in_plane(back)
    expert_out = in_plane(after(expert_out, back))
    grad_normed2 = combined(pick, after(back, sums))
    sums = lax.psum_scatter(
        sums, "dp", scatter_dimension=0, tiled=True, axis_index_groups=column_groups
    )

    grad_top = out_grad.astype(F32)
    grad_from_norm2, grad_gain2 = norm_back(grad_normed2, hidden1, inverse2, norm2_gain)
    grad_hidden1 = grad_top + grad_from_norm2
    grad_branch = grad_hidden1.astype(BF16)
    grad_attended = contract(w_out, grad_branch, NT).astype(BF16)
    grad_query_pre, *grad_blocks = attend_back(
        query, grad_attended, log_total, cosine, sine, blocks, group
    )
    returned = [
        passed_along(grad_blocks[number], -hop) for number, hop in enumerate(range(HOPS, 0, -1))
    ]
    kv_total = grad_blocks[-1]
    for part in returned:
        kv_total = kv_total + part.astype(F32)
    kv_rows = local_kv * HD
    grad_key_pre = rotate(kv_total[:kv_rows], cosine, -sine).astype(BF16)
    grad_value = kv_total[kv_rows:].astype(BF16)

    grad_norm1_part = (
        contract(grad_query_pre, w_query, ((0,), (1,)))
        + contract(grad_key_pre, w_key, ((0,), (1,)))
        + contract(grad_value, w_value, ((0,), (1,)))
    ).astype(BF16)

    grad_normed1 = grad_norm1_part.astype(F32) + swapped(grad_norm1_part).astype(F32)
    grad_from_norm1, grad_gain1 = norm_back(grad_normed1, x_float, inverse1, norm1_gain)
    input_grad = grad_hidden1 + grad_from_norm1
    peak = jnp.max(peaks, axis=1)
    peak_high = peak.astype(BF16).astype(F32)
    places = jnp.arange(dp_size)[:, None] == lax.axis_index("dp")
    peak_row = jnp.where(places, jnp.concatenate([peak_high, peak - peak_high])[None], 0.0)
    extra = jnp.stack([grad_gain1, grad_gain2, peak_row.reshape(-1)])
    extra = jnp.pad(extra, ((0, MORE - len(extra)), (0, 0)))
    grad_qkv = jnp.concatenate([grad_query_pre, grad_key_pre, grad_value])
    parts = weight_grads(normed1, grad_qkv, attended, grad_branch, extra)
    parts, sums, expert_out = lax.optimization_barrier((parts, sums, expert_out))
    summed = lax.psum(parts, "dp")
    output = (hidden1 + combined(gated, expert_out)).astype(BF16)
    grad_gate, grad_up, grad_down = jnp.split(sums[0].astype(F32), 3, axis=1)
    grad_down = grad_down.T
    all_peaks = summed[:, 2 - MORE].astype(F32).reshape(dp_size, 2 * local_heads)
    head_peaks = jnp.max(all_peaks[:, :local_heads] + all_peaks[:, local_heads:], axis=0)
    factor = clip_limit / jnp.maximum(head_peaks, clip_limit)
    key_factor = jnp.min(factor.reshape(local_kv, group), axis=1)
    scale_query = jnp.repeat(jnp.sqrt(factor), HD)[None, :]
    scale_key = jnp.repeat(jnp.sqrt(key_factor), HD)[None, :]
    grad_wo, grad_wq, grad_wk, grad_wv, totals, clipped_query, clipped_key = unpack(
        summed, w_query, w_key, scale_query, scale_key
    )
    return (
        output,
        input_grad,
        grad_wq,
        grad_wk,
        grad_wv,
        grad_wo,
        totals[0],
        totals[1],
        grad_gate[None],
        grad_up[None],
        grad_down[None],
        clipped_query,
        clipped_key,
        head_peaks,
    )


def solution(mesh):
    in_specs = (
        P("dp", None),
        P("dp", None),
        P(),
        P(),
        P(None, "tensor"),
        P(None, "tensor"),
        P(None, "tensor"),
        P("tensor", None),
        P("dp", None, "tensor"),
        P("dp", None, "tensor"),
        P("dp", "tensor", None),
        P("dp", None),
        P("dp", None),
        P("dp"),
        P("dp"),
        P("tensor"),
    )
    out_specs = (
        P("dp", None),
        P("dp", None),
        P(None, "tensor"),
        P(None, "tensor"),
        P(None, "tensor"),
        P("tensor", None),
        P(),
        P(),
        P("dp", None, "tensor"),
        P("dp", None, "tensor"),
        P("dp", "tensor", None),
        P(None, "tensor"),
        P(None, "tensor"),
        P("tensor"),
    )
    return jax.shard_map(shards, mesh=mesh, in_specs=in_specs, out_specs=out_specs, check_vma=False)
```

```python
import functools
import math

import jax
import jax.numpy as jnp
import numpy as np
from jax import lax
from jax.experimental import pallas as pl
from jax.experimental.pallas import tpu as pltpu
from jax.sharding import PartitionSpec as P

HD = 64
TOP = 8
CAP = 64
HOPS = 4
RANK_ROWS = 32
PLANE = 16
SEGMENTS = 3
EARLY = 2
AUX = 16
LANES = 256
MORE = 128

EPS = 1e-06
ROPE_BASE = 10000.0
NEG_FILL = -1e30
BF16 = jnp.bfloat16
F32 = jnp.float32


def contract(left, right, dims):
    return lax.dot_general(left, right, (dims, ((), ())), preferred_element_type=F32)


NN = ((1,), (0,))
NT = ((1,), (1,))
TN = ((0,), (0,))


def swapped(array):
    return lax.ppermute(array, "tensor", [(0, 1), (1, 0)])


def after(array, other):
    return lax.optimization_barrier((array, other))[0]


def passed_along(value, steps):
    count = lax.axis_size("dp")
    first, last = (max(0, -steps), min(count, count - steps))
    return lax.ppermute(value, "dp", [(s, s + steps) for s in range(first, last)])


def rope_tables(count, dp_size):
    freq = np.exp(np.arange(HD // 2) * (-2.0 * math.log(ROPE_BASE) / HD))
    base = np.arange(dp_size)[:, None] * count * freq[None, :]
    local = freq[:, None] * np.arange(count)[None, :]
    index = lax.axis_index("dp")
    cos_base = jnp.asarray(np.cos(base), F32)[index][:, None]
    sin_base = jnp.asarray(np.sin(base), F32)[index][:, None]
    cos_local, sin_local = (jnp.asarray(np.cos(local), F32), jnp.asarray(np.sin(local), F32))
    return (
        cos_base * cos_local - sin_base * sin_local,
        sin_base * cos_local + cos_base * sin_local,
    )


def rotate(values, cosine, sine):
    half = HD // 2
    heads = values.reshape(-1, HD, values.shape[-1])
    first, second = (heads[:, :half], heads[:, half:])
    turned = jnp.concatenate(
        [first * cosine - second * sine, second * cosine + first * sine], axis=1
    )
    return turned.reshape(values.shape)


def fill_bias(blocks, bias):
    tok = bias.shape[1]
    rows = blocks[-1].shape[0] - AUX
    own = blocks[-1][rows:, :].astype(F32)
    seq_q, piece_q = (own[0:1, :], own[1:2, :])
    for number, block in enumerate(blocks):
        side = jnp.transpose(block[rows:, :].astype(F32))
        keep = side[:, 0:1] == seq_q
        if number == len(blocks) - 1:
            at_key = lax.broadcasted_iota(jnp.int32, (tok, tok), 0)
            at_query = lax.broadcasted_iota(jnp.int32, (tok, tok), 1)
            piece = (side[:, 1:2] == piece_q) & (piece_q > 0.0)
            keep = keep & ((at_key <= at_query) | piece)
        bias[number * tok : (number + 1) * tok, :] = jnp.where(keep, 0.0, NEG_FILL)


def all_keys(blocks, start):
    return jnp.concatenate([block[pl.ds(start, HD), :] for block in blocks], axis=1)


def attend_kernel(group, q_ref, k4, k3, k2, k1, k0, out_ref, log_ref, peak_ref, bias):
    blocks = (k4, k3, k2, k1, k0)
    fill_bias(blocks, bias)
    kv_rows = (k0.shape[0] - AUX) // 2

    def one_group(g, _):
        at = pl.multiple_of(g * HD, HD)
        keys = all_keys(blocks, at)
        values = all_keys(blocks, kv_rows + at)
        for j in range(group):
            head = g * group + j
            here = pl.ds(pl.multiple_of(head * HD, HD), HD)
            scores = contract(keys, q_ref[here, :], TN) + bias[...]
            peak = jnp.max(scores, axis=0, keepdims=True)
            weight = jnp.exp(scores - peak)
            total = jnp.sum(weight, axis=0, keepdims=True)
            mixed = contract(values, weight.astype(BF16), NN) * (1.0 / total)
            out_ref[here, :] = mixed.astype(BF16)
            log_ref[pl.ds(head, 1), :] = peak + jnp.log(total)
            peak_ref[pl.ds(head, 1), :] = peak
        return 0

    lax.fori_loop(0, kv_rows // HD, one_group, 0)


def attend(q, blocks, group):
    rows, tok = q.shape
    heads = rows // HD
    return pl.pallas_call(
        functools.partial(attend_kernel, group),
        out_shape=(
            jax.ShapeDtypeStruct((rows, tok), BF16),
            jax.ShapeDtypeStruct((heads, tok), F32),
            jax.ShapeDtypeStruct((heads, tok), F32),
        ),
        scratch_shapes=[pltpu.VMEM((len(blocks) * tok, tok), F32)],
        compiler_params=pltpu.CompilerParams(vmem_limit_bytes=48 << 20),
        cost_estimate=pl.CostEstimate(
            flops=4 * rows * tok * tok * len(blocks),
            bytes_accessed=4 * rows * tok + 2 * len(blocks) * 528 * tok,
            transcendentals=heads * tok * tok * len(blocks),
        ),
    )(q, *blocks)


def attend_back_kernel(
    group, q_ref, g_ref, log_ref, cos_ref, sin_ref, k4, k3, k2, k1, k0,
    dq_ref, d4, d3, d2, d1, d0, bias,
):
    blocks = (k4, k3, k2, k1, k0)
    grads = (d4, d3, d2, d1, d0)
    fill_bias(blocks, bias)
    kv_rows = (k0.shape[0] - AUX) // 2
    tok = bias.shape[1]
    half = HD // 2

    def one_group(g, _):
        at = pl.multiple_of(g * HD, HD)
        keys = all_keys(blocks, at)
        values = all_keys(blocks, kv_rows + at)
        key_sum = value_sum = None
        for j in range(group):
            head = g * group + j
            start = pl.multiple_of(head * HD, HD)
            query, grad = (q_ref[pl.ds(start, HD), :], g_ref[pl.ds(start, HD), :])
            scores = contract(keys, query, TN) + bias[...]
            probs = jnp.exp(scores - log_ref[pl.ds(head, 1), :])
            grad_probs = contract(values, grad, TN)
            delta = jnp.sum(probs * grad_probs, axis=0, keepdims=True)
            grad_scores = (probs * (grad_probs - delta)).astype(BF16)
            key_part = contract(query, grad_scores, NT)
            value_part = contract(grad, probs.astype(BF16), NT)
            key_sum = key_part if key_sum is None else key_sum + key_part
            value_sum = value_part if value_sum is None else value_sum + value_part
            turned = contract(keys, grad_scores, NN) * (HD**-0.5)
            first, second = (turned[:half], turned[half:])
            cosine, sine = (cos_ref[...], sin_ref[...])
            dq_ref[pl.ds(start, half), :] = (first * cosine + second * sine).astype(BF16)
            dq_ref[pl.ds(start + half, half), :] = (second * cosine - first * sine).astype(BF16)
        for number, grad_ref in enumerate(grads):
            piece = slice(number * tok, (number + 1) * tok)
            grad_ref[pl.ds(at, HD), :] = key_sum[:, piece].astype(grad_ref.dtype)
            grad_ref[pl.ds(kv_rows + at, HD), :] = value_sum[:, piece].astype(grad_ref.dtype)
        return 0

    lax.fori_loop(0, kv_rows // HD, one_group, 0)


def attend_back(q, grad, log_total, cosine, sine, blocks, group):
    rows, tok = q.shape
    kv = blocks[0].shape[0] - AUX
    return pl.pallas_call(
        functools.partial(attend_back_kernel, group),
        out_shape=(
            jax.ShapeDtypeStruct((rows, tok), BF16),
            *(jax.ShapeDtypeStruct((kv, tok), BF16) for _ in blocks[1:]),
            jax.ShapeDtypeStruct((kv, tok), F32),
        ),
        scratch_shapes=[pltpu.VMEM((len(blocks) * tok, tok), F32)],
        compiler_params=pltpu.CompilerParams(vmem_limit_bytes=48 << 20),
        cost_estimate=pl.CostEstimate(
            flops=500 * rows * tok * tok * len(blocks),
            bytes_accessed=6 * rows * tok + 4 * len(blocks) * 528 * tok,
            transcendentals=rows // HD * tok * tok * len(blocks),
        ),
    )(q, grad, log_total, cosine, sine, *blocks)


def pack_weights_kernel(gate_ref, up_ref, down_ref, out_ref):
    hidden = gate_ref.shape[1]
    out_ref[:, :hidden] = gate_ref[...]
    out_ref[:, hidden : 2 * hidden] = up_ref[...]
    out_ref[:, 2 * hidden :] = jnp.transpose(down_ref[...].astype(F32)).astype(BF16)


def pack_weights(gate, up, down):
    width, hidden = gate.shape
    thin = pl.BlockSpec((LANES, hidden), lambda i: (i, 0))
    return pl.pallas_call(
        pack_weights_kernel,
        grid=(width // LANES,),
        in_specs=[thin, thin, pl.BlockSpec((hidden, LANES), lambda i: (0, i))],
        out_specs=pl.BlockSpec((LANES, 3 * hidden), lambda i: (i, 0)),
        out_shape=jax.ShapeDtypeStruct((width, 3 * hidden), BF16),
        cost_estimate=pl.CostEstimate(
            flops=width * hidden, bytes_accessed=12 * width * hidden, transcendentals=0
        ),
    )(gate, up, down)


def expert_kernel(x_ref, g_ref, own_ref, peer_ref, dx_ref, own_acts, peer_acts):
    width = x_ref.shape[-1]
    rows, grads = (x_ref[...].reshape(-1, width), g_ref[...].reshape(-1, width))
    hidden = own_ref.shape[-1] // 3
    back = None
    for weights, acts in ((own_ref, own_acts), (peer_ref, peer_acts)):
        both = contract(rows, weights[0, :, : 2 * hidden], NN)
        grad_inner = contract(grads, weights[0, :, 2 * hidden :], NN)
        gate_act, up_act = (both[:, :hidden], both[:, hidden:])
        sigmoid = 1.0 / (1.0 + jnp.exp(-gate_act))
        silu = gate_act * sigmoid
        dgate = grad_inner * up_act * (sigmoid * (1.0 + gate_act * (1.0 - sigmoid)))
        acts[0, :, :hidden] = dgate.astype(BF16)
        acts[0, :, hidden : 2 * hidden] = (grad_inner * silu).astype(BF16)
        acts[0, :, 2 * hidden :] = (silu * up_act).astype(BF16)
        part = contract(acts[0, :, : 2 * hidden], weights[0, :, : 2 * hidden], NT)
        back = part if back is None else back + part
    dx_ref[...] = back.astype(BF16).reshape(dx_ref.shape)


def expert_back(rows, grads, own, peer):
    sources, lines, width = rows.shape
    segments, triple = (lines // RANK_ROWS, own.shape[-1])
    count = sources * RANK_ROWS
    wide = pl.BlockSpec((sources, RANK_ROWS, width), lambda s: (0, s, 0))
    weight = pl.BlockSpec((1, width, triple), lambda s: (s, 0, 0))
    act = pl.BlockSpec((1, count, triple), lambda s: (s, 0, 0))
    return pl.pallas_call(
        expert_kernel,
        grid=(segments,),
        in_specs=[wide, wide, weight, weight],
        out_specs=[wide, act, act],
        out_shape=[
            jax.ShapeDtypeStruct(rows.shape, BF16),
            jax.ShapeDtypeStruct((segments, count, triple), BF16),
            jax.ShapeDtypeStruct((segments, count, triple), BF16),
        ],
        compiler_params=pltpu.CompilerParams(vmem_limit_bytes=56 << 20),
        cost_estimate=pl.CostEstimate(
            flops=7 * sources * lines * width * triple,
            bytes_accessed=6 * sources * lines * width + 4 * segments * width * triple,
            transcendentals=2 * sources * lines * triple // 3,
        ),
    )(rows, grads, own, peer)


def expert_sums_kernel(x_ref, g_ref, own_acts, peer_acts, own_ref, peer_ref, sum_own, *outs):
    width = x_ref.shape[-1]
    rows, grads = (x_ref[...].reshape(-1, width), g_ref[...].reshape(-1, width))
    hidden = own_ref.shape[-1]
    early_ref, late_ref = outs[3:]
    segment = pl.program_id(0)
    out = None
    for side, (acts, weights) in enumerate(((own_acts, own_ref), (peer_acts, peer_ref))):
        first = contract(rows, acts[0, :, : 2 * hidden], TN).astype(BF16)
        second = contract(grads, acts[0, :, 2 * hidden :], TN).astype(BF16)
        if side == 0:
            sum_own[0, :, : 2 * hidden] = first
            sum_own[0, :, 2 * hidden :] = second
        else:
            outs[0][0] = first[:, :hidden]
            outs[1][0] = first[:, hidden:]
            outs[2][0] = second
        part = contract(acts[0, :, 2 * hidden :], weights[0], NT)
        out = part if out is None else out + part
    out = out.astype(BF16).reshape(x_ref.shape)

    @pl.when(segment < EARLY)
    def _():
        early_ref[...] = out

    @pl.when(segment >= EARLY)
    def _():
        late_ref[...] = out


def expert_sums(rows, grads, own_acts, peer_acts, own, peer):
    sources, lines, width = rows.shape
    segments, triple = (lines // RANK_ROWS, own.shape[-1])
    hidden = triple // 3
    count = sources * RANK_ROWS
    block = (sources, RANK_ROWS, width)
    wide = pl.BlockSpec(block, lambda s: (0, s, 0))
    down = pl.BlockSpec((1, width, hidden), lambda s: (s, 0, 2))
    act = pl.BlockSpec((1, count, triple), lambda s: (s, 0, 0))
    return pl.pallas_call(
        expert_sums_kernel,
        grid=(segments,),
        in_specs=[wide, wide, act, act, down, down],
        out_specs=[pl.BlockSpec((1, width, triple), lambda s: (s, 0, 0))]
        + [pl.BlockSpec((1, width, hidden), lambda s: (s, 0, 0))] * 3
        + [
            pl.BlockSpec(block, lambda s: (0, jnp.minimum(s, EARLY - 1), 0)),
            pl.BlockSpec(block, lambda s: (0, jnp.maximum(s - EARLY, 0), 0)),
        ],
        out_shape=[jax.ShapeDtypeStruct((segments, width, triple), BF16)]
        + [jax.ShapeDtypeStruct((segments, width, hidden), BF16)] * 3
        + [
            jax.ShapeDtypeStruct((sources, EARLY * RANK_ROWS, width), BF16),
            jax.ShapeDtypeStruct((sources, (segments - EARLY) * RANK_ROWS, width), BF16),
        ],
        compiler_params=pltpu.CompilerParams(vmem_limit_bytes=60 << 20),
        cost_estimate=pl.CostEstimate(
            flops=6 * sources * lines * width * triple,
            bytes_accessed=6 * sources * lines * width + 5 * segments * width * triple,
            transcendentals=0,
        ),
    )(rows, grads, own_acts, peer_acts, own, peer)


def both_cores_kernel(own_ref, *refs):
    out_ref = refs[-1]
    hidden = refs[0].shape[-1]

    @pl.when(pl.program_id(0) < SEGMENTS)
    def _():
        for kind, peer_ref in enumerate(refs[:-1]):
            here = slice(kind * hidden, (kind + 1) * hidden)
            total = own_ref[0, :, here].astype(F32) + peer_ref[0].astype(F32)
            out_ref[0, :, here] = total.astype(BF16)

    @pl.when(pl.program_id(0) >= SEGMENTS)
    def _():
        out_ref[...] = jnp.zeros_like(out_ref)


def both_cores(own, peers, slots):
    segments, width, triple = own.shape
    rows = width // 2
    last = segments - 1
    part = pl.BlockSpec((1, rows, triple), lambda s, r: (jnp.minimum(s, last), r, 0))
    thin = pl.BlockSpec((1, rows, triple // 3), lambda s, r: (jnp.minimum(s, last), r, 0))
    return pl.pallas_call(
        both_cores_kernel,
        grid=(slots, 2),
        in_specs=[part] + [thin] * 3,
        out_specs=pl.BlockSpec((1, rows, triple), lambda s, r: (s, r, 0)),
        out_shape=jax.ShapeDtypeStruct((slots, width, triple), BF16),
        cost_estimate=pl.CostEstimate(
            flops=slots * width * triple, bytes_accessed=6 * slots * width * triple, transcendentals=0
        ),
    )(own, *peers)


def weight_grads_kernel(normed_ref, qkv_ref, attended_ref, branch_ref, extra_ref, out_ref):
    width = branch_ref.shape[1]
    columns = width + qkv_ref.shape[0]
    out_ref[:, :width] = contract(attended_ref[...], branch_ref[...], NN).astype(BF16)
    out_ref[:, width:columns] = contract(normed_ref[...], qkv_ref[...], ((0,), (1,))).astype(BF16)
    out_ref[:, columns:] = jnp.transpose(extra_ref[...]).astype(BF16)


def weight_grads(normed, grad_qkv, attended, branch, extra):
    tok, model = normed.shape
    width, columns = (attended.shape[0], grad_qkv.shape[0])
    half = width // LANES
    every = width + columns + MORE
    return pl.pallas_call(
        weight_grads_kernel,
        grid=(model // LANES,),
        in_specs=[
            pl.BlockSpec((tok, LANES), lambda i: (0, i)),
            pl.BlockSpec((columns, tok), lambda i: (0, 0)),
            pl.BlockSpec((LANES, tok), lambda i: (i % half, 0)),
            pl.BlockSpec((tok, width), lambda i: (0, i // half)),
            pl.BlockSpec((MORE, LANES), lambda i: (0, i)),
        ],
        out_specs=pl.BlockSpec((LANES, every), lambda i: (i, 0)),
        out_shape=jax.ShapeDtypeStruct((model, every), BF16),
        cost_estimate=pl.CostEstimate(
            flops=2 * tok * model * every,
            bytes_accessed=2 * model * every + 4 * tok * model,
            transcendentals=0,
        ),
    )(normed, grad_qkv, attended, branch, extra)


def unpack_kernel(
    in_ref, query_ref, key_ref, sq_ref, sk_ref,
    wo_ref, wq_ref, wk_ref, wv_ref, sum_ref, cq_ref, ck_ref,
):
    at = 0
    for target in (wo_ref, wq_ref, wk_ref, wv_ref):
        size = target.shape[1]
        target[...] = in_ref[:, at : at + size].astype(F32)
        at += size
    sum_ref[...] = jnp.transpose(in_ref[:, at:].astype(F32))[: sum_ref.shape[0]]
    cq_ref[...] = (query_ref[...].astype(F32) * sq_ref[...]).astype(BF16)
    ck_ref[...] = (key_ref[...].astype(F32) * sk_ref[...]).astype(BF16)


def unpack(summed, w_query, w_key, scale_query, scale_key):
    total, every = summed.shape
    width, narrow = (w_query.shape[1], w_key.shape[1])
    steps = total // LANES
    wide = pl.BlockSpec((LANES, width), lambda i: (i, 0))
    thin = pl.BlockSpec((LANES, narrow), lambda i: (i, 0))
    return pl.pallas_call(
        unpack_kernel,
        grid=(steps,),
        in_specs=[
            pl.BlockSpec((LANES, every), lambda i: (i, 0)),
            wide,
            thin,
            pl.BlockSpec((1, width), lambda i: (0, 0)),
            pl.BlockSpec((1, narrow), lambda i: (0, 0)),
        ],
        out_specs=[
            pl.BlockSpec((LANES, width), lambda i: (i % (steps // 2), i // (steps // 2))),
            wide,
            thin,
            thin,
            pl.BlockSpec((8, LANES), lambda i: (0, i)),
            wide,
            thin,
        ],
        out_shape=[
            jax.ShapeDtypeStruct((total // 2, 2 * width), F32),
            jax.ShapeDtypeStruct((total, width), F32),
            jax.ShapeDtypeStruct((total, narrow), F32),
            jax.ShapeDtypeStruct((total, narrow), F32),
            jax.ShapeDtypeStruct((8, total), F32),
            jax.ShapeDtypeStruct((total, width), BF16),
            jax.ShapeDtypeStruct((total, narrow), BF16),
        ],
        compiler_params=pltpu.CompilerParams(vmem_limit_bytes=60 << 20),
        cost_estimate=pl.CostEstimate(
            flops=total * every, bytes_accessed=8 * total * every, transcendentals=0
        ),
    )(summed, w_query, w_key, scale_query, scale_key)


def rms_scale(values):
    return lax.rsqrt(jnp.mean(values * values, axis=-1, keepdims=True) + EPS)


def norm_back(grad_normed, hidden, inverse, gain):
    weighted = grad_normed * gain
    grad_gain = jnp.sum(grad_normed * hidden * inverse, axis=0)
    grad_hidden = inverse * weighted - hidden * inverse**3 * jnp.mean(
        weighted * hidden, axis=-1, keepdims=True
    )
    return (grad_hidden, grad_gain)


def shards(
    tokens,
    out_grad,
    norm1_gain,
    norm2_gain,
    w_query,
    w_key,
    w_value,
    w_out,
    w_gate,
    w_up,
    w_down,
    route_ids,
    route_logits,
    seq_ids,
    piece_ids,
    clip_limit,
):
    tok_dev, model_width = tokens.shape
    dp_size = lax.axis_size("dp")
    tensor_size = lax.axis_size("tensor")
    core = lax.axis_index("tensor")
    local_heads = w_query.shape[1] // HD
    local_kv = w_key.shape[1] // HD
    group = local_heads // local_kv
    plane_groups = [list(range(at, at + PLANE)) for at in range(0, dp_size, PLANE)]
    column_groups = [list(range(at, dp_size, PLANE)) for at in range(PLANE)]


    picks = route_ids.T
    logits = route_logits.T
    gate_exp = jnp.exp(logits - jnp.max(logits, axis=0, keepdims=True))
    gates = gate_exp / jnp.sum(gate_exp, axis=0, keepdims=True)
    number = jnp.arange(PLANE * SEGMENTS, dtype=jnp.int32)
    number = number % SEGMENTS * PLANE + number // SEGMENTS
    same = picks[None] == number[:, None, None]
    member = jnp.any(same, axis=1)
    gate_of = jnp.sum(jnp.where(same, gates[None], 0.0), axis=1)
    place = jnp.arange(tok_dev, dtype=jnp.int32)
    before = (place[:, None] < place[None, :]).astype(BF16)
    rank = contract(member.astype(BF16), before, NN)
    rank = jnp.where(member, rank, -1.0)
    wanted = (tensor_size * jnp.arange(RANK_ROWS, dtype=jnp.int32) + core).astype(F32)
    chosen = rank[:, None, :] == wanted[None, :, None]
    pick = chosen.astype(BF16).reshape(-1, tok_dev)
    gated = jnp.where(chosen, gate_of[:, None, :], 0.0)
    slot_gate = jnp.sum(gated, axis=2).reshape(-1, 1)
    gated = gated.astype(BF16).reshape(-1, tok_dev)

    def in_plane(rows):
        rows = rows.reshape(PLANE, -1, model_width)
        return lax.all_to_all(rows, "dp", 0, 0, tiled=True, axis_index_groups=plane_groups)

    grad_rows = (contract(pick, out_grad, NN) * slot_gate).astype(BF16)

    cosine, sine = rope_tables(tok_dev, dp_size)
    x_float = tokens.astype(F32)
    inverse1 = rms_scale(x_float)
    normed1 = (x_float * inverse1 * norm1_gain).astype(BF16)
    query = rotate(contract(w_query, normed1, ((0,), (1,))), cosine, sine)
    query = (query * (HD**-0.5)).astype(BF16)
    key = rotate(contract(w_key, normed1, ((0,), (1,))), cosine, sine).astype(BF16)
    value = contract(w_value, normed1, ((0,), (1,))).astype(BF16)
    side = jnp.concatenate(
        [(seq_ids + 1)[None], piece_ids[None], jnp.zeros((AUX - 2, tok_dev), jnp.int32)]
    ).astype(BF16)
    block = jnp.concatenate([key, value, side])
    blocks = tuple(passed_along(block, hop) for hop in range(HOPS, 0, -1)) + (block,)
    blocks, grad_rows = lax.optimization_barrier((blocks, grad_rows))
    packed_w = pack_weights(w_gate[0], w_up[0], w_down[0])
    own = lax.all_gather(packed_w, "dp", axis=0, axis_index_groups=column_groups)
    grad_rows = in_plane(grad_rows)
    attended, log_total, peaks = attend(query, blocks, group)
    attn_part = contract(attended, w_out, TN)
    hidden1 = x_float + (attn_part + swapped(attn_part))
    inverse2 = rms_scale(hidden1)
    normed2 = (hidden1 * inverse2 * norm2_gain).astype(BF16)

    rows_out = contract(pick, normed2, NN).astype(BF16)
    rows_out = after(rows_out, grad_rows)
    own = after(own, rows_out)
    peer = swapped(own)
    rows_in = in_plane(rows_out)
    back, own_acts, peer_acts = expert_back(rows_in, grad_rows, own, peer)

    def combined(weights, rows):
        part = contract(weights, rows.reshape(-1, model_width), TN).astype(BF16)
        return part.astype(F32) + swapped(part).astype(F32)

    sum_own, *sum_peer, out_early, out_late = expert_sums(rows_in, grad_rows, own_acts, peer_acts, own, peer)
    sums = both_cores(sum_own, [swapped(part) for part in sum_peer], dp_size // PLANE)
    back = in_plane(back)
    out_early = in_plane(after(out_early, back))
    grad_normed2 = combined(pick, after(back, sums))
    sums = lax.psum_scatter(
        sums, "dp", scatter_dimension=0, tiled=True, axis_index_groups=column_groups
    )

    grad_top = out_grad.astype(F32)
    grad_from_norm2, grad_gain2 = norm_back(grad_normed2, hidden1, inverse2, norm2_gain)
    grad_hidden1 = grad_top + grad_from_norm2
    grad_branch = grad_hidden1.astype(BF16)
    grad_attended = contract(w_out, grad_branch, NT).astype(BF16)
    grad_query_pre, *grad_blocks = attend_back(
        query, grad_attended, log_total, cosine, sine, blocks, group
    )
    returned = [
        passed_along(grad_blocks[number], -hop) for number, hop in enumerate(range(HOPS, 0, -1))
    ]
    out_late = in_plane(after(out_late, (returned, out_early)))
    kv_total = grad_blocks[-1]
    for part in returned:
        kv_total = kv_total + part.astype(F32)
    kv_rows = local_kv * HD
    grad_key_pre = rotate(kv_total[:kv_rows], cosine, -sine).astype(BF16)
    grad_value = kv_total[kv_rows:].astype(BF16)

    grad_norm1_part = (
        contract(grad_query_pre, w_query, ((0,), (1,)))
        + contract(grad_key_pre, w_key, ((0,), (1,)))
        + contract(grad_value, w_value, ((0,), (1,)))
    ).astype(BF16)

    grad_normed1 = grad_norm1_part.astype(F32) + swapped(grad_norm1_part).astype(F32)
    grad_from_norm1, grad_gain1 = norm_back(grad_normed1, x_float, inverse1, norm1_gain)
    input_grad = grad_hidden1 + grad_from_norm1
    peak = jnp.max(peaks, axis=1)
    peak_high = peak.astype(BF16).astype(F32)
    places = jnp.arange(dp_size)[:, None] == lax.axis_index("dp")
    peak_row = jnp.where(places, jnp.concatenate([peak_high, peak - peak_high])[None], 0.0)
    extra = jnp.stack([grad_gain1, grad_gain2, peak_row.reshape(-1)])
    extra = jnp.pad(extra, ((0, MORE - len(extra)), (0, 0)))
    grad_qkv = jnp.concatenate([grad_query_pre, grad_key_pre, grad_value])
    parts = weight_grads(normed1, grad_qkv, attended, grad_branch, extra)
    parts, sums, out_early, out_late = lax.optimization_barrier((parts, sums, out_early, out_late))
    summed = lax.psum(parts, "dp")
    expert_out = jnp.concatenate([out_early, out_late], axis=1)
    output = (hidden1 + combined(gated, expert_out)).astype(BF16)
    grad_gate, grad_up, grad_down = jnp.split(sums[0].astype(F32), 3, axis=1)
    grad_down = grad_down.T
    all_peaks = summed[:, 2 - MORE].astype(F32).reshape(dp_size, 2 * local_heads)
    head_peaks = jnp.max(all_peaks[:, :local_heads] + all_peaks[:, local_heads:], axis=0)
    factor = clip_limit / jnp.maximum(head_peaks, clip_limit)
    key_factor = jnp.min(factor.reshape(local_kv, group), axis=1)
    scale_query = jnp.repeat(jnp.sqrt(factor), HD)[None, :]
    scale_key = jnp.repeat(jnp.sqrt(key_factor), HD)[None, :]
    grad_wo, grad_wq, grad_wk, grad_wv, totals, clipped_query, clipped_key = unpack(
        summed, w_query, w_key, scale_query, scale_key
    )
    return (
        output,
        input_grad,
        grad_wq,
        grad_wk,
        grad_wv,
        grad_wo,
        totals[0],
        totals[1],
        grad_gate[None],
        grad_up[None],
        grad_down[None],
        clipped_query,
        clipped_key,
        head_peaks,
    )


def solution(mesh):
    in_specs = (
        P("dp", None),
        P("dp", None),
        P(),
        P(),
        P(None, "tensor"),
        P(None, "tensor"),
        P(None, "tensor"),
        P("tensor", None),
        P("dp", None, "tensor"),
        P("dp", None, "tensor"),
        P("dp", "tensor", None),
        P("dp", None),
        P("dp", None),
        P("dp"),
        P("dp"),
        P("tensor"),
    )
    out_specs = (
        P("dp", None),
        P("dp", None),
        P(None, "tensor"),
        P(None, "tensor"),
        P(None, "tensor"),
        P("tensor", None),
        P(),
        P(),
        P("dp", None, "tensor"),
        P("dp", None, "tensor"),
        P("dp", "tensor", None),
        P(None, "tensor"),
        P(None, "tensor"),
        P("tensor"),
    )
    return jax.shard_map(shards, mesh=mesh, in_specs=in_specs, out_specs=out_specs, check_vma=False)
```

```python
import functools
import math

import jax
import jax.numpy as jnp
import numpy as np
from jax import lax
from jax.experimental import pallas as pl
from jax.experimental.pallas import tpu as pltpu
from jax.sharding import PartitionSpec as P

HD = 64
TOP = 8
CAP = 64
HOPS = 4
RANK_ROWS = 32
PLANE = 16
SEGMENTS = 3
EARLY = 1
AUX = 16
LANES = 256
MORE = 128

EPS = 1e-06
ROPE_BASE = 10000.0
NEG_FILL = -1e30
BF16 = jnp.bfloat16
F32 = jnp.float32


def contract(left, right, dims):
    return lax.dot_general(left, right, (dims, ((), ())), preferred_element_type=F32)


NN = ((1,), (0,))
NT = ((1,), (1,))
TN = ((0,), (0,))


def swapped(array):
    return lax.ppermute(array, "tensor", [(0, 1), (1, 0)])


def after(array, other):
    return lax.optimization_barrier((array, other))[0]


def passed_along(value, steps):
    count = lax.axis_size("dp")
    first, last = (max(0, -steps), min(count, count - steps))
    return lax.ppermute(value, "dp", [(s, s + steps) for s in range(first, last)])


def rope_tables(count, dp_size):
    freq = np.exp(np.arange(HD // 2) * (-2.0 * math.log(ROPE_BASE) / HD))
    base = np.arange(dp_size)[:, None] * count * freq[None, :]
    local = freq[:, None] * np.arange(count)[None, :]
    index = lax.axis_index("dp")
    cos_base = jnp.asarray(np.cos(base), F32)[index][:, None]
    sin_base = jnp.asarray(np.sin(base), F32)[index][:, None]
    cos_local, sin_local = (jnp.asarray(np.cos(local), F32), jnp.asarray(np.sin(local), F32))
    return (
        cos_base * cos_local - sin_base * sin_local,
        sin_base * cos_local + cos_base * sin_local,
    )


def rotate(values, cosine, sine):
    half = HD // 2
    heads = values.reshape(-1, HD, values.shape[-1])
    first, second = (heads[:, :half], heads[:, half:])
    turned = jnp.concatenate(
        [first * cosine - second * sine, second * cosine + first * sine], axis=1
    )
    return turned.reshape(values.shape)


def fill_bias(blocks, bias):
    tok = bias.shape[1]
    rows = blocks[-1].shape[0] - AUX
    own = blocks[-1][rows:, :].astype(F32)
    seq_q, piece_q = (own[0:1, :], own[1:2, :])
    for number, block in enumerate(blocks):
        side = jnp.transpose(block[rows:, :].astype(F32))
        keep = side[:, 0:1] == seq_q
        if number == len(blocks) - 1:
            at_key = lax.broadcasted_iota(jnp.int32, (tok, tok), 0)
            at_query = lax.broadcasted_iota(jnp.int32, (tok, tok), 1)
            piece = (side[:, 1:2] == piece_q) & (piece_q > 0.0)
            keep = keep & ((at_key <= at_query) | piece)
        bias[number * tok : (number + 1) * tok, :] = jnp.where(keep, 0.0, NEG_FILL)


def all_keys(blocks, start):
    return jnp.concatenate([block[pl.ds(start, HD), :] for block in blocks], axis=1)


def attend_kernel(group, q_ref, k4, k3, k2, k1, k0, out_ref, log_ref, peak_ref, bias):
    blocks = (k4, k3, k2, k1, k0)
    fill_bias(blocks, bias)
    kv_rows = (k0.shape[0] - AUX) // 2

    def one_group(g, _):
        at = pl.multiple_of(g * HD, HD)
        keys = all_keys(blocks, at)
        values = all_keys(blocks, kv_rows + at)
        for j in range(group):
            head = g * group + j
            here = pl.ds(pl.multiple_of(head * HD, HD), HD)
            scores = contract(keys, q_ref[here, :], TN) + bias[...]
            peak = jnp.max(scores, axis=0, keepdims=True)
            weight = jnp.exp(scores - peak)
            total = jnp.sum(weight, axis=0, keepdims=True)
            mixed = contract(values, weight.astype(BF16), NN) * (1.0 / total)
            out_ref[here, :] = mixed.astype(BF16)
            log_ref[pl.ds(head, 1), :] = peak + jnp.log(total)
            peak_ref[pl.ds(head, 1), :] = peak
        return 0

    lax.fori_loop(0, kv_rows // HD, one_group, 0)


def attend(q, blocks, group):
    rows, tok = q.shape
    heads = rows // HD
    return pl.pallas_call(
        functools.partial(attend_kernel, group),
        out_shape=(
            jax.ShapeDtypeStruct((rows, tok), BF16),
            jax.ShapeDtypeStruct((heads, tok), F32),
            jax.ShapeDtypeStruct((heads, tok), F32),
        ),
        scratch_shapes=[pltpu.VMEM((len(blocks) * tok, tok), F32)],
        compiler_params=pltpu.CompilerParams(vmem_limit_bytes=48 << 20),
        cost_estimate=pl.CostEstimate(
            flops=4 * rows * tok * tok * len(blocks),
            bytes_accessed=4 * rows * tok + 2 * len(blocks) * 528 * tok,
            transcendentals=heads * tok * tok * len(blocks),
        ),
    )(q, *blocks)


def attend_back_kernel(
    group, q_ref, g_ref, log_ref, cos_ref, sin_ref, k4, k3, k2, k1, k0,
    dq_ref, d4, d3, d2, d1, d0, bias,
):
    blocks = (k4, k3, k2, k1, k0)
    grads = (d4, d3, d2, d1, d0)
    fill_bias(blocks, bias)
    kv_rows = (k0.shape[0] - AUX) // 2
    tok = bias.shape[1]
    half = HD // 2

    def one_group(g, _):
        at = pl.multiple_of(g * HD, HD)
        keys = all_keys(blocks, at)
        values = all_keys(blocks, kv_rows + at)
        key_sum = value_sum = None
        for j in range(group):
            head = g * group + j
            start = pl.multiple_of(head * HD, HD)
            query, grad = (q_ref[pl.ds(start, HD), :], g_ref[pl.ds(start, HD), :])
            scores = contract(keys, query, TN) + bias[...]
            probs = jnp.exp(scores - log_ref[pl.ds(head, 1), :])
            grad_probs = contract(values, grad, TN)
            delta = jnp.sum(probs * grad_probs, axis=0, keepdims=True)
            grad_scores = (probs * (grad_probs - delta)).astype(BF16)
            key_part = contract(query, grad_scores, NT)
            value_part = contract(grad, probs.astype(BF16), NT)
            key_sum = key_part if key_sum is None else key_sum + key_part
            value_sum = value_part if value_sum is None else value_sum + value_part
            turned = contract(keys, grad_scores, NN) * (HD**-0.5)
            first, second = (turned[:half], turned[half:])
            cosine, sine = (cos_ref[...], sin_ref[...])
            dq_ref[pl.ds(start, half), :] = (first * cosine + second * sine).astype(BF16)
            dq_ref[pl.ds(start + half, half), :] = (second * cosine - first * sine).astype(BF16)
        for number, grad_ref in enumerate(grads):
            piece = slice(number * tok, (number + 1) * tok)
            grad_ref[pl.ds(at, HD), :] = key_sum[:, piece].astype(grad_ref.dtype)
            grad_ref[pl.ds(kv_rows + at, HD), :] = value_sum[:, piece].astype(grad_ref.dtype)
        return 0

    lax.fori_loop(0, kv_rows // HD, one_group, 0)


def attend_back(q, grad, log_total, cosine, sine, blocks, group):
    rows, tok = q.shape
    kv = blocks[0].shape[0] - AUX
    return pl.pallas_call(
        functools.partial(attend_back_kernel, group),
        out_shape=(
            jax.ShapeDtypeStruct((rows, tok), BF16),
            *(jax.ShapeDtypeStruct((kv, tok), BF16) for _ in blocks[1:]),
            jax.ShapeDtypeStruct((kv, tok), F32),
        ),
        scratch_shapes=[pltpu.VMEM((len(blocks) * tok, tok), F32)],
        compiler_params=pltpu.CompilerParams(vmem_limit_bytes=48 << 20),
        cost_estimate=pl.CostEstimate(
            flops=500 * rows * tok * tok * len(blocks),
            bytes_accessed=6 * rows * tok + 4 * len(blocks) * 528 * tok,
            transcendentals=rows // HD * tok * tok * len(blocks),
        ),
    )(q, grad, log_total, cosine, sine, *blocks)


def pack_weights_kernel(gate_ref, up_ref, down_ref, out_ref):
    hidden = gate_ref.shape[1]
    out_ref[:, :hidden] = gate_ref[...]
    out_ref[:, hidden : 2 * hidden] = up_ref[...]
    out_ref[:, 2 * hidden :] = jnp.transpose(down_ref[...].astype(F32)).astype(BF16)


def pack_weights(gate, up, down):
    width, hidden = gate.shape
    thin = pl.BlockSpec((LANES, hidden), lambda i: (i, 0))
    return pl.pallas_call(
        pack_weights_kernel,
        grid=(width // LANES,),
        in_specs=[thin, thin, pl.BlockSpec((hidden, LANES), lambda i: (0, i))],
        out_specs=pl.BlockSpec((LANES, 3 * hidden), lambda i: (i, 0)),
        out_shape=jax.ShapeDtypeStruct((width, 3 * hidden), BF16),
        cost_estimate=pl.CostEstimate(
            flops=width * hidden, bytes_accessed=12 * width * hidden, transcendentals=0
        ),
    )(gate, up, down)


def expert_first_kernel(x_ref, own_ref, peer_ref, out_ref):
    width = x_ref.shape[-1]
    rows = x_ref[...].reshape(-1, width)
    hidden = own_ref.shape[-1] // 3
    out = None
    for weights in (own_ref, peer_ref):
        both = contract(rows, weights[0, :, : 2 * hidden], NN)
        gate_act, up_act = (both[:, :hidden], both[:, hidden:])
        inner = gate_act * (1.0 / (1.0 + jnp.exp(-gate_act))) * up_act
        part = contract(inner.astype(BF16), weights[0, :, 2 * hidden :], NT)
        out = part if out is None else out + part
    out_ref[...] = out.astype(BF16).reshape(out_ref.shape)


def expert_first(rows, own, peer):
    sources, _, width = rows.shape
    triple = own.shape[-1]
    step = sources // 2
    part = pl.BlockSpec((step, RANK_ROWS, width), lambda s, j: (j, s, 0))
    weight = pl.BlockSpec((1, width, triple), lambda s, j: (s, 0, 0))
    return pl.pallas_call(
        expert_first_kernel,
        grid=(EARLY, 2),
        in_specs=[part, weight, weight],
        out_specs=part,
        out_shape=jax.ShapeDtypeStruct((sources, EARLY * RANK_ROWS, width), BF16),
        compiler_params=pltpu.CompilerParams(vmem_limit_bytes=56 << 20),
        cost_estimate=pl.CostEstimate(
            flops=4 * sources * EARLY * RANK_ROWS * width * triple,
            bytes_accessed=4 * sources * EARLY * RANK_ROWS * width + 4 * EARLY * width * triple,
            transcendentals=sources * EARLY * RANK_ROWS * triple * 2 // 3,
        ),
    )(rows, own, peer)


def expert_kernel(x_ref, g_ref, own_ref, peer_ref, dx_ref, own_acts, peer_acts):
    width = x_ref.shape[-1]
    rows, grads = (x_ref[...].reshape(-1, width), g_ref[...].reshape(-1, width))
    hidden = own_ref.shape[-1] // 3
    back = None
    for weights, acts in ((own_ref, own_acts), (peer_ref, peer_acts)):
        both = contract(rows, weights[0, :, : 2 * hidden], NN)
        grad_inner = contract(grads, weights[0, :, 2 * hidden :], NN)
        gate_act, up_act = (both[:, :hidden], both[:, hidden:])
        sigmoid = 1.0 / (1.0 + jnp.exp(-gate_act))
        silu = gate_act * sigmoid
        dgate = grad_inner * up_act * (sigmoid * (1.0 + gate_act * (1.0 - sigmoid)))
        acts[0, :, :hidden] = dgate.astype(BF16)
        acts[0, :, hidden : 2 * hidden] = (grad_inner * silu).astype(BF16)
        acts[0, :, 2 * hidden :] = (silu * up_act).astype(BF16)
        part = contract(acts[0, :, : 2 * hidden], weights[0, :, : 2 * hidden], NT)
        back = part if back is None else back + part
    dx_ref[...] = back.astype(BF16).reshape(dx_ref.shape)


def expert_back(rows, grads, own, peer):
    sources, lines, width = rows.shape
    segments, triple = (lines // RANK_ROWS, own.shape[-1])
    count = sources * RANK_ROWS
    wide = pl.BlockSpec((sources, RANK_ROWS, width), lambda s: (0, s, 0))
    weight = pl.BlockSpec((1, width, triple), lambda s: (s, 0, 0))
    act = pl.BlockSpec((1, count, triple), lambda s: (s, 0, 0))
    return pl.pallas_call(
        expert_kernel,
        grid=(segments,),
        in_specs=[wide, wide, weight, weight],
        out_specs=[wide, act, act],
        out_shape=[
            jax.ShapeDtypeStruct(rows.shape, BF16),
            jax.ShapeDtypeStruct((segments, count, triple), BF16),
            jax.ShapeDtypeStruct((segments, count, triple), BF16),
        ],
        compiler_params=pltpu.CompilerParams(vmem_limit_bytes=56 << 20),
        cost_estimate=pl.CostEstimate(
            flops=7 * sources * lines * width * triple,
            bytes_accessed=6 * sources * lines * width + 4 * segments * width * triple,
            transcendentals=2 * sources * lines * triple // 3,
        ),
    )(rows, grads, own, peer)


def expert_sums_kernel(x_ref, g_ref, own_acts, peer_acts, own_ref, peer_ref, sum_own, *outs):
    width = x_ref.shape[-1]
    rows, grads = (x_ref[...].reshape(-1, width), g_ref[...].reshape(-1, width))
    hidden = own_ref.shape[-1]
    late_ref = outs[3]
    segment = pl.program_id(0)
    for side, acts in enumerate((own_acts, peer_acts)):
        first = contract(rows, acts[0, :, : 2 * hidden], TN).astype(BF16)
        second = contract(grads, acts[0, :, 2 * hidden :], TN).astype(BF16)
        if side == 0:
            sum_own[0, :, : 2 * hidden] = first
            sum_own[0, :, 2 * hidden :] = second
        else:
            outs[0][0] = first[:, :hidden]
            outs[1][0] = first[:, hidden:]
            outs[2][0] = second

    @pl.when(segment >= EARLY)
    def _():
        out = contract(own_acts[0, :, 2 * hidden :], own_ref[0], NT)
        out = out + contract(peer_acts[0, :, 2 * hidden :], peer_ref[0], NT)
        late_ref[...] = out.astype(BF16).reshape(x_ref.shape)


def expert_sums(rows, grads, own_acts, peer_acts, own, peer):
    sources, lines, width = rows.shape
    segments, triple = (lines // RANK_ROWS, own.shape[-1])
    hidden = triple // 3
    count = sources * RANK_ROWS
    block = (sources, RANK_ROWS, width)
    wide = pl.BlockSpec(block, lambda s: (0, s, 0))
    down = pl.BlockSpec((1, width, hidden), lambda s: (s, 0, 2))
    act = pl.BlockSpec((1, count, triple), lambda s: (s, 0, 0))
    return pl.pallas_call(
        expert_sums_kernel,
        grid=(segments,),
        in_specs=[wide, wide, act, act, down, down],
        out_specs=[pl.BlockSpec((1, width, triple), lambda s: (s, 0, 0))]
        + [pl.BlockSpec((1, width, hidden), lambda s: (s, 0, 0))] * 3
        + [pl.BlockSpec(block, lambda s: (0, jnp.maximum(s - EARLY, 0), 0))],
        out_shape=[jax.ShapeDtypeStruct((segments, width, triple), BF16)]
        + [jax.ShapeDtypeStruct((segments, width, hidden), BF16)] * 3
        + [jax.ShapeDtypeStruct((sources, (segments - EARLY) * RANK_ROWS, width), BF16)],
        compiler_params=pltpu.CompilerParams(vmem_limit_bytes=60 << 20),
        cost_estimate=pl.CostEstimate(
            flops=6 * sources * lines * width * triple,
            bytes_accessed=6 * sources * lines * width + 5 * segments * width * triple,
            transcendentals=0,
        ),
    )(rows, grads, own_acts, peer_acts, own, peer)


def both_cores_kernel(own_ref, *refs):
    out_ref = refs[-1]
    hidden = refs[0].shape[-1]

    @pl.when(pl.program_id(0) < SEGMENTS)
    def _():
        for kind, peer_ref in enumerate(refs[:-1]):
            here = slice(kind * hidden, (kind + 1) * hidden)
            total = own_ref[0, :, here].astype(F32) + peer_ref[0].astype(F32)
            out_ref[0, :, here] = total.astype(BF16)

    @pl.when(pl.program_id(0) >= SEGMENTS)
    def _():
        out_ref[...] = jnp.zeros_like(out_ref)


def both_cores(own, peers, slots):
    segments, width, triple = own.shape
    rows = width // 2
    last = segments - 1
    part = pl.BlockSpec((1, rows, triple), lambda s, r: (jnp.minimum(s, last), r, 0))
    thin = pl.BlockSpec((1, rows, triple // 3), lambda s, r: (jnp.minimum(s, last), r, 0))
    return pl.pallas_call(
        both_cores_kernel,
        grid=(slots, 2),
        in_specs=[part] + [thin] * 3,
        out_specs=pl.BlockSpec((1, rows, triple), lambda s, r: (s, r, 0)),
        out_shape=jax.ShapeDtypeStruct((slots, width, triple), BF16),
        cost_estimate=pl.CostEstimate(
            flops=slots * width * triple, bytes_accessed=6 * slots * width * triple, transcendentals=0
        ),
    )(own, *peers)


def weight_grads_kernel(normed_ref, qkv_ref, attended_ref, branch_ref, extra_ref, out_ref):
    width = branch_ref.shape[1]
    columns = width + qkv_ref.shape[0]
    out_ref[:, :width] = contract(attended_ref[...], branch_ref[...], NN).astype(BF16)
    out_ref[:, width:columns] = contract(normed_ref[...], qkv_ref[...], ((0,), (1,))).astype(BF16)
    out_ref[:, columns:] = jnp.transpose(extra_ref[...]).astype(BF16)


def weight_grads(normed, grad_qkv, attended, branch, extra):
    tok, model = normed.shape
    width, columns = (attended.shape[0], grad_qkv.shape[0])
    half = width // LANES
    every = width + columns + MORE
    return pl.pallas_call(
        weight_grads_kernel,
        grid=(model // LANES,),
        in_specs=[
            pl.BlockSpec((tok, LANES), lambda i: (0, i)),
            pl.BlockSpec((columns, tok), lambda i: (0, 0)),
            pl.BlockSpec((LANES, tok), lambda i: (i % half, 0)),
            pl.BlockSpec((tok, width), lambda i: (0, i // half)),
            pl.BlockSpec((MORE, LANES), lambda i: (0, i)),
        ],
        out_specs=pl.BlockSpec((LANES, every), lambda i: (i, 0)),
        out_shape=jax.ShapeDtypeStruct((model, every), BF16),
        cost_estimate=pl.CostEstimate(
            flops=2 * tok * model * every,
            bytes_accessed=2 * model * every + 4 * tok * model,
            transcendentals=0,
        ),
    )(normed, grad_qkv, attended, branch, extra)


def unpack_kernel(
    in_ref, query_ref, key_ref, sq_ref, sk_ref,
    wo_ref, wq_ref, wk_ref, wv_ref, sum_ref, cq_ref, ck_ref,
):
    at = 0
    for target in (wo_ref, wq_ref, wk_ref, wv_ref):
        size = target.shape[1]
        target[...] = in_ref[:, at : at + size].astype(F32)
        at += size
    sum_ref[...] = jnp.transpose(in_ref[:, at:].astype(F32))[: sum_ref.shape[0]]
    cq_ref[...] = (query_ref[...].astype(F32) * sq_ref[...]).astype(BF16)
    ck_ref[...] = (key_ref[...].astype(F32) * sk_ref[...]).astype(BF16)


def unpack(summed, w_query, w_key, scale_query, scale_key):
    total, every = summed.shape
    width, narrow = (w_query.shape[1], w_key.shape[1])
    steps = total // LANES
    wide = pl.BlockSpec((LANES, width), lambda i: (i, 0))
    thin = pl.BlockSpec((LANES, narrow), lambda i: (i, 0))
    return pl.pallas_call(
        unpack_kernel,
        grid=(steps,),
        in_specs=[
            pl.BlockSpec((LANES, every), lambda i: (i, 0)),
            wide,
            thin,
            pl.BlockSpec((1, width), lambda i: (0, 0)),
            pl.BlockSpec((1, narrow), lambda i: (0, 0)),
        ],
        out_specs=[
            pl.BlockSpec((LANES, width), lambda i: (i % (steps // 2), i // (steps // 2))),
            wide,
            thin,
            thin,
            pl.BlockSpec((8, LANES), lambda i: (0, i)),
            wide,
            thin,
        ],
        out_shape=[
            jax.ShapeDtypeStruct((total // 2, 2 * width), F32),
            jax.ShapeDtypeStruct((total, width), F32),
            jax.ShapeDtypeStruct((total, narrow), F32),
            jax.ShapeDtypeStruct((total, narrow), F32),
            jax.ShapeDtypeStruct((8, total), F32),
            jax.ShapeDtypeStruct((total, width), BF16),
            jax.ShapeDtypeStruct((total, narrow), BF16),
        ],
        compiler_params=pltpu.CompilerParams(vmem_limit_bytes=60 << 20),
        cost_estimate=pl.CostEstimate(
            flops=total * every, bytes_accessed=8 * total * every, transcendentals=0
        ),
    )(summed, w_query, w_key, scale_query, scale_key)


def rms_scale(values):
    return lax.rsqrt(jnp.mean(values * values, axis=-1, keepdims=True) + EPS)


def norm_back(grad_normed, hidden, inverse, gain):
    weighted = grad_normed * gain
    grad_gain = jnp.sum(grad_normed * hidden * inverse, axis=0)
    grad_hidden = inverse * weighted - hidden * inverse**3 * jnp.mean(
        weighted * hidden, axis=-1, keepdims=True
    )
    return (grad_hidden, grad_gain)


def shards(
    tokens,
    out_grad,
    norm1_gain,
    norm2_gain,
    w_query,
    w_key,
    w_value,
    w_out,
    w_gate,
    w_up,
    w_down,
    route_ids,
    route_logits,
    seq_ids,
    piece_ids,
    clip_limit,
):
    tok_dev, model_width = tokens.shape
    dp_size = lax.axis_size("dp")
    tensor_size = lax.axis_size("tensor")
    core = lax.axis_index("tensor")
    local_heads = w_query.shape[1] // HD
    local_kv = w_key.shape[1] // HD
    group = local_heads // local_kv
    plane_groups = [list(range(at, at + PLANE)) for at in range(0, dp_size, PLANE)]
    column_groups = [list(range(at, dp_size, PLANE)) for at in range(PLANE)]


    picks = route_ids.T
    logits = route_logits.T
    gate_exp = jnp.exp(logits - jnp.max(logits, axis=0, keepdims=True))
    gates = gate_exp / jnp.sum(gate_exp, axis=0, keepdims=True)
    number = jnp.arange(PLANE * SEGMENTS, dtype=jnp.int32)
    number = number % SEGMENTS * PLANE + number // SEGMENTS
    same = picks[None] == number[:, None, None]
    member = jnp.any(same, axis=1)
    gate_of = jnp.sum(jnp.where(same, gates[None], 0.0), axis=1)
    place = jnp.arange(tok_dev, dtype=jnp.int32)
    before = (place[:, None] < place[None, :]).astype(BF16)
    rank = contract(member.astype(BF16), before, NN)
    rank = jnp.where(member, rank, -1.0)
    wanted = (tensor_size * jnp.arange(RANK_ROWS, dtype=jnp.int32) + core).astype(F32)
    chosen = rank[:, None, :] == wanted[None, :, None]
    pick = chosen.astype(BF16).reshape(-1, tok_dev)
    gated = jnp.where(chosen, gate_of[:, None, :], 0.0)
    slot_gate = jnp.sum(gated, axis=2).reshape(-1, 1)
    gated = gated.astype(BF16).reshape(-1, tok_dev)

    def in_plane(rows):
        rows = rows.reshape(PLANE, -1, model_width)
        return lax.all_to_all(rows, "dp", 0, 0, tiled=True, axis_index_groups=plane_groups)

    grad_rows = (contract(pick, out_grad, NN) * slot_gate).astype(BF16)

    cosine, sine = rope_tables(tok_dev, dp_size)
    x_float = tokens.astype(F32)
    inverse1 = rms_scale(x_float)
    normed1 = (x_float * inverse1 * norm1_gain).astype(BF16)
    query = rotate(contract(w_query, normed1, ((0,), (1,))), cosine, sine)
    query = (query * (HD**-0.5)).astype(BF16)
    key = rotate(contract(w_key, normed1, ((0,), (1,))), cosine, sine).astype(BF16)
    value = contract(w_value, normed1, ((0,), (1,))).astype(BF16)
    side = jnp.concatenate(
        [(seq_ids + 1)[None], piece_ids[None], jnp.zeros((AUX - 2, tok_dev), jnp.int32)]
    ).astype(BF16)
    block = jnp.concatenate([key, value, side])
    blocks = tuple(passed_along(block, hop) for hop in range(HOPS, 0, -1)) + (block,)
    blocks, grad_rows = lax.optimization_barrier((blocks, grad_rows))
    packed_w = pack_weights(w_gate[0], w_up[0], w_down[0])
    own = lax.all_gather(packed_w, "dp", axis=0, axis_index_groups=column_groups)
    grad_rows = in_plane(grad_rows)
    attended, log_total, peaks = attend(query, blocks, group)
    attn_part = contract(attended, w_out, TN)
    hidden1 = x_float + (attn_part + swapped(attn_part))
    inverse2 = rms_scale(hidden1)
    normed2 = (hidden1 * inverse2 * norm2_gain).astype(BF16)

    rows_out = contract(pick, normed2, NN).astype(BF16)
    rows_out = after(rows_out, grad_rows)
    own = after(own, rows_out)
    peer = swapped(own)
    rows_in = in_plane(rows_out)
    out_early = in_plane(expert_first(rows_in, own, peer))
    back, own_acts, peer_acts = expert_back(rows_in, grad_rows, own, peer)

    def combined(weights, rows):
        part = contract(weights, rows.reshape(-1, model_width), TN).astype(BF16)
        return part.astype(F32) + swapped(part).astype(F32)

    sum_own, *sum_peer, out_late = expert_sums(rows_in, grad_rows, own_acts, peer_acts, own, peer)
    sums = both_cores(sum_own, [swapped(part) for part in sum_peer], dp_size // PLANE)
    back = in_plane(after(back, out_early))
    out_late = in_plane(after(out_late, back))
    grad_normed2 = combined(pick, after(back, sums))
    sums = lax.psum_scatter(
        sums, "dp", scatter_dimension=0, tiled=True, axis_index_groups=column_groups
    )

    grad_top = out_grad.astype(F32)
    grad_from_norm2, grad_gain2 = norm_back(grad_normed2, hidden1, inverse2, norm2_gain)
    grad_hidden1 = grad_top + grad_from_norm2
    grad_branch = grad_hidden1.astype(BF16)
    grad_attended = contract(w_out, grad_branch, NT).astype(BF16)
    grad_query_pre, *grad_blocks = attend_back(
        query, grad_attended, log_total, cosine, sine, blocks, group
    )
    returned = [
        passed_along(grad_blocks[number], -hop) for number, hop in enumerate(range(HOPS, 0, -1))
    ]
    kv_total = grad_blocks[-1]
    for part in returned:
        kv_total = kv_total + part.astype(F32)
    kv_rows = local_kv * HD
    grad_key_pre = rotate(kv_total[:kv_rows], cosine, -sine).astype(BF16)
    grad_value = kv_total[kv_rows:].astype(BF16)

    grad_norm1_part = (
        contract(grad_query_pre, w_query, ((0,), (1,)))
        + contract(grad_key_pre, w_key, ((0,), (1,)))
        + contract(grad_value, w_value, ((0,), (1,)))
    ).astype(BF16)

    grad_normed1 = grad_norm1_part.astype(F32) + swapped(grad_norm1_part).astype(F32)
    grad_from_norm1, grad_gain1 = norm_back(grad_normed1, x_float, inverse1, norm1_gain)
    input_grad = grad_hidden1 + grad_from_norm1
    peak = jnp.max(peaks, axis=1)
    peak_high = peak.astype(BF16).astype(F32)
    places = jnp.arange(dp_size)[:, None] == lax.axis_index("dp")
    peak_row = jnp.where(places, jnp.concatenate([peak_high, peak - peak_high])[None], 0.0)
    extra = jnp.stack([grad_gain1, grad_gain2, peak_row.reshape(-1)])
    extra = jnp.pad(extra, ((0, MORE - len(extra)), (0, 0)))
    grad_qkv = jnp.concatenate([grad_query_pre, grad_key_pre, grad_value])
    parts = weight_grads(normed1, grad_qkv, attended, grad_branch, extra)
    parts, sums, out_early, out_late = lax.optimization_barrier((parts, sums, out_early, out_late))
    summed = lax.psum(parts, "dp")
    expert_out = jnp.concatenate([out_early, out_late], axis=1)
    output = (hidden1 + combined(gated, expert_out)).astype(BF16)
    grad_gate, grad_up, grad_down = jnp.split(sums[0].astype(F32), 3, axis=1)
    grad_down = grad_down.T
    all_peaks = summed[:, 2 - MORE].astype(F32).reshape(dp_size, 2 * local_heads)
    head_peaks = jnp.max(all_peaks[:, :local_heads] + all_peaks[:, local_heads:], axis=0)
    factor = clip_limit / jnp.maximum(head_peaks, clip_limit)
    key_factor = jnp.min(factor.reshape(local_kv, group), axis=1)
    scale_query = jnp.repeat(jnp.sqrt(factor), HD)[None, :]
    scale_key = jnp.repeat(jnp.sqrt(key_factor), HD)[None, :]
    grad_wo, grad_wq, grad_wk, grad_wv, totals, clipped_query, clipped_key = unpack(
        summed, w_query, w_key, scale_query, scale_key
    )
    return (
        output,
        input_grad,
        grad_wq,
        grad_wk,
        grad_wv,
        grad_wo,
        totals[0],
        totals[1],
        grad_gate[None],
        grad_up[None],
        grad_down[None],
        clipped_query,
        clipped_key,
        head_peaks,
    )


def solution(mesh):
    in_specs = (
        P("dp", None),
        P("dp", None),
        P(),
        P(),
        P(None, "tensor"),
        P(None, "tensor"),
        P(None, "tensor"),
        P("tensor", None),
        P("dp", None, "tensor"),
        P("dp", None, "tensor"),
        P("dp", "tensor", None),
        P("dp", None),
        P("dp", None),
        P("dp"),
        P("dp"),
        P("tensor"),
    )
    out_specs = (
        P("dp", None),
        P("dp", None),
        P(None, "tensor"),
        P(None, "tensor"),
        P(None, "tensor"),
        P("tensor", None),
        P(),
        P(),
        P("dp", None, "tensor"),
        P("dp", None, "tensor"),
        P("dp", "tensor", None),
        P(None, "tensor"),
        P(None, "tensor"),
        P("tensor"),
    )
    return jax.shard_map(shards, mesh=mesh, in_specs=in_specs, out_specs=out_specs, check_vma=False)
```

```python
import functools
import math

import jax
import jax.numpy as jnp
import numpy as np
from jax import lax
from jax.experimental import pallas as pl
from jax.experimental.pallas import tpu as pltpu
from jax.sharding import PartitionSpec as P

HD = 64
TOP = 8
CAP = 64
HOPS = 4
RANK_ROWS = 32
PLANE = 16
SEGMENTS = 3
EARLY = 1
AUX = 16
LANES = 256
MORE = 128

EPS = 1e-06
ROPE_BASE = 10000.0
NEG_FILL = -1e30
BF16 = jnp.bfloat16
F32 = jnp.float32


def contract(left, right, dims):
    return lax.dot_general(left, right, (dims, ((), ())), preferred_element_type=F32)


NN = ((1,), (0,))
NT = ((1,), (1,))
TN = ((0,), (0,))


def swapped(array):
    return lax.ppermute(array, "tensor", [(0, 1), (1, 0)])


def after(array, other):
    return lax.optimization_barrier((array, other))[0]


def passed_along(value, steps):
    count = lax.axis_size("dp")
    first, last = (max(0, -steps), min(count, count - steps))
    return lax.ppermute(value, "dp", [(s, s + steps) for s in range(first, last)])


def rope_tables(count, dp_size):
    freq = np.exp(np.arange(HD // 2) * (-2.0 * math.log(ROPE_BASE) / HD))
    base = np.arange(dp_size)[:, None] * count * freq[None, :]
    local = freq[:, None] * np.arange(count)[None, :]
    index = lax.axis_index("dp")
    cos_base = jnp.asarray(np.cos(base), F32)[index][:, None]
    sin_base = jnp.asarray(np.sin(base), F32)[index][:, None]
    cos_local, sin_local = (jnp.asarray(np.cos(local), F32), jnp.asarray(np.sin(local), F32))
    return (
        cos_base * cos_local - sin_base * sin_local,
        sin_base * cos_local + cos_base * sin_local,
    )


def rotate(values, cosine, sine):
    half = HD // 2
    heads = values.reshape(-1, HD, values.shape[-1])
    first, second = (heads[:, :half], heads[:, half:])
    turned = jnp.concatenate(
        [first * cosine - second * sine, second * cosine + first * sine], axis=1
    )
    return turned.reshape(values.shape)


def fill_bias(blocks, bias):
    tok = bias.shape[1]
    rows = blocks[-1].shape[0] - AUX
    own = blocks[-1][rows:, :].astype(F32)
    seq_q, piece_q = (own[0:1, :], own[1:2, :])
    for number, block in enumerate(blocks):
        side = jnp.transpose(block[rows:, :].astype(F32))
        keep = side[:, 0:1] == seq_q
        if number == len(blocks) - 1:
            at_key = lax.broadcasted_iota(jnp.int32, (tok, tok), 0)
            at_query = lax.broadcasted_iota(jnp.int32, (tok, tok), 1)
            piece = (side[:, 1:2] == piece_q) & (piece_q > 0.0)
            keep = keep & ((at_key <= at_query) | piece)
        bias[number * tok : (number + 1) * tok, :] = jnp.where(keep, 0.0, NEG_FILL)


def all_keys(blocks, start):
    return jnp.concatenate([block[pl.ds(start, HD), :] for block in blocks], axis=1)


def attend_kernel(group, q_ref, k4, k3, k2, k1, k0, out_ref, log_ref, peak_ref, bias):
    blocks = (k4, k3, k2, k1, k0)
    fill_bias(blocks, bias)
    kv_rows = (k0.shape[0] - AUX) // 2

    def one_group(g, _):
        at = pl.multiple_of(g * HD, HD)
        keys = all_keys(blocks, at)
        values = all_keys(blocks, kv_rows + at)
        for j in range(group):
            head = g * group + j
            here = pl.ds(pl.multiple_of(head * HD, HD), HD)
            scores = contract(keys, q_ref[here, :], TN) + bias[...]
            peak = jnp.max(scores, axis=0, keepdims=True)
            weight = jnp.exp(scores - peak)
            total = jnp.sum(weight, axis=0, keepdims=True)
            mixed = contract(values, weight.astype(BF16), NN) * (1.0 / total)
            out_ref[here, :] = mixed.astype(BF16)
            log_ref[pl.ds(head, 1), :] = peak + jnp.log(total)
            peak_ref[pl.ds(head, 1), :] = peak
        return 0

    lax.fori_loop(0, kv_rows // HD, one_group, 0)


def attend(q, blocks, group):
    rows, tok = q.shape
    heads = rows // HD
    return pl.pallas_call(
        functools.partial(attend_kernel, group),
        out_shape=(
            jax.ShapeDtypeStruct((rows, tok), BF16),
            jax.ShapeDtypeStruct((heads, tok), F32),
            jax.ShapeDtypeStruct((heads, tok), F32),
        ),
        scratch_shapes=[pltpu.VMEM((len(blocks) * tok, tok), F32)],
        compiler_params=pltpu.CompilerParams(vmem_limit_bytes=48 << 20),
        cost_estimate=pl.CostEstimate(
            flops=4 * rows * tok * tok * len(blocks),
            bytes_accessed=4 * rows * tok + 2 * len(blocks) * 528 * tok,
            transcendentals=heads * tok * tok * len(blocks),
        ),
    )(q, *blocks)


def attend_back_kernel(
    group, q_ref, g_ref, log_ref, cos_ref, sin_ref, k4, k3, k2, k1, k0,
    dq_ref, d4, d3, d2, d1, d0, bias,
):
    blocks = (k4, k3, k2, k1, k0)
    grads = (d4, d3, d2, d1, d0)
    fill_bias(blocks, bias)
    kv_rows = (k0.shape[0] - AUX) // 2
    tok = bias.shape[1]
    half = HD // 2

    def one_group(g, _):
        at = pl.multiple_of(g * HD, HD)
        keys = all_keys(blocks, at)
        values = all_keys(blocks, kv_rows + at)
        key_sum = value_sum = None
        for j in range(group):
            head = g * group + j
            start = pl.multiple_of(head * HD, HD)
            query, grad = (q_ref[pl.ds(start, HD), :], g_ref[pl.ds(start, HD), :])
            scores = contract(keys, query, TN) + bias[...]
            probs = jnp.exp(scores - log_ref[pl.ds(head, 1), :])
            grad_probs = contract(values, grad, TN)
            delta = jnp.sum(probs * grad_probs, axis=0, keepdims=True)
            grad_scores = (probs * (grad_probs - delta)).astype(BF16)
            key_part = contract(query, grad_scores, NT)
            value_part = contract(grad, probs.astype(BF16), NT)
            key_sum = key_part if key_sum is None else key_sum + key_part
            value_sum = value_part if value_sum is None else value_sum + value_part
            turned = contract(keys, grad_scores, NN) * (HD**-0.5)
            first, second = (turned[:half], turned[half:])
            cosine, sine = (cos_ref[...], sin_ref[...])
            dq_ref[pl.ds(start, half), :] = (first * cosine + second * sine).astype(BF16)
            dq_ref[pl.ds(start + half, half), :] = (second * cosine - first * sine).astype(BF16)
        for number, grad_ref in enumerate(grads):
            piece = slice(number * tok, (number + 1) * tok)
            grad_ref[pl.ds(at, HD), :] = key_sum[:, piece].astype(grad_ref.dtype)
            grad_ref[pl.ds(kv_rows + at, HD), :] = value_sum[:, piece].astype(grad_ref.dtype)
        return 0

    lax.fori_loop(0, kv_rows // HD, one_group, 0)


def attend_back(q, grad, log_total, cosine, sine, blocks, group):
    rows, tok = q.shape
    kv = blocks[0].shape[0] - AUX
    return pl.pallas_call(
        functools.partial(attend_back_kernel, group),
        out_shape=(
            jax.ShapeDtypeStruct((rows, tok), BF16),
            *(jax.ShapeDtypeStruct((kv, tok), BF16) for _ in blocks[1:]),
            jax.ShapeDtypeStruct((kv, tok), F32),
        ),
        scratch_shapes=[pltpu.VMEM((len(blocks) * tok, tok), F32)],
        compiler_params=pltpu.CompilerParams(vmem_limit_bytes=48 << 20),
        cost_estimate=pl.CostEstimate(
            flops=500 * rows * tok * tok * len(blocks),
            bytes_accessed=6 * rows * tok + 4 * len(blocks) * 528 * tok,
            transcendentals=rows // HD * tok * tok * len(blocks),
        ),
    )(q, grad, log_total, cosine, sine, *blocks)


def pack_weights_kernel(gate_ref, up_ref, down_ref, out_ref):
    hidden = gate_ref.shape[1]
    out_ref[:, :hidden] = gate_ref[...]
    out_ref[:, hidden : 2 * hidden] = up_ref[...]
    out_ref[:, 2 * hidden :] = jnp.transpose(down_ref[...].astype(F32)).astype(BF16)


def pack_weights(gate, up, down):
    width, hidden = gate.shape
    rows = width // 2
    thin = pl.BlockSpec((rows, hidden), lambda i: (i, 0))
    return pl.pallas_call(
        pack_weights_kernel,
        grid=(2,),
        in_specs=[thin, thin, pl.BlockSpec((hidden, rows), lambda i: (0, i))],
        out_specs=pl.BlockSpec((rows, 3 * hidden), lambda i: (i, 0)),
        out_shape=jax.ShapeDtypeStruct((width, 3 * hidden), BF16),
        cost_estimate=pl.CostEstimate(
            flops=width * hidden, bytes_accessed=12 * width * hidden, transcendentals=0
        ),
    )(gate, up, down)


def expert_first_kernel(x_ref, own_ref, peer_ref, out_ref):
    width = x_ref.shape[-1]
    rows = x_ref[...].reshape(-1, width)
    hidden = own_ref.shape[-1] // 3
    out = None
    for weights in (own_ref, peer_ref):
        both = contract(rows, weights[0, :, : 2 * hidden], NN)
        gate_act, up_act = (both[:, :hidden], both[:, hidden:])
        inner = gate_act * (1.0 / (1.0 + jnp.exp(-gate_act))) * up_act
        part = contract(inner.astype(BF16), weights[0, :, 2 * hidden :], NT)
        out = part if out is None else out + part
    out_ref[...] = out.astype(BF16).reshape(out_ref.shape)


def expert_first(rows, own, peer):
    sources, _, width = rows.shape
    triple = own.shape[-1]
    step = sources // 2
    part = pl.BlockSpec((step, RANK_ROWS, width), lambda s, j: (j, s, 0))
    weight = pl.BlockSpec((1, width, triple), lambda s, j: (s, 0, 0))
    return pl.pallas_call(
        expert_first_kernel,
        grid=(EARLY, 2),
        in_specs=[part, weight, weight],
        out_specs=part,
        out_shape=jax.ShapeDtypeStruct((sources, EARLY * RANK_ROWS, width), BF16),
        compiler_params=pltpu.CompilerParams(vmem_limit_bytes=56 << 20),
        cost_estimate=pl.CostEstimate(
            flops=4 * sources * EARLY * RANK_ROWS * width * triple,
            bytes_accessed=4 * sources * EARLY * RANK_ROWS * width + 4 * EARLY * width * triple,
            transcendentals=sources * EARLY * RANK_ROWS * triple * 2 // 3,
        ),
    )(rows, own, peer)


def of_segment(early_ref, late_ref):
    width = early_ref.shape[-1]
    chosen = jnp.where(pl.program_id(0) < EARLY, early_ref[...], late_ref[...])
    return chosen.reshape(-1, width)


def expert_kernel(x_ref, g1_ref, g2_ref, own_ref, peer_ref, dx_ref, own_acts, peer_acts):
    width = x_ref.shape[-1]
    rows, grads = (x_ref[...].reshape(-1, width), of_segment(g1_ref, g2_ref))
    hidden = own_ref.shape[-1] // 3
    back = None
    for weights, acts in ((own_ref, own_acts), (peer_ref, peer_acts)):
        both = contract(rows, weights[0, :, : 2 * hidden], NN)
        grad_inner = contract(grads, weights[0, :, 2 * hidden :], NN)
        gate_act, up_act = (both[:, :hidden], both[:, hidden:])
        sigmoid = 1.0 / (1.0 + jnp.exp(-gate_act))
        silu = gate_act * sigmoid
        dgate = grad_inner * up_act * (sigmoid * (1.0 + gate_act * (1.0 - sigmoid)))
        acts[0, :, :hidden] = dgate.astype(BF16)
        acts[0, :, hidden : 2 * hidden] = (grad_inner * silu).astype(BF16)
        acts[0, :, 2 * hidden :] = (silu * up_act).astype(BF16)
        part = contract(acts[0, :, : 2 * hidden], weights[0, :, : 2 * hidden], NT)
        back = part if back is None else back + part
    dx_ref[...] = back.astype(BF16).reshape(dx_ref.shape)


def segment_specs(block):
    return [
        pl.BlockSpec(block, lambda s: (0, s, 0)),
        pl.BlockSpec(block, lambda s: (0, jnp.minimum(s, EARLY - 1), 0)),
        pl.BlockSpec(block, lambda s: (0, jnp.maximum(s - EARLY, 0), 0)),
    ]


def expert_back(rows, grads, own, peer):
    sources, lines, width = rows.shape
    segments, triple = (lines // RANK_ROWS, own.shape[-1])
    count = sources * RANK_ROWS
    specs = segment_specs((sources, RANK_ROWS, width))
    wide = specs[0]
    weight = pl.BlockSpec((1, width, triple), lambda s: (s, 0, 0))
    act = pl.BlockSpec((1, count, triple), lambda s: (s, 0, 0))
    return pl.pallas_call(
        expert_kernel,
        grid=(segments,),
        in_specs=[*specs, weight, weight],
        out_specs=[wide, act, act],
        out_shape=[
            jax.ShapeDtypeStruct(rows.shape, BF16),
            jax.ShapeDtypeStruct((segments, count, triple), BF16),
            jax.ShapeDtypeStruct((segments, count, triple), BF16),
        ],
        compiler_params=pltpu.CompilerParams(vmem_limit_bytes=56 << 20),
        cost_estimate=pl.CostEstimate(
            flops=7 * sources * lines * width * triple,
            bytes_accessed=6 * sources * lines * width + 4 * segments * width * triple,
            transcendentals=2 * sources * lines * triple // 3,
        ),
    )(rows, *grads, own, peer)


def expert_sums_kernel(x_ref, g1_ref, g2_ref, own_acts, peer_acts, own_ref, peer_ref, sum_own, *outs):
    width = x_ref.shape[-1]
    rows, grads = (x_ref[...].reshape(-1, width), of_segment(g1_ref, g2_ref))
    hidden = own_ref.shape[-1]
    late_ref = outs[3]
    segment = pl.program_id(0)
    for side, acts in enumerate((own_acts, peer_acts)):
        first = contract(rows, acts[0, :, : 2 * hidden], TN).astype(BF16)
        second = contract(grads, acts[0, :, 2 * hidden :], TN).astype(BF16)
        if side == 0:
            sum_own[0, :, : 2 * hidden] = first
            sum_own[0, :, 2 * hidden :] = second
        else:
            outs[0][0] = first[:, :hidden]
            outs[1][0] = first[:, hidden:]
            outs[2][0] = second

    @pl.when(segment >= EARLY)
    def _():
        out = contract(own_acts[0, :, 2 * hidden :], own_ref[0], NT)
        out = out + contract(peer_acts[0, :, 2 * hidden :], peer_ref[0], NT)
        late_ref[...] = out.astype(BF16).reshape(x_ref.shape)


def expert_sums(rows, grads, own_acts, peer_acts, own, peer):
    sources, lines, width = rows.shape
    segments, triple = (lines // RANK_ROWS, own.shape[-1])
    hidden = triple // 3
    count = sources * RANK_ROWS
    block = (sources, RANK_ROWS, width)
    down = pl.BlockSpec((1, width, hidden), lambda s: (s, 0, 2))
    act = pl.BlockSpec((1, count, triple), lambda s: (s, 0, 0))
    return pl.pallas_call(
        expert_sums_kernel,
        grid=(segments,),
        in_specs=[*segment_specs(block), act, act, down, down],
        out_specs=[pl.BlockSpec((1, width, triple), lambda s: (s, 0, 0))]
        + [pl.BlockSpec((1, width, hidden), lambda s: (s, 0, 0))] * 3
        + [pl.BlockSpec(block, lambda s: (0, jnp.maximum(s - EARLY, 0), 0))],
        out_shape=[jax.ShapeDtypeStruct((segments, width, triple), BF16)]
        + [jax.ShapeDtypeStruct((segments, width, hidden), BF16)] * 3
        + [jax.ShapeDtypeStruct((sources, (segments - EARLY) * RANK_ROWS, width), BF16)],
        compiler_params=pltpu.CompilerParams(vmem_limit_bytes=60 << 20),
        cost_estimate=pl.CostEstimate(
            flops=6 * sources * lines * width * triple,
            bytes_accessed=6 * sources * lines * width + 5 * segments * width * triple,
            transcendentals=0,
        ),
    )(rows, *grads, own_acts, peer_acts, own, peer)


def both_cores_kernel(own_ref, *refs):
    out_ref = refs[-1]
    hidden = refs[0].shape[-1]

    @pl.when(pl.program_id(0) < SEGMENTS)
    def _():
        for kind, peer_ref in enumerate(refs[:-1]):
            here = slice(kind * hidden, (kind + 1) * hidden)
            total = own_ref[0, :, here].astype(F32) + peer_ref[0].astype(F32)
            out_ref[0, :, here] = total.astype(BF16)

    @pl.when(pl.program_id(0) >= SEGMENTS)
    def _():
        out_ref[...] = jnp.zeros_like(out_ref)


def both_cores(own, peers, slots):
    segments, width, triple = own.shape
    rows = width // 2
    last = segments - 1
    part = pl.BlockSpec((1, rows, triple), lambda s, r: (jnp.minimum(s, last), r, 0))
    thin = pl.BlockSpec((1, rows, triple // 3), lambda s, r: (jnp.minimum(s, last), r, 0))
    return pl.pallas_call(
        both_cores_kernel,
        grid=(slots, 2),
        in_specs=[part] + [thin] * 3,
        out_specs=pl.BlockSpec((1, rows, triple), lambda s, r: (s, r, 0)),
        out_shape=jax.ShapeDtypeStruct((slots, width, triple), BF16),
        cost_estimate=pl.CostEstimate(
            flops=slots * width * triple, bytes_accessed=6 * slots * width * triple, transcendentals=0
        ),
    )(own, *peers)


def first_grads_kernel(normed_ref, query_ref, attended_ref, branch_ref, out_ref):
    width = branch_ref.shape[1]
    out_ref[:, :width] = contract(attended_ref[...], branch_ref[...], NN).astype(BF16)
    out_ref[:, width:] = contract(normed_ref[...], query_ref[...], ((0,), (1,))).astype(BF16)


def last_grads_kernel(normed_ref, kv_ref, extra_ref, _, out_ref):
    columns = kv_ref.shape[0]
    out_ref[:, :columns] = contract(normed_ref[...], kv_ref[...], ((0,), (1,))).astype(BF16)
    out_ref[:, columns : columns + MORE] = jnp.transpose(extra_ref[...]).astype(BF16)
    out_ref[:, columns + MORE :] = jnp.zeros((out_ref.shape[0], MORE), BF16)


def first_grads(normed, grad_query, attended, branch, every):
    tok, model = normed.shape
    width = attended.shape[0]
    half = width // LANES
    return pl.pallas_call(
        first_grads_kernel,
        grid=(model // LANES,),
        in_specs=[
            pl.BlockSpec((tok, LANES), lambda i: (0, i)),
            pl.BlockSpec((width, tok), lambda i: (0, 0)),
            pl.BlockSpec((LANES, tok), lambda i: (i % half, 0)),
            pl.BlockSpec((tok, width), lambda i: (0, i // half)),
        ],
        out_specs=pl.BlockSpec((LANES, 2 * width), lambda i: (i, 0)),
        out_shape=jax.ShapeDtypeStruct((model, every), BF16),
        cost_estimate=pl.CostEstimate(
            flops=4 * tok * model * width, bytes_accessed=4 * model * width, transcendentals=0
        ),
    )(normed, grad_query, attended, branch)


def last_grads(normed, grad_kv, extra, parts):
    tok, model = normed.shape
    columns = grad_kv.shape[0]
    every = parts.shape[1]
    size = columns + 2 * MORE
    return pl.pallas_call(
        last_grads_kernel,
        grid=(model // LANES,),
        in_specs=[
            pl.BlockSpec((tok, LANES), lambda i: (0, i)),
            pl.BlockSpec((columns, tok), lambda i: (0, 0)),
            pl.BlockSpec((MORE, LANES), lambda i: (0, i)),
            pl.BlockSpec(memory_space=pl.ANY),
        ],
        out_specs=pl.BlockSpec((LANES, size), lambda i: (i, (every - size) // size)),
        out_shape=jax.ShapeDtypeStruct(parts.shape, BF16),
        input_output_aliases={3: 0},
        cost_estimate=pl.CostEstimate(
            flops=2 * tok * model * columns, bytes_accessed=2 * model * size, transcendentals=0
        ),
    )(normed, grad_kv, extra, parts)


def unpack_kernel(
    devices, in_ref, query_ref, key_ref, clip_ref,
    wo_ref, wq_ref, wk_ref, wv_ref, sum_ref, cq_ref, ck_ref, peak_ref, sq_ref, sk_ref,
):
    at = 0
    group = cq_ref.shape[1] // ck_ref.shape[1]
    heads = cq_ref.shape[1] // HD
    start = 2 * (wo_ref.shape[1] + wk_ref.shape[1])

    @pl.when(pl.program_id(0) == 0)
    def _():
        lines = in_ref[:devices, start : start + MORE].astype(F32)
        high, low = (lines[:, 2 : 2 + heads], lines[:, 2 + heads : 2 + 2 * heads])
        peak = jnp.max(high + low, axis=0, keepdims=True)
        clip = clip_ref[...]
        scale = jnp.sqrt(clip / jnp.maximum(peak, clip))
        peak_ref[...] = peak
        each = lax.broadcasted_iota(jnp.int32, sq_ref.shape, 1) // HD
        of_key = lax.broadcasted_iota(jnp.int32, sk_ref.shape, 1) // HD
        query_scale, key_scale = (jnp.zeros(sq_ref.shape, F32), jnp.zeros(sk_ref.shape, F32))
        for h in range(heads):
            query_scale = jnp.where(each == h, scale[:, h : h + 1], query_scale)
        for g in range(heads // group):
            least = jnp.min(scale[:, g * group : (g + 1) * group], axis=1, keepdims=True)
            key_scale = jnp.where(of_key == g, least, key_scale)
        sq_ref[...] = query_scale
        sk_ref[...] = key_scale

    for target in (wo_ref, wq_ref, wk_ref, wv_ref):
        size = target.shape[1]
        target[...] = in_ref[:, at : at + size].astype(F32)
        at += size
    sum_ref[...] = jnp.transpose(in_ref[:, at : at + MORE].astype(F32))[: sum_ref.shape[0]]
    cq_ref[...] = (query_ref[...].astype(F32) * sq_ref[...]).astype(BF16)
    ck_ref[...] = (key_ref[...].astype(F32) * sk_ref[...]).astype(BF16)


def unpack(summed, w_query, w_key, clip_limit, devices):
    total, every = summed.shape
    width, narrow = (w_query.shape[1], w_key.shape[1])
    steps = total // LANES
    wide = pl.BlockSpec((LANES, width), lambda i: (i, 0))
    thin = pl.BlockSpec((LANES, narrow), lambda i: (i, 0))
    heads = width // HD
    line = pl.BlockSpec((1, heads), lambda i: (0, 0))
    return pl.pallas_call(
        functools.partial(unpack_kernel, devices),
        grid=(steps,),
        in_specs=[
            pl.BlockSpec((LANES, every), lambda i: (i, 0)),
            wide,
            thin,
            line,
        ],
        out_specs=[
            pl.BlockSpec((LANES, width), lambda i: (i % (steps // 2), i // (steps // 2))),
            wide,
            thin,
            thin,
            pl.BlockSpec((8, LANES), lambda i: (0, i)),
            wide,
            thin,
            line,
        ],
        scratch_shapes=[pltpu.VMEM((1, width), F32), pltpu.VMEM((1, narrow), F32)],
        out_shape=[
            jax.ShapeDtypeStruct((total // 2, 2 * width), F32),
            jax.ShapeDtypeStruct((total, width), F32),
            jax.ShapeDtypeStruct((total, narrow), F32),
            jax.ShapeDtypeStruct((total, narrow), F32),
            jax.ShapeDtypeStruct((8, total), F32),
            jax.ShapeDtypeStruct((total, width), BF16),
            jax.ShapeDtypeStruct((total, narrow), BF16),
            jax.ShapeDtypeStruct((1, heads), F32),
        ],
        compiler_params=pltpu.CompilerParams(vmem_limit_bytes=60 << 20),
        cost_estimate=pl.CostEstimate(
            flops=total * every, bytes_accessed=8 * total * every, transcendentals=0
        ),
    )(summed, w_query, w_key, clip_limit.reshape(1, heads))


def rms_scale(values):
    return lax.rsqrt(jnp.mean(values * values, axis=-1, keepdims=True) + EPS)


def norm_back(grad_normed, hidden, inverse, gain):
    weighted = grad_normed * gain
    grad_gain = jnp.sum(grad_normed * hidden * inverse, axis=0)
    grad_hidden = inverse * weighted - hidden * inverse**3 * jnp.mean(
        weighted * hidden, axis=-1, keepdims=True
    )
    return (grad_hidden, grad_gain)


def shards(
    tokens,
    out_grad,
    norm1_gain,
    norm2_gain,
    w_query,
    w_key,
    w_value,
    w_out,
    w_gate,
    w_up,
    w_down,
    route_ids,
    route_logits,
    seq_ids,
    piece_ids,
    clip_limit,
):
    tok_dev, model_width = tokens.shape
    dp_size = lax.axis_size("dp")
    tensor_size = lax.axis_size("tensor")
    core = lax.axis_index("tensor")
    local_heads = w_query.shape[1] // HD
    local_kv = w_key.shape[1] // HD
    group = local_heads // local_kv
    plane_groups = [list(range(at, at + PLANE)) for at in range(0, dp_size, PLANE)]
    column_groups = [list(range(at, dp_size, PLANE)) for at in range(PLANE)]


    picks = route_ids.T
    logits = route_logits.T
    gate_exp = jnp.exp(logits - jnp.max(logits, axis=0, keepdims=True))
    gates = gate_exp / jnp.sum(gate_exp, axis=0, keepdims=True)
    number = jnp.arange(PLANE * SEGMENTS, dtype=jnp.int32)
    number = number % SEGMENTS * PLANE + number // SEGMENTS
    same = picks[None] == number[:, None, None]
    member = jnp.any(same, axis=1)
    gate_of = jnp.sum(jnp.where(same, gates[None], 0.0), axis=1)
    place = jnp.arange(tok_dev, dtype=jnp.int32)
    before = (place[:, None] < place[None, :]).astype(BF16)
    rank = contract(member.astype(BF16), before, NN)
    rank = jnp.where(member, rank, -1.0)
    wanted = (tensor_size * jnp.arange(RANK_ROWS, dtype=jnp.int32) + core).astype(F32)
    chosen = rank[:, None, :] == wanted[None, :, None]
    pick = chosen.astype(BF16).reshape(-1, tok_dev)
    gated = jnp.where(chosen, gate_of[:, None, :], 0.0)
    slot_gate = jnp.sum(gated, axis=2).reshape(-1, 1)
    gated = gated.astype(BF16).reshape(-1, tok_dev)

    def in_plane(rows):
        rows = rows.reshape(PLANE, -1, model_width)
        return lax.all_to_all(rows, "dp", 0, 0, tiled=True, axis_index_groups=plane_groups)

    def grads_for(first, last):
        shape = (PLANE, SEGMENTS * RANK_ROWS, -1)
        part = pick.reshape(shape)[:, first * RANK_ROWS : last * RANK_ROWS].reshape(-1, tok_dev)
        gate = slot_gate.reshape(shape)[:, first * RANK_ROWS : last * RANK_ROWS].reshape(-1, 1)
        return (contract(part, out_grad, NN) * gate).astype(BF16)

    grads_early = in_plane(grads_for(0, EARLY))
    grads_late = grads_for(EARLY, SEGMENTS)

    cosine, sine = rope_tables(tok_dev, dp_size)
    x_float = tokens.astype(F32)
    inverse1 = rms_scale(x_float)
    normed1 = (x_float * inverse1 * norm1_gain).astype(BF16)
    query = rotate(contract(w_query, normed1, ((0,), (1,))), cosine, sine)
    query = (query * (HD**-0.5)).astype(BF16)
    key = rotate(contract(w_key, normed1, ((0,), (1,))), cosine, sine).astype(BF16)
    value = contract(w_value, normed1, ((0,), (1,))).astype(BF16)
    side = jnp.concatenate(
        [(seq_ids + 1)[None], piece_ids[None], jnp.zeros((AUX - 2, tok_dev), jnp.int32)]
    ).astype(BF16)
    block = jnp.concatenate([key, value, side])
    blocks = tuple(passed_along(block, hop) for hop in range(HOPS, 0, -1)) + (block,)
    blocks, grads_early, grads_late = lax.optimization_barrier((blocks, grads_early, grads_late))
    packed_w = pack_weights(w_gate[0], w_up[0], w_down[0])
    own = lax.all_gather(packed_w, "dp", axis=0, axis_index_groups=column_groups)
    grad_rows = (grads_early, in_plane(grads_late))
    attended, log_total, peaks = attend(query, blocks, group)
    attn_part = contract(attended, w_out, TN)
    hidden1 = x_float + (attn_part + swapped(attn_part))
    inverse2 = rms_scale(hidden1)
    normed2 = (hidden1 * inverse2 * norm2_gain).astype(BF16)

    rows_out = contract(pick, normed2, NN).astype(BF16)
    rows_out = after(rows_out, grad_rows[1])
    own = after(own, rows_out)
    peer = swapped(own)
    rows_in = in_plane(rows_out)
    out_early = in_plane(expert_first(rows_in, own, peer))
    back, own_acts, peer_acts = expert_back(rows_in, grad_rows, own, peer)

    def combined(weights, rows):
        part = contract(weights, rows.reshape(-1, model_width), TN).astype(BF16)
        return part.astype(F32) + swapped(part).astype(F32)

    sum_own, *sum_peer, out_late = expert_sums(rows_in, grad_rows, own_acts, peer_acts, own, peer)
    sums = both_cores(sum_own, [swapped(part) for part in sum_peer], dp_size // PLANE)
    back = in_plane(after(back, out_early))
    out_late = in_plane(after(out_late, back))
    grad_normed2 = combined(pick, after(back, sums))
    sums = lax.psum_scatter(
        sums, "dp", scatter_dimension=0, tiled=True, axis_index_groups=column_groups
    )

    grad_top = out_grad.astype(F32)
    grad_from_norm2, grad_gain2 = norm_back(grad_normed2, hidden1, inverse2, norm2_gain)
    grad_hidden1 = grad_top + grad_from_norm2
    grad_branch = grad_hidden1.astype(BF16)
    grad_attended = contract(w_out, grad_branch, NT).astype(BF16)
    grad_query_pre, *grad_blocks = attend_back(
        query, grad_attended, log_total, cosine, sine, blocks, group
    )
    every = 2 * w_query.shape[1] + 2 * w_key.shape[1] + 2 * MORE
    parts = first_grads(normed1, grad_query_pre, attended, grad_branch, every)
    returned = [
        passed_along(grad_blocks[number], -hop) for number, hop in enumerate(range(HOPS, 0, -1))
    ]
    returned = after(returned, parts)
    kv_total = grad_blocks[-1]
    for part in returned:
        kv_total = kv_total + part.astype(F32)
    kv_rows = local_kv * HD
    grad_key_pre = rotate(kv_total[:kv_rows], cosine, -sine).astype(BF16)
    grad_value = kv_total[kv_rows:].astype(BF16)

    grad_norm1_part = (
        contract(grad_query_pre, w_query, ((0,), (1,)))
        + contract(grad_key_pre, w_key, ((0,), (1,)))
        + contract(grad_value, w_value, ((0,), (1,)))
    ).astype(BF16)

    grad_normed1 = grad_norm1_part.astype(F32) + swapped(grad_norm1_part).astype(F32)
    grad_from_norm1, grad_gain1 = norm_back(grad_normed1, x_float, inverse1, norm1_gain)
    input_grad = grad_hidden1 + grad_from_norm1
    peak = jnp.max(peaks, axis=1)
    peak_high = peak.astype(BF16).astype(F32)
    peak_pair = jnp.concatenate([peak_high, peak - peak_high])
    places = jnp.arange(model_width)[None] == lax.axis_index("dp")
    peak_rows = jnp.where(places, peak_pair[:, None], 0.0)
    extra = jnp.concatenate([grad_gain1[None], grad_gain2[None], peak_rows])
    extra = jnp.pad(extra, ((0, MORE - len(extra)), (0, 0)))
    parts = last_grads(normed1, jnp.concatenate([grad_key_pre, grad_value]), extra, parts)
    parts, sums, out_early, out_late = lax.optimization_barrier((parts, sums, out_early, out_late))
    summed = lax.psum(parts, "dp")
    expert_out = jnp.concatenate([out_early, out_late], axis=1)
    output = (hidden1 + combined(gated, expert_out)).astype(BF16)
    grad_gate, grad_up, grad_down = jnp.split(sums[0].astype(F32), 3, axis=1)
    grad_down = grad_down.T
    grad_wo, grad_wq, grad_wk, grad_wv, totals, clipped_query, clipped_key, head_peaks = unpack(
        summed, w_query, w_key, clip_limit, dp_size
    )
    return (
        output,
        input_grad,
        grad_wq,
        grad_wk,
        grad_wv,
        grad_wo,
        totals[0],
        totals[1],
        grad_gate[None],
        grad_up[None],
        grad_down[None],
        clipped_query,
        clipped_key,
        head_peaks.reshape(-1),
    )


def solution(mesh):
    in_specs = (
        P("dp", None),
        P("dp", None),
        P(),
        P(),
        P(None, "tensor"),
        P(None, "tensor"),
        P(None, "tensor"),
        P("tensor", None),
        P("dp", None, "tensor"),
        P("dp", None, "tensor"),
        P("dp", "tensor", None),
        P("dp", None),
        P("dp", None),
        P("dp"),
        P("dp"),
        P("tensor"),
    )
    out_specs = (
        P("dp", None),
        P("dp", None),
        P(None, "tensor"),
        P(None, "tensor"),
        P(None, "tensor"),
        P("tensor", None),
        P(),
        P(),
        P("dp", None, "tensor"),
        P("dp", None, "tensor"),
        P("dp", "tensor", None),
        P(None, "tensor"),
        P(None, "tensor"),
        P("tensor"),
    )
    return jax.shard_map(shards, mesh=mesh, in_specs=in_specs, out_specs=out_specs, check_vma=False)
```

```python
import functools
import math

import jax
import jax.numpy as jnp
import numpy as np
from jax import lax
from jax.experimental import pallas as pl
from jax.experimental.pallas import tpu as pltpu
from jax.sharding import PartitionSpec as P

HD = 64
TOP = 8
CAP = 64
HOPS = 4
RANK_ROWS = 32
PLANE = 16
SEGMENTS = 3
EARLY = 1
AUX = 16
LANES = 256
MORE = 128

EPS = 1e-06
ROPE_BASE = 10000.0
NEG_FILL = -1e30
BF16 = jnp.bfloat16
F32 = jnp.float32


def contract(left, right, dims):
    return lax.dot_general(left, right, (dims, ((), ())), preferred_element_type=F32)


NN = ((1,), (0,))
NT = ((1,), (1,))
TN = ((0,), (0,))


def swapped(array):
    return lax.ppermute(array, "tensor", [(0, 1), (1, 0)])


def after(array, other):
    return lax.optimization_barrier((array, other))[0]


def passed_along(value, steps):
    count = lax.axis_size("dp")
    first, last = (max(0, -steps), min(count, count - steps))
    return lax.ppermute(value, "dp", [(s, s + steps) for s in range(first, last)])


def rope_tables(count, dp_size):
    freq = np.exp(np.arange(HD // 2) * (-2.0 * math.log(ROPE_BASE) / HD))
    base = np.arange(dp_size)[:, None] * count * freq[None, :]
    local = freq[:, None] * np.arange(count)[None, :]
    index = lax.axis_index("dp")
    cos_base = jnp.asarray(np.cos(base), F32)[index][:, None]
    sin_base = jnp.asarray(np.sin(base), F32)[index][:, None]
    cos_local, sin_local = (jnp.asarray(np.cos(local), F32), jnp.asarray(np.sin(local), F32))
    return (
        cos_base * cos_local - sin_base * sin_local,
        sin_base * cos_local + cos_base * sin_local,
    )


def rotate(values, cosine, sine):
    half = HD // 2
    heads = values.reshape(-1, HD, values.shape[-1])
    first, second = (heads[:, :half], heads[:, half:])
    turned = jnp.concatenate(
        [first * cosine - second * sine, second * cosine + first * sine], axis=1
    )
    return turned.reshape(values.shape)


def fill_bias(blocks, bias):
    tok = bias.shape[1]
    rows = blocks[-1].shape[0] - AUX
    own = blocks[-1][rows:, :].astype(F32)
    seq_q, piece_q = (own[0:1, :], own[1:2, :])
    for number, block in enumerate(blocks):
        side = jnp.transpose(block[rows:, :].astype(F32))
        keep = side[:, 0:1] == seq_q
        if number == len(blocks) - 1:
            at_key = lax.broadcasted_iota(jnp.int32, (tok, tok), 0)
            at_query = lax.broadcasted_iota(jnp.int32, (tok, tok), 1)
            piece = (side[:, 1:2] == piece_q) & (piece_q > 0.0)
            keep = keep & ((at_key <= at_query) | piece)
        bias[number * tok : (number + 1) * tok, :] = jnp.where(keep, 0.0, NEG_FILL)


def all_keys(blocks, start):
    return jnp.concatenate([block[pl.ds(start, HD), :] for block in blocks], axis=1)


def attend_kernel(group, q_ref, k4, k3, k2, k1, k0, out_ref, log_ref, peak_ref, bias):
    blocks = (k4, k3, k2, k1, k0)
    fill_bias(blocks, bias)
    kv_rows = (k0.shape[0] - AUX) // 2

    def one_group(g, _):
        at = pl.multiple_of(g * HD, HD)
        keys = all_keys(blocks, at)
        values = all_keys(blocks, kv_rows + at)
        for j in range(group):
            head = g * group + j
            here = pl.ds(pl.multiple_of(head * HD, HD), HD)
            scores = contract(keys, q_ref[here, :], TN) + bias[...]
            peak = jnp.max(scores, axis=0, keepdims=True)
            weight = jnp.exp(scores - peak)
            total = jnp.sum(weight, axis=0, keepdims=True)
            mixed = contract(values, weight.astype(BF16), NN) * (1.0 / total)
            out_ref[here, :] = mixed.astype(BF16)
            log_ref[pl.ds(head, 1), :] = peak + jnp.log(total)
            peak_ref[pl.ds(head, 1), :] = peak
        return 0

    lax.fori_loop(0, kv_rows // HD, one_group, 0)


def attend(q, blocks, group):
    rows, tok = q.shape
    heads = rows // HD
    return pl.pallas_call(
        functools.partial(attend_kernel, group),
        out_shape=(
            jax.ShapeDtypeStruct((rows, tok), BF16),
            jax.ShapeDtypeStruct((heads, tok), F32),
            jax.ShapeDtypeStruct((heads, tok), F32),
        ),
        scratch_shapes=[pltpu.VMEM((len(blocks) * tok, tok), F32)],
        compiler_params=pltpu.CompilerParams(vmem_limit_bytes=48 << 20),
        cost_estimate=pl.CostEstimate(
            flops=4 * rows * tok * tok * len(blocks),
            bytes_accessed=4 * rows * tok + 2 * len(blocks) * 528 * tok,
            transcendentals=heads * tok * tok * len(blocks),
        ),
    )(q, *blocks)


def attend_back_kernel(
    group, q_ref, g_ref, log_ref, cos_ref, sin_ref, k4, k3, k2, k1, k0,
    dq_ref, d4, d3, d2, d1, d0, bias,
):
    blocks = (k4, k3, k2, k1, k0)
    grads = (d4, d3, d2, d1, d0)
    fill_bias(blocks, bias)
    kv_rows = (k0.shape[0] - AUX) // 2
    tok = bias.shape[1]
    half = HD // 2

    def one_group(g, _):
        at = pl.multiple_of(g * HD, HD)
        keys = all_keys(blocks, at)
        values = all_keys(blocks, kv_rows + at)
        key_sum = value_sum = None
        for j in range(group):
            head = g * group + j
            start = pl.multiple_of(head * HD, HD)
            query, grad = (q_ref[pl.ds(start, HD), :], g_ref[pl.ds(start, HD), :])
            scores = contract(keys, query, TN) + bias[...]
            probs = jnp.exp(scores - log_ref[pl.ds(head, 1), :])
            grad_probs = contract(values, grad, TN)
            delta = jnp.sum(probs * grad_probs, axis=0, keepdims=True)
            grad_scores = (probs * (grad_probs - delta)).astype(BF16)
            key_part = contract(query, grad_scores, NT)
            value_part = contract(grad, probs.astype(BF16), NT)
            key_sum = key_part if key_sum is None else key_sum + key_part
            value_sum = value_part if value_sum is None else value_sum + value_part
            turned = contract(keys, grad_scores, NN) * (HD**-0.5)
            first, second = (turned[:half], turned[half:])
            cosine, sine = (cos_ref[...], sin_ref[...])
            dq_ref[pl.ds(start, half), :] = (first * cosine + second * sine).astype(BF16)
            dq_ref[pl.ds(start + half, half), :] = (second * cosine - first * sine).astype(BF16)
        for number, grad_ref in enumerate(grads):
            piece = slice(number * tok, (number + 1) * tok)
            grad_ref[pl.ds(at, HD), :] = key_sum[:, piece].astype(grad_ref.dtype)
            grad_ref[pl.ds(kv_rows + at, HD), :] = value_sum[:, piece].astype(grad_ref.dtype)
        return 0

    lax.fori_loop(0, kv_rows // HD, one_group, 0)


def attend_back(q, grad, log_total, cosine, sine, blocks, group):
    rows, tok = q.shape
    kv = blocks[0].shape[0] - AUX
    return pl.pallas_call(
        functools.partial(attend_back_kernel, group),
        out_shape=(
            jax.ShapeDtypeStruct((rows, tok), BF16),
            *(jax.ShapeDtypeStruct((kv, tok), BF16) for _ in blocks[1:]),
            jax.ShapeDtypeStruct((kv, tok), F32),
        ),
        scratch_shapes=[pltpu.VMEM((len(blocks) * tok, tok), F32)],
        compiler_params=pltpu.CompilerParams(vmem_limit_bytes=48 << 20),
        cost_estimate=pl.CostEstimate(
            flops=500 * rows * tok * tok * len(blocks),
            bytes_accessed=6 * rows * tok + 4 * len(blocks) * 528 * tok,
            transcendentals=rows // HD * tok * tok * len(blocks),
        ),
    )(q, grad, log_total, cosine, sine, *blocks)


def pack_weights_kernel(gate_ref, up_ref, down_ref, out_ref):
    hidden = gate_ref.shape[1]
    out_ref[:, :hidden] = gate_ref[...]
    out_ref[:, hidden : 2 * hidden] = up_ref[...]
    out_ref[:, 2 * hidden :] = jnp.transpose(down_ref[...].astype(F32)).astype(BF16)


def pack_weights(gate, up, down):
    width, hidden = gate.shape
    rows = width // 2
    thin = pl.BlockSpec((rows, hidden), lambda i: (i, 0))
    return pl.pallas_call(
        pack_weights_kernel,
        grid=(2,),
        in_specs=[thin, thin, pl.BlockSpec((hidden, rows), lambda i: (0, i))],
        out_specs=pl.BlockSpec((rows, 3 * hidden), lambda i: (i, 0)),
        out_shape=jax.ShapeDtypeStruct((width, 3 * hidden), BF16),
        cost_estimate=pl.CostEstimate(
            flops=width * hidden, bytes_accessed=12 * width * hidden, transcendentals=0
        ),
    )(gate, up, down)


def expert_first_kernel(x_ref, own_ref, peer_ref, out_ref):
    width = x_ref.shape[-1]
    rows = x_ref[...].reshape(-1, width)
    hidden = own_ref.shape[-1] // 3
    out = None
    for weights in (own_ref, peer_ref):
        both = contract(rows, weights[0, :, : 2 * hidden], NN)
        gate_act, up_act = (both[:, :hidden], both[:, hidden:])
        inner = gate_act * (1.0 / (1.0 + jnp.exp(-gate_act))) * up_act
        part = contract(inner.astype(BF16), weights[0, :, 2 * hidden :], NT)
        out = part if out is None else out + part
    out_ref[...] = out.astype(BF16).reshape(out_ref.shape)


def expert_first(rows, own, peer):
    sources, _, width = rows.shape
    triple = own.shape[-1]
    step = sources // 2
    part = pl.BlockSpec((step, RANK_ROWS, width), lambda s, j: (j, s, 0))
    weight = pl.BlockSpec((1, width, triple), lambda s, j: (s, 0, 0))
    return pl.pallas_call(
        expert_first_kernel,
        grid=(EARLY, 2),
        in_specs=[part, weight, weight],
        out_specs=part,
        out_shape=jax.ShapeDtypeStruct((sources, EARLY * RANK_ROWS, width), BF16),
        compiler_params=pltpu.CompilerParams(vmem_limit_bytes=56 << 20),
        cost_estimate=pl.CostEstimate(
            flops=4 * sources * EARLY * RANK_ROWS * width * triple,
            bytes_accessed=4 * sources * EARLY * RANK_ROWS * width + 4 * EARLY * width * triple,
            transcendentals=sources * EARLY * RANK_ROWS * triple * 2 // 3,
        ),
    )(rows, own, peer)


def of_segment(early_ref, late_ref):
    width = early_ref.shape[-1]
    chosen = jnp.where(pl.program_id(0) < EARLY, early_ref[...], late_ref[...])
    return chosen.reshape(-1, width)


def expert_kernel(x1_ref, x2_ref, g1_ref, g2_ref, own_ref, peer_ref, dx_ref, own_acts, peer_acts):
    rows, grads = (of_segment(x1_ref, x2_ref), of_segment(g1_ref, g2_ref))
    hidden = own_ref.shape[-1] // 3
    back = None
    for weights, acts in ((own_ref, own_acts), (peer_ref, peer_acts)):
        both = contract(rows, weights[0, :, : 2 * hidden], NN)
        grad_inner = contract(grads, weights[0, :, 2 * hidden :], NN)
        gate_act, up_act = (both[:, :hidden], both[:, hidden:])
        sigmoid = 1.0 / (1.0 + jnp.exp(-gate_act))
        silu = gate_act * sigmoid
        dgate = grad_inner * up_act * (sigmoid * (1.0 + gate_act * (1.0 - sigmoid)))
        acts[0, :, :hidden] = dgate.astype(BF16)
        acts[0, :, hidden : 2 * hidden] = (grad_inner * silu).astype(BF16)
        acts[0, :, 2 * hidden :] = (silu * up_act).astype(BF16)
        part = contract(acts[0, :, : 2 * hidden], weights[0, :, : 2 * hidden], NT)
        back = part if back is None else back + part
    dx_ref[...] = back.astype(BF16).reshape(dx_ref.shape)


def segment_specs(block):
    return [
        pl.BlockSpec(block, lambda s: (0, s, 0)),
        pl.BlockSpec(block, lambda s: (0, jnp.minimum(s, EARLY - 1), 0)),
        pl.BlockSpec(block, lambda s: (0, jnp.maximum(s - EARLY, 0), 0)),
    ]


def expert_back(rows, grads, own, peer):
    sources, _, width = rows[0].shape
    segments, triple = (SEGMENTS, own.shape[-1])
    lines = segments * RANK_ROWS
    count = sources * RANK_ROWS
    specs = segment_specs((sources, RANK_ROWS, width))
    wide = specs[0]
    weight = pl.BlockSpec((1, width, triple), lambda s: (s, 0, 0))
    act = pl.BlockSpec((1, count, triple), lambda s: (s, 0, 0))
    return pl.pallas_call(
        expert_kernel,
        grid=(segments,),
        in_specs=[*specs[1:], *specs[1:], weight, weight],
        out_specs=[wide, act, act],
        out_shape=[
            jax.ShapeDtypeStruct((sources, lines, width), BF16),
            jax.ShapeDtypeStruct((segments, count, triple), BF16),
            jax.ShapeDtypeStruct((segments, count, triple), BF16),
        ],
        compiler_params=pltpu.CompilerParams(vmem_limit_bytes=56 << 20),
        cost_estimate=pl.CostEstimate(
            flops=7 * sources * lines * width * triple,
            bytes_accessed=6 * sources * lines * width + 4 * segments * width * triple,
            transcendentals=2 * sources * lines * triple // 3,
        ),
    )(*rows, *grads, own, peer)


def expert_sums_kernel(
    x1_ref, x2_ref, g1_ref, g2_ref, own_acts, peer_acts, own_ref, peer_ref, sum_own, *outs
):
    rows, grads = (of_segment(x1_ref, x2_ref), of_segment(g1_ref, g2_ref))
    hidden = own_ref.shape[-1]
    late_ref = outs[3]
    segment = pl.program_id(0)
    for side, acts in enumerate((own_acts, peer_acts)):
        first = contract(rows, acts[0, :, : 2 * hidden], TN).astype(BF16)
        second = contract(grads, acts[0, :, 2 * hidden :], TN).astype(BF16)
        if side == 0:
            sum_own[0, :, : 2 * hidden] = first
            sum_own[0, :, 2 * hidden :] = second
        else:
            outs[0][0] = first[:, :hidden]
            outs[1][0] = first[:, hidden:]
            outs[2][0] = second

    @pl.when(segment >= EARLY)
    def _():
        out = contract(own_acts[0, :, 2 * hidden :], own_ref[0], NT)
        out = out + contract(peer_acts[0, :, 2 * hidden :], peer_ref[0], NT)
        late_ref[...] = out.astype(BF16).reshape(late_ref.shape)


def expert_sums(rows, grads, own_acts, peer_acts, own, peer):
    sources, _, width = rows[0].shape
    segments, triple = (SEGMENTS, own.shape[-1])
    lines = segments * RANK_ROWS
    hidden = triple // 3
    count = sources * RANK_ROWS
    block = (sources, RANK_ROWS, width)
    down = pl.BlockSpec((1, width, hidden), lambda s: (s, 0, 2))
    act = pl.BlockSpec((1, count, triple), lambda s: (s, 0, 0))
    return pl.pallas_call(
        expert_sums_kernel,
        grid=(segments,),
        in_specs=[*segment_specs(block)[1:] * 2, act, act, down, down],
        out_specs=[pl.BlockSpec((1, width, triple), lambda s: (s, 0, 0))]
        + [pl.BlockSpec((1, width, hidden), lambda s: (s, 0, 0))] * 3
        + [pl.BlockSpec(block, lambda s: (0, jnp.maximum(s - EARLY, 0), 0))],
        out_shape=[jax.ShapeDtypeStruct((segments, width, triple), BF16)]
        + [jax.ShapeDtypeStruct((segments, width, hidden), BF16)] * 3
        + [jax.ShapeDtypeStruct((sources, (segments - EARLY) * RANK_ROWS, width), BF16)],
        compiler_params=pltpu.CompilerParams(vmem_limit_bytes=60 << 20),
        cost_estimate=pl.CostEstimate(
            flops=6 * sources * lines * width * triple,
            bytes_accessed=6 * sources * lines * width + 5 * segments * width * triple,
            transcendentals=0,
        ),
    )(*rows, *grads, own_acts, peer_acts, own, peer)


def both_cores_kernel(own_ref, *refs):
    out_ref = refs[-1]
    hidden = refs[0].shape[-1]

    @pl.when(pl.program_id(0) < SEGMENTS)
    def _():
        for kind, peer_ref in enumerate(refs[:-1]):
            here = slice(kind * hidden, (kind + 1) * hidden)
            total = own_ref[0, :, here].astype(F32) + peer_ref[0].astype(F32)
            out_ref[0, :, here] = total.astype(BF16)

    @pl.when(pl.program_id(0) >= SEGMENTS)
    def _():
        out_ref[...] = jnp.zeros_like(out_ref)


def both_cores(own, peers, slots):
    segments, width, triple = own.shape
    rows = width // 2
    last = segments - 1
    part = pl.BlockSpec((1, rows, triple), lambda s, r: (jnp.minimum(s, last), r, 0))
    thin = pl.BlockSpec((1, rows, triple // 3), lambda s, r: (jnp.minimum(s, last), r, 0))
    return pl.pallas_call(
        both_cores_kernel,
        grid=(slots, 2),
        in_specs=[part] + [thin] * 3,
        out_specs=pl.BlockSpec((1, rows, triple), lambda s, r: (s, r, 0)),
        out_shape=jax.ShapeDtypeStruct((slots, width, triple), BF16),
        cost_estimate=pl.CostEstimate(
            flops=slots * width * triple, bytes_accessed=6 * slots * width * triple, transcendentals=0
        ),
    )(own, *peers)


def first_grads_kernel(normed_ref, query_ref, attended_ref, branch_ref, out_ref):
    width = branch_ref.shape[1]
    out_ref[:, :width] = contract(attended_ref[...], branch_ref[...], NN).astype(BF16)
    out_ref[:, width:] = contract(normed_ref[...], query_ref[...], ((0,), (1,))).astype(BF16)


def last_grads_kernel(normed_ref, kv_ref, extra_ref, _, out_ref):
    columns = kv_ref.shape[0]
    out_ref[:, :columns] = contract(normed_ref[...], kv_ref[...], ((0,), (1,))).astype(BF16)
    out_ref[:, columns : columns + MORE] = jnp.transpose(extra_ref[...]).astype(BF16)
    out_ref[:, columns + MORE :] = jnp.zeros((out_ref.shape[0], MORE), BF16)


def first_grads(normed, grad_query, attended, branch, every):
    tok, model = normed.shape
    width = attended.shape[0]
    half = width // LANES
    return pl.pallas_call(
        first_grads_kernel,
        grid=(model // LANES,),
        in_specs=[
            pl.BlockSpec((tok, LANES), lambda i: (0, i)),
            pl.BlockSpec((width, tok), lambda i: (0, 0)),
            pl.BlockSpec((LANES, tok), lambda i: (i % half, 0)),
            pl.BlockSpec((tok, width), lambda i: (0, i // half)),
        ],
        out_specs=pl.BlockSpec((LANES, 2 * width), lambda i: (i, 0)),
        out_shape=jax.ShapeDtypeStruct((model, every), BF16),
        cost_estimate=pl.CostEstimate(
            flops=4 * tok * model * width, bytes_accessed=4 * model * width, transcendentals=0
        ),
    )(normed, grad_query, attended, branch)


def last_grads(normed, grad_kv, extra, parts):
    tok, model = normed.shape
    columns = grad_kv.shape[0]
    every = parts.shape[1]
    size = columns + 2 * MORE
    return pl.pallas_call(
        last_grads_kernel,
        grid=(model // LANES,),
        in_specs=[
            pl.BlockSpec((tok, LANES), lambda i: (0, i)),
            pl.BlockSpec((columns, tok), lambda i: (0, 0)),
            pl.BlockSpec((MORE, LANES), lambda i: (0, i)),
            pl.BlockSpec(memory_space=pl.ANY),
        ],
        out_specs=pl.BlockSpec((LANES, size), lambda i: (i, (every - size) // size)),
        out_shape=jax.ShapeDtypeStruct(parts.shape, BF16),
        input_output_aliases={3: 0},
        cost_estimate=pl.CostEstimate(
            flops=2 * tok * model * columns, bytes_accessed=2 * model * size, transcendentals=0
        ),
    )(normed, grad_kv, extra, parts)


def unpack_kernel(
    devices, in_ref, query_ref, key_ref, clip_ref,
    wo_ref, wq_ref, wk_ref, wv_ref, sum_ref, cq_ref, ck_ref, peak_ref, sq_ref, sk_ref,
):
    at = 0
    group = cq_ref.shape[1] // ck_ref.shape[1]
    heads = cq_ref.shape[1] // HD
    start = 2 * (wo_ref.shape[1] + wk_ref.shape[1])

    @pl.when(pl.program_id(0) == 0)
    def _():
        lines = in_ref[:devices, start : start + MORE].astype(F32)
        high, low = (lines[:, 2 : 2 + heads], lines[:, 2 + heads : 2 + 2 * heads])
        peak = jnp.max(high + low, axis=0, keepdims=True)
        clip = clip_ref[...]
        scale = jnp.sqrt(clip / jnp.maximum(peak, clip))
        peak_ref[...] = peak
        each = lax.broadcasted_iota(jnp.int32, sq_ref.shape, 1) // HD
        of_key = lax.broadcasted_iota(jnp.int32, sk_ref.shape, 1) // HD
        query_scale, key_scale = (jnp.zeros(sq_ref.shape, F32), jnp.zeros(sk_ref.shape, F32))
        for h in range(heads):
            query_scale = jnp.where(each == h, scale[:, h : h + 1], query_scale)
        for g in range(heads // group):
            least = jnp.min(scale[:, g * group : (g + 1) * group], axis=1, keepdims=True)
            key_scale = jnp.where(of_key == g, least, key_scale)
        sq_ref[...] = query_scale
        sk_ref[...] = key_scale

    for target in (wo_ref, wq_ref, wk_ref, wv_ref):
        size = target.shape[1]
        target[...] = in_ref[:, at : at + size].astype(F32)
        at += size
    sum_ref[...] = jnp.transpose(in_ref[:, at : at + MORE].astype(F32))[: sum_ref.shape[0]]
    cq_ref[...] = (query_ref[...].astype(F32) * sq_ref[...]).astype(BF16)
    ck_ref[...] = (key_ref[...].astype(F32) * sk_ref[...]).astype(BF16)


def unpack(summed, w_query, w_key, clip_limit, devices):
    total, every = summed.shape
    width, narrow = (w_query.shape[1], w_key.shape[1])
    steps = total // LANES
    wide = pl.BlockSpec((LANES, width), lambda i: (i, 0))
    thin = pl.BlockSpec((LANES, narrow), lambda i: (i, 0))
    heads = width // HD
    line = pl.BlockSpec((1, heads), lambda i: (0, 0))
    return pl.pallas_call(
        functools.partial(unpack_kernel, devices),
        grid=(steps,),
        in_specs=[
            pl.BlockSpec((LANES, every), lambda i: (i, 0)),
            wide,
            thin,
            line,
        ],
        out_specs=[
            pl.BlockSpec((LANES, width), lambda i: (i % (steps // 2), i // (steps // 2))),
            wide,
            thin,
            thin,
            pl.BlockSpec((8, LANES), lambda i: (0, i)),
            wide,
            thin,
            line,
        ],
        scratch_shapes=[pltpu.VMEM((1, width), F32), pltpu.VMEM((1, narrow), F32)],
        out_shape=[
            jax.ShapeDtypeStruct((total // 2, 2 * width), F32),
            jax.ShapeDtypeStruct((total, width), F32),
            jax.ShapeDtypeStruct((total, narrow), F32),
            jax.ShapeDtypeStruct((total, narrow), F32),
            jax.ShapeDtypeStruct((8, total), F32),
            jax.ShapeDtypeStruct((total, width), BF16),
            jax.ShapeDtypeStruct((total, narrow), BF16),
            jax.ShapeDtypeStruct((1, heads), F32),
        ],
        compiler_params=pltpu.CompilerParams(vmem_limit_bytes=60 << 20),
        cost_estimate=pl.CostEstimate(
            flops=total * every, bytes_accessed=8 * total * every, transcendentals=0
        ),
    )(summed, w_query, w_key, clip_limit.reshape(1, heads))


def rms_scale(values):
    return lax.rsqrt(jnp.mean(values * values, axis=-1, keepdims=True) + EPS)


def norm_back(grad_normed, hidden, inverse, gain):
    weighted = grad_normed * gain
    grad_gain = jnp.sum(grad_normed * hidden * inverse, axis=0)
    grad_hidden = inverse * weighted - hidden * inverse**3 * jnp.mean(
        weighted * hidden, axis=-1, keepdims=True
    )
    return (grad_hidden, grad_gain)


def shards(
    tokens,
    out_grad,
    norm1_gain,
    norm2_gain,
    w_query,
    w_key,
    w_value,
    w_out,
    w_gate,
    w_up,
    w_down,
    route_ids,
    route_logits,
    seq_ids,
    piece_ids,
    clip_limit,
):
    tok_dev, model_width = tokens.shape
    dp_size = lax.axis_size("dp")
    tensor_size = lax.axis_size("tensor")
    core = lax.axis_index("tensor")
    local_heads = w_query.shape[1] // HD
    local_kv = w_key.shape[1] // HD
    group = local_heads // local_kv
    plane_groups = [list(range(at, at + PLANE)) for at in range(0, dp_size, PLANE)]
    column_groups = [list(range(at, dp_size, PLANE)) for at in range(PLANE)]


    picks = route_ids.T
    logits = route_logits.T
    gate_exp = jnp.exp(logits - jnp.max(logits, axis=0, keepdims=True))
    gates = gate_exp / jnp.sum(gate_exp, axis=0, keepdims=True)
    number = jnp.arange(PLANE * SEGMENTS, dtype=jnp.int32)
    number = number % SEGMENTS * PLANE + number // SEGMENTS
    same = picks[None] == number[:, None, None]
    member = jnp.any(same, axis=1)
    gate_of = jnp.sum(jnp.where(same, gates[None], 0.0), axis=1)
    place = jnp.arange(tok_dev, dtype=jnp.int32)
    before = (place[:, None] < place[None, :]).astype(BF16)
    rank = contract(member.astype(BF16), before, NN)
    rank = jnp.where(member, rank, -1.0)
    wanted = (tensor_size * jnp.arange(RANK_ROWS, dtype=jnp.int32) + core).astype(F32)
    chosen = rank[:, None, :] == wanted[None, :, None]
    pick = chosen.astype(BF16).reshape(-1, tok_dev)
    gated = jnp.where(chosen, gate_of[:, None, :], 0.0)
    slot_gate = jnp.sum(gated, axis=2).reshape(-1, 1)
    gated = gated.astype(BF16).reshape(-1, tok_dev)

    def in_plane(rows):
        rows = rows.reshape(PLANE, -1, model_width)
        return lax.all_to_all(rows, "dp", 0, 0, tiled=True, axis_index_groups=plane_groups)

    shape = (PLANE, SEGMENTS * RANK_ROWS, -1)
    picks_of = tuple(
        pick.reshape(shape)[:, first * RANK_ROWS : last * RANK_ROWS].reshape(-1, tok_dev)
        for first, last in ((0, EARLY), (EARLY, SEGMENTS))
    )
    gates_of = tuple(
        slot_gate.reshape(shape)[:, first * RANK_ROWS : last * RANK_ROWS].reshape(-1, 1)
        for first, last in ((0, EARLY), (EARLY, SEGMENTS))
    )

    def grads_for(part):
        return (contract(picks_of[part], out_grad, NN) * gates_of[part]).astype(BF16)

    grads_early = in_plane(grads_for(0))
    grads_late = grads_for(1)

    cosine, sine = rope_tables(tok_dev, dp_size)
    x_float = tokens.astype(F32)
    inverse1 = rms_scale(x_float)
    normed1 = (x_float * inverse1 * norm1_gain).astype(BF16)
    query = rotate(contract(w_query, normed1, ((0,), (1,))), cosine, sine)
    query = (query * (HD**-0.5)).astype(BF16)
    key = rotate(contract(w_key, normed1, ((0,), (1,))), cosine, sine).astype(BF16)
    value = contract(w_value, normed1, ((0,), (1,))).astype(BF16)
    side = jnp.concatenate(
        [(seq_ids + 1)[None], piece_ids[None], jnp.zeros((AUX - 2, tok_dev), jnp.int32)]
    ).astype(BF16)
    block = jnp.concatenate([key, value, side])
    blocks = tuple(passed_along(block, hop) for hop in range(HOPS, 0, -1)) + (block,)
    blocks, grads_early, grads_late = lax.optimization_barrier((blocks, grads_early, grads_late))
    packed_w = pack_weights(w_gate[0], w_up[0], w_down[0])
    own = lax.all_gather(packed_w, "dp", axis=0, axis_index_groups=column_groups)
    grad_rows = (grads_early, in_plane(grads_late))
    attended, log_total, peaks = attend(query, blocks, group)
    attn_part = contract(attended, w_out, TN)
    hidden1 = x_float + (attn_part + swapped(attn_part))
    inverse2 = rms_scale(hidden1)
    normed2 = (hidden1 * inverse2 * norm2_gain).astype(BF16)

    rows_early, rows_late = (contract(part, normed2, NN).astype(BF16) for part in picks_of)
    rows_early, rows_late, *_ = lax.optimization_barrier((rows_early, rows_late, grad_rows[1]))
    rows_early = in_plane(rows_early)
    own = after(own, rows_early)
    peer = swapped(own)
    rows_late = in_plane(after(rows_late, rows_early))
    rows_in = (rows_early, rows_late)
    out_early = in_plane(after(expert_first(rows_early, own, peer), rows_late))
    back, own_acts, peer_acts = expert_back(rows_in, grad_rows, own, peer)

    def combined(weights, rows):
        part = contract(weights, rows.reshape(-1, model_width), TN).astype(BF16)
        return part.astype(F32) + swapped(part).astype(F32)

    sum_own, *sum_peer, out_late = expert_sums(rows_in, grad_rows, own_acts, peer_acts, own, peer)
    sums = both_cores(sum_own, [swapped(part) for part in sum_peer], dp_size // PLANE)
    back = in_plane(after(back, out_early))
    out_late = in_plane(after(out_late, back))
    grad_normed2 = combined(pick, after(back, sums))
    sums = lax.psum_scatter(
        sums, "dp", scatter_dimension=0, tiled=True, axis_index_groups=column_groups
    )

    grad_top = out_grad.astype(F32)
    grad_from_norm2, grad_gain2 = norm_back(grad_normed2, hidden1, inverse2, norm2_gain)
    grad_hidden1 = grad_top + grad_from_norm2
    grad_branch = grad_hidden1.astype(BF16)
    grad_attended = contract(w_out, grad_branch, NT).astype(BF16)
    grad_query_pre, *grad_blocks = attend_back(
        query, grad_attended, log_total, cosine, sine, blocks, group
    )
    every = 2 * w_query.shape[1] + 2 * w_key.shape[1] + 2 * MORE
    parts = first_grads(normed1, grad_query_pre, attended, grad_branch, every)
    returned = [
        passed_along(grad_blocks[number], -hop) for number, hop in enumerate(range(HOPS, 0, -1))
    ]
    returned = after(returned, parts)
    kv_total = grad_blocks[-1]
    for part in returned:
        kv_total = kv_total + part.astype(F32)
    kv_rows = local_kv * HD
    grad_key_pre = rotate(kv_total[:kv_rows], cosine, -sine).astype(BF16)
    grad_value = kv_total[kv_rows:].astype(BF16)

    grad_norm1_part = (
        contract(grad_query_pre, w_query, ((0,), (1,)))
        + contract(grad_key_pre, w_key, ((0,), (1,)))
        + contract(grad_value, w_value, ((0,), (1,)))
    ).astype(BF16)

    grad_normed1 = grad_norm1_part.astype(F32) + swapped(grad_norm1_part).astype(F32)
    grad_from_norm1, grad_gain1 = norm_back(grad_normed1, x_float, inverse1, norm1_gain)
    input_grad = grad_hidden1 + grad_from_norm1
    peak = jnp.max(peaks, axis=1)
    peak_high = peak.astype(BF16).astype(F32)
    peak_pair = jnp.concatenate([peak_high, peak - peak_high])
    places = jnp.arange(model_width)[None] == lax.axis_index("dp")
    peak_rows = jnp.where(places, peak_pair[:, None], 0.0)
    extra = jnp.concatenate([grad_gain1[None], grad_gain2[None], peak_rows])
    extra = jnp.pad(extra, ((0, MORE - len(extra)), (0, 0)))
    parts = last_grads(normed1, jnp.concatenate([grad_key_pre, grad_value]), extra, parts)
    parts, sums, out_early, out_late = lax.optimization_barrier((parts, sums, out_early, out_late))
    summed = lax.psum(parts, "dp")
    expert_out = jnp.concatenate([out_early, out_late], axis=1)
    output = (hidden1 + combined(gated, expert_out)).astype(BF16)
    grad_gate, grad_up, grad_down = jnp.split(sums[0].astype(F32), 3, axis=1)
    grad_down = grad_down.T
    grad_wo, grad_wq, grad_wk, grad_wv, totals, clipped_query, clipped_key, head_peaks = unpack(
        summed, w_query, w_key, clip_limit, dp_size
    )
    return (
        output,
        input_grad,
        grad_wq,
        grad_wk,
        grad_wv,
        grad_wo,
        totals[0],
        totals[1],
        grad_gate[None],
        grad_up[None],
        grad_down[None],
        clipped_query,
        clipped_key,
        head_peaks.reshape(-1),
    )


def solution(mesh):
    in_specs = (
        P("dp", None),
        P("dp", None),
        P(),
        P(),
        P(None, "tensor"),
        P(None, "tensor"),
        P(None, "tensor"),
        P("tensor", None),
        P("dp", None, "tensor"),
        P("dp", None, "tensor"),
        P("dp", "tensor", None),
        P("dp", None),
        P("dp", None),
        P("dp"),
        P("dp"),
        P("tensor"),
    )
    out_specs = (
        P("dp", None),
        P("dp", None),
        P(None, "tensor"),
        P(None, "tensor"),
        P(None, "tensor"),
        P("tensor", None),
        P(),
        P(),
        P("dp", None, "tensor"),
        P("dp", None, "tensor"),
        P("dp", "tensor", None),
        P(None, "tensor"),
        P(None, "tensor"),
        P("tensor"),
    )
    return jax.shard_map(shards, mesh=mesh, in_specs=in_specs, out_specs=out_specs, check_vma=False)
```

```python
import functools
import math

import jax
import jax.numpy as jnp
import numpy as np
from jax import lax
from jax.experimental import pallas as pl
from jax.experimental.pallas import tpu as pltpu
from jax.sharding import PartitionSpec as P

HD = 64
TOP = 8
CAP = 64
HOPS = 4
RANK_ROWS = 32
PLANE = 16
SEGMENTS = 3
EARLY = 1
AUX = 16
LANES = 256
MORE = 128

EPS = 1e-06
ROPE_BASE = 10000.0
NEG_FILL = -1e30
BF16 = jnp.bfloat16
F32 = jnp.float32


def contract(left, right, dims):
    return lax.dot_general(left, right, (dims, ((), ())), preferred_element_type=F32)


NN = ((1,), (0,))
NT = ((1,), (1,))
TN = ((0,), (0,))


def swapped(array):
    return lax.ppermute(array, "tensor", [(0, 1), (1, 0)])


def after(array, other):
    return lax.optimization_barrier((array, other))[0]


def passed_along(value, steps):
    count = lax.axis_size("dp")
    first, last = (max(0, -steps), min(count, count - steps))
    return lax.ppermute(value, "dp", [(s, s + steps) for s in range(first, last)])


def rope_tables(count, dp_size):
    freq = np.exp(np.arange(HD // 2) * (-2.0 * math.log(ROPE_BASE) / HD))
    base = np.arange(dp_size)[:, None] * count * freq[None, :]
    local = freq[:, None] * np.arange(count)[None, :]
    index = lax.axis_index("dp")
    cos_base = jnp.asarray(np.cos(base), F32)[index][:, None]
    sin_base = jnp.asarray(np.sin(base), F32)[index][:, None]
    cos_local, sin_local = (jnp.asarray(np.cos(local), F32), jnp.asarray(np.sin(local), F32))
    return (
        cos_base * cos_local - sin_base * sin_local,
        sin_base * cos_local + cos_base * sin_local,
    )


def rotate(values, cosine, sine):
    half = HD // 2
    heads = values.reshape(-1, HD, values.shape[-1])
    first, second = (heads[:, :half], heads[:, half:])
    turned = jnp.concatenate(
        [first * cosine - second * sine, second * cosine + first * sine], axis=1
    )
    return turned.reshape(values.shape)


def fill_bias(blocks, bias):
    tok = bias.shape[1]
    rows = blocks[-1].shape[0] - AUX
    own = blocks[-1][rows:, :].astype(F32)
    seq_q, piece_q = (own[0:1, :], own[1:2, :])
    for number, block in enumerate(blocks):
        side = jnp.transpose(block[rows:, :].astype(F32))
        keep = side[:, 0:1] == seq_q
        if number == len(blocks) - 1:
            at_key = lax.broadcasted_iota(jnp.int32, (tok, tok), 0)
            at_query = lax.broadcasted_iota(jnp.int32, (tok, tok), 1)
            piece = (side[:, 1:2] == piece_q) & (piece_q > 0.0)
            keep = keep & ((at_key <= at_query) | piece)
        bias[number * tok : (number + 1) * tok, :] = jnp.where(keep, 0.0, NEG_FILL)


def all_keys(blocks, start):
    return jnp.concatenate([block[pl.ds(start, HD), :] for block in blocks], axis=1)


def attend_kernel(group, q_ref, k4, k3, k2, k1, k0, out_ref, log_ref, peak_ref, bias):
    blocks = (k4, k3, k2, k1, k0)
    fill_bias(blocks, bias)
    kv_rows = (k0.shape[0] - AUX) // 2

    def one_head(head, _):
        at = pl.multiple_of(head // group * HD, HD)
        keys = all_keys(blocks, at)
        values = all_keys(blocks, kv_rows + at)
        here = pl.ds(pl.multiple_of(head * HD, HD), HD)
        scores = contract(keys, q_ref[here, :], TN) + bias[...]
        peak = jnp.max(scores, axis=0, keepdims=True)
        weight = jnp.exp(scores - peak)
        total = jnp.sum(weight, axis=0, keepdims=True)
        mixed = contract(values, weight.astype(BF16), NN) * (1.0 / total)
        out_ref[here, :] = mixed.astype(BF16)
        log_ref[pl.ds(head, 1), :] = peak + jnp.log(total)
        peak_ref[pl.ds(head, 1), :] = peak
        return 0

    lax.fori_loop(0, group * kv_rows // HD, one_head, 0)


def attend(q, blocks, group):
    rows, tok = q.shape
    heads = rows // HD
    return pl.pallas_call(
        functools.partial(attend_kernel, group),
        out_shape=(
            jax.ShapeDtypeStruct((rows, tok), BF16),
            jax.ShapeDtypeStruct((heads, tok), F32),
            jax.ShapeDtypeStruct((heads, tok), F32),
        ),
        scratch_shapes=[pltpu.VMEM((len(blocks) * tok, tok), F32)],
        compiler_params=pltpu.CompilerParams(vmem_limit_bytes=48 << 20),
        cost_estimate=pl.CostEstimate(
            flops=4 * rows * tok * tok * len(blocks),
            bytes_accessed=4 * rows * tok + 2 * len(blocks) * 528 * tok,
            transcendentals=heads * tok * tok * len(blocks),
        ),
    )(q, *blocks)


def attend_back_kernel(
    group, q_ref, g_ref, log_ref, cos_ref, sin_ref, k4, k3, k2, k1, k0,
    dq_ref, d4, d3, d2, d1, d0, bias,
):
    blocks = (k4, k3, k2, k1, k0)
    grads = (d4, d3, d2, d1, d0)
    fill_bias(blocks, bias)
    kv_rows = (k0.shape[0] - AUX) // 2
    tok = bias.shape[1]
    half = HD // 2

    def one_group(g, _):
        at = pl.multiple_of(g * HD, HD)
        keys = all_keys(blocks, at)
        values = all_keys(blocks, kv_rows + at)

        def one_head(head, sums):
            start = pl.multiple_of(head * HD, HD)
            query, grad = (q_ref[pl.ds(start, HD), :], g_ref[pl.ds(start, HD), :])
            scores = contract(keys, query, TN) + bias[...]
            probs = jnp.exp(scores - log_ref[pl.ds(head, 1), :])
            grad_probs = contract(values, grad, TN)
            delta = jnp.sum(probs * grad_probs, axis=0, keepdims=True)
            grad_scores = (probs * (grad_probs - delta)).astype(BF16)
            turned = contract(keys, grad_scores, NN) * (HD**-0.5)
            first, second = (turned[:half], turned[half:])
            cosine, sine = (cos_ref[...], sin_ref[...])
            dq_ref[pl.ds(start, half), :] = (first * cosine + second * sine).astype(BF16)
            dq_ref[pl.ds(start + half, half), :] = (second * cosine - first * sine).astype(BF16)
            return (
                sums[0] + contract(query, grad_scores, NT),
                sums[1] + contract(grad, probs.astype(BF16), NT),
            )

        zero = jnp.zeros(keys.shape, F32)
        key_sum, value_sum = lax.fori_loop(g * group, (g + 1) * group, one_head, (zero, zero))
        for number, grad_ref in enumerate(grads):
            piece = slice(number * tok, (number + 1) * tok)
            grad_ref[pl.ds(at, HD), :] = key_sum[:, piece].astype(grad_ref.dtype)
            grad_ref[pl.ds(kv_rows + at, HD), :] = value_sum[:, piece].astype(grad_ref.dtype)
        return 0

    lax.fori_loop(0, kv_rows // HD, one_group, 0)


def attend_back(q, grad, log_total, cosine, sine, blocks, group):
    rows, tok = q.shape
    kv = blocks[0].shape[0] - AUX
    return pl.pallas_call(
        functools.partial(attend_back_kernel, group),
        out_shape=(
            jax.ShapeDtypeStruct((rows, tok), BF16),
            *(jax.ShapeDtypeStruct((kv, tok), BF16) for _ in blocks[1:]),
            jax.ShapeDtypeStruct((kv, tok), F32),
        ),
        scratch_shapes=[pltpu.VMEM((len(blocks) * tok, tok), F32)],
        compiler_params=pltpu.CompilerParams(vmem_limit_bytes=48 << 20),
        cost_estimate=pl.CostEstimate(
            flops=500 * rows * tok * tok * len(blocks),
            bytes_accessed=6 * rows * tok + 4 * len(blocks) * 528 * tok,
            transcendentals=rows // HD * tok * tok * len(blocks),
        ),
    )(q, grad, log_total, cosine, sine, *blocks)


def pack_weights_kernel(gate_ref, up_ref, down_ref, out_ref):
    hidden = gate_ref.shape[1]
    out_ref[:, :hidden] = gate_ref[...]
    out_ref[:, hidden : 2 * hidden] = up_ref[...]
    out_ref[:, 2 * hidden :] = jnp.transpose(down_ref[...].astype(F32)).astype(BF16)


def pack_weights(gate, up, down):
    width, hidden = gate.shape
    rows = width // 2
    thin = pl.BlockSpec((rows, hidden), lambda i: (i, 0))
    return pl.pallas_call(
        pack_weights_kernel,
        grid=(2,),
        in_specs=[thin, thin, pl.BlockSpec((hidden, rows), lambda i: (0, i))],
        out_specs=pl.BlockSpec((rows, 3 * hidden), lambda i: (i, 0)),
        out_shape=jax.ShapeDtypeStruct((width, 3 * hidden), BF16),
        cost_estimate=pl.CostEstimate(
            flops=width * hidden, bytes_accessed=12 * width * hidden, transcendentals=0
        ),
    )(gate, up, down)


def expert_first_kernel(x_ref, own_ref, peer_ref, out_ref):
    width = x_ref.shape[-1]
    rows = x_ref[...].reshape(-1, width)
    hidden = own_ref.shape[-1] // 3
    out = None
    for weights in (own_ref, peer_ref):
        both = contract(rows, weights[0, :, : 2 * hidden], NN)
        gate_act, up_act = (both[:, :hidden], both[:, hidden:])
        inner = gate_act * (1.0 / (1.0 + jnp.exp(-gate_act))) * up_act
        part = contract(inner.astype(BF16), weights[0, :, 2 * hidden :], NT)
        out = part if out is None else out + part
    out_ref[...] = out.astype(BF16).reshape(out_ref.shape)


def expert_first(rows, own, peer):
    sources, _, width = rows.shape
    triple = own.shape[-1]
    step = sources // 2
    part = pl.BlockSpec((step, RANK_ROWS, width), lambda s, j: (j, s, 0))
    weight = pl.BlockSpec((1, width, triple), lambda s, j: (s, 0, 0))
    return pl.pallas_call(
        expert_first_kernel,
        grid=(EARLY, 2),
        in_specs=[part, weight, weight],
        out_specs=part,
        out_shape=jax.ShapeDtypeStruct((sources, EARLY * RANK_ROWS, width), BF16),
        compiler_params=pltpu.CompilerParams(vmem_limit_bytes=56 << 20),
        cost_estimate=pl.CostEstimate(
            flops=4 * sources * EARLY * RANK_ROWS * width * triple,
            bytes_accessed=4 * sources * EARLY * RANK_ROWS * width + 4 * EARLY * width * triple,
            transcendentals=sources * EARLY * RANK_ROWS * triple * 2 // 3,
        ),
    )(rows, own, peer)


def of_segment(early_ref, late_ref, sources=slice(None), lanes=slice(None)):
    early, late = (ref[sources, :, lanes] for ref in (early_ref, late_ref))
    chosen = jnp.where(pl.program_id(0) < EARLY, early, late)
    return chosen.reshape(-1, chosen.shape[-1])


def expert_kernel(x_ref, g1_ref, g2_ref, own_ref, peer_ref, dx_ref, own_acts, peer_acts):
    hidden = own_ref.shape[-1] // 3
    sources = x_ref.shape[0] // 2
    count = sources * RANK_ROWS

    def one_half(half, _):
        here = pl.ds(half * sources, sources)
        there = pl.ds(pl.multiple_of(half * count, count), count)
        rows = x_ref[here].reshape(count, -1)
        grads = of_segment(g1_ref, g2_ref, here)
        back = None
        for weights, acts in ((own_ref, own_acts), (peer_ref, peer_acts)):
            both = contract(rows, weights[0, :, : 2 * hidden], NN)
            grad_inner = contract(grads, weights[0, :, 2 * hidden :], NN)
            gate_act, up_act = (both[:, :hidden], both[:, hidden:])
            sigmoid = 1.0 / (1.0 + jnp.exp(-gate_act))
            silu = gate_act * sigmoid
            dgate = grad_inner * up_act * (sigmoid * (1.0 + gate_act * (1.0 - sigmoid)))
            acts[0, there, :hidden] = dgate.astype(BF16)
            acts[0, there, hidden : 2 * hidden] = (grad_inner * silu).astype(BF16)
            acts[0, there, 2 * hidden :] = (silu * up_act).astype(BF16)
            part = contract(acts[0, there, : 2 * hidden], weights[0, :, : 2 * hidden], NT)
            back = part if back is None else back + part
        dx_ref[here] = back.astype(BF16).reshape(sources, RANK_ROWS, -1)
        return 0

    lax.fori_loop(0, 2, one_half, 0)


def segment_specs(block):
    return [
        pl.BlockSpec(block, lambda s: (0, s, 0)),
        pl.BlockSpec(block, lambda s: (0, jnp.minimum(s, EARLY - 1), 0)),
        pl.BlockSpec(block, lambda s: (0, jnp.maximum(s - EARLY, 0), 0)),
    ]


def expert_back(rows, grads, own, peer):
    sources, lines, width = rows.shape
    segments, triple = (lines // RANK_ROWS, own.shape[-1])
    count = sources * RANK_ROWS
    specs = segment_specs((sources, RANK_ROWS, width))
    wide = specs[0]
    weight = pl.BlockSpec((1, width, triple), lambda s: (s, 0, 0))
    act = pl.BlockSpec((1, count, triple), lambda s: (s, 0, 0))
    return pl.pallas_call(
        expert_kernel,
        grid=(segments,),
        in_specs=[*specs, weight, weight],
        out_specs=[wide, act, act],
        out_shape=[
            jax.ShapeDtypeStruct(rows.shape, BF16),
            jax.ShapeDtypeStruct((segments, count, triple), BF16),
            jax.ShapeDtypeStruct((segments, count, triple), BF16),
        ],
        compiler_params=pltpu.CompilerParams(vmem_limit_bytes=56 << 20),
        cost_estimate=pl.CostEstimate(
            flops=7 * sources * lines * width * triple,
            bytes_accessed=6 * sources * lines * width + 4 * segments * width * triple,
            transcendentals=2 * sources * lines * triple // 3,
        ),
    )(rows, *grads, own, peer)


def expert_sums_kernel(x_ref, g1_ref, g2_ref, own_acts, peer_acts, own_ref, peer_ref, sum_own, *outs):
    width = x_ref.shape[-1]
    hidden = own_ref.shape[-1]
    late_ref = outs[3]
    chunk = width // 3

    def one_chunk(c, _):
        lanes = pl.ds(pl.multiple_of(c * chunk, chunk), chunk)
        rows = x_ref[:, :, lanes].reshape(-1, chunk)
        grads = of_segment(g1_ref, g2_ref, slice(None), lanes)
        for side, acts in enumerate((own_acts, peer_acts)):
            first = contract(rows, acts[0, :, : 2 * hidden], TN).astype(BF16)
            second = contract(grads, acts[0, :, 2 * hidden :], TN).astype(BF16)
            if side == 0:
                sum_own[0, lanes, : 2 * hidden] = first
                sum_own[0, lanes, 2 * hidden :] = second
            else:
                outs[0][0, lanes, :] = first[:, :hidden]
                outs[1][0, lanes, :] = first[:, hidden:]
                outs[2][0, lanes, :] = second
        return 0

    lax.fori_loop(0, 3, one_chunk, 0)
    sources = x_ref.shape[0] // 2
    count = sources * RANK_ROWS

    def one_half(half, _):
        there = pl.ds(pl.multiple_of(half * count, count), count)
        out = contract(own_acts[0, there, 2 * hidden :], own_ref[0], NT)
        out = out + contract(peer_acts[0, there, 2 * hidden :], peer_ref[0], NT)
        late_ref[pl.ds(half * sources, sources)] = out.astype(BF16).reshape(sources, RANK_ROWS, -1)
        return 0

    @pl.when(pl.program_id(0) >= EARLY)
    def _():
        lax.fori_loop(0, 2, one_half, 0)


def expert_sums(rows, grads, own_acts, peer_acts, own, peer):
    sources, lines, width = rows.shape
    segments, triple = (lines // RANK_ROWS, own.shape[-1])
    hidden = triple // 3
    count = sources * RANK_ROWS
    block = (sources, RANK_ROWS, width)
    down = pl.BlockSpec((1, width, hidden), lambda s: (s, 0, 2))
    act = pl.BlockSpec((1, count, triple), lambda s: (s, 0, 0))
    return pl.pallas_call(
        expert_sums_kernel,
        grid=(segments,),
        in_specs=[*segment_specs(block), act, act, down, down],
        out_specs=[pl.BlockSpec((1, width, triple), lambda s: (s, 0, 0))]
        + [pl.BlockSpec((1, width, hidden), lambda s: (s, 0, 0))] * 3
        + [pl.BlockSpec(block, lambda s: (0, jnp.maximum(s - EARLY, 0), 0))],
        out_shape=[jax.ShapeDtypeStruct((segments, width, triple), BF16)]
        + [jax.ShapeDtypeStruct((segments, width, hidden), BF16)] * 3
        + [jax.ShapeDtypeStruct((sources, (segments - EARLY) * RANK_ROWS, width), BF16)],
        compiler_params=pltpu.CompilerParams(vmem_limit_bytes=60 << 20),
        cost_estimate=pl.CostEstimate(
            flops=6 * sources * lines * width * triple,
            bytes_accessed=6 * sources * lines * width + 5 * segments * width * triple,
            transcendentals=0,
        ),
    )(rows, *grads, own_acts, peer_acts, own, peer)


def both_cores_kernel(own_ref, *refs):
    out_ref = refs[-1]
    hidden = refs[0].shape[-1]

    @pl.when(pl.program_id(0) < SEGMENTS)
    def _():
        for kind, peer_ref in enumerate(refs[:-1]):
            here = slice(kind * hidden, (kind + 1) * hidden)
            total = own_ref[0, :, here].astype(F32) + peer_ref[0].astype(F32)
            out_ref[0, :, here] = total.astype(BF16)

    @pl.when(pl.program_id(0) >= SEGMENTS)
    def _():
        out_ref[...] = jnp.zeros_like(out_ref)


def both_cores(own, peers, slots):
    segments, width, triple = own.shape
    rows = width // 2
    last = segments - 1
    part = pl.BlockSpec((1, rows, triple), lambda s, r: (jnp.minimum(s, last), r, 0))
    thin = pl.BlockSpec((1, rows, triple // 3), lambda s, r: (jnp.minimum(s, last), r, 0))
    return pl.pallas_call(
        both_cores_kernel,
        grid=(slots, 2),
        in_specs=[part] + [thin] * 3,
        out_specs=pl.BlockSpec((1, rows, triple), lambda s, r: (s, r, 0)),
        out_shape=jax.ShapeDtypeStruct((slots, width, triple), BF16),
        cost_estimate=pl.CostEstimate(
            flops=slots * width * triple, bytes_accessed=6 * slots * width * triple, transcendentals=0
        ),
    )(own, *peers)


def first_grads_kernel(normed_ref, query_ref, attended_ref, branch_ref, out_ref):
    width = branch_ref.shape[1]
    out_ref[:, :width] = contract(attended_ref[...], branch_ref[...], NN).astype(BF16)
    out_ref[:, width:] = contract(normed_ref[...], query_ref[...], ((0,), (1,))).astype(BF16)


def last_grads_kernel(normed_ref, kv_ref, extra_ref, _, out_ref):
    columns = kv_ref.shape[0]
    out_ref[:, :columns] = contract(normed_ref[...], kv_ref[...], ((0,), (1,))).astype(BF16)
    out_ref[:, columns : columns + MORE] = jnp.transpose(extra_ref[...]).astype(BF16)
    out_ref[:, columns + MORE :] = jnp.zeros((out_ref.shape[0], MORE), BF16)


def first_grads(normed, grad_query, attended, branch, every):
    tok, model = normed.shape
    width = attended.shape[0]
    half = width // LANES
    return pl.pallas_call(
        first_grads_kernel,
        grid=(model // LANES,),
        in_specs=[
            pl.BlockSpec((tok, LANES), lambda i: (0, i)),
            pl.BlockSpec((width, tok), lambda i: (0, 0)),
            pl.BlockSpec((LANES, tok), lambda i: (i % half, 0)),
            pl.BlockSpec((tok, width), lambda i: (0, i // half)),
        ],
        out_specs=pl.BlockSpec((LANES, 2 * width), lambda i: (i, 0)),
        out_shape=jax.ShapeDtypeStruct((model, every), BF16),
        cost_estimate=pl.CostEstimate(
            flops=4 * tok * model * width, bytes_accessed=4 * model * width, transcendentals=0
        ),
    )(normed, grad_query, attended, branch)


def last_grads(normed, grad_kv, extra, parts):
    tok, model = normed.shape
    columns = grad_kv.shape[0]
    every = parts.shape[1]
    size = columns + 2 * MORE
    return pl.pallas_call(
        last_grads_kernel,
        grid=(model // LANES,),
        in_specs=[
            pl.BlockSpec((tok, LANES), lambda i: (0, i)),
            pl.BlockSpec((columns, tok), lambda i: (0, 0)),
            pl.BlockSpec((MORE, LANES), lambda i: (0, i)),
            pl.BlockSpec(memory_space=pl.ANY),
        ],
        out_specs=pl.BlockSpec((LANES, size), lambda i: (i, (every - size) // size)),
        out_shape=jax.ShapeDtypeStruct(parts.shape, BF16),
        input_output_aliases={3: 0},
        cost_estimate=pl.CostEstimate(
            flops=2 * tok * model * columns, bytes_accessed=2 * model * size, transcendentals=0
        ),
    )(normed, grad_kv, extra, parts)


def unpack_kernel(
    devices, in_ref, query_ref, key_ref, clip_ref,
    wo_ref, wq_ref, wk_ref, wv_ref, sum_ref, cq_ref, ck_ref, peak_ref, sq_ref, sk_ref,
):
    at = 0
    group = cq_ref.shape[1] // ck_ref.shape[1]
    heads = cq_ref.shape[1] // HD
    start = 2 * (wo_ref.shape[1] + wk_ref.shape[1])

    @pl.when(pl.program_id(0) == 0)
    def _():
        lines = in_ref[:devices, start : start + MORE].astype(F32)
        high, low = (lines[:, 2 : 2 + heads], lines[:, 2 + heads : 2 + 2 * heads])
        peak = jnp.max(high + low, axis=0, keepdims=True)
        clip = clip_ref[...]
        scale = jnp.sqrt(clip / jnp.maximum(peak, clip))
        peak_ref[...] = peak
        each = lax.broadcasted_iota(jnp.int32, sq_ref.shape, 1) // HD
        of_key = lax.broadcasted_iota(jnp.int32, sk_ref.shape, 1) // HD
        query_scale, key_scale = (jnp.zeros(sq_ref.shape, F32), jnp.zeros(sk_ref.shape, F32))
        for h in range(heads):
            query_scale = jnp.where(each == h, scale[:, h : h + 1], query_scale)
        for g in range(heads // group):
            least = jnp.min(scale[:, g * group : (g + 1) * group], axis=1, keepdims=True)
            key_scale = jnp.where(of_key == g, least, key_scale)
        sq_ref[...] = query_scale
        sk_ref[...] = key_scale

    for target in (wo_ref, wq_ref, wk_ref, wv_ref):
        size = target.shape[1]
        target[...] = in_ref[:, at : at + size].astype(F32)
        at += size
    sum_ref[...] = jnp.transpose(in_ref[:, at : at + MORE].astype(F32))[: sum_ref.shape[0]]
    cq_ref[...] = (query_ref[...].astype(F32) * sq_ref[...]).astype(BF16)
    ck_ref[...] = (key_ref[...].astype(F32) * sk_ref[...]).astype(BF16)


def unpack(summed, w_query, w_key, clip_limit, devices):
    total, every = summed.shape
    width, narrow = (w_query.shape[1], w_key.shape[1])
    steps = total // LANES
    wide = pl.BlockSpec((LANES, width), lambda i: (i, 0))
    thin = pl.BlockSpec((LANES, narrow), lambda i: (i, 0))
    heads = width // HD
    line = pl.BlockSpec((1, heads), lambda i: (0, 0))
    return pl.pallas_call(
        functools.partial(unpack_kernel, devices),
        grid=(steps,),
        in_specs=[
            pl.BlockSpec((LANES, every), lambda i: (i, 0)),
            wide,
            thin,
            line,
        ],
        out_specs=[
            pl.BlockSpec((LANES, width), lambda i: (i % (steps // 2), i // (steps // 2))),
            wide,
            thin,
            thin,
            pl.BlockSpec((8, LANES), lambda i: (0, i)),
            wide,
            thin,
            line,
        ],
        scratch_shapes=[pltpu.VMEM((1, width), F32), pltpu.VMEM((1, narrow), F32)],
        out_shape=[
            jax.ShapeDtypeStruct((total // 2, 2 * width), F32),
            jax.ShapeDtypeStruct((total, width), F32),
            jax.ShapeDtypeStruct((total, narrow), F32),
            jax.ShapeDtypeStruct((total, narrow), F32),
            jax.ShapeDtypeStruct((8, total), F32),
            jax.ShapeDtypeStruct((total, width), BF16),
            jax.ShapeDtypeStruct((total, narrow), BF16),
            jax.ShapeDtypeStruct((1, heads), F32),
        ],
        compiler_params=pltpu.CompilerParams(vmem_limit_bytes=60 << 20),
        cost_estimate=pl.CostEstimate(
            flops=total * every, bytes_accessed=8 * total * every, transcendentals=0
        ),
    )(summed, w_query, w_key, clip_limit.reshape(1, heads))


def rms_scale(values):
    return lax.rsqrt(jnp.mean(values * values, axis=-1, keepdims=True) + EPS)


def norm_back(grad_normed, hidden, inverse, gain):
    weighted = grad_normed * gain
    grad_gain = jnp.sum(grad_normed * hidden * inverse, axis=0)
    grad_hidden = inverse * weighted - hidden * inverse**3 * jnp.mean(
        weighted * hidden, axis=-1, keepdims=True
    )
    return (grad_hidden, grad_gain)


def shards(
    tokens,
    out_grad,
    norm1_gain,
    norm2_gain,
    w_query,
    w_key,
    w_value,
    w_out,
    w_gate,
    w_up,
    w_down,
    route_ids,
    route_logits,
    seq_ids,
    piece_ids,
    clip_limit,
):
    tok_dev, model_width = tokens.shape
    dp_size = lax.axis_size("dp")
    tensor_size = lax.axis_size("tensor")
    core = lax.axis_index("tensor")
    local_heads = w_query.shape[1] // HD
    local_kv = w_key.shape[1] // HD
    group = local_heads // local_kv
    plane_groups = [list(range(at, at + PLANE)) for at in range(0, dp_size, PLANE)]
    column_groups = [list(range(at, dp_size, PLANE)) for at in range(PLANE)]


    picks = route_ids.T
    logits = route_logits.T
    gate_exp = jnp.exp(logits - jnp.max(logits, axis=0, keepdims=True))
    gates = gate_exp / jnp.sum(gate_exp, axis=0, keepdims=True)
    number = jnp.arange(PLANE * SEGMENTS, dtype=jnp.int32)
    number = number % SEGMENTS * PLANE + number // SEGMENTS
    same = picks[None] == number[:, None, None]
    member = jnp.any(same, axis=1)
    gate_of = jnp.sum(jnp.where(same, gates[None], 0.0), axis=1)
    place = jnp.arange(tok_dev, dtype=jnp.int32)
    before = (place[:, None] < place[None, :]).astype(BF16)
    rank = contract(member.astype(BF16), before, NN)
    rank = jnp.where(member, rank, -1.0)
    wanted = (tensor_size * jnp.arange(RANK_ROWS, dtype=jnp.int32) + core).astype(F32)
    chosen = rank[:, None, :] == wanted[None, :, None]
    pick = chosen.astype(BF16).reshape(-1, tok_dev)
    gated = jnp.where(chosen, gate_of[:, None, :], 0.0)
    slot_gate = jnp.sum(gated, axis=2).reshape(-1, 1)
    gated = gated.astype(BF16).reshape(-1, tok_dev)

    def in_plane(rows):
        rows = rows.reshape(PLANE, -1, model_width)
        return lax.all_to_all(rows, "dp", 0, 0, tiled=True, axis_index_groups=plane_groups)

    def grads_for(first, last):
        shape = (PLANE, SEGMENTS * RANK_ROWS, -1)
        part = pick.reshape(shape)[:, first * RANK_ROWS : last * RANK_ROWS].reshape(-1, tok_dev)
        gate = slot_gate.reshape(shape)[:, first * RANK_ROWS : last * RANK_ROWS].reshape(-1, 1)
        return (contract(part, out_grad, NN) * gate).astype(BF16)

    grads_early = in_plane(grads_for(0, EARLY))
    grads_late = grads_for(EARLY, SEGMENTS)

    cosine, sine = rope_tables(tok_dev, dp_size)
    x_float = tokens.astype(F32)
    inverse1 = rms_scale(x_float)
    normed1 = (x_float * inverse1 * norm1_gain).astype(BF16)
    query = rotate(contract(w_query, normed1, ((0,), (1,))), cosine, sine)
    query = (query * (HD**-0.5)).astype(BF16)
    key = rotate(contract(w_key, normed1, ((0,), (1,))), cosine, sine).astype(BF16)
    value = contract(w_value, normed1, ((0,), (1,))).astype(BF16)
    side = jnp.concatenate(
        [(seq_ids + 1)[None], piece_ids[None], jnp.zeros((AUX - 2, tok_dev), jnp.int32)]
    ).astype(BF16)
    block = jnp.concatenate([key, value, side])
    blocks = tuple(passed_along(block, hop) for hop in range(HOPS, 0, -1)) + (block,)
    blocks, grads_early, grads_late = lax.optimization_barrier((blocks, grads_early, grads_late))
    packed_w = pack_weights(w_gate[0], w_up[0], w_down[0])
    own = lax.all_gather(packed_w, "dp", axis=0, axis_index_groups=column_groups)
    grad_rows = (grads_early, in_plane(grads_late))
    attended, log_total, peaks = attend(query, blocks, group)
    attn_part = contract(attended, w_out, TN)
    hidden1 = x_float + (attn_part + swapped(attn_part))
    inverse2 = rms_scale(hidden1)
    normed2 = (hidden1 * inverse2 * norm2_gain).astype(BF16)

    rows_out = contract(pick, normed2, NN).astype(BF16)
    rows_out = after(rows_out, grad_rows[1])
    own = after(own, rows_out)
    peer = swapped(own)
    rows_in = in_plane(rows_out)
    out_early = in_plane(expert_first(rows_in, own, peer))
    back, own_acts, peer_acts = expert_back(rows_in, grad_rows, own, peer)

    def combined(weights, rows):
        part = contract(weights, rows.reshape(-1, model_width), TN).astype(BF16)
        return part.astype(F32) + swapped(part).astype(F32)

    sum_own, *sum_peer, out_late = expert_sums(rows_in, grad_rows, own_acts, peer_acts, own, peer)
    sums = both_cores(sum_own, [swapped(part) for part in sum_peer], dp_size // PLANE)
    back = in_plane(after(back, out_early))
    out_late = in_plane(after(out_late, back))
    grad_normed2 = combined(pick, after(back, sums))
    sums = lax.psum_scatter(
        sums, "dp", scatter_dimension=0, tiled=True, axis_index_groups=column_groups
    )

    grad_top = out_grad.astype(F32)
    grad_from_norm2, grad_gain2 = norm_back(grad_normed2, hidden1, inverse2, norm2_gain)
    grad_hidden1 = grad_top + grad_from_norm2
    grad_branch = grad_hidden1.astype(BF16)
    grad_attended = contract(w_out, grad_branch, NT).astype(BF16)
    grad_query_pre, *grad_blocks = attend_back(
        query, grad_attended, log_total, cosine, sine, blocks, group
    )
    every = 2 * w_query.shape[1] + 2 * w_key.shape[1] + 2 * MORE
    parts = first_grads(normed1, grad_query_pre, attended, grad_branch, every)
    returned = [
        passed_along(grad_blocks[number], -hop) for number, hop in enumerate(range(HOPS, 0, -1))
    ]
    returned = after(returned, parts)
    kv_total = grad_blocks[-1]
    for part in returned:
        kv_total = kv_total + part.astype(F32)
    kv_rows = local_kv * HD
    grad_key_pre = rotate(kv_total[:kv_rows], cosine, -sine).astype(BF16)
    grad_value = kv_total[kv_rows:].astype(BF16)

    grad_norm1_part = (
        contract(grad_query_pre, w_query, ((0,), (1,)))
        + contract(grad_key_pre, w_key, ((0,), (1,)))
        + contract(grad_value, w_value, ((0,), (1,)))
    ).astype(BF16)

    grad_normed1 = grad_norm1_part.astype(F32) + swapped(grad_norm1_part).astype(F32)
    grad_from_norm1, grad_gain1 = norm_back(grad_normed1, x_float, inverse1, norm1_gain)
    input_grad = grad_hidden1 + grad_from_norm1
    peak = jnp.max(peaks, axis=1)
    peak_high = peak.astype(BF16).astype(F32)
    peak_pair = jnp.concatenate([peak_high, peak - peak_high])
    places = jnp.arange(model_width)[None] == lax.axis_index("dp")
    peak_rows = jnp.where(places, peak_pair[:, None], 0.0)
    extra = jnp.concatenate([grad_gain1[None], grad_gain2[None], peak_rows])
    extra = jnp.pad(extra, ((0, MORE - len(extra)), (0, 0)))
    parts = last_grads(normed1, jnp.concatenate([grad_key_pre, grad_value]), extra, parts)
    parts, sums, out_early, out_late = lax.optimization_barrier((parts, sums, out_early, out_late))
    summed = lax.psum(parts, "dp")
    expert_out = jnp.concatenate([out_early, out_late], axis=1)
    output = (hidden1 + combined(gated, expert_out)).astype(BF16)
    grad_gate, grad_up, grad_down = jnp.split(sums[0].astype(F32), 3, axis=1)
    grad_down = grad_down.T
    grad_wo, grad_wq, grad_wk, grad_wv, totals, clipped_query, clipped_key, head_peaks = unpack(
        summed, w_query, w_key, clip_limit, dp_size
    )
    return (
        output,
        input_grad,
        grad_wq,
        grad_wk,
        grad_wv,
        grad_wo,
        totals[0],
        totals[1],
        grad_gate[None],
        grad_up[None],
        grad_down[None],
        clipped_query,
        clipped_key,
        head_peaks.reshape(-1),
    )


def solution(mesh):
    in_specs = (
        P("dp", None),
        P("dp", None),
        P(),
        P(),
        P(None, "tensor"),
        P(None, "tensor"),
        P(None, "tensor"),
        P("tensor", None),
        P("dp", None, "tensor"),
        P("dp", None, "tensor"),
        P("dp", "tensor", None),
        P("dp", None),
        P("dp", None),
        P("dp"),
        P("dp"),
        P("tensor"),
    )
    out_specs = (
        P("dp", None),
        P("dp", None),
        P(None, "tensor"),
        P(None, "tensor"),
        P(None, "tensor"),
        P("tensor", None),
        P(),
        P(),
        P("dp", None, "tensor"),
        P("dp", None, "tensor"),
        P("dp", "tensor", None),
        P(None, "tensor"),
        P(None, "tensor"),
        P("tensor"),
    )
    return jax.shard_map(shards, mesh=mesh, in_specs=in_specs, out_specs=out_specs, check_vma=False)
```

```python
import functools
import math

import jax
import jax.numpy as jnp
import numpy as np
from jax import lax
from jax.experimental import pallas as pl
from jax.experimental.pallas import tpu as pltpu
from jax.sharding import PartitionSpec as P

HD = 64
TOP = 8
CAP = 64
HOPS = 4
RANK_ROWS = 32
PLANE = 16
SEGMENTS = 3
EARLY = 1
AUX = 16
LANES = 256
MORE = 128

EPS = 1e-06
ROPE_BASE = 10000.0
NEG_FILL = -1e30
BF16 = jnp.bfloat16
F32 = jnp.float32


def contract(left, right, dims):
    return lax.dot_general(left, right, (dims, ((), ())), preferred_element_type=F32)


NN = ((1,), (0,))
NT = ((1,), (1,))
TN = ((0,), (0,))


def swapped(array):
    return lax.ppermute(array, "tensor", [(0, 1), (1, 0)])


def after(array, other):
    return lax.optimization_barrier((array, other))[0]


def passed_along(value, steps):
    count = lax.axis_size("dp")
    first, last = (max(0, -steps), min(count, count - steps))
    return lax.ppermute(value, "dp", [(s, s + steps) for s in range(first, last)])


def rope_tables(count, dp_size):
    freq = np.exp(np.arange(HD // 2) * (-2.0 * math.log(ROPE_BASE) / HD))
    base = np.arange(dp_size)[:, None] * count * freq[None, :]
    local = freq[:, None] * np.arange(count)[None, :]
    index = lax.axis_index("dp")
    cos_base = jnp.asarray(np.cos(base), F32)[index][:, None]
    sin_base = jnp.asarray(np.sin(base), F32)[index][:, None]
    cos_local, sin_local = (jnp.asarray(np.cos(local), F32), jnp.asarray(np.sin(local), F32))
    return (
        cos_base * cos_local - sin_base * sin_local,
        sin_base * cos_local + cos_base * sin_local,
    )


def rotate(values, cosine, sine):
    half = HD // 2
    heads = values.reshape(-1, HD, values.shape[-1])
    first, second = (heads[:, :half], heads[:, half:])
    turned = jnp.concatenate(
        [first * cosine - second * sine, second * cosine + first * sine], axis=1
    )
    return turned.reshape(values.shape)


def fill_bias(blocks, bias):
    tok = bias.shape[1]
    rows = blocks[-1].shape[0] - AUX
    own = blocks[-1][rows:, :].astype(F32)
    seq_q, piece_q = (own[0:1, :], own[1:2, :])
    for number, block in enumerate(blocks):
        side = jnp.transpose(block[rows:, :].astype(F32))
        keep = side[:, 0:1] == seq_q
        if number == len(blocks) - 1:
            at_key = lax.broadcasted_iota(jnp.int32, (tok, tok), 0)
            at_query = lax.broadcasted_iota(jnp.int32, (tok, tok), 1)
            piece = (side[:, 1:2] == piece_q) & (piece_q > 0.0)
            keep = keep & ((at_key <= at_query) | piece)
        bias[number * tok : (number + 1) * tok, :] = jnp.where(keep, 0.0, NEG_FILL)


def all_keys(blocks, start):
    return jnp.concatenate([block[pl.ds(start, HD), :] for block in blocks], axis=1)


def attend_kernel(group, q_ref, k4, k3, k2, k1, k0, out_ref, log_ref, peak_ref, bias):
    blocks = (k4, k3, k2, k1, k0)
    fill_bias(blocks, bias)
    kv_rows = (k0.shape[0] - AUX) // 2

    def one_head(head, _):
        at = pl.multiple_of(head // group * HD, HD)
        keys = all_keys(blocks, at)
        values = all_keys(blocks, kv_rows + at)
        here = pl.ds(pl.multiple_of(head * HD, HD), HD)
        scores = contract(keys, q_ref[here, :], TN) + bias[...]
        peak = jnp.max(scores, axis=0, keepdims=True)
        weight = jnp.exp(scores - peak)
        total = jnp.sum(weight, axis=0, keepdims=True)
        mixed = contract(values, weight.astype(BF16), NN) * (1.0 / total)
        out_ref[here, :] = mixed.astype(BF16)
        log_ref[pl.ds(head, 1), :] = peak + jnp.log(total)
        peak_ref[pl.ds(head, 1), :] = peak
        return 0

    lax.fori_loop(0, group * kv_rows // HD, one_head, 0)


def attend(q, blocks, group):
    rows, tok = q.shape
    heads = rows // HD
    return pl.pallas_call(
        functools.partial(attend_kernel, group),
        out_shape=(
            jax.ShapeDtypeStruct((rows, tok), BF16),
            jax.ShapeDtypeStruct((heads, tok), F32),
            jax.ShapeDtypeStruct((heads, tok), F32),
        ),
        scratch_shapes=[pltpu.VMEM((len(blocks) * tok, tok), F32)],
        compiler_params=pltpu.CompilerParams(vmem_limit_bytes=48 << 20),
        cost_estimate=pl.CostEstimate(
            flops=4 * rows * tok * tok * len(blocks),
            bytes_accessed=4 * rows * tok + 2 * len(blocks) * 528 * tok,
            transcendentals=heads * tok * tok * len(blocks),
        ),
    )(q, *blocks)


def attend_back_kernel(
    group, q_ref, g_ref, log_ref, cos_ref, sin_ref, k4, k3, k2, k1, k0,
    dq_ref, d4, d3, d2, d1, d0, bias,
):
    blocks = (k4, k3, k2, k1, k0)
    grads = (d4, d3, d2, d1, d0)
    fill_bias(blocks, bias)
    kv_rows = (k0.shape[0] - AUX) // 2
    tok = bias.shape[1]
    half = HD // 2

    def one_group(g, _):
        at = pl.multiple_of(g * HD, HD)
        keys = all_keys(blocks, at)
        values = all_keys(blocks, kv_rows + at)

        def one_head(head, sums):
            start = pl.multiple_of(head * HD, HD)
            query, grad = (q_ref[pl.ds(start, HD), :], g_ref[pl.ds(start, HD), :])
            scores = contract(keys, query, TN) + bias[...]
            probs = jnp.exp(scores - log_ref[pl.ds(head, 1), :])
            grad_probs = contract(values, grad, TN)
            delta = jnp.sum(probs * grad_probs, axis=0, keepdims=True)
            grad_scores = (probs * (grad_probs - delta)).astype(BF16)
            turned = contract(keys, grad_scores, NN) * (HD**-0.5)
            first, second = (turned[:half], turned[half:])
            cosine, sine = (cos_ref[...], sin_ref[...])
            dq_ref[pl.ds(start, half), :] = (first * cosine + second * sine).astype(BF16)
            dq_ref[pl.ds(start + half, half), :] = (second * cosine - first * sine).astype(BF16)
            return (
                sums[0] + contract(query, grad_scores, NT),
                sums[1] + contract(grad, probs.astype(BF16), NT),
            )

        zero = jnp.zeros(keys.shape, F32)
        key_sum, value_sum = lax.fori_loop(g * group, (g + 1) * group, one_head, (zero, zero))
        for number, grad_ref in enumerate(grads):
            piece = slice(number * tok, (number + 1) * tok)
            grad_ref[pl.ds(at, HD), :] = key_sum[:, piece].astype(grad_ref.dtype)
            grad_ref[pl.ds(kv_rows + at, HD), :] = value_sum[:, piece].astype(grad_ref.dtype)
        return 0

    lax.fori_loop(0, kv_rows // HD, one_group, 0)


def attend_back(q, grad, log_total, cosine, sine, blocks, group):
    rows, tok = q.shape
    kv = blocks[0].shape[0] - AUX
    return pl.pallas_call(
        functools.partial(attend_back_kernel, group),
        out_shape=(
            jax.ShapeDtypeStruct((rows, tok), BF16),
            *(jax.ShapeDtypeStruct((kv, tok), BF16) for _ in blocks[1:]),
            jax.ShapeDtypeStruct((kv, tok), F32),
        ),
        scratch_shapes=[pltpu.VMEM((len(blocks) * tok, tok), F32)],
        compiler_params=pltpu.CompilerParams(vmem_limit_bytes=48 << 20),
        cost_estimate=pl.CostEstimate(
            flops=500 * rows * tok * tok * len(blocks),
            bytes_accessed=6 * rows * tok + 4 * len(blocks) * 528 * tok,
            transcendentals=rows // HD * tok * tok * len(blocks),
        ),
    )(q, grad, log_total, cosine, sine, *blocks)


def dispatch_kernel(pick_ref, rows_ref, *refs):
    rows = contract(pick_ref[...], rows_ref[...], NN)
    for gate_ref in refs[:-1]:
        rows = rows * jnp.sum(gate_ref[...], axis=1, keepdims=True)
    refs[-1][...] = rows.astype(BF16)


def dispatch(pick, rows, *gates):
    slots, tok = pick.shape
    width = rows.shape[1]
    return pl.pallas_call(
        dispatch_kernel,
        grid=(slots // LANES,),
        in_specs=[
            pl.BlockSpec((LANES, tok), lambda i: (i, 0)),
            pl.BlockSpec((tok, width), lambda i: (0, 0)),
        ]
        + [pl.BlockSpec((LANES, tok), lambda i: (i, 0))] * len(gates),
        out_specs=pl.BlockSpec((LANES, width), lambda i: (i, 0)),
        out_shape=jax.ShapeDtypeStruct((slots, width), BF16),
        cost_estimate=pl.CostEstimate(
            flops=2 * slots * tok * width, bytes_accessed=2 * slots * (width + tok), transcendentals=0
        ),
    )(pick, rows, *gates)


def combine_kernel(weight_ref, rows_ref, out_ref):
    rows = rows_ref[...].reshape(weight_ref.shape[0], -1)
    out_ref[...] = contract(weight_ref[...], rows, TN).astype(BF16)


def combine(weights, rows):
    sources, lines, width = rows.shape
    slots, tok = weights.shape
    part = 512
    return pl.pallas_call(
        combine_kernel,
        grid=(width // part,),
        in_specs=[
            pl.BlockSpec((slots, tok), lambda i: (0, 0)),
            pl.BlockSpec((sources, lines, part), lambda i: (0, 0, i)),
        ],
        out_specs=pl.BlockSpec((tok, part), lambda i: (0, i)),
        out_shape=jax.ShapeDtypeStruct((tok, width), BF16),
        cost_estimate=pl.CostEstimate(
            flops=2 * slots * tok * width, bytes_accessed=2 * slots * (width + tok), transcendentals=0
        ),
    )(weights, rows)


def project_kernel(
    x_ref, gain_ref, wq_ref, wk_ref, wv_ref, cos_ref, sin_ref, side_ref,
    normed_ref, inverse_ref, q_ref, block_ref,
):
    x = x_ref[...].astype(F32)
    inverse = lax.rsqrt(jnp.mean(x * x, axis=-1, keepdims=True) + EPS)
    inverse_ref[...] = inverse
    normed_ref[...] = (x * inverse * gain_ref[...]).astype(BF16)
    kv = wk_ref.shape[1]
    step, half = (2 * HD, HD // 2)
    block_ref[2 * kv :, :] = side_ref[...]

    def columns(weight_ref, c):
        lanes = pl.ds(pl.multiple_of(c * step, step), step)
        return contract(weight_ref[:, lanes], normed_ref[...], ((0,), (1,)))

    def rotated(weight_ref, out_ref, scale):
        def one(c, _):
            both = columns(weight_ref, c)
            cosine, sine = (cos_ref[...] * scale, sin_ref[...] * scale)
            for head in range(2):
                first, second = (both[head * HD : head * HD + half], both[head * HD + half : (head + 1) * HD])
                at = pl.multiple_of(c * step + head * HD, HD)
                out_ref[pl.ds(at, half), :] = (first * cosine - second * sine).astype(BF16)
                out_ref[pl.ds(at + half, half), :] = (second * cosine + first * sine).astype(BF16)
            return 0

        lax.fori_loop(0, weight_ref.shape[1] // step, one, 0)

    def one_value(c, _):
        at = pl.multiple_of(kv + c * step, step)
        block_ref[pl.ds(at, step), :] = columns(wv_ref, c).astype(BF16)
        return 0

    rotated(wk_ref, block_ref, 1.0)
    lax.fori_loop(0, kv // step, one_value, 0)
    rotated(wq_ref, q_ref, HD**-0.5)


def project(tokens, gain, w_query, w_key, w_value, cosine, sine, side):
    tok, model = tokens.shape
    width, kv = (w_query.shape[1], w_key.shape[1])
    return pl.pallas_call(
        project_kernel,
        out_shape=(
            jax.ShapeDtypeStruct((tok, model), BF16),
            jax.ShapeDtypeStruct((tok, 1), F32),
            jax.ShapeDtypeStruct((width, tok), BF16),
            jax.ShapeDtypeStruct((2 * kv + AUX, tok), BF16),
        ),
        compiler_params=pltpu.CompilerParams(vmem_limit_bytes=40 << 20),
        cost_estimate=pl.CostEstimate(
            flops=2 * tok * model * (width + 2 * kv),
            bytes_accessed=2 * model * (width + 2 * kv + 3 * tok),
            transcendentals=0,
        ),
    )(tokens, gain, w_query, w_key, w_value, cosine, sine, side)


def pack_weights_kernel(gate_ref, up_ref, down_ref, out_ref):
    hidden = gate_ref.shape[1]
    out_ref[:, :hidden] = gate_ref[...]
    out_ref[:, hidden : 2 * hidden] = up_ref[...]
    out_ref[:, 2 * hidden :] = jnp.transpose(down_ref[...].astype(F32)).astype(BF16)


def pack_weights(gate, up, down):
    width, hidden = gate.shape
    rows = width // 2
    thin = pl.BlockSpec((rows, hidden), lambda i: (i, 0))
    return pl.pallas_call(
        pack_weights_kernel,
        grid=(2,),
        in_specs=[thin, thin, pl.BlockSpec((hidden, rows), lambda i: (0, i))],
        out_specs=pl.BlockSpec((rows, 3 * hidden), lambda i: (i, 0)),
        out_shape=jax.ShapeDtypeStruct((width, 3 * hidden), BF16),
        cost_estimate=pl.CostEstimate(
            flops=width * hidden, bytes_accessed=12 * width * hidden, transcendentals=0
        ),
    )(gate, up, down)


def expert_first_kernel(x_ref, own_ref, peer_ref, out_ref):
    width = x_ref.shape[-1]
    rows = x_ref[...].reshape(-1, width)
    hidden = own_ref.shape[-1] // 3
    out = None
    for weights in (own_ref, peer_ref):
        both = contract(rows, weights[0, :, : 2 * hidden], NN)
        gate_act, up_act = (both[:, :hidden], both[:, hidden:])
        inner = gate_act * (1.0 / (1.0 + jnp.exp(-gate_act))) * up_act
        part = contract(inner.astype(BF16), weights[0, :, 2 * hidden :], NT)
        out = part if out is None else out + part
    out_ref[...] = out.astype(BF16).reshape(out_ref.shape)


def expert_first(rows, own, peer):
    sources, _, width = rows.shape
    triple = own.shape[-1]
    step = sources // 2
    part = pl.BlockSpec((step, RANK_ROWS, width), lambda s, j: (j, s, 0))
    weight = pl.BlockSpec((1, width, triple), lambda s, j: (s, 0, 0))
    return pl.pallas_call(
        expert_first_kernel,
        grid=(EARLY, 2),
        in_specs=[part, weight, weight],
        out_specs=part,
        out_shape=jax.ShapeDtypeStruct((sources, EARLY * RANK_ROWS, width), BF16),
        compiler_params=pltpu.CompilerParams(vmem_limit_bytes=56 << 20),
        cost_estimate=pl.CostEstimate(
            flops=4 * sources * EARLY * RANK_ROWS * width * triple,
            bytes_accessed=4 * sources * EARLY * RANK_ROWS * width + 4 * EARLY * width * triple,
            transcendentals=sources * EARLY * RANK_ROWS * triple * 2 // 3,
        ),
    )(rows, own, peer)


def of_segment(early_ref, late_ref, sources=slice(None), lanes=slice(None)):
    early, late = (ref[sources, :, lanes] for ref in (early_ref, late_ref))
    chosen = jnp.where(pl.program_id(0) < EARLY, early, late)
    return chosen.reshape(-1, chosen.shape[-1])


def expert_kernel(x_ref, g1_ref, g2_ref, own_ref, peer_ref, dx_ref, own_acts, peer_acts):
    hidden = own_ref.shape[-1] // 3
    sources = x_ref.shape[0] // 2
    count = sources * RANK_ROWS

    def one_half(half, _):
        here = pl.ds(half * sources, sources)
        there = pl.ds(pl.multiple_of(half * count, count), count)
        rows = x_ref[here].reshape(count, -1)
        grads = of_segment(g1_ref, g2_ref, here)
        back = None
        for weights, acts in ((own_ref, own_acts), (peer_ref, peer_acts)):
            both = contract(rows, weights[0, :, : 2 * hidden], NN)
            grad_inner = contract(grads, weights[0, :, 2 * hidden :], NN)
            gate_act, up_act = (both[:, :hidden], both[:, hidden:])
            sigmoid = 1.0 / (1.0 + jnp.exp(-gate_act))
            silu = gate_act * sigmoid
            dgate = grad_inner * up_act * (sigmoid * (1.0 + gate_act * (1.0 - sigmoid)))
            acts[0, there, :hidden] = dgate.astype(BF16)
            acts[0, there, hidden : 2 * hidden] = (grad_inner * silu).astype(BF16)
            acts[0, there, 2 * hidden :] = (silu * up_act).astype(BF16)
            part = contract(acts[0, there, : 2 * hidden], weights[0, :, : 2 * hidden], NT)
            back = part if back is None else back + part
        dx_ref[here] = back.astype(BF16).reshape(sources, RANK_ROWS, -1)
        return 0

    lax.fori_loop(0, 2, one_half, 0)


def segment_specs(block):
    return [
        pl.BlockSpec(block, lambda s: (0, s, 0)),
        pl.BlockSpec(block, lambda s: (0, jnp.minimum(s, EARLY - 1), 0)),
        pl.BlockSpec(block, lambda s: (0, jnp.maximum(s - EARLY, 0), 0)),
    ]


def expert_back(rows, grads, own, peer):
    sources, lines, width = rows.shape
    segments, triple = (lines // RANK_ROWS, own.shape[-1])
    count = sources * RANK_ROWS
    specs = segment_specs((sources, RANK_ROWS, width))
    wide = specs[0]
    weight = pl.BlockSpec((1, width, triple), lambda s: (s, 0, 0))
    act = pl.BlockSpec((1, count, triple), lambda s: (s, 0, 0))
    return pl.pallas_call(
        expert_kernel,
        grid=(segments,),
        in_specs=[*specs, weight, weight],
        out_specs=[wide, act, act],
        out_shape=[
            jax.ShapeDtypeStruct(rows.shape, BF16),
            jax.ShapeDtypeStruct((segments, count, triple), BF16),
            jax.ShapeDtypeStruct((segments, count, triple), BF16),
        ],
        compiler_params=pltpu.CompilerParams(vmem_limit_bytes=56 << 20),
        cost_estimate=pl.CostEstimate(
            flops=7 * sources * lines * width * triple,
            bytes_accessed=6 * sources * lines * width + 4 * segments * width * triple,
            transcendentals=2 * sources * lines * triple // 3,
        ),
    )(rows, *grads, own, peer)


def expert_sums_kernel(x_ref, g1_ref, g2_ref, own_acts, peer_acts, own_ref, peer_ref, sum_own, *outs):
    width = x_ref.shape[-1]
    hidden = own_ref.shape[-1]
    late_ref = outs[3]
    chunk = width // 3

    def one_chunk(c, _):
        lanes = pl.ds(pl.multiple_of(c * chunk, chunk), chunk)
        rows = x_ref[:, :, lanes].reshape(-1, chunk)
        grads = of_segment(g1_ref, g2_ref, slice(None), lanes)
        for side, acts in enumerate((own_acts, peer_acts)):
            first = contract(rows, acts[0, :, : 2 * hidden], TN).astype(BF16)
            second = contract(grads, acts[0, :, 2 * hidden :], TN).astype(BF16)
            if side == 0:
                sum_own[0, lanes, : 2 * hidden] = first
                sum_own[0, lanes, 2 * hidden :] = second
            else:
                outs[0][0, lanes, :] = first[:, :hidden]
                outs[1][0, lanes, :] = first[:, hidden:]
                outs[2][0, lanes, :] = second
        return 0

    lax.fori_loop(0, 3, one_chunk, 0)
    sources = x_ref.shape[0] // 2
    count = sources * RANK_ROWS

    def one_half(half, _):
        there = pl.ds(pl.multiple_of(half * count, count), count)
        out = contract(own_acts[0, there, 2 * hidden :], own_ref[0], NT)
        out = out + contract(peer_acts[0, there, 2 * hidden :], peer_ref[0], NT)
        late_ref[pl.ds(half * sources, sources)] = out.astype(BF16).reshape(sources, RANK_ROWS, -1)
        return 0

    @pl.when(pl.program_id(0) >= EARLY)
    def _():
        lax.fori_loop(0, 2, one_half, 0)


def expert_sums(rows, grads, own_acts, peer_acts, own, peer):
    sources, lines, width = rows.shape
    segments, triple = (lines // RANK_ROWS, own.shape[-1])
    hidden = triple // 3
    count = sources * RANK_ROWS
    block = (sources, RANK_ROWS, width)
    down = pl.BlockSpec((1, width, hidden), lambda s: (s, 0, 2))
    act = pl.BlockSpec((1, count, triple), lambda s: (s, 0, 0))
    return pl.pallas_call(
        expert_sums_kernel,
        grid=(segments,),
        in_specs=[*segment_specs(block), act, act, down, down],
        out_specs=[pl.BlockSpec((1, width, triple), lambda s: (s, 0, 0))]
        + [pl.BlockSpec((1, width, hidden), lambda s: (s, 0, 0))] * 3
        + [pl.BlockSpec(block, lambda s: (0, jnp.maximum(s - EARLY, 0), 0))],
        out_shape=[jax.ShapeDtypeStruct((segments, width, triple), BF16)]
        + [jax.ShapeDtypeStruct((segments, width, hidden), BF16)] * 3
        + [jax.ShapeDtypeStruct((sources, (segments - EARLY) * RANK_ROWS, width), BF16)],
        compiler_params=pltpu.CompilerParams(vmem_limit_bytes=60 << 20),
        cost_estimate=pl.CostEstimate(
            flops=6 * sources * lines * width * triple,
            bytes_accessed=6 * sources * lines * width + 5 * segments * width * triple,
            transcendentals=0,
        ),
    )(rows, *grads, own_acts, peer_acts, own, peer)


def both_cores_kernel(own_ref, *refs):
    out_ref = refs[-1]
    hidden = refs[0].shape[-1]

    @pl.when(pl.program_id(0) < SEGMENTS)
    def _():
        for kind, peer_ref in enumerate(refs[:-1]):
            here = slice(kind * hidden, (kind + 1) * hidden)
            total = own_ref[0, :, here].astype(F32) + peer_ref[0].astype(F32)
            out_ref[0, :, here] = total.astype(BF16)

    @pl.when(pl.program_id(0) >= SEGMENTS)
    def _():
        out_ref[...] = jnp.zeros_like(out_ref)


def both_cores(own, peers, slots):
    segments, width, triple = own.shape
    rows = width // 2
    last = segments - 1
    part = pl.BlockSpec((1, rows, triple), lambda s, r: (jnp.minimum(s, last), r, 0))
    thin = pl.BlockSpec((1, rows, triple // 3), lambda s, r: (jnp.minimum(s, last), r, 0))
    return pl.pallas_call(
        both_cores_kernel,
        grid=(slots, 2),
        in_specs=[part] + [thin] * 3,
        out_specs=pl.BlockSpec((1, rows, triple), lambda s, r: (s, r, 0)),
        out_shape=jax.ShapeDtypeStruct((slots, width, triple), BF16),
        cost_estimate=pl.CostEstimate(
            flops=slots * width * triple, bytes_accessed=6 * slots * width * triple, transcendentals=0
        ),
    )(own, *peers)


def first_grads_kernel(normed_ref, query_ref, attended_ref, branch_ref, out_ref):
    width = branch_ref.shape[1]
    out_ref[:, :width] = contract(attended_ref[...], branch_ref[...], NN).astype(BF16)
    out_ref[:, width:] = contract(normed_ref[...], query_ref[...], ((0,), (1,))).astype(BF16)


def last_grads_kernel(normed_ref, kv_ref, extra_ref, _, out_ref):
    columns = kv_ref.shape[0]
    out_ref[:, :columns] = contract(normed_ref[...], kv_ref[...], ((0,), (1,))).astype(BF16)
    out_ref[:, columns : columns + MORE] = jnp.transpose(extra_ref[...]).astype(BF16)
    out_ref[:, columns + MORE :] = jnp.zeros((out_ref.shape[0], MORE), BF16)


def first_grads(normed, grad_query, attended, branch, every):
    tok, model = normed.shape
    width = attended.shape[0]
    half = width // LANES
    return pl.pallas_call(
        first_grads_kernel,
        grid=(model // LANES,),
        in_specs=[
            pl.BlockSpec((tok, LANES), lambda i: (0, i)),
            pl.BlockSpec((width, tok), lambda i: (0, 0)),
            pl.BlockSpec((LANES, tok), lambda i: (i % half, 0)),
            pl.BlockSpec((tok, width), lambda i: (0, i // half)),
        ],
        out_specs=pl.BlockSpec((LANES, 2 * width), lambda i: (i, 0)),
        out_shape=jax.ShapeDtypeStruct((model, every), BF16),
        cost_estimate=pl.CostEstimate(
            flops=4 * tok * model * width, bytes_accessed=4 * model * width, transcendentals=0
        ),
    )(normed, grad_query, attended, branch)


def last_grads(normed, grad_kv, extra, parts):
    tok, model = normed.shape
    columns = grad_kv.shape[0]
    every = parts.shape[1]
    size = columns + 2 * MORE
    return pl.pallas_call(
        last_grads_kernel,
        grid=(model // LANES,),
        in_specs=[
            pl.BlockSpec((tok, LANES), lambda i: (0, i)),
            pl.BlockSpec((columns, tok), lambda i: (0, 0)),
            pl.BlockSpec((MORE, LANES), lambda i: (0, i)),
            pl.BlockSpec(memory_space=pl.ANY),
        ],
        out_specs=pl.BlockSpec((LANES, size), lambda i: (i, (every - size) // size)),
        out_shape=jax.ShapeDtypeStruct(parts.shape, BF16),
        input_output_aliases={3: 0},
        cost_estimate=pl.CostEstimate(
            flops=2 * tok * model * columns, bytes_accessed=2 * model * size, transcendentals=0
        ),
    )(normed, grad_kv, extra, parts)


def unpack_kernel(
    devices, in_ref, query_ref, key_ref, clip_ref,
    wo_ref, wq_ref, wk_ref, wv_ref, sum_ref, cq_ref, ck_ref, peak_ref, sq_ref, sk_ref,
):
    at = 0
    group = cq_ref.shape[1] // ck_ref.shape[1]
    heads = cq_ref.shape[1] // HD
    start = 2 * (wo_ref.shape[1] + wk_ref.shape[1])

    @pl.when(pl.program_id(0) == 0)
    def _():
        lines = in_ref[:devices, start : start + MORE].astype(F32)
        high, low = (lines[:, 2 : 2 + heads], lines[:, 2 + heads : 2 + 2 * heads])
        peak = jnp.max(high + low, axis=0, keepdims=True)
        clip = clip_ref[...]
        scale = jnp.sqrt(clip / jnp.maximum(peak, clip))
        peak_ref[...] = peak
        each = lax.broadcasted_iota(jnp.int32, sq_ref.shape, 1) // HD
        of_key = lax.broadcasted_iota(jnp.int32, sk_ref.shape, 1) // HD
        query_scale, key_scale = (jnp.zeros(sq_ref.shape, F32), jnp.zeros(sk_ref.shape, F32))
        for h in range(heads):
            query_scale = jnp.where(each == h, scale[:, h : h + 1], query_scale)
        for g in range(heads // group):
            least = jnp.min(scale[:, g * group : (g + 1) * group], axis=1, keepdims=True)
            key_scale = jnp.where(of_key == g, least, key_scale)
        sq_ref[...] = query_scale
        sk_ref[...] = key_scale

    for target in (wo_ref, wq_ref, wk_ref, wv_ref):
        size = target.shape[1]
        target[...] = in_ref[:, at : at + size].astype(F32)
        at += size
    sum_ref[...] = jnp.transpose(in_ref[:, at : at + MORE].astype(F32))[: sum_ref.shape[0]]
    cq_ref[...] = (query_ref[...].astype(F32) * sq_ref[...]).astype(BF16)
    ck_ref[...] = (key_ref[...].astype(F32) * sk_ref[...]).astype(BF16)


def unpack(summed, w_query, w_key, clip_limit, devices):
    total, every = summed.shape
    width, narrow = (w_query.shape[1], w_key.shape[1])
    steps = total // LANES
    wide = pl.BlockSpec((LANES, width), lambda i: (i, 0))
    thin = pl.BlockSpec((LANES, narrow), lambda i: (i, 0))
    heads = width // HD
    line = pl.BlockSpec((1, heads), lambda i: (0, 0))
    return pl.pallas_call(
        functools.partial(unpack_kernel, devices),
        grid=(steps,),
        in_specs=[
            pl.BlockSpec((LANES, every), lambda i: (i, 0)),
            wide,
            thin,
            line,
        ],
        out_specs=[
            pl.BlockSpec((LANES, width), lambda i: (i % (steps // 2), i // (steps // 2))),
            wide,
            thin,
            thin,
            pl.BlockSpec((8, LANES), lambda i: (0, i)),
            wide,
            thin,
            line,
        ],
        scratch_shapes=[pltpu.VMEM((1, width), F32), pltpu.VMEM((1, narrow), F32)],
        out_shape=[
            jax.ShapeDtypeStruct((total // 2, 2 * width), F32),
            jax.ShapeDtypeStruct((total, width), F32),
            jax.ShapeDtypeStruct((total, narrow), F32),
            jax.ShapeDtypeStruct((total, narrow), F32),
            jax.ShapeDtypeStruct((8, total), F32),
            jax.ShapeDtypeStruct((total, width), BF16),
            jax.ShapeDtypeStruct((total, narrow), BF16),
            jax.ShapeDtypeStruct((1, heads), F32),
        ],
        compiler_params=pltpu.CompilerParams(vmem_limit_bytes=60 << 20),
        cost_estimate=pl.CostEstimate(
            flops=total * every, bytes_accessed=8 * total * every, transcendentals=0
        ),
    )(summed, w_query, w_key, clip_limit.reshape(1, heads))


def rms_scale(values):
    return lax.rsqrt(jnp.mean(values * values, axis=-1, keepdims=True) + EPS)


def norm_back(grad_normed, hidden, inverse, gain):
    weighted = grad_normed * gain
    grad_gain = jnp.sum(grad_normed * hidden * inverse, axis=0)
    grad_hidden = inverse * weighted - hidden * inverse**3 * jnp.mean(
        weighted * hidden, axis=-1, keepdims=True
    )
    return (grad_hidden, grad_gain)


def shards(
    tokens,
    out_grad,
    norm1_gain,
    norm2_gain,
    w_query,
    w_key,
    w_value,
    w_out,
    w_gate,
    w_up,
    w_down,
    route_ids,
    route_logits,
    seq_ids,
    piece_ids,
    clip_limit,
):
    tok_dev, model_width = tokens.shape
    dp_size = lax.axis_size("dp")
    tensor_size = lax.axis_size("tensor")
    core = lax.axis_index("tensor")
    local_heads = w_query.shape[1] // HD
    local_kv = w_key.shape[1] // HD
    group = local_heads // local_kv
    plane_groups = [list(range(at, at + PLANE)) for at in range(0, dp_size, PLANE)]
    column_groups = [list(range(at, dp_size, PLANE)) for at in range(PLANE)]


    picks = route_ids.T
    logits = route_logits.T
    gate_exp = jnp.exp(logits - jnp.max(logits, axis=0, keepdims=True))
    gates = gate_exp / jnp.sum(gate_exp, axis=0, keepdims=True)
    number = jnp.arange(PLANE * SEGMENTS, dtype=jnp.int32)
    number = number % SEGMENTS * PLANE + number // SEGMENTS
    same = picks[None] == number[:, None, None]
    member = jnp.any(same, axis=1)
    gate_of = jnp.sum(jnp.where(same, gates[None], 0.0), axis=1)
    place = jnp.arange(tok_dev, dtype=jnp.int32)
    before = (place[:, None] < place[None, :]).astype(BF16)
    rank = contract(member.astype(BF16), before, NN)
    rank = jnp.where(member, rank, -1.0)
    wanted = (tensor_size * jnp.arange(RANK_ROWS, dtype=jnp.int32) + core).astype(F32)
    chosen = rank[:, None, :] == wanted[None, :, None]
    pick = chosen.astype(BF16).reshape(-1, tok_dev)
    gated = jnp.where(chosen, gate_of[:, None, :], 0.0)
    gated = gated.reshape(-1, tok_dev)

    def in_plane(rows):
        rows = rows.reshape(PLANE, -1, model_width)
        return lax.all_to_all(rows, "dp", 0, 0, tiled=True, axis_index_groups=plane_groups)

    def grads_for(first, last):
        shape = (PLANE, SEGMENTS * RANK_ROWS, -1)
        part = pick.reshape(shape)[:, first * RANK_ROWS : last * RANK_ROWS].reshape(-1, tok_dev)
        gate = gated.reshape(shape)[:, first * RANK_ROWS : last * RANK_ROWS].reshape(-1, tok_dev)
        return dispatch(part, out_grad, gate)

    grads_early = in_plane(grads_for(0, EARLY))
    grads_late = grads_for(EARLY, SEGMENTS)

    cosine, sine = rope_tables(tok_dev, dp_size)
    x_float = tokens.astype(F32)
    side = jnp.concatenate(
        [(seq_ids + 1)[None], piece_ids[None], jnp.zeros((AUX - 2, tok_dev), jnp.int32)]
    ).astype(BF16)
    normed1, inverse1, query, block = project(
        tokens, norm1_gain[None], w_query, w_key, w_value, cosine, sine, side
    )
    blocks = tuple(passed_along(block, hop) for hop in range(HOPS, 0, -1)) + (block,)
    blocks, grads_early, grads_late = lax.optimization_barrier((blocks, grads_early, grads_late))
    packed_w = pack_weights(w_gate[0], w_up[0], w_down[0])
    own = lax.all_gather(packed_w, "dp", axis=0, axis_index_groups=column_groups)
    grad_rows = (grads_early, in_plane(grads_late))
    attended, log_total, peaks = attend(query, blocks, group)
    attn_part = contract(attended, w_out, TN)
    hidden1 = x_float + (attn_part + swapped(attn_part))
    inverse2 = rms_scale(hidden1)
    normed2 = (hidden1 * inverse2 * norm2_gain).astype(BF16)

    rows_out = dispatch(pick, normed2)
    rows_out = after(rows_out, grad_rows[1])
    own = after(own, rows_out)
    peer = swapped(own)
    rows_in = in_plane(rows_out)
    out_early = in_plane(expert_first(rows_in, own, peer))
    back, own_acts, peer_acts = expert_back(rows_in, grad_rows, own, peer)

    def combined(weights, rows):
        part = combine(weights, rows)
        return part.astype(F32) + swapped(part).astype(F32)

    sum_own, *sum_peer, out_late = expert_sums(rows_in, grad_rows, own_acts, peer_acts, own, peer)
    sums = both_cores(sum_own, [swapped(part) for part in sum_peer], dp_size // PLANE)
    back = in_plane(after(back, out_early))
    out_late = in_plane(after(out_late, back))
    grad_normed2 = combined(pick, after(back, sums))
    sums = lax.psum_scatter(
        sums, "dp", scatter_dimension=0, tiled=True, axis_index_groups=column_groups
    )

    grad_top = out_grad.astype(F32)
    grad_from_norm2, grad_gain2 = norm_back(grad_normed2, hidden1, inverse2, norm2_gain)
    grad_hidden1 = grad_top + grad_from_norm2
    grad_branch = grad_hidden1.astype(BF16)
    grad_attended = contract(w_out, grad_branch, NT).astype(BF16)
    grad_query_pre, *grad_blocks = attend_back(
        query, grad_attended, log_total, cosine, sine, blocks, group
    )
    every = 2 * w_query.shape[1] + 2 * w_key.shape[1] + 2 * MORE
    parts = first_grads(normed1, grad_query_pre, attended, grad_branch, every)
    returned = [
        passed_along(grad_blocks[number], -hop) for number, hop in enumerate(range(HOPS, 0, -1))
    ]
    returned = after(returned, parts)
    kv_total = grad_blocks[-1]
    for part in returned:
        kv_total = kv_total + part.astype(F32)
    kv_rows = local_kv * HD
    grad_key_pre = rotate(kv_total[:kv_rows], cosine, -sine).astype(BF16)
    grad_value = kv_total[kv_rows:].astype(BF16)

    grad_norm1_part = (
        contract(grad_query_pre, w_query, ((0,), (1,)))
        + contract(grad_key_pre, w_key, ((0,), (1,)))
        + contract(grad_value, w_value, ((0,), (1,)))
    ).astype(BF16)

    grad_normed1 = grad_norm1_part.astype(F32) + swapped(grad_norm1_part).astype(F32)
    grad_from_norm1, grad_gain1 = norm_back(grad_normed1, x_float, inverse1, norm1_gain)
    input_grad = grad_hidden1 + grad_from_norm1
    peak = jnp.max(peaks, axis=1)
    peak_high = peak.astype(BF16).astype(F32)
    peak_pair = jnp.concatenate([peak_high, peak - peak_high])
    places = jnp.arange(model_width)[None] == lax.axis_index("dp")
    peak_rows = jnp.where(places, peak_pair[:, None], 0.0)
    extra = jnp.concatenate([grad_gain1[None], grad_gain2[None], peak_rows])
    extra = jnp.pad(extra, ((0, MORE - len(extra)), (0, 0)))
    parts = last_grads(normed1, jnp.concatenate([grad_key_pre, grad_value]), extra, parts)
    parts, sums, out_early, out_late = lax.optimization_barrier((parts, sums, out_early, out_late))
    summed = lax.psum(parts, "dp")
    expert_out = jnp.concatenate([out_early, out_late], axis=1)
    output = (hidden1 + combined(gated.astype(BF16), expert_out)).astype(BF16)
    grad_gate, grad_up, grad_down = jnp.split(sums[0].astype(F32), 3, axis=1)
    grad_down = grad_down.T
    grad_wo, grad_wq, grad_wk, grad_wv, totals, clipped_query, clipped_key, head_peaks = unpack(
        summed, w_query, w_key, clip_limit, dp_size
    )
    return (
        output,
        input_grad,
        grad_wq,
        grad_wk,
        grad_wv,
        grad_wo,
        totals[0],
        totals[1],
        grad_gate[None],
        grad_up[None],
        grad_down[None],
        clipped_query,
        clipped_key,
        head_peaks.reshape(-1),
    )


def solution(mesh):
    in_specs = (
        P("dp", None),
        P("dp", None),
        P(),
        P(),
        P(None, "tensor"),
        P(None, "tensor"),
        P(None, "tensor"),
        P("tensor", None),
        P("dp", None, "tensor"),
        P("dp", None, "tensor"),
        P("dp", "tensor", None),
        P("dp", None),
        P("dp", None),
        P("dp"),
        P("dp"),
        P("tensor"),
    )
    out_specs = (
        P("dp", None),
        P("dp", None),
        P(None, "tensor"),
        P(None, "tensor"),
        P(None, "tensor"),
        P("tensor", None),
        P(),
        P(),
        P("dp", None, "tensor"),
        P("dp", None, "tensor"),
        P("dp", "tensor", None),
        P(None, "tensor"),
        P(None, "tensor"),
        P("tensor"),
    )
    return jax.shard_map(shards, mesh=mesh, in_specs=in_specs, out_specs=out_specs, check_vma=False)
```

```python
import functools
import math

import jax
import jax.numpy as jnp
import numpy as np
from jax import lax
from jax.experimental import pallas as pl
from jax.experimental.pallas import tpu as pltpu
from jax.sharding import PartitionSpec as P

HD = 64
TOP = 8
CAP = 64
HOPS = 4
RANK_ROWS = 32
PLANE = 16
SEGMENTS = 3
EARLY = 1
AUX = 16
LANES = 256
MORE = 128

EPS = 1e-06
ROPE_BASE = 10000.0
NEG_FILL = -1e30
BF16 = jnp.bfloat16
F32 = jnp.float32


def contract(left, right, dims):
    return lax.dot_general(left, right, (dims, ((), ())), preferred_element_type=F32)


NN = ((1,), (0,))
NT = ((1,), (1,))
TN = ((0,), (0,))


def swapped(array):
    return lax.ppermute(array, "tensor", [(0, 1), (1, 0)])


def after(array, other):
    return lax.optimization_barrier((array, other))[0]


def passed_along(value, steps):
    count = lax.axis_size("dp")
    first, last = (max(0, -steps), min(count, count - steps))
    return lax.ppermute(value, "dp", [(s, s + steps) for s in range(first, last)])


def rope_tables(count, dp_size):
    freq = np.exp(np.arange(HD // 2) * (-2.0 * math.log(ROPE_BASE) / HD))
    base = np.arange(dp_size)[:, None] * count * freq[None, :]
    local = freq[:, None] * np.arange(count)[None, :]
    index = lax.axis_index("dp")
    cos_base = jnp.asarray(np.cos(base), F32)[index][:, None]
    sin_base = jnp.asarray(np.sin(base), F32)[index][:, None]
    cos_local, sin_local = (jnp.asarray(np.cos(local), F32), jnp.asarray(np.sin(local), F32))
    return (
        cos_base * cos_local - sin_base * sin_local,
        sin_base * cos_local + cos_base * sin_local,
    )


def rotate(values, cosine, sine):
    half = HD // 2
    heads = values.reshape(-1, HD, values.shape[-1])
    first, second = (heads[:, :half], heads[:, half:])
    turned = jnp.concatenate(
        [first * cosine - second * sine, second * cosine + first * sine], axis=1
    )
    return turned.reshape(values.shape)


def fill_bias(blocks, bias):
    tok = bias.shape[1]
    rows = blocks[-1].shape[0] - AUX
    own = blocks[-1][rows:, :].astype(F32)
    seq_q, piece_q = (own[0:1, :], own[1:2, :])
    for number, block in enumerate(blocks):
        side = jnp.transpose(block[rows:, :].astype(F32))
        keep = side[:, 0:1] == seq_q
        if number == len(blocks) - 1:
            at_key = lax.broadcasted_iota(jnp.int32, (tok, tok), 0)
            at_query = lax.broadcasted_iota(jnp.int32, (tok, tok), 1)
            piece = (side[:, 1:2] == piece_q) & (piece_q > 0.0)
            keep = keep & ((at_key <= at_query) | piece)
        bias[number * tok : (number + 1) * tok, :] = jnp.where(keep, 0.0, NEG_FILL)


def all_keys(blocks, start):
    return jnp.concatenate([block[pl.ds(start, HD), :] for block in blocks], axis=1)


def attend_kernel(group, q_ref, k4, k3, k2, k1, k0, out_ref, log_ref, peak_ref, bias):
    blocks = (k4, k3, k2, k1, k0)
    fill_bias(blocks, bias)
    kv_rows = (k0.shape[0] - AUX) // 2

    def one_head(head, _):
        at = pl.multiple_of(head // group * HD, HD)
        keys = all_keys(blocks, at)
        values = all_keys(blocks, kv_rows + at)
        here = pl.ds(pl.multiple_of(head * HD, HD), HD)
        scores = contract(keys, q_ref[here, :], TN) + bias[...]
        peak = jnp.max(scores, axis=0, keepdims=True)
        weight = jnp.exp(scores - peak)
        total = jnp.sum(weight, axis=0, keepdims=True)
        mixed = contract(values, weight.astype(BF16), NN) * (1.0 / total)
        out_ref[here, :] = mixed.astype(BF16)
        log_ref[pl.ds(head, 1), :] = peak + jnp.log(total)
        peak_ref[pl.ds(head, 1), :] = peak
        return 0

    lax.fori_loop(0, group * kv_rows // HD, one_head, 0)


def attend(q, blocks, group):
    rows, tok = q.shape
    heads = rows // HD
    return pl.pallas_call(
        functools.partial(attend_kernel, group),
        out_shape=(
            jax.ShapeDtypeStruct((rows, tok), BF16),
            jax.ShapeDtypeStruct((heads, tok), F32),
            jax.ShapeDtypeStruct((heads, tok), F32),
        ),
        scratch_shapes=[pltpu.VMEM((len(blocks) * tok, tok), F32)],
        compiler_params=pltpu.CompilerParams(vmem_limit_bytes=48 << 20),
        cost_estimate=pl.CostEstimate(
            flops=4 * rows * tok * tok * len(blocks),
            bytes_accessed=4 * rows * tok + 2 * len(blocks) * 528 * tok,
            transcendentals=heads * tok * tok * len(blocks),
        ),
    )(q, *blocks)


def attend_back_kernel(
    group, q_ref, g_ref, log_ref, cos_ref, sin_ref, k4, k3, k2, k1, k0,
    dq_ref, d4, d3, d2, d1, d0, bias,
):
    blocks = (k4, k3, k2, k1, k0)
    grads = (d4, d3, d2, d1, d0)
    fill_bias(blocks, bias)
    kv_rows = (k0.shape[0] - AUX) // 2
    tok = bias.shape[1]
    half = HD // 2

    def one_group(g, _):
        at = pl.multiple_of(g * HD, HD)
        keys = all_keys(blocks, at)
        values = all_keys(blocks, kv_rows + at)

        def one_head(head, sums):
            start = pl.multiple_of(head * HD, HD)
            query, grad = (q_ref[pl.ds(start, HD), :], g_ref[pl.ds(start, HD), :])
            scores = contract(keys, query, TN) + bias[...]
            probs = jnp.exp(scores - log_ref[pl.ds(head, 1), :])
            grad_probs = contract(values, grad, TN)
            delta = jnp.sum(probs * grad_probs, axis=0, keepdims=True)
            grad_scores = (probs * (grad_probs - delta)).astype(BF16)
            turned = contract(keys, grad_scores, NN) * (HD**-0.5)
            first, second = (turned[:half], turned[half:])
            cosine, sine = (cos_ref[...], sin_ref[...])
            dq_ref[pl.ds(start, half), :] = (first * cosine + second * sine).astype(BF16)
            dq_ref[pl.ds(start + half, half), :] = (second * cosine - first * sine).astype(BF16)
            return (
                sums[0] + contract(query, grad_scores, NT),
                sums[1] + contract(grad, probs.astype(BF16), NT),
            )

        zero = jnp.zeros(keys.shape, F32)
        key_sum, value_sum = lax.fori_loop(g * group, (g + 1) * group, one_head, (zero, zero))
        for number, grad_ref in enumerate(grads):
            piece = slice(number * tok, (number + 1) * tok)
            grad_ref[pl.ds(at, HD), :] = key_sum[:, piece].astype(grad_ref.dtype)
            grad_ref[pl.ds(kv_rows + at, HD), :] = value_sum[:, piece].astype(grad_ref.dtype)
        return 0

    lax.fori_loop(0, kv_rows // HD, one_group, 0)


def attend_back(q, grad, log_total, cosine, sine, blocks, group):
    rows, tok = q.shape
    kv = blocks[0].shape[0] - AUX
    return pl.pallas_call(
        functools.partial(attend_back_kernel, group),
        out_shape=(
            jax.ShapeDtypeStruct((rows, tok), BF16),
            *(jax.ShapeDtypeStruct((kv, tok), BF16) for _ in blocks[1:]),
            jax.ShapeDtypeStruct((kv, tok), F32),
        ),
        scratch_shapes=[pltpu.VMEM((len(blocks) * tok, tok), F32)],
        compiler_params=pltpu.CompilerParams(vmem_limit_bytes=48 << 20),
        cost_estimate=pl.CostEstimate(
            flops=500 * rows * tok * tok * len(blocks),
            bytes_accessed=6 * rows * tok + 4 * len(blocks) * 528 * tok,
            transcendentals=rows // HD * tok * tok * len(blocks),
        ),
    )(q, grad, log_total, cosine, sine, *blocks)


def dispatch_kernel(pick_ref, rows_ref, *refs):
    rows = contract(pick_ref[...], rows_ref[...], NN)
    for gate_ref in refs[:-1]:
        rows = rows * jnp.sum(gate_ref[...], axis=1, keepdims=True)
    refs[-1][...] = rows.astype(BF16)


def dispatch(pick, rows, *gates):
    slots, tok = pick.shape
    width = rows.shape[1]
    return pl.pallas_call(
        dispatch_kernel,
        grid=(slots // LANES,),
        in_specs=[
            pl.BlockSpec((LANES, tok), lambda i: (i, 0)),
            pl.BlockSpec((tok, width), lambda i: (0, 0)),
        ]
        + [pl.BlockSpec((LANES, tok), lambda i: (i, 0))] * len(gates),
        out_specs=pl.BlockSpec((LANES, width), lambda i: (i, 0)),
        out_shape=jax.ShapeDtypeStruct((slots, width), BF16),
        cost_estimate=pl.CostEstimate(
            flops=2 * slots * tok * width, bytes_accessed=2 * slots * (width + tok), transcendentals=0
        ),
    )(pick, rows, *gates)


def combine_kernel(weight_ref, rows_ref, out_ref):
    rows = rows_ref[...].reshape(weight_ref.shape[1], -1)
    out_ref[...] = contract(weight_ref[...], rows, NN).astype(BF16)


def combine(weights, rows):
    sources, lines, width = rows.shape
    tok, slots = weights.shape
    part = 512
    return pl.pallas_call(
        combine_kernel,
        grid=(width // part,),
        in_specs=[
            pl.BlockSpec((tok, slots), lambda i: (0, 0)),
            pl.BlockSpec((sources, lines, part), lambda i: (0, 0, i)),
        ],
        out_specs=pl.BlockSpec((tok, part), lambda i: (0, i)),
        out_shape=jax.ShapeDtypeStruct((tok, width), BF16),
        cost_estimate=pl.CostEstimate(
            flops=2 * slots * tok * width, bytes_accessed=2 * slots * (width + tok), transcendentals=0
        ),
    )(weights, rows)


def project_kernel(
    x_ref, gain_ref, wq_ref, wk_ref, wv_ref, cos_ref, sin_ref, side_ref,
    normed_ref, inverse_ref, q_ref, block_ref,
):
    x = x_ref[...].astype(F32)
    inverse = lax.rsqrt(jnp.mean(x * x, axis=-1, keepdims=True) + EPS)
    inverse_ref[...] = inverse
    normed_ref[...] = (x * inverse * gain_ref[...]).astype(BF16)
    kv = wk_ref.shape[1]
    step, half = (2 * HD, HD // 2)
    block_ref[2 * kv :, :] = side_ref[...]

    def columns(weight_ref, c):
        lanes = pl.ds(pl.multiple_of(c * step, step), step)
        return contract(weight_ref[:, lanes], normed_ref[...], ((0,), (1,)))

    def rotated(weight_ref, out_ref, scale):
        def one(c, _):
            both = columns(weight_ref, c)
            cosine, sine = (cos_ref[...] * scale, sin_ref[...] * scale)
            for head in range(2):
                first, second = (both[head * HD : head * HD + half], both[head * HD + half : (head + 1) * HD])
                at = pl.multiple_of(c * step + head * HD, HD)
                out_ref[pl.ds(at, half), :] = (first * cosine - second * sine).astype(BF16)
                out_ref[pl.ds(at + half, half), :] = (second * cosine + first * sine).astype(BF16)
            return 0

        lax.fori_loop(0, weight_ref.shape[1] // step, one, 0)

    def one_value(c, _):
        at = pl.multiple_of(kv + c * step, step)
        block_ref[pl.ds(at, step), :] = columns(wv_ref, c).astype(BF16)
        return 0

    rotated(wk_ref, block_ref, 1.0)
    lax.fori_loop(0, kv // step, one_value, 0)
    rotated(wq_ref, q_ref, HD**-0.5)


def project(tokens, gain, w_query, w_key, w_value, cosine, sine, side):
    tok, model = tokens.shape
    width, kv = (w_query.shape[1], w_key.shape[1])
    return pl.pallas_call(
        project_kernel,
        out_shape=(
            jax.ShapeDtypeStruct((tok, model), BF16),
            jax.ShapeDtypeStruct((tok, 1), F32),
            jax.ShapeDtypeStruct((width, tok), BF16),
            jax.ShapeDtypeStruct((2 * kv + AUX, tok), BF16),
        ),
        compiler_params=pltpu.CompilerParams(vmem_limit_bytes=40 << 20),
        cost_estimate=pl.CostEstimate(
            flops=2 * tok * model * (width + 2 * kv),
            bytes_accessed=2 * model * (width + 2 * kv + 3 * tok),
            transcendentals=0,
        ),
    )(tokens, gain, w_query, w_key, w_value, cosine, sine, side)


def pack_weights_kernel(gate_ref, up_ref, down_ref, out_ref):
    hidden = gate_ref.shape[1]
    out_ref[:, :hidden] = gate_ref[...]
    out_ref[:, hidden : 2 * hidden] = up_ref[...]
    out_ref[:, 2 * hidden :] = jnp.transpose(down_ref[...].astype(F32)).astype(BF16)


def pack_weights(gate, up, down):
    width, hidden = gate.shape
    rows = width // 2
    thin = pl.BlockSpec((rows, hidden), lambda i: (i, 0))
    return pl.pallas_call(
        pack_weights_kernel,
        grid=(2,),
        in_specs=[thin, thin, pl.BlockSpec((hidden, rows), lambda i: (0, i))],
        out_specs=pl.BlockSpec((rows, 3 * hidden), lambda i: (i, 0)),
        out_shape=jax.ShapeDtypeStruct((width, 3 * hidden), BF16),
        cost_estimate=pl.CostEstimate(
            flops=width * hidden, bytes_accessed=12 * width * hidden, transcendentals=0
        ),
    )(gate, up, down)


def expert_first_kernel(x_ref, own_ref, peer_ref, out_ref):
    width = x_ref.shape[-1]
    rows = x_ref[...].reshape(-1, width)
    hidden = own_ref.shape[-1] // 3
    out = None
    for weights in (own_ref, peer_ref):
        both = contract(rows, weights[0, :, : 2 * hidden], NN)
        gate_act, up_act = (both[:, :hidden], both[:, hidden:])
        inner = gate_act * (1.0 / (1.0 + jnp.exp(-gate_act))) * up_act
        part = contract(inner.astype(BF16), weights[0, :, 2 * hidden :], NT)
        out = part if out is None else out + part
    out_ref[...] = out.astype(BF16).reshape(out_ref.shape)


def expert_first(rows, own, peer):
    sources, _, width = rows.shape
    triple = own.shape[-1]
    step = sources // 2
    part = pl.BlockSpec((step, RANK_ROWS, width), lambda s, j: (j, s, 0))
    weight = pl.BlockSpec((1, width, triple), lambda s, j: (s, 0, 0))
    return pl.pallas_call(
        expert_first_kernel,
        grid=(EARLY, 2),
        in_specs=[part, weight, weight],
        out_specs=part,
        out_shape=jax.ShapeDtypeStruct((sources, EARLY * RANK_ROWS, width), BF16),
        compiler_params=pltpu.CompilerParams(vmem_limit_bytes=56 << 20),
        cost_estimate=pl.CostEstimate(
            flops=4 * sources * EARLY * RANK_ROWS * width * triple,
            bytes_accessed=4 * sources * EARLY * RANK_ROWS * width + 4 * EARLY * width * triple,
            transcendentals=sources * EARLY * RANK_ROWS * triple * 2 // 3,
        ),
    )(rows, own, peer)


def of_segment(early_ref, late_ref, sources=slice(None), lanes=slice(None)):
    early, late = (ref[sources, :, lanes] for ref in (early_ref, late_ref))
    chosen = jnp.where(pl.program_id(0) < EARLY, early, late)
    return chosen.reshape(-1, chosen.shape[-1])


def expert_kernel(x_ref, g1_ref, g2_ref, own_ref, peer_ref, dx_ref, own_acts, peer_acts):
    hidden = own_ref.shape[-1] // 3
    sources = x_ref.shape[0] // 2
    count = sources * RANK_ROWS

    def one_half(half, _):
        here = pl.ds(half * sources, sources)
        there = pl.ds(pl.multiple_of(half * count, count), count)
        rows = x_ref[here].reshape(count, -1)
        grads = of_segment(g1_ref, g2_ref, here)
        back = None
        for weights, acts in ((own_ref, own_acts), (peer_ref, peer_acts)):
            both = contract(rows, weights[0, :, : 2 * hidden], NN)
            grad_inner = contract(grads, weights[0, :, 2 * hidden :], NN)
            gate_act, up_act = (both[:, :hidden], both[:, hidden:])
            sigmoid = 1.0 / (1.0 + jnp.exp(-gate_act))
            silu = gate_act * sigmoid
            dgate = grad_inner * up_act * (sigmoid * (1.0 + gate_act * (1.0 - sigmoid)))
            acts[0, there, :hidden] = dgate.astype(BF16)
            acts[0, there, hidden : 2 * hidden] = (grad_inner * silu).astype(BF16)
            acts[0, there, 2 * hidden :] = (silu * up_act).astype(BF16)
            part = contract(acts[0, there, : 2 * hidden], weights[0, :, : 2 * hidden], NT)
            back = part if back is None else back + part
        dx_ref[here] = back.astype(BF16).reshape(sources, RANK_ROWS, -1)
        return 0

    lax.fori_loop(0, 2, one_half, 0)


def segment_specs(block):
    return [
        pl.BlockSpec(block, lambda s: (0, s, 0)),
        pl.BlockSpec(block, lambda s: (0, jnp.minimum(s, EARLY - 1), 0)),
        pl.BlockSpec(block, lambda s: (0, jnp.maximum(s - EARLY, 0), 0)),
    ]


def expert_back(rows, grads, own, peer):
    sources, lines, width = rows.shape
    segments, triple = (lines // RANK_ROWS, own.shape[-1])
    count = sources * RANK_ROWS
    specs = segment_specs((sources, RANK_ROWS, width))
    wide = specs[0]
    weight = pl.BlockSpec((1, width, triple), lambda s: (s, 0, 0))
    act = pl.BlockSpec((1, count, triple), lambda s: (s, 0, 0))
    return pl.pallas_call(
        expert_kernel,
        grid=(segments,),
        in_specs=[*specs, weight, weight],
        out_specs=[wide, act, act],
        out_shape=[
            jax.ShapeDtypeStruct(rows.shape, BF16),
            jax.ShapeDtypeStruct((segments, count, triple), BF16),
            jax.ShapeDtypeStruct((segments, count, triple), BF16),
        ],
        compiler_params=pltpu.CompilerParams(vmem_limit_bytes=56 << 20),
        cost_estimate=pl.CostEstimate(
            flops=7 * sources * lines * width * triple,
            bytes_accessed=6 * sources * lines * width + 4 * segments * width * triple,
            transcendentals=2 * sources * lines * triple // 3,
        ),
    )(rows, *grads, own, peer)


def expert_sums_kernel(x_ref, g1_ref, g2_ref, own_acts, peer_acts, own_ref, peer_ref, sum_own, *outs):
    width = x_ref.shape[-1]
    hidden = own_ref.shape[-1]
    late_ref = outs[3]
    chunk = width // 3

    def one_chunk(c, _):
        lanes = pl.ds(pl.multiple_of(c * chunk, chunk), chunk)
        rows = x_ref[:, :, lanes].reshape(-1, chunk)
        grads = of_segment(g1_ref, g2_ref, slice(None), lanes)
        for side, acts in enumerate((own_acts, peer_acts)):
            first = contract(rows, acts[0, :, : 2 * hidden], TN).astype(BF16)
            second = contract(grads, acts[0, :, 2 * hidden :], TN).astype(BF16)
            if side == 0:
                sum_own[0, lanes, : 2 * hidden] = first
                sum_own[0, lanes, 2 * hidden :] = second
            else:
                outs[0][0, lanes, :] = first[:, :hidden]
                outs[1][0, lanes, :] = first[:, hidden:]
                outs[2][0, lanes, :] = second
        return 0

    lax.fori_loop(0, 3, one_chunk, 0)
    sources = x_ref.shape[0] // 2
    count = sources * RANK_ROWS

    def one_half(half, _):
        there = pl.ds(pl.multiple_of(half * count, count), count)
        out = contract(own_acts[0, there, 2 * hidden :], own_ref[0], NT)
        out = out + contract(peer_acts[0, there, 2 * hidden :], peer_ref[0], NT)
        late_ref[pl.ds(half * sources, sources)] = out.astype(BF16).reshape(sources, RANK_ROWS, -1)
        return 0

    @pl.when(pl.program_id(0) >= EARLY)
    def _():
        lax.fori_loop(0, 2, one_half, 0)


def expert_sums(rows, grads, own_acts, peer_acts, own, peer):
    sources, lines, width = rows.shape
    segments, triple = (lines // RANK_ROWS, own.shape[-1])
    hidden = triple // 3
    count = sources * RANK_ROWS
    block = (sources, RANK_ROWS, width)
    down = pl.BlockSpec((1, width, hidden), lambda s: (s, 0, 2))
    act = pl.BlockSpec((1, count, triple), lambda s: (s, 0, 0))
    return pl.pallas_call(
        expert_sums_kernel,
        grid=(segments,),
        in_specs=[*segment_specs(block), act, act, down, down],
        out_specs=[pl.BlockSpec((1, width, triple), lambda s: (s, 0, 0))]
        + [pl.BlockSpec((1, width, hidden), lambda s: (s, 0, 0))] * 3
        + [pl.BlockSpec(block, lambda s: (0, jnp.maximum(s - EARLY, 0), 0))],
        out_shape=[jax.ShapeDtypeStruct((segments, width, triple), BF16)]
        + [jax.ShapeDtypeStruct((segments, width, hidden), BF16)] * 3
        + [jax.ShapeDtypeStruct((sources, (segments - EARLY) * RANK_ROWS, width), BF16)],
        compiler_params=pltpu.CompilerParams(vmem_limit_bytes=60 << 20),
        cost_estimate=pl.CostEstimate(
            flops=6 * sources * lines * width * triple,
            bytes_accessed=6 * sources * lines * width + 5 * segments * width * triple,
            transcendentals=0,
        ),
    )(rows, *grads, own_acts, peer_acts, own, peer)


def both_cores_kernel(own_ref, *refs):
    out_ref = refs[-1]
    hidden = refs[0].shape[-1]

    @pl.when(pl.program_id(0) < SEGMENTS)
    def _():
        for kind, peer_ref in enumerate(refs[:-1]):
            here = slice(kind * hidden, (kind + 1) * hidden)
            total = own_ref[0, :, here].astype(F32) + peer_ref[0].astype(F32)
            out_ref[0, :, here] = total.astype(BF16)

    @pl.when(pl.program_id(0) >= SEGMENTS)
    def _():
        out_ref[...] = jnp.zeros_like(out_ref)


def both_cores(own, peers, slots):
    segments, width, triple = own.shape
    rows = width // 2
    last = segments - 1
    part = pl.BlockSpec((1, rows, triple), lambda s, r: (jnp.minimum(s, last), r, 0))
    thin = pl.BlockSpec((1, rows, triple // 3), lambda s, r: (jnp.minimum(s, last), r, 0))
    return pl.pallas_call(
        both_cores_kernel,
        grid=(slots, 2),
        in_specs=[part] + [thin] * 3,
        out_specs=pl.BlockSpec((1, rows, triple), lambda s, r: (s, r, 0)),
        out_shape=jax.ShapeDtypeStruct((slots, width, triple), BF16),
        cost_estimate=pl.CostEstimate(
            flops=slots * width * triple, bytes_accessed=6 * slots * width * triple, transcendentals=0
        ),
    )(own, *peers)


def first_grads_kernel(normed_ref, query_ref, attended_ref, branch_ref, out_ref):
    width = branch_ref.shape[1]
    out_ref[:, :width] = contract(attended_ref[...], branch_ref[...], NN).astype(BF16)
    out_ref[:, width:] = contract(normed_ref[...], query_ref[...], ((0,), (1,))).astype(BF16)


def key_grads_kernel(normed_ref, kv_ref, _, out_ref):
    out_ref[...] = contract(normed_ref[...], kv_ref[...], ((0,), (1,))).astype(BF16)


def gain_rows_kernel(gain_ref, extra_ref, _, out_ref):
    line = lax.broadcasted_iota(jnp.int32, extra_ref.shape, 0)
    lines = jnp.where(line == 0, gain_ref[...], extra_ref[...])
    out_ref[:, :MORE] = jnp.transpose(lines).astype(BF16)
    out_ref[:, MORE:] = jnp.zeros((out_ref.shape[0], MORE), BF16)


def first_grads(normed, grad_query, attended, branch, every):
    tok, model = normed.shape
    width = attended.shape[0]
    half = width // LANES
    return pl.pallas_call(
        first_grads_kernel,
        grid=(model // LANES,),
        in_specs=[
            pl.BlockSpec((tok, LANES), lambda i: (0, i)),
            pl.BlockSpec((width, tok), lambda i: (0, 0)),
            pl.BlockSpec((LANES, tok), lambda i: (i % half, 0)),
            pl.BlockSpec((tok, width), lambda i: (0, i // half)),
        ],
        out_specs=pl.BlockSpec((LANES, 2 * width), lambda i: (i, 0)),
        out_shape=jax.ShapeDtypeStruct((model, every), BF16),
        cost_estimate=pl.CostEstimate(
            flops=4 * tok * model * width, bytes_accessed=4 * model * width, transcendentals=0
        ),
    )(normed, grad_query, attended, branch)


def key_grads(normed, grad_kv, parts):
    tok, model = normed.shape
    columns = grad_kv.shape[0]
    rows = 2 * LANES
    at = (parts.shape[1] - columns - 2 * MORE) // columns
    return pl.pallas_call(
        key_grads_kernel,
        grid=(model // rows,),
        in_specs=[
            pl.BlockSpec((tok, rows), lambda i: (0, i)),
            pl.BlockSpec((columns, tok), lambda i: (0, 0)),
            pl.BlockSpec(memory_space=pl.ANY),
        ],
        out_specs=pl.BlockSpec((rows, columns), lambda i: (i, at)),
        out_shape=jax.ShapeDtypeStruct(parts.shape, BF16),
        input_output_aliases={2: 0},
        cost_estimate=pl.CostEstimate(
            flops=2 * tok * model * columns, bytes_accessed=2 * model * columns, transcendentals=0
        ),
    )(normed, grad_kv, parts)


def gain_rows(gain, extra, parts):
    model = gain.shape[1]
    rows = 2 * LANES
    at = parts.shape[1] // (2 * MORE) - 1
    return pl.pallas_call(
        gain_rows_kernel,
        grid=(model // rows,),
        in_specs=[
            pl.BlockSpec((1, rows), lambda i: (0, i)),
            pl.BlockSpec((MORE, rows), lambda i: (0, i)),
            pl.BlockSpec(memory_space=pl.ANY),
        ],
        out_specs=pl.BlockSpec((rows, 2 * MORE), lambda i: (i, at)),
        out_shape=jax.ShapeDtypeStruct(parts.shape, BF16),
        input_output_aliases={2: 0},
        cost_estimate=pl.CostEstimate(
            flops=model * MORE, bytes_accessed=8 * model * MORE, transcendentals=0
        ),
    )(gain, extra, parts)


def unpack_kernel(
    devices, in_ref, query_ref, key_ref, clip_ref,
    wo_ref, wq_ref, wk_ref, wv_ref, gain1_ref, gain2_ref, cq_ref, ck_ref, peak_ref, sq_ref, sk_ref,
):
    at = 0
    group = cq_ref.shape[1] // ck_ref.shape[1]
    heads = cq_ref.shape[1] // HD
    start = 2 * (wo_ref.shape[1] + wk_ref.shape[1])

    @pl.when(pl.program_id(0) == 0)
    def _():
        lines = in_ref[:devices, start : start + MORE].astype(F32)
        high, low = (lines[:, 2 : 2 + heads], lines[:, 2 + heads : 2 + 2 * heads])
        peak = jnp.max(high + low, axis=0, keepdims=True)
        clip = clip_ref[...]
        scale = jnp.sqrt(clip / jnp.maximum(peak, clip))
        peak_ref[...] = peak
        each = lax.broadcasted_iota(jnp.int32, sq_ref.shape, 1) // HD
        of_key = lax.broadcasted_iota(jnp.int32, sk_ref.shape, 1) // HD
        query_scale, key_scale = (jnp.zeros(sq_ref.shape, F32), jnp.zeros(sk_ref.shape, F32))
        for h in range(heads):
            query_scale = jnp.where(each == h, scale[:, h : h + 1], query_scale)
        for g in range(heads // group):
            least = jnp.min(scale[:, g * group : (g + 1) * group], axis=1, keepdims=True)
            key_scale = jnp.where(of_key == g, least, key_scale)
        sq_ref[...] = query_scale
        sk_ref[...] = key_scale

    for target in (wo_ref, wq_ref, wk_ref, wv_ref):
        size = target.shape[1]
        target[...] = in_ref[:, at : at + size].astype(F32)
        at += size
    lines = jnp.transpose(in_ref[:, at : at + MORE].astype(F32))
    gain1_ref[...] = lines[0:1, :]
    gain2_ref[...] = lines[1:2, :]
    cq_ref[...] = (query_ref[...].astype(F32) * sq_ref[...]).astype(BF16)
    ck_ref[...] = (key_ref[...].astype(F32) * sk_ref[...]).astype(BF16)


def unpack(summed, w_query, w_key, clip_limit, devices):
    total, every = summed.shape
    width, narrow = (w_query.shape[1], w_key.shape[1])
    steps = total // LANES
    wide = pl.BlockSpec((LANES, width), lambda i: (i, 0))
    thin = pl.BlockSpec((LANES, narrow), lambda i: (i, 0))
    heads = width // HD
    line = pl.BlockSpec((1, heads), lambda i: (0, 0))
    return pl.pallas_call(
        functools.partial(unpack_kernel, devices),
        grid=(steps,),
        in_specs=[
            pl.BlockSpec((LANES, every), lambda i: (i, 0)),
            wide,
            thin,
            line,
        ],
        out_specs=[
            pl.BlockSpec((LANES, width), lambda i: (i % (steps // 2), i // (steps // 2))),
            wide,
            thin,
            thin,
            pl.BlockSpec((1, LANES), lambda i: (0, i)),
            pl.BlockSpec((1, LANES), lambda i: (0, i)),
            wide,
            thin,
            line,
        ],
        scratch_shapes=[pltpu.VMEM((1, width), F32), pltpu.VMEM((1, narrow), F32)],
        out_shape=[
            jax.ShapeDtypeStruct((total // 2, 2 * width), F32),
            jax.ShapeDtypeStruct((total, width), F32),
            jax.ShapeDtypeStruct((total, narrow), F32),
            jax.ShapeDtypeStruct((total, narrow), F32),
            jax.ShapeDtypeStruct((1, total), F32),
            jax.ShapeDtypeStruct((1, total), F32),
            jax.ShapeDtypeStruct((total, width), BF16),
            jax.ShapeDtypeStruct((total, narrow), BF16),
            jax.ShapeDtypeStruct((1, heads), F32),
        ],
        compiler_params=pltpu.CompilerParams(vmem_limit_bytes=60 << 20),
        cost_estimate=pl.CostEstimate(
            flops=total * every, bytes_accessed=8 * total * every, transcendentals=0
        ),
    )(summed, w_query, w_key, clip_limit.reshape(1, heads))


def rms_scale(values):
    return lax.rsqrt(jnp.mean(values * values, axis=-1, keepdims=True) + EPS)


def norm_back(grad_normed, hidden, inverse, gain):
    weighted = grad_normed * gain
    grad_gain = jnp.sum(grad_normed * hidden * inverse, axis=0)
    grad_hidden = inverse * weighted - hidden * inverse**3 * jnp.mean(
        weighted * hidden, axis=-1, keepdims=True
    )
    return (grad_hidden, grad_gain)


def shards(
    tokens,
    out_grad,
    norm1_gain,
    norm2_gain,
    w_query,
    w_key,
    w_value,
    w_out,
    w_gate,
    w_up,
    w_down,
    route_ids,
    route_logits,
    seq_ids,
    piece_ids,
    clip_limit,
):
    tok_dev, model_width = tokens.shape
    dp_size = lax.axis_size("dp")
    tensor_size = lax.axis_size("tensor")
    core = lax.axis_index("tensor")
    local_heads = w_query.shape[1] // HD
    local_kv = w_key.shape[1] // HD
    group = local_heads // local_kv
    plane_groups = [list(range(at, at + PLANE)) for at in range(0, dp_size, PLANE)]
    column_groups = [list(range(at, dp_size, PLANE)) for at in range(PLANE)]


    picks = route_ids.T
    logits = route_logits.T
    gate_exp = jnp.exp(logits - jnp.max(logits, axis=0, keepdims=True))
    gates = gate_exp / jnp.sum(gate_exp, axis=0, keepdims=True)
    number = jnp.arange(PLANE * SEGMENTS, dtype=jnp.int32)
    number = number % SEGMENTS * PLANE + number // SEGMENTS
    same = picks[None] == number[:, None, None]
    member = jnp.any(same, axis=1)
    gate_of = jnp.sum(jnp.where(same, gates[None], 0.0), axis=1)
    place = jnp.arange(tok_dev, dtype=jnp.int32)
    before = (place[:, None] < place[None, :]).astype(BF16)
    rank = contract(member.astype(BF16), before, NN)
    rank = jnp.where(member, rank, -1.0)
    wanted = (tensor_size * jnp.arange(RANK_ROWS, dtype=jnp.int32) + core).astype(F32)
    chosen = rank[:, None, :] == wanted[None, :, None]
    pick = chosen.astype(BF16).reshape(-1, tok_dev)
    gated = jnp.where(chosen, gate_of[:, None, :], 0.0)
    gated = gated.reshape(-1, tok_dev)
    pick_back, gated_back = (pick.T, gated.astype(BF16).T)

    def in_plane(rows):
        rows = rows.reshape(PLANE, -1, model_width)
        return lax.all_to_all(rows, "dp", 0, 0, tiled=True, axis_index_groups=plane_groups)

    def grads_for(first, last):
        shape = (PLANE, SEGMENTS * RANK_ROWS, -1)
        part = pick.reshape(shape)[:, first * RANK_ROWS : last * RANK_ROWS].reshape(-1, tok_dev)
        gate = gated.reshape(shape)[:, first * RANK_ROWS : last * RANK_ROWS].reshape(-1, tok_dev)
        return dispatch(part, out_grad, gate)

    grads_early = in_plane(grads_for(0, EARLY))
    grads_late = grads_for(EARLY, SEGMENTS)

    cosine, sine = rope_tables(tok_dev, dp_size)
    x_float = tokens.astype(F32)
    side = jnp.concatenate(
        [(seq_ids + 1)[None], piece_ids[None], jnp.zeros((AUX - 2, tok_dev), jnp.int32)]
    ).astype(BF16)
    normed1, inverse1, query, block = project(
        tokens, norm1_gain[None], w_query, w_key, w_value, cosine, sine, side
    )
    blocks = tuple(passed_along(block, hop) for hop in range(HOPS, 0, -1)) + (block,)
    blocks, grads_early, grads_late = lax.optimization_barrier((blocks, grads_early, grads_late))
    packed_w = pack_weights(w_gate[0], w_up[0], w_down[0])
    own = lax.all_gather(packed_w, "dp", axis=0, axis_index_groups=column_groups)
    grad_rows = (grads_early, in_plane(grads_late))
    attended, log_total, peaks = attend(query, blocks, group)
    attn_part = contract(attended, w_out, TN)
    hidden1 = x_float + (attn_part + swapped(attn_part))
    inverse2 = rms_scale(hidden1)
    normed2 = (hidden1 * inverse2 * norm2_gain).astype(BF16)

    rows_out = dispatch(pick, normed2)
    rows_out = after(rows_out, grad_rows[1])
    own = after(own, rows_out)
    peer = swapped(own)
    rows_in = in_plane(rows_out)
    out_early = in_plane(expert_first(rows_in, own, peer))
    back, own_acts, peer_acts = expert_back(rows_in, grad_rows, own, peer)

    def combined(weights, rows):
        part = combine(weights, rows)
        return part.astype(F32) + swapped(part).astype(F32)

    sum_own, *sum_peer, out_late = expert_sums(rows_in, grad_rows, own_acts, peer_acts, own, peer)
    sums = both_cores(sum_own, [swapped(part) for part in sum_peer], dp_size // PLANE)
    back = in_plane(after(back, out_early))
    out_late = in_plane(after(out_late, back))
    grad_normed2 = combined(pick_back, after(back, sums))
    sums = lax.psum_scatter(
        sums, "dp", scatter_dimension=0, tiled=True, axis_index_groups=column_groups
    )

    grad_top = out_grad.astype(F32)
    grad_from_norm2, grad_gain2 = norm_back(grad_normed2, hidden1, inverse2, norm2_gain)
    grad_hidden1 = grad_top + grad_from_norm2
    grad_branch = grad_hidden1.astype(BF16)
    grad_attended = contract(w_out, grad_branch, NT).astype(BF16)
    grad_query_pre, *grad_blocks = attend_back(
        query, grad_attended, log_total, cosine, sine, blocks, group
    )
    every = 2 * w_query.shape[1] + 2 * w_key.shape[1] + 2 * MORE
    parts = first_grads(normed1, grad_query_pre, attended, grad_branch, every)
    returned = [
        passed_along(grad_blocks[number], -hop) for number, hop in enumerate(range(HOPS, 0, -1))
    ]
    returned = after(returned, parts)
    kv_total = grad_blocks[-1]
    for part in returned:
        kv_total = kv_total + part.astype(F32)
    kv_rows = local_kv * HD
    grad_key_pre = rotate(kv_total[:kv_rows], cosine, -sine).astype(BF16)
    grad_value = kv_total[kv_rows:].astype(BF16)

    grad_norm1_part = (
        contract(grad_query_pre, w_query, ((0,), (1,)))
        + contract(grad_key_pre, w_key, ((0,), (1,)))
        + contract(grad_value, w_value, ((0,), (1,)))
    ).astype(BF16)

    grad_normed1 = grad_norm1_part.astype(F32) + swapped(grad_norm1_part).astype(F32)
    grad_from_norm1, grad_gain1 = norm_back(grad_normed1, x_float, inverse1, norm1_gain)
    input_grad = grad_hidden1 + grad_from_norm1
    peak = jnp.max(peaks, axis=1)
    peak_high = peak.astype(BF16).astype(F32)
    peak_pair = jnp.concatenate([peak_high, peak - peak_high])
    places = jnp.arange(model_width)[None] == lax.axis_index("dp")
    peak_rows = jnp.where(places, peak_pair[:, None], 0.0)
    extra = jnp.concatenate([jnp.zeros((1, model_width), F32), grad_gain2[None], peak_rows])
    extra = jnp.pad(extra, ((0, MORE - len(extra)), (0, 0)))
    parts = key_grads(normed1, jnp.concatenate([grad_key_pre, grad_value]), parts)
    parts = gain_rows(grad_gain1[None], extra, parts)
    parts, sums, out_early, out_late = lax.optimization_barrier((parts, sums, out_early, out_late))
    summed = lax.psum(parts, "dp")
    expert_out = jnp.concatenate([out_early, out_late], axis=1)
    output = (hidden1 + combined(gated_back, expert_out)).astype(BF16)
    grad_gate, grad_up, grad_down = jnp.split(sums[0].astype(F32), 3, axis=1)
    grad_down = grad_down.T
    grad_wo, grad_wq, grad_wk, grad_wv, sum1, sum2, clipped_query, clipped_key, head_peaks = unpack(
        summed, w_query, w_key, clip_limit, dp_size
    )
    return (
        output,
        input_grad,
        grad_wq,
        grad_wk,
        grad_wv,
        grad_wo,
        sum1.reshape(-1),
        sum2.reshape(-1),
        grad_gate[None],
        grad_up[None],
        grad_down[None],
        clipped_query,
        clipped_key,
        head_peaks.reshape(-1),
    )


def solution(mesh):
    in_specs = (
        P("dp", None),
        P("dp", None),
        P(),
        P(),
        P(None, "tensor"),
        P(None, "tensor"),
        P(None, "tensor"),
        P("tensor", None),
        P("dp", None, "tensor"),
        P("dp", None, "tensor"),
        P("dp", "tensor", None),
        P("dp", None),
        P("dp", None),
        P("dp"),
        P("dp"),
        P("tensor"),
    )
    out_specs = (
        P("dp", None),
        P("dp", None),
        P(None, "tensor"),
        P(None, "tensor"),
        P(None, "tensor"),
        P("tensor", None),
        P(),
        P(),
        P("dp", None, "tensor"),
        P("dp", None, "tensor"),
        P("dp", "tensor", None),
        P(None, "tensor"),
        P(None, "tensor"),
        P("tensor"),
    )
    return jax.shard_map(shards, mesh=mesh, in_specs=in_specs, out_specs=out_specs, check_vma=False)
```

```python
import functools
import math

import jax
import jax.numpy as jnp
import numpy as np
from jax import lax
from jax.experimental import pallas as pl
from jax.experimental.pallas import tpu as pltpu
from jax.sharding import PartitionSpec as P

HD = 64
TOP = 8
CAP = 64
HOPS = 4
RANK_ROWS = 32
PLANE = 16
SEGMENTS = 3
EARLY = 1
FIRST = 2
AUX = 16
LANES = 256
MORE = 128

EPS = 1e-06
ROPE_BASE = 10000.0
NEG_FILL = -1e30
BF16 = jnp.bfloat16
F32 = jnp.float32


def contract(left, right, dims):
    return lax.dot_general(left, right, (dims, ((), ())), preferred_element_type=F32)


NN = ((1,), (0,))
NT = ((1,), (1,))
TN = ((0,), (0,))


def swapped(array):
    return lax.ppermute(array, "tensor", [(0, 1), (1, 0)])


def after(array, other):
    return lax.optimization_barrier((array, other))[0]


def passed_along(value, steps):
    count = lax.axis_size("dp")
    first, last = (max(0, -steps), min(count, count - steps))
    return lax.ppermute(value, "dp", [(s, s + steps) for s in range(first, last)])


def rope_tables(count, dp_size):
    freq = np.exp(np.arange(HD // 2) * (-2.0 * math.log(ROPE_BASE) / HD))
    base = np.arange(dp_size)[:, None] * count * freq[None, :]
    local = freq[:, None] * np.arange(count)[None, :]
    index = lax.axis_index("dp")
    cos_base = jnp.asarray(np.cos(base), F32)[index][:, None]
    sin_base = jnp.asarray(np.sin(base), F32)[index][:, None]
    cos_local, sin_local = (jnp.asarray(np.cos(local), F32), jnp.asarray(np.sin(local), F32))
    return (
        cos_base * cos_local - sin_base * sin_local,
        sin_base * cos_local + cos_base * sin_local,
    )


def rotate(values, cosine, sine):
    half = HD // 2
    heads = values.reshape(-1, HD, values.shape[-1])
    first, second = (heads[:, :half], heads[:, half:])
    turned = jnp.concatenate(
        [first * cosine - second * sine, second * cosine + first * sine], axis=1
    )
    return turned.reshape(values.shape)


def fill_bias(blocks, bias):
    tok = bias.shape[1]
    rows = blocks[-1].shape[0] - AUX
    own = blocks[-1][rows:, :].astype(F32)
    seq_q, piece_q = (own[0:1, :], own[1:2, :])
    for number, block in enumerate(blocks):
        side = jnp.transpose(block[rows:, :].astype(F32))
        keep = side[:, 0:1] == seq_q
        if number == len(blocks) - 1:
            at_key = lax.broadcasted_iota(jnp.int32, (tok, tok), 0)
            at_query = lax.broadcasted_iota(jnp.int32, (tok, tok), 1)
            piece = (side[:, 1:2] == piece_q) & (piece_q > 0.0)
            keep = keep & ((at_key <= at_query) | piece)
        bias[number * tok : (number + 1) * tok, :] = jnp.where(keep, 0.0, NEG_FILL)


def all_keys(blocks, start):
    return jnp.concatenate([block[pl.ds(start, HD), :] for block in blocks], axis=1)


def attend_kernel(group, q_ref, k4, k3, k2, k1, k0, out_ref, log_ref, peak_ref, bias):
    blocks = (k4, k3, k2, k1, k0)
    fill_bias(blocks, bias)
    kv_rows = (k0.shape[0] - AUX) // 2

    def one_head(head, _):
        at = pl.multiple_of(head // group * HD, HD)
        keys = all_keys(blocks, at)
        values = all_keys(blocks, kv_rows + at)
        here = pl.ds(pl.multiple_of(head * HD, HD), HD)
        scores = contract(keys, q_ref[here, :], TN) + bias[...]
        peak = jnp.max(scores, axis=0, keepdims=True)
        weight = jnp.exp(scores - peak)
        total = jnp.sum(weight, axis=0, keepdims=True)
        mixed = contract(values, weight.astype(BF16), NN) * (1.0 / total)
        out_ref[here, :] = mixed.astype(BF16)
        log_ref[pl.ds(head, 1), :] = peak + jnp.log(total)
        peak_ref[pl.ds(head, 1), :] = peak
        return 0

    lax.fori_loop(0, group * kv_rows // HD, one_head, 0)


def attend(q, blocks, group):
    rows, tok = q.shape
    heads = rows // HD
    return pl.pallas_call(
        functools.partial(attend_kernel, group),
        out_shape=(
            jax.ShapeDtypeStruct((rows, tok), BF16),
            jax.ShapeDtypeStruct((heads, tok), F32),
            jax.ShapeDtypeStruct((heads, tok), F32),
        ),
        scratch_shapes=[pltpu.VMEM((len(blocks) * tok, tok), F32)],
        compiler_params=pltpu.CompilerParams(vmem_limit_bytes=48 << 20),
        cost_estimate=pl.CostEstimate(
            flops=4 * rows * tok * tok * len(blocks),
            bytes_accessed=4 * rows * tok + 2 * len(blocks) * 528 * tok,
            transcendentals=heads * tok * tok * len(blocks),
        ),
    )(q, *blocks)


def attend_back_kernel(
    group, q_ref, g_ref, log_ref, cos_ref, sin_ref, k4, k3, k2, k1, k0,
    dq_ref, d4, d3, d2, d1, d0, bias,
):
    blocks = (k4, k3, k2, k1, k0)
    grads = (d4, d3, d2, d1, d0)
    fill_bias(blocks, bias)
    kv_rows = (k0.shape[0] - AUX) // 2
    tok = bias.shape[1]
    half = HD // 2

    def one_group(g, _):
        at = pl.multiple_of(g * HD, HD)
        keys = all_keys(blocks, at)
        values = all_keys(blocks, kv_rows + at)
        key_sum = value_sum = None
        for j in range(group):
            head = g * group + j
            start = pl.multiple_of(head * HD, HD)
            query, grad = (q_ref[pl.ds(start, HD), :], g_ref[pl.ds(start, HD), :])
            scores = contract(keys, query, TN) + bias[...]
            probs = jnp.exp(scores - log_ref[pl.ds(head, 1), :])
            grad_probs = contract(values, grad, TN)
            delta = jnp.sum(probs * grad_probs, axis=0, keepdims=True)
            grad_scores = (probs * (grad_probs - delta)).astype(BF16)
            key_part = contract(query, grad_scores, NT)
            value_part = contract(grad, probs.astype(BF16), NT)
            key_sum = key_part if key_sum is None else key_sum + key_part
            value_sum = value_part if value_sum is None else value_sum + value_part
            turned = contract(keys, grad_scores, NN) * (HD**-0.5)
            first, second = (turned[:half], turned[half:])
            cosine, sine = (cos_ref[...], sin_ref[...])
            dq_ref[pl.ds(start, half), :] = (first * cosine + second * sine).astype(BF16)
            dq_ref[pl.ds(start + half, half), :] = (second * cosine - first * sine).astype(BF16)
        for number, grad_ref in enumerate(grads):
            piece = slice(number * tok, (number + 1) * tok)
            grad_ref[pl.ds(at, HD), :] = key_sum[:, piece].astype(grad_ref.dtype)
            grad_ref[pl.ds(kv_rows + at, HD), :] = value_sum[:, piece].astype(grad_ref.dtype)
        return 0

    lax.fori_loop(0, kv_rows // HD, one_group, 0)


def attend_back(q, grad, log_total, cosine, sine, blocks, group):
    rows, tok = q.shape
    kv = blocks[0].shape[0] - AUX
    return pl.pallas_call(
        functools.partial(attend_back_kernel, group),
        out_shape=(
            jax.ShapeDtypeStruct((rows, tok), BF16),
            *(jax.ShapeDtypeStruct((kv, tok), BF16) for _ in blocks[1:]),
            jax.ShapeDtypeStruct((kv, tok), F32),
        ),
        scratch_shapes=[pltpu.VMEM((len(blocks) * tok, tok), F32)],
        compiler_params=pltpu.CompilerParams(vmem_limit_bytes=48 << 20),
        cost_estimate=pl.CostEstimate(
            flops=500 * rows * tok * tok * len(blocks),
            bytes_accessed=6 * rows * tok + 4 * len(blocks) * 528 * tok,
            transcendentals=rows // HD * tok * tok * len(blocks),
        ),
    )(q, grad, log_total, cosine, sine, *blocks)


def dispatch_kernel(pick_ref, rows_ref, *refs):
    rows = contract(pick_ref[...], rows_ref[...], NN)
    for gate_ref in refs[:-1]:
        rows = rows * jnp.sum(gate_ref[...], axis=1, keepdims=True)
    refs[-1][...] = rows.astype(BF16)


def dispatch(pick, rows, *gates):
    slots, tok = pick.shape
    width = rows.shape[1]
    return pl.pallas_call(
        dispatch_kernel,
        grid=(slots // LANES,),
        in_specs=[
            pl.BlockSpec((LANES, tok), lambda i: (i, 0)),
            pl.BlockSpec((tok, width), lambda i: (0, 0)),
        ]
        + [pl.BlockSpec((LANES, tok), lambda i: (i, 0))] * len(gates),
        out_specs=pl.BlockSpec((LANES, width), lambda i: (i, 0)),
        out_shape=jax.ShapeDtypeStruct((slots, width), BF16),
        cost_estimate=pl.CostEstimate(
            flops=2 * slots * tok * width, bytes_accessed=2 * slots * (width + tok), transcendentals=0
        ),
    )(pick, rows, *gates)


def combine_kernel(weight_ref, rows_ref, out_ref):
    rows = rows_ref[...].reshape(weight_ref.shape[0], -1)
    out_ref[...] = contract(weight_ref[...], rows, TN).astype(BF16)


def combine(weights, rows):
    sources, lines, width = rows.shape
    slots, tok = weights.shape
    part = 512
    return pl.pallas_call(
        combine_kernel,
        grid=(width // part,),
        in_specs=[
            pl.BlockSpec((slots, tok), lambda i: (0, 0)),
            pl.BlockSpec((sources, lines, part), lambda i: (0, 0, i)),
        ],
        out_specs=pl.BlockSpec((tok, part), lambda i: (0, i)),
        out_shape=jax.ShapeDtypeStruct((tok, width), BF16),
        cost_estimate=pl.CostEstimate(
            flops=2 * slots * tok * width, bytes_accessed=2 * slots * (width + tok), transcendentals=0
        ),
    )(weights, rows)


def project_kernel(
    x_ref, gain_ref, wq_ref, wk_ref, wv_ref, cos_ref, sin_ref, side_ref,
    normed_ref, inverse_ref, q_ref, block_ref,
):
    x = x_ref[...].astype(F32)
    inverse = lax.rsqrt(jnp.mean(x * x, axis=-1, keepdims=True) + EPS)
    inverse_ref[...] = inverse
    normed_ref[...] = (x * inverse * gain_ref[...]).astype(BF16)
    kv = wk_ref.shape[1]
    step, half = (2 * HD, HD // 2)
    block_ref[2 * kv :, :] = side_ref[...]

    def columns(weight_ref, c):
        lanes = pl.ds(pl.multiple_of(c * step, step), step)
        return contract(weight_ref[:, lanes], normed_ref[...], ((0,), (1,)))

    def rotated(weight_ref, out_ref, scale):
        def one(c, _):
            both = columns(weight_ref, c)
            cosine, sine = (cos_ref[...] * scale, sin_ref[...] * scale)
            for head in range(2):
                first, second = (both[head * HD : head * HD + half], both[head * HD + half : (head + 1) * HD])
                at = pl.multiple_of(c * step + head * HD, HD)
                out_ref[pl.ds(at, half), :] = (first * cosine - second * sine).astype(BF16)
                out_ref[pl.ds(at + half, half), :] = (second * cosine + first * sine).astype(BF16)
            return 0

        lax.fori_loop(0, weight_ref.shape[1] // step, one, 0)

    def one_value(c, _):
        at = pl.multiple_of(kv + c * step, step)
        block_ref[pl.ds(at, step), :] = columns(wv_ref, c).astype(BF16)
        return 0

    rotated(wk_ref, block_ref, 1.0)
    lax.fori_loop(0, kv // step, one_value, 0)
    rotated(wq_ref, q_ref, HD**-0.5)


def project(tokens, gain, w_query, w_key, w_value, cosine, sine, side):
    tok, model = tokens.shape
    width, kv = (w_query.shape[1], w_key.shape[1])
    return pl.pallas_call(
        project_kernel,
        out_shape=(
            jax.ShapeDtypeStruct((tok, model), BF16),
            jax.ShapeDtypeStruct((tok, 1), F32),
            jax.ShapeDtypeStruct((width, tok), BF16),
            jax.ShapeDtypeStruct((2 * kv + AUX, tok), BF16),
        ),
        compiler_params=pltpu.CompilerParams(vmem_limit_bytes=40 << 20),
        cost_estimate=pl.CostEstimate(
            flops=2 * tok * model * (width + 2 * kv),
            bytes_accessed=2 * model * (width + 2 * kv + 3 * tok),
            transcendentals=0,
        ),
    )(tokens, gain, w_query, w_key, w_value, cosine, sine, side)


def pack_weights_kernel(gate_ref, up_ref, down_ref, out_ref):
    hidden = gate_ref.shape[1]
    out_ref[:, :hidden] = gate_ref[...]
    out_ref[:, hidden : 2 * hidden] = up_ref[...]
    out_ref[:, 2 * hidden :] = jnp.transpose(down_ref[...].astype(F32)).astype(BF16)


def pack_weights(gate, up, down):
    width, hidden = gate.shape
    rows = width // 2
    thin = pl.BlockSpec((rows, hidden), lambda i: (i, 0))
    return pl.pallas_call(
        pack_weights_kernel,
        grid=(2,),
        in_specs=[thin, thin, pl.BlockSpec((hidden, rows), lambda i: (0, i))],
        out_specs=pl.BlockSpec((rows, 3 * hidden), lambda i: (i, 0)),
        out_shape=jax.ShapeDtypeStruct((width, 3 * hidden), BF16),
        cost_estimate=pl.CostEstimate(
            flops=width * hidden, bytes_accessed=12 * width * hidden, transcendentals=0
        ),
    )(gate, up, down)


def expert_first_kernel(x_ref, own_ref, peer_ref, out_ref):
    width = x_ref.shape[-1]
    rows = x_ref[...].reshape(-1, width)
    hidden = own_ref.shape[-1] // 3
    out = None
    for weights in (own_ref, peer_ref):
        both = contract(rows, weights[0, :, : 2 * hidden], NN)
        gate_act, up_act = (both[:, :hidden], both[:, hidden:])
        inner = gate_act * (1.0 / (1.0 + jnp.exp(-gate_act))) * up_act
        part = contract(inner.astype(BF16), weights[0, :, 2 * hidden :], NT)
        out = part if out is None else out + part
    out_ref[...] = out.astype(BF16).reshape(out_ref.shape)


def expert_first(rows, own, peer):
    sources, _, width = rows.shape
    triple = own.shape[-1]
    step = sources // 2
    part = pl.BlockSpec((step, RANK_ROWS, width), lambda s, j: (j, s, 0))
    weight = pl.BlockSpec((1, width, triple), lambda s, j: (s, 0, 0))
    return pl.pallas_call(
        expert_first_kernel,
        grid=(FIRST, 2),
        in_specs=[part, weight, weight],
        out_specs=part,
        out_shape=jax.ShapeDtypeStruct((sources, FIRST * RANK_ROWS, width), BF16),
        compiler_params=pltpu.CompilerParams(vmem_limit_bytes=56 << 20),
        cost_estimate=pl.CostEstimate(
            flops=4 * sources * FIRST * RANK_ROWS * width * triple,
            bytes_accessed=4 * sources * FIRST * RANK_ROWS * width + 4 * FIRST * width * triple,
            transcendentals=sources * FIRST * RANK_ROWS * triple * 2 // 3,
        ),
    )(rows, own, peer)


def of_segment(split, early_ref, late_ref, sources=slice(None), lanes=slice(None)):
    early, late = (ref[sources, :, lanes] for ref in (early_ref, late_ref))
    chosen = jnp.where(pl.program_id(0) < split, early, late)
    return chosen.reshape(-1, chosen.shape[-1])


def expert_kernel(x1_ref, x2_ref, g1_ref, g2_ref, own_ref, peer_ref, dx_ref, own_acts, peer_acts):
    hidden = own_ref.shape[-1] // 3
    sources = dx_ref.shape[0] // 2
    count = sources * RANK_ROWS

    def one_half(half, _):
        here = pl.ds(half * sources, sources)
        there = pl.ds(pl.multiple_of(half * count, count), count)
        rows = of_segment(FIRST, x1_ref, x2_ref, here)
        grads = of_segment(EARLY, g1_ref, g2_ref, here)
        back = None
        for weights, acts in ((own_ref, own_acts), (peer_ref, peer_acts)):
            both = contract(rows, weights[0, :, : 2 * hidden], NN)
            grad_inner = contract(grads, weights[0, :, 2 * hidden :], NN)
            gate_act, up_act = (both[:, :hidden], both[:, hidden:])
            sigmoid = 1.0 / (1.0 + jnp.exp(-gate_act))
            silu = gate_act * sigmoid
            dgate = grad_inner * up_act * (sigmoid * (1.0 + gate_act * (1.0 - sigmoid)))
            acts[0, there, :hidden] = dgate.astype(BF16)
            acts[0, there, hidden : 2 * hidden] = (grad_inner * silu).astype(BF16)
            acts[0, there, 2 * hidden :] = (silu * up_act).astype(BF16)
            part = contract(acts[0, there, : 2 * hidden], weights[0, :, : 2 * hidden], NT)
            back = part if back is None else back + part
        dx_ref[here] = back.astype(BF16).reshape(sources, RANK_ROWS, -1)
        return 0

    lax.fori_loop(0, 2, one_half, 0)


def segment_specs(block, split):
    return [
        pl.BlockSpec(block, lambda s: (0, jnp.minimum(s, split - 1), 0)),
        pl.BlockSpec(block, lambda s: (0, jnp.maximum(s - split, 0), 0)),
    ]


def expert_back(rows, grads, own, peer):
    sources, _, width = rows[0].shape
    segments, triple = (SEGMENTS, own.shape[-1])
    lines, count = (segments * RANK_ROWS, sources * RANK_ROWS)
    block = (sources, RANK_ROWS, width)
    specs = segment_specs(block, FIRST) + segment_specs(block, EARLY)
    wide = pl.BlockSpec(block, lambda s: (0, s, 0))
    weight = pl.BlockSpec((1, width, triple), lambda s: (s, 0, 0))
    act = pl.BlockSpec((1, count, triple), lambda s: (s, 0, 0))
    return pl.pallas_call(
        expert_kernel,
        grid=(segments,),
        in_specs=[*specs, weight, weight],
        out_specs=[wide, act, act],
        out_shape=[
            jax.ShapeDtypeStruct((sources, lines, width), BF16),
            jax.ShapeDtypeStruct((segments, count, triple), BF16),
            jax.ShapeDtypeStruct((segments, count, triple), BF16),
        ],
        compiler_params=pltpu.CompilerParams(vmem_limit_bytes=56 << 20),
        cost_estimate=pl.CostEstimate(
            flops=7 * sources * lines * width * triple,
            bytes_accessed=6 * sources * lines * width + 4 * segments * width * triple,
            transcendentals=2 * sources * lines * triple // 3,
        ),
    )(*rows, *grads, own, peer)


def expert_sums_kernel(
    x1_ref, x2_ref, g1_ref, g2_ref, own_acts, peer_acts, own_ref, peer_ref, sum_own, *outs
):
    width = x1_ref.shape[-1]
    hidden = own_ref.shape[-1]
    late_ref = outs[3]
    chunk = width // 3

    def one_chunk(c, _):
        lanes = pl.ds(pl.multiple_of(c * chunk, chunk), chunk)
        rows = of_segment(FIRST, x1_ref, x2_ref, slice(None), lanes)
        grads = of_segment(EARLY, g1_ref, g2_ref, slice(None), lanes)
        for side, acts in enumerate((own_acts, peer_acts)):
            first = contract(rows, acts[0, :, : 2 * hidden], TN).astype(BF16)
            second = contract(grads, acts[0, :, 2 * hidden :], TN).astype(BF16)
            if side == 0:
                sum_own[0, lanes, : 2 * hidden] = first
                sum_own[0, lanes, 2 * hidden :] = second
            else:
                outs[0][0, lanes, :] = first[:, :hidden]
                outs[1][0, lanes, :] = first[:, hidden:]
                outs[2][0, lanes, :] = second
        return 0

    lax.fori_loop(0, 3, one_chunk, 0)
    sources = x1_ref.shape[0] // 2
    count = sources * RANK_ROWS

    def one_half(half, _):
        there = pl.ds(pl.multiple_of(half * count, count), count)
        out = contract(own_acts[0, there, 2 * hidden :], own_ref[0], NT)
        out = out + contract(peer_acts[0, there, 2 * hidden :], peer_ref[0], NT)
        late_ref[pl.ds(half * sources, sources)] = out.astype(BF16).reshape(sources, RANK_ROWS, -1)
        return 0

    @pl.when(pl.program_id(0) >= FIRST)
    def _():
        lax.fori_loop(0, 2, one_half, 0)


def expert_sums(rows, grads, own_acts, peer_acts, own, peer):
    sources, _, width = rows[0].shape
    segments, triple = (SEGMENTS, own.shape[-1])
    lines = segments * RANK_ROWS
    hidden = triple // 3
    count = sources * RANK_ROWS
    block = (sources, RANK_ROWS, width)
    down = pl.BlockSpec((1, width, hidden), lambda s: (s, 0, 2))
    act = pl.BlockSpec((1, count, triple), lambda s: (s, 0, 0))
    return pl.pallas_call(
        expert_sums_kernel,
        grid=(segments,),
        in_specs=[*segment_specs(block, FIRST), *segment_specs(block, EARLY), act, act, down, down],
        out_specs=[pl.BlockSpec((1, width, triple), lambda s: (s, 0, 0))]
        + [pl.BlockSpec((1, width, hidden), lambda s: (s, 0, 0))] * 3
        + [pl.BlockSpec(block, lambda s: (0, jnp.maximum(s - FIRST, 0), 0))],
        out_shape=[jax.ShapeDtypeStruct((segments, width, triple), BF16)]
        + [jax.ShapeDtypeStruct((segments, width, hidden), BF16)] * 3
        + [jax.ShapeDtypeStruct((sources, (segments - FIRST) * RANK_ROWS, width), BF16)],
        compiler_params=pltpu.CompilerParams(vmem_limit_bytes=60 << 20),
        cost_estimate=pl.CostEstimate(
            flops=6 * sources * lines * width * triple,
            bytes_accessed=6 * sources * lines * width + 5 * segments * width * triple,
            transcendentals=0,
        ),
    )(*rows, *grads, own_acts, peer_acts, own, peer)


def both_cores_kernel(own_ref, *refs):
    out_ref = refs[-1]
    hidden = refs[0].shape[-1]

    @pl.when(pl.program_id(0) < SEGMENTS)
    def _():
        for kind, peer_ref in enumerate(refs[:-1]):
            here = slice(kind * hidden, (kind + 1) * hidden)
            total = own_ref[0, :, here].astype(F32) + peer_ref[0].astype(F32)
            out_ref[0, :, here] = total.astype(BF16)

    @pl.when(pl.program_id(0) >= SEGMENTS)
    def _():
        out_ref[...] = jnp.zeros_like(out_ref)


def both_cores(own, peers, slots):
    segments, width, triple = own.shape
    rows = width // 2
    last = segments - 1
    part = pl.BlockSpec((1, rows, triple), lambda s, r: (jnp.minimum(s, last), r, 0))
    thin = pl.BlockSpec((1, rows, triple // 3), lambda s, r: (jnp.minimum(s, last), r, 0))
    return pl.pallas_call(
        both_cores_kernel,
        grid=(slots, 2),
        in_specs=[part] + [thin] * 3,
        out_specs=pl.BlockSpec((1, rows, triple), lambda s, r: (s, r, 0)),
        out_shape=jax.ShapeDtypeStruct((slots, width, triple), BF16),
        cost_estimate=pl.CostEstimate(
            flops=slots * width * triple, bytes_accessed=6 * slots * width * triple, transcendentals=0
        ),
    )(own, *peers)


def first_grads_kernel(normed_ref, query_ref, attended_ref, branch_ref, out_ref):
    width = branch_ref.shape[1]
    out_ref[:, :width] = contract(attended_ref[...], branch_ref[...], NN).astype(BF16)
    out_ref[:, width:] = contract(normed_ref[...], query_ref[...], ((0,), (1,))).astype(BF16)


def last_grads_kernel(normed_ref, kv_ref, extra_ref, _, out_ref):
    columns = kv_ref.shape[0]
    out_ref[:, :columns] = contract(normed_ref[...], kv_ref[...], ((0,), (1,))).astype(BF16)
    out_ref[:, columns : columns + MORE] = jnp.transpose(extra_ref[...]).astype(BF16)
    out_ref[:, columns + MORE :] = jnp.zeros((out_ref.shape[0], MORE), BF16)


def first_grads(normed, grad_query, attended, branch, every):
    tok, model = normed.shape
    width = attended.shape[0]
    half = width // LANES
    return pl.pallas_call(
        first_grads_kernel,
        grid=(model // LANES,),
        in_specs=[
            pl.BlockSpec((tok, LANES), lambda i: (0, i)),
            pl.BlockSpec((width, tok), lambda i: (0, 0)),
            pl.BlockSpec((LANES, tok), lambda i: (i % half, 0)),
            pl.BlockSpec((tok, width), lambda i: (0, i // half)),
        ],
        out_specs=pl.BlockSpec((LANES, 2 * width), lambda i: (i, 0)),
        out_shape=jax.ShapeDtypeStruct((model, every), BF16),
        cost_estimate=pl.CostEstimate(
            flops=4 * tok * model * width, bytes_accessed=4 * model * width, transcendentals=0
        ),
    )(normed, grad_query, attended, branch)


def last_grads(normed, grad_kv, extra, parts):
    tok, model = normed.shape
    columns = grad_kv.shape[0]
    every = parts.shape[1]
    size = columns + 2 * MORE
    return pl.pallas_call(
        last_grads_kernel,
        grid=(model // LANES,),
        in_specs=[
            pl.BlockSpec((tok, LANES), lambda i: (0, i)),
            pl.BlockSpec((columns, tok), lambda i: (0, 0)),
            pl.BlockSpec((MORE, LANES), lambda i: (0, i)),
            pl.BlockSpec(memory_space=pl.ANY),
        ],
        out_specs=pl.BlockSpec((LANES, size), lambda i: (i, (every - size) // size)),
        out_shape=jax.ShapeDtypeStruct(parts.shape, BF16),
        input_output_aliases={3: 0},
        cost_estimate=pl.CostEstimate(
            flops=2 * tok * model * columns, bytes_accessed=2 * model * size, transcendentals=0
        ),
    )(normed, grad_kv, extra, parts)


def unpack_kernel(
    devices, in_ref, query_ref, key_ref, clip_ref,
    wo_ref, wq_ref, wk_ref, wv_ref, sum_ref, cq_ref, ck_ref, peak_ref, sq_ref, sk_ref,
):
    at = 0
    group = cq_ref.shape[1] // ck_ref.shape[1]
    heads = cq_ref.shape[1] // HD
    start = 2 * (wo_ref.shape[1] + wk_ref.shape[1])

    @pl.when(pl.program_id(0) == 0)
    def _():
        lines = in_ref[:devices, start : start + MORE].astype(F32)
        high, low = (lines[:, 2 : 2 + heads], lines[:, 2 + heads : 2 + 2 * heads])
        peak = jnp.max(high + low, axis=0, keepdims=True)
        clip = clip_ref[...]
        scale = jnp.sqrt(clip / jnp.maximum(peak, clip))
        peak_ref[...] = peak
        each = lax.broadcasted_iota(jnp.int32, sq_ref.shape, 1) // HD
        of_key = lax.broadcasted_iota(jnp.int32, sk_ref.shape, 1) // HD
        query_scale, key_scale = (jnp.zeros(sq_ref.shape, F32), jnp.zeros(sk_ref.shape, F32))
        for h in range(heads):
            query_scale = jnp.where(each == h, scale[:, h : h + 1], query_scale)
        for g in range(heads // group):
            least = jnp.min(scale[:, g * group : (g + 1) * group], axis=1, keepdims=True)
            key_scale = jnp.where(of_key == g, least, key_scale)
        sq_ref[...] = query_scale
        sk_ref[...] = key_scale

    for target in (wo_ref, wq_ref, wk_ref, wv_ref):
        size = target.shape[1]
        target[...] = in_ref[:, at : at + size].astype(F32)
        at += size
    sum_ref[...] = jnp.transpose(in_ref[:, at : at + MORE].astype(F32))[: sum_ref.shape[0]]
    cq_ref[...] = (query_ref[...].astype(F32) * sq_ref[...]).astype(BF16)
    ck_ref[...] = (key_ref[...].astype(F32) * sk_ref[...]).astype(BF16)


def unpack(summed, w_query, w_key, clip_limit, devices):
    total, every = summed.shape
    width, narrow = (w_query.shape[1], w_key.shape[1])
    steps = total // LANES
    wide = pl.BlockSpec((LANES, width), lambda i: (i, 0))
    thin = pl.BlockSpec((LANES, narrow), lambda i: (i, 0))
    heads = width // HD
    line = pl.BlockSpec((1, heads), lambda i: (0, 0))
    return pl.pallas_call(
        functools.partial(unpack_kernel, devices),
        grid=(steps,),
        in_specs=[
            pl.BlockSpec((LANES, every), lambda i: (i, 0)),
            wide,
            thin,
            line,
        ],
        out_specs=[
            pl.BlockSpec((LANES, width), lambda i: (i % (steps // 2), i // (steps // 2))),
            wide,
            thin,
            thin,
            pl.BlockSpec((8, LANES), lambda i: (0, i)),
            wide,
            thin,
            line,
        ],
        scratch_shapes=[pltpu.VMEM((1, width), F32), pltpu.VMEM((1, narrow), F32)],
        out_shape=[
            jax.ShapeDtypeStruct((total // 2, 2 * width), F32),
            jax.ShapeDtypeStruct((total, width), F32),
            jax.ShapeDtypeStruct((total, narrow), F32),
            jax.ShapeDtypeStruct((total, narrow), F32),
            jax.ShapeDtypeStruct((8, total), F32),
            jax.ShapeDtypeStruct((total, width), BF16),
            jax.ShapeDtypeStruct((total, narrow), BF16),
            jax.ShapeDtypeStruct((1, heads), F32),
        ],
        compiler_params=pltpu.CompilerParams(vmem_limit_bytes=60 << 20),
        cost_estimate=pl.CostEstimate(
            flops=total * every, bytes_accessed=8 * total * every, transcendentals=0
        ),
    )(summed, w_query, w_key, clip_limit.reshape(1, heads))


def rms_scale(values):
    return lax.rsqrt(jnp.mean(values * values, axis=-1, keepdims=True) + EPS)


def norm_back(grad_normed, hidden, inverse, gain):
    weighted = grad_normed * gain
    grad_gain = jnp.sum(grad_normed * hidden * inverse, axis=0)
    grad_hidden = inverse * weighted - hidden * inverse**3 * jnp.mean(
        weighted * hidden, axis=-1, keepdims=True
    )
    return (grad_hidden, grad_gain)


def shards(
    tokens,
    out_grad,
    norm1_gain,
    norm2_gain,
    w_query,
    w_key,
    w_value,
    w_out,
    w_gate,
    w_up,
    w_down,
    route_ids,
    route_logits,
    seq_ids,
    piece_ids,
    clip_limit,
):
    tok_dev, model_width = tokens.shape
    dp_size = lax.axis_size("dp")
    tensor_size = lax.axis_size("tensor")
    core = lax.axis_index("tensor")
    local_heads = w_query.shape[1] // HD
    local_kv = w_key.shape[1] // HD
    group = local_heads // local_kv
    plane_groups = [list(range(at, at + PLANE)) for at in range(0, dp_size, PLANE)]
    column_groups = [list(range(at, dp_size, PLANE)) for at in range(PLANE)]


    picks = route_ids.T
    logits = route_logits.T
    gate_exp = jnp.exp(logits - jnp.max(logits, axis=0, keepdims=True))
    gates = gate_exp / jnp.sum(gate_exp, axis=0, keepdims=True)
    number = jnp.arange(PLANE * SEGMENTS, dtype=jnp.int32)
    number = number % SEGMENTS * PLANE + number // SEGMENTS
    same = picks[None] == number[:, None, None]
    member = jnp.any(same, axis=1)
    gate_of = jnp.sum(jnp.where(same, gates[None], 0.0), axis=1)
    place = jnp.arange(tok_dev, dtype=jnp.int32)
    before = (place[:, None] < place[None, :]).astype(BF16)
    rank = contract(member.astype(BF16), before, NN)
    rank = jnp.where(member, rank, -1.0)
    wanted = (tensor_size * jnp.arange(RANK_ROWS, dtype=jnp.int32) + core).astype(F32)
    chosen = rank[:, None, :] == wanted[None, :, None]
    pick = chosen.astype(BF16).reshape(-1, tok_dev)
    gated = jnp.where(chosen, gate_of[:, None, :], 0.0)
    gated = gated.reshape(-1, tok_dev)

    def in_plane(rows):
        rows = rows.reshape(PLANE, -1, model_width)
        return lax.all_to_all(rows, "dp", 0, 0, tiled=True, axis_index_groups=plane_groups)

    def grads_for(first, last):
        shape = (PLANE, SEGMENTS * RANK_ROWS, -1)
        part = pick.reshape(shape)[:, first * RANK_ROWS : last * RANK_ROWS].reshape(-1, tok_dev)
        gate = gated.reshape(shape)[:, first * RANK_ROWS : last * RANK_ROWS].reshape(-1, tok_dev)
        return dispatch(part, out_grad, gate)

    grads_early = in_plane(grads_for(0, EARLY))
    grads_late = grads_for(EARLY, SEGMENTS)

    cosine, sine = rope_tables(tok_dev, dp_size)
    x_float = tokens.astype(F32)
    side = jnp.concatenate(
        [(seq_ids + 1)[None], piece_ids[None], jnp.zeros((AUX - 2, tok_dev), jnp.int32)]
    ).astype(BF16)
    normed1, inverse1, query, block = project(
        tokens, norm1_gain[None], w_query, w_key, w_value, cosine, sine, side
    )
    blocks = tuple(passed_along(block, hop) for hop in range(HOPS, 0, -1)) + (block,)
    blocks, grads_early, grads_late = lax.optimization_barrier((blocks, grads_early, grads_late))
    packed_w = pack_weights(w_gate[0], w_up[0], w_down[0])
    own = lax.all_gather(packed_w, "dp", axis=0, axis_index_groups=column_groups)
    grad_rows = (grads_early, in_plane(grads_late))
    attended, log_total, peaks = attend(query, blocks, group)
    attn_part = contract(attended, w_out, TN)
    hidden1 = x_float + (attn_part + swapped(attn_part))
    inverse2 = rms_scale(hidden1)
    normed2 = (hidden1 * inverse2 * norm2_gain).astype(BF16)

    shape = (PLANE, SEGMENTS * RANK_ROWS, -1)
    first_pick, last_pick = (
        pick.reshape(shape)[:, first * RANK_ROWS : last * RANK_ROWS].reshape(-1, tok_dev)
        for first, last in ((0, FIRST), (FIRST, SEGMENTS))
    )
    rows_first, rows_last, *_ = lax.optimization_barrier(
        (dispatch(first_pick, normed2), dispatch(last_pick, normed2), grad_rows[1])
    )
    rows_first = in_plane(rows_first)
    own = after(own, rows_first)
    peer = swapped(own)
    rows_last = in_plane(after(rows_last, rows_first))
    rows_in = (rows_first, rows_last)
    out_early = in_plane(after(expert_first(rows_first, own, peer), rows_last))
    back, own_acts, peer_acts = expert_back(rows_in, grad_rows, own, peer)

    def combined(weights, rows):
        part = combine(weights, rows)
        return part.astype(F32) + swapped(part).astype(F32)

    sum_own, *sum_peer, out_late = expert_sums(rows_in, grad_rows, own_acts, peer_acts, own, peer)
    sums = both_cores(sum_own, [swapped(part) for part in sum_peer], dp_size // PLANE)
    back = in_plane(after(back, out_early))
    out_late = in_plane(after(out_late, back))
    grad_normed2 = combined(pick, after(back, sums))
    sums = lax.psum_scatter(
        sums, "dp", scatter_dimension=0, tiled=True, axis_index_groups=column_groups
    )

    grad_top = out_grad.astype(F32)
    grad_from_norm2, grad_gain2 = norm_back(grad_normed2, hidden1, inverse2, norm2_gain)
    grad_hidden1 = grad_top + grad_from_norm2
    grad_branch = grad_hidden1.astype(BF16)
    grad_attended = contract(w_out, grad_branch, NT).astype(BF16)
    grad_query_pre, *grad_blocks = attend_back(
        query, grad_attended, log_total, cosine, sine, blocks, group
    )
    every = 2 * w_query.shape[1] + 2 * w_key.shape[1] + 2 * MORE
    parts = first_grads(normed1, grad_query_pre, attended, grad_branch, every)
    returned = [
        passed_along(grad_blocks[number], -hop) for number, hop in enumerate(range(HOPS, 0, -1))
    ]
    returned = after(returned, parts)
    kv_total = grad_blocks[-1]
    for part in returned:
        kv_total = kv_total + part.astype(F32)
    kv_rows = local_kv * HD
    grad_key_pre = rotate(kv_total[:kv_rows], cosine, -sine).astype(BF16)
    grad_value = kv_total[kv_rows:].astype(BF16)

    grad_norm1_part = (
        contract(grad_query_pre, w_query, ((0,), (1,)))
        + contract(grad_key_pre, w_key, ((0,), (1,)))
        + contract(grad_value, w_value, ((0,), (1,)))
    ).astype(BF16)

    grad_normed1 = grad_norm1_part.astype(F32) + swapped(grad_norm1_part).astype(F32)
    grad_from_norm1, grad_gain1 = norm_back(grad_normed1, x_float, inverse1, norm1_gain)
    input_grad = grad_hidden1 + grad_from_norm1
    peak = jnp.max(peaks, axis=1)
    peak_high = peak.astype(BF16).astype(F32)
    peak_pair = jnp.concatenate([peak_high, peak - peak_high])
    places = jnp.arange(model_width)[None] == lax.axis_index("dp")
    peak_rows = jnp.where(places, peak_pair[:, None], 0.0)
    extra = jnp.concatenate([grad_gain1[None], grad_gain2[None], peak_rows])
    extra = jnp.pad(extra, ((0, MORE - len(extra)), (0, 0)))
    parts = last_grads(normed1, jnp.concatenate([grad_key_pre, grad_value]), extra, parts)
    parts, sums, out_early, out_late = lax.optimization_barrier((parts, sums, out_early, out_late))
    summed = lax.psum(parts, "dp")
    expert_out = jnp.concatenate([out_early, out_late], axis=1)
    output = (hidden1 + combined(gated.astype(BF16), expert_out)).astype(BF16)
    grad_gate, grad_up, grad_down = jnp.split(sums[0].astype(F32), 3, axis=1)
    grad_down = grad_down.T
    grad_wo, grad_wq, grad_wk, grad_wv, totals, clipped_query, clipped_key, head_peaks = unpack(
        summed, w_query, w_key, clip_limit, dp_size
    )
    return (
        output,
        input_grad,
        grad_wq,
        grad_wk,
        grad_wv,
        grad_wo,
        totals[0],
        totals[1],
        grad_gate[None],
        grad_up[None],
        grad_down[None],
        clipped_query,
        clipped_key,
        head_peaks.reshape(-1),
    )


def solution(mesh):
    in_specs = (
        P("dp", None),
        P("dp", None),
        P(),
        P(),
        P(None, "tensor"),
        P(None, "tensor"),
        P(None, "tensor"),
        P("tensor", None),
        P("dp", None, "tensor"),
        P("dp", None, "tensor"),
        P("dp", "tensor", None),
        P("dp", None),
        P("dp", None),
        P("dp"),
        P("dp"),
        P("tensor"),
    )
    out_specs = (
        P("dp", None),
        P("dp", None),
        P(None, "tensor"),
        P(None, "tensor"),
        P(None, "tensor"),
        P("tensor", None),
        P(),
        P(),
        P("dp", None, "tensor"),
        P("dp", None, "tensor"),
        P("dp", "tensor", None),
        P(None, "tensor"),
        P(None, "tensor"),
        P("tensor"),
    )
    return jax.shard_map(shards, mesh=mesh, in_specs=in_specs, out_specs=out_specs, check_vma=False)
```

```python
import functools
import math

import jax
import jax.numpy as jnp
import numpy as np
from jax import lax
from jax.experimental import pallas as pl
from jax.experimental.pallas import tpu as pltpu
from jax.sharding import PartitionSpec as P

HD = 64
TOP = 8
CAP = 64
HOPS = 4
RANK_ROWS = 32
PLANE = 16
SEGMENTS = 3
EARLY = 1
AUX = 16
LANES = 256
MORE = 128

EPS = 1e-06
ROPE_BASE = 10000.0
NEG_FILL = -1e30
BF16 = jnp.bfloat16
F32 = jnp.float32


def contract(left, right, dims):
    return lax.dot_general(left, right, (dims, ((), ())), preferred_element_type=F32)


NN = ((1,), (0,))
NT = ((1,), (1,))
TN = ((0,), (0,))


def swapped(array):
    return lax.ppermute(array, "tensor", [(0, 1), (1, 0)])


def after(array, other):
    return lax.optimization_barrier((array, other))[0]


def passed_along(value, steps):
    count = lax.axis_size("dp")
    first, last = (max(0, -steps), min(count, count - steps))
    return lax.ppermute(value, "dp", [(s, s + steps) for s in range(first, last)])


def rope_tables(count, dp_size):
    freq = np.exp(np.arange(HD // 2) * (-2.0 * math.log(ROPE_BASE) / HD))
    base = np.arange(dp_size)[:, None] * count * freq[None, :]
    local = freq[:, None] * np.arange(count)[None, :]
    index = lax.axis_index("dp")
    cos_base = jnp.asarray(np.cos(base), F32)[index][:, None]
    sin_base = jnp.asarray(np.sin(base), F32)[index][:, None]
    cos_local, sin_local = (jnp.asarray(np.cos(local), F32), jnp.asarray(np.sin(local), F32))
    return (
        cos_base * cos_local - sin_base * sin_local,
        sin_base * cos_local + cos_base * sin_local,
    )


def rotate(values, cosine, sine):
    half = HD // 2
    heads = values.reshape(-1, HD, values.shape[-1])
    first, second = (heads[:, :half], heads[:, half:])
    turned = jnp.concatenate(
        [first * cosine - second * sine, second * cosine + first * sine], axis=1
    )
    return turned.reshape(values.shape)


def fill_bias(blocks, bias):
    tok = bias.shape[1]
    rows = blocks[-1].shape[0] - AUX
    own = blocks[-1][rows:, :].astype(F32)
    seq_q, piece_q = (own[0:1, :], own[1:2, :])
    for number, block in enumerate(blocks):
        side = jnp.transpose(block[rows:, :].astype(F32))
        keep = side[:, 0:1] == seq_q
        if number == len(blocks) - 1:
            at_key = lax.broadcasted_iota(jnp.int32, (tok, tok), 0)
            at_query = lax.broadcasted_iota(jnp.int32, (tok, tok), 1)
            piece = (side[:, 1:2] == piece_q) & (piece_q > 0.0)
            keep = keep & ((at_key <= at_query) | piece)
        bias[number * tok : (number + 1) * tok, :] = jnp.where(keep, 0.0, NEG_FILL)


def all_keys(blocks, start):
    return jnp.concatenate([block[pl.ds(start, HD), :] for block in blocks], axis=1)


def attend_kernel(group, q_ref, k4, k3, k2, k1, k0, out_ref, log_ref, peak_ref, bias):
    blocks = (k4, k3, k2, k1, k0)
    fill_bias(blocks, bias)
    kv_rows = (k0.shape[0] - AUX) // 2

    def one_head(head, _):
        at = pl.multiple_of(head // group * HD, HD)
        keys = all_keys(blocks, at)
        values = all_keys(blocks, kv_rows + at)
        here = pl.ds(pl.multiple_of(head * HD, HD), HD)
        scores = contract(keys, q_ref[here, :], TN) + bias[...]
        peak = jnp.max(scores, axis=0, keepdims=True)
        weight = jnp.exp(scores - peak)
        total = jnp.sum(weight, axis=0, keepdims=True)
        mixed = contract(values, weight.astype(BF16), NN) * (1.0 / total)
        out_ref[here, :] = mixed.astype(BF16)
        log_ref[pl.ds(head, 1), :] = peak + jnp.log(total)
        peak_ref[pl.ds(head, 1), :] = peak
        return 0

    lax.fori_loop(0, group * kv_rows // HD, one_head, 0)


def attend(q, blocks, group):
    rows, tok = q.shape
    heads = rows // HD
    return pl.pallas_call(
        functools.partial(attend_kernel, group),
        out_shape=(
            jax.ShapeDtypeStruct((rows, tok), BF16),
            jax.ShapeDtypeStruct((heads, tok), F32),
            jax.ShapeDtypeStruct((heads, tok), F32),
        ),
        scratch_shapes=[pltpu.VMEM((len(blocks) * tok, tok), F32)],
        compiler_params=pltpu.CompilerParams(vmem_limit_bytes=48 << 20),
        cost_estimate=pl.CostEstimate(
            flops=4 * rows * tok * tok * len(blocks),
            bytes_accessed=4 * rows * tok + 2 * len(blocks) * 528 * tok,
            transcendentals=heads * tok * tok * len(blocks),
        ),
    )(q, *blocks)


def attend_back_kernel(
    group, q_ref, g_ref, log_ref, cos_ref, sin_ref, k4, k3, k2, k1, k0,
    dq_ref, d4, d3, d2, d1, d0, bias,
):
    blocks = (k4, k3, k2, k1, k0)
    grads = (d4, d3, d2, d1, d0)
    fill_bias(blocks, bias)
    kv_rows = (k0.shape[0] - AUX) // 2
    tok = bias.shape[1]
    half = HD // 2

    def one_group(g, _):
        at = pl.multiple_of(g * HD, HD)
        keys = all_keys(blocks, at)
        values = all_keys(blocks, kv_rows + at)

        def one_head(head, sums):
            start = pl.multiple_of(head * HD, HD)
            query, grad = (q_ref[pl.ds(start, HD), :], g_ref[pl.ds(start, HD), :])
            scores = contract(keys, query, TN) + bias[...]
            probs = jnp.exp(scores - log_ref[pl.ds(head, 1), :])
            grad_probs = contract(values, grad, TN)
            delta = jnp.sum(probs * grad_probs, axis=0, keepdims=True)
            grad_scores = (probs * (grad_probs - delta)).astype(BF16)
            turned = contract(keys, grad_scores, NN) * (HD**-0.5)
            first, second = (turned[:half], turned[half:])
            cosine, sine = (cos_ref[...], sin_ref[...])
            dq_ref[pl.ds(start, half), :] = (first * cosine + second * sine).astype(BF16)
            dq_ref[pl.ds(start + half, half), :] = (second * cosine - first * sine).astype(BF16)
            return (
                sums[0] + contract(query, grad_scores, NT),
                sums[1] + contract(grad, probs.astype(BF16), NT),
            )

        zero = jnp.zeros(keys.shape, F32)
        key_sum, value_sum = lax.fori_loop(g * group, (g + 1) * group, one_head, (zero, zero))
        for number, grad_ref in enumerate(grads):
            piece = slice(number * tok, (number + 1) * tok)
            grad_ref[pl.ds(at, HD), :] = key_sum[:, piece].astype(grad_ref.dtype)
            grad_ref[pl.ds(kv_rows + at, HD), :] = value_sum[:, piece].astype(grad_ref.dtype)
        return 0

    lax.fori_loop(0, kv_rows // HD, one_group, 0)


def attend_back(q, grad, log_total, cosine, sine, blocks, group):
    rows, tok = q.shape
    kv = blocks[0].shape[0] - AUX
    return pl.pallas_call(
        functools.partial(attend_back_kernel, group),
        out_shape=(
            jax.ShapeDtypeStruct((rows, tok), BF16),
            *(jax.ShapeDtypeStruct((kv, tok), BF16) for _ in blocks[1:]),
            jax.ShapeDtypeStruct((kv, tok), F32),
        ),
        scratch_shapes=[pltpu.VMEM((len(blocks) * tok, tok), F32)],
        compiler_params=pltpu.CompilerParams(vmem_limit_bytes=48 << 20),
        cost_estimate=pl.CostEstimate(
            flops=500 * rows * tok * tok * len(blocks),
            bytes_accessed=6 * rows * tok + 4 * len(blocks) * 528 * tok,
            transcendentals=rows // HD * tok * tok * len(blocks),
        ),
    )(q, grad, log_total, cosine, sine, *blocks)


def dispatch_kernel(pick_ref, rows_ref, *refs):
    rows = contract(pick_ref[...], rows_ref[...], NN)
    for gate_ref in refs[:-1]:
        rows = rows * jnp.sum(gate_ref[...], axis=1, keepdims=True)
    refs[-1][...] = rows.astype(BF16)


def dispatch(pick, rows, *gates):
    slots, tok = pick.shape
    width = rows.shape[1]
    return pl.pallas_call(
        dispatch_kernel,
        grid=(slots // LANES,),
        in_specs=[
            pl.BlockSpec((LANES, tok), lambda i: (i, 0)),
            pl.BlockSpec((tok, width), lambda i: (0, 0)),
        ]
        + [pl.BlockSpec((LANES, tok), lambda i: (i, 0))] * len(gates),
        out_specs=pl.BlockSpec((LANES, width), lambda i: (i, 0)),
        out_shape=jax.ShapeDtypeStruct((slots, width), BF16),
        cost_estimate=pl.CostEstimate(
            flops=2 * slots * tok * width, bytes_accessed=2 * slots * (width + tok), transcendentals=0
        ),
    )(pick, rows, *gates)


def combine_kernel(weight_ref, rows_ref, out_ref):
    rows = rows_ref[...].reshape(weight_ref.shape[0], -1)
    out_ref[...] = contract(weight_ref[...], rows, TN).astype(BF16)


def combine(weights, rows):
    sources, lines, width = rows.shape
    slots, tok = weights.shape
    part = 512
    return pl.pallas_call(
        combine_kernel,
        grid=(width // part,),
        in_specs=[
            pl.BlockSpec((slots, tok), lambda i: (0, 0)),
            pl.BlockSpec((sources, lines, part), lambda i: (0, 0, i)),
        ],
        out_specs=pl.BlockSpec((tok, part), lambda i: (0, i)),
        out_shape=jax.ShapeDtypeStruct((tok, width), BF16),
        cost_estimate=pl.CostEstimate(
            flops=2 * slots * tok * width, bytes_accessed=2 * slots * (width + tok), transcendentals=0
        ),
    )(weights, rows)


def project_kernel(
    x_ref, gain_ref, wq_ref, wk_ref, wv_ref, cos_ref, sin_ref, side_ref,
    normed_ref, inverse_ref, q_ref, block_ref,
):
    x = x_ref[...].astype(F32)
    inverse = lax.rsqrt(jnp.mean(x * x, axis=-1, keepdims=True) + EPS)
    inverse_ref[...] = inverse
    normed_ref[...] = (x * inverse * gain_ref[...]).astype(BF16)
    kv = wk_ref.shape[1]
    step, half = (2 * HD, HD // 2)
    block_ref[2 * kv :, :] = side_ref[...]

    def columns(weight_ref, c):
        lanes = pl.ds(pl.multiple_of(c * step, step), step)
        return contract(weight_ref[:, lanes], normed_ref[...], ((0,), (1,)))

    def rotated(weight_ref, out_ref, scale):
        def one(c, _):
            both = columns(weight_ref, c)
            cosine, sine = (cos_ref[...] * scale, sin_ref[...] * scale)
            for head in range(2):
                first, second = (both[head * HD : head * HD + half], both[head * HD + half : (head + 1) * HD])
                at = pl.multiple_of(c * step + head * HD, HD)
                out_ref[pl.ds(at, half), :] = (first * cosine - second * sine).astype(BF16)
                out_ref[pl.ds(at + half, half), :] = (second * cosine + first * sine).astype(BF16)
            return 0

        lax.fori_loop(0, weight_ref.shape[1] // step, one, 0)

    def one_value(c, _):
        at = pl.multiple_of(kv + c * step, step)
        block_ref[pl.ds(at, step), :] = columns(wv_ref, c).astype(BF16)
        return 0

    rotated(wk_ref, block_ref, 1.0)
    lax.fori_loop(0, kv // step, one_value, 0)
    rotated(wq_ref, q_ref, HD**-0.5)


def project(tokens, gain, w_query, w_key, w_value, cosine, sine, side):
    tok, model = tokens.shape
    width, kv = (w_query.shape[1], w_key.shape[1])
    return pl.pallas_call(
        project_kernel,
        out_shape=(
            jax.ShapeDtypeStruct((tok, model), BF16),
            jax.ShapeDtypeStruct((tok, 1), F32),
            jax.ShapeDtypeStruct((width, tok), BF16),
            jax.ShapeDtypeStruct((2 * kv + AUX, tok), BF16),
        ),
        compiler_params=pltpu.CompilerParams(vmem_limit_bytes=40 << 20),
        cost_estimate=pl.CostEstimate(
            flops=2 * tok * model * (width + 2 * kv),
            bytes_accessed=2 * model * (width + 2 * kv + 3 * tok),
            transcendentals=0,
        ),
    )(tokens, gain, w_query, w_key, w_value, cosine, sine, side)


def pack_weights_kernel(gate_ref, up_ref, down_ref, out_ref):
    hidden = gate_ref.shape[1]
    out_ref[:, :hidden] = gate_ref[...]
    out_ref[:, hidden : 2 * hidden] = up_ref[...]
    out_ref[:, 2 * hidden :] = jnp.transpose(down_ref[...].astype(F32)).astype(BF16)


def pack_weights(gate, up, down):
    width, hidden = gate.shape
    rows = width // 2
    thin = pl.BlockSpec((rows, hidden), lambda i: (i, 0))
    return pl.pallas_call(
        pack_weights_kernel,
        grid=(2,),
        in_specs=[thin, thin, pl.BlockSpec((hidden, rows), lambda i: (0, i))],
        out_specs=pl.BlockSpec((rows, 3 * hidden), lambda i: (i, 0)),
        out_shape=jax.ShapeDtypeStruct((width, 3 * hidden), BF16),
        cost_estimate=pl.CostEstimate(
            flops=width * hidden, bytes_accessed=12 * width * hidden, transcendentals=0
        ),
    )(gate, up, down)


def expert_first_kernel(x_ref, own_ref, peer_ref, out_ref):
    width = x_ref.shape[-1]
    rows = x_ref[...].reshape(-1, width)
    hidden = own_ref.shape[-1] // 3
    out = None
    for weights in (own_ref, peer_ref):
        both = contract(rows, weights[0, :, : 2 * hidden], NN)
        gate_act, up_act = (both[:, :hidden], both[:, hidden:])
        inner = gate_act * (1.0 / (1.0 + jnp.exp(-gate_act))) * up_act
        part = contract(inner.astype(BF16), weights[0, :, 2 * hidden :], NT)
        out = part if out is None else out + part
    out_ref[...] = out.astype(BF16).reshape(out_ref.shape)


def expert_first(rows, own, peer):
    sources, _, width = rows.shape
    triple = own.shape[-1]
    step = sources // 2
    part = pl.BlockSpec((step, RANK_ROWS, width), lambda s, j: (j, s, 0))
    weight = pl.BlockSpec((1, width, triple), lambda s, j: (s, 0, 0))
    return pl.pallas_call(
        expert_first_kernel,
        grid=(EARLY, 2),
        in_specs=[part, weight, weight],
        out_specs=part,
        out_shape=jax.ShapeDtypeStruct((sources, EARLY * RANK_ROWS, width), BF16),
        compiler_params=pltpu.CompilerParams(vmem_limit_bytes=56 << 20),
        cost_estimate=pl.CostEstimate(
            flops=4 * sources * EARLY * RANK_ROWS * width * triple,
            bytes_accessed=4 * sources * EARLY * RANK_ROWS * width + 4 * EARLY * width * triple,
            transcendentals=sources * EARLY * RANK_ROWS * triple * 2 // 3,
        ),
    )(rows, own, peer)


def of_segment(early_ref, late_ref, sources=slice(None), lanes=slice(None)):
    early, late = (ref[sources, :, lanes] for ref in (early_ref, late_ref))
    chosen = jnp.where(pl.program_id(0) < EARLY, early, late)
    return chosen.reshape(-1, chosen.shape[-1])


def expert_kernel(x_ref, g1_ref, g2_ref, own_ref, peer_ref, dx_ref, own_acts, peer_acts):
    hidden = own_ref.shape[-1] // 3
    sources = x_ref.shape[0] // 2
    count = sources * RANK_ROWS

    def one_half(half, _):
        here = pl.ds(half * sources, sources)
        there = pl.ds(pl.multiple_of(half * count, count), count)
        rows = x_ref[here].reshape(count, -1)
        grads = of_segment(g1_ref, g2_ref, here)
        back = None
        for weights, acts in ((own_ref, own_acts), (peer_ref, peer_acts)):
            both = contract(rows, weights[0, :, : 2 * hidden], NN)
            grad_inner = contract(grads, weights[0, :, 2 * hidden :], NN)
            gate_act, up_act = (both[:, :hidden], both[:, hidden:])
            sigmoid = 1.0 / (1.0 + jnp.exp(-gate_act))
            silu = gate_act * sigmoid
            dgate = grad_inner * up_act * (sigmoid * (1.0 + gate_act * (1.0 - sigmoid)))
            acts[0, there, :hidden] = dgate.astype(BF16)
            acts[0, there, hidden : 2 * hidden] = (grad_inner * silu).astype(BF16)
            acts[0, there, 2 * hidden :] = (silu * up_act).astype(BF16)
            part = contract(acts[0, there, : 2 * hidden], weights[0, :, : 2 * hidden], NT)
            back = part if back is None else back + part
        dx_ref[here] = back.astype(BF16).reshape(sources, RANK_ROWS, -1)
        return 0

    lax.fori_loop(0, 2, one_half, 0)


def segment_specs(block):
    return [
        pl.BlockSpec(block, lambda s: (0, s, 0)),
        pl.BlockSpec(block, lambda s: (0, jnp.minimum(s, EARLY - 1), 0)),
        pl.BlockSpec(block, lambda s: (0, jnp.maximum(s - EARLY, 0), 0)),
    ]


def expert_back(rows, grads, own, peer):
    sources, lines, width = rows.shape
    segments, triple = (lines // RANK_ROWS, own.shape[-1])
    count = sources * RANK_ROWS
    specs = segment_specs((sources, RANK_ROWS, width))
    wide = specs[0]
    weight = pl.BlockSpec((1, width, triple), lambda s: (s, 0, 0))
    act = pl.BlockSpec((1, count, triple), lambda s: (s, 0, 0))
    return pl.pallas_call(
        expert_kernel,
        grid=(segments,),
        in_specs=[*specs, weight, weight],
        out_specs=[wide, act, act],
        out_shape=[
            jax.ShapeDtypeStruct(rows.shape, BF16),
            jax.ShapeDtypeStruct((segments, count, triple), BF16),
            jax.ShapeDtypeStruct((segments, count, triple), BF16),
        ],
        compiler_params=pltpu.CompilerParams(vmem_limit_bytes=56 << 20),
        cost_estimate=pl.CostEstimate(
            flops=7 * sources * lines * width * triple,
            bytes_accessed=6 * sources * lines * width + 4 * segments * width * triple,
            transcendentals=2 * sources * lines * triple // 3,
        ),
    )(rows, *grads, own, peer)


def expert_sums_kernel(x_ref, g1_ref, g2_ref, own_acts, peer_acts, own_ref, peer_ref, sum_own, *outs):
    width = x_ref.shape[-1]
    hidden = own_ref.shape[-1]
    late_ref = outs[3]
    chunk = width // 3

    def one_chunk(c, _):
        lanes = pl.ds(pl.multiple_of(c * chunk, chunk), chunk)
        rows = x_ref[:, :, lanes].reshape(-1, chunk)
        grads = of_segment(g1_ref, g2_ref, slice(None), lanes)
        for side, acts in enumerate((own_acts, peer_acts)):
            first = contract(rows, acts[0, :, : 2 * hidden], TN).astype(BF16)
            second = contract(grads, acts[0, :, 2 * hidden :], TN).astype(BF16)
            if side == 0:
                sum_own[0, lanes, : 2 * hidden] = first
                sum_own[0, lanes, 2 * hidden :] = second
            else:
                outs[0][0, lanes, :] = first[:, :hidden]
                outs[1][0, lanes, :] = first[:, hidden:]
                outs[2][0, lanes, :] = second
        return 0

    lax.fori_loop(0, 3, one_chunk, 0)
    sources = x_ref.shape[0] // 2
    count = sources * RANK_ROWS

    def one_half(half, _):
        there = pl.ds(pl.multiple_of(half * count, count), count)
        out = contract(own_acts[0, there, 2 * hidden :], own_ref[0], NT)
        out = out + contract(peer_acts[0, there, 2 * hidden :], peer_ref[0], NT)
        late_ref[pl.ds(half * sources, sources)] = out.astype(BF16).reshape(sources, RANK_ROWS, -1)
        return 0

    @pl.when(pl.program_id(0) >= EARLY)
    def _():
        lax.fori_loop(0, 2, one_half, 0)


def expert_sums(rows, grads, own_acts, peer_acts, own, peer):
    sources, lines, width = rows.shape
    segments, triple = (lines // RANK_ROWS, own.shape[-1])
    hidden = triple // 3
    count = sources * RANK_ROWS
    block = (sources, RANK_ROWS, width)
    down = pl.BlockSpec((1, width, hidden), lambda s: (s, 0, 2))
    act = pl.BlockSpec((1, count, triple), lambda s: (s, 0, 0))
    return pl.pallas_call(
        expert_sums_kernel,
        grid=(segments,),
        in_specs=[*segment_specs(block), act, act, down, down],
        out_specs=[pl.BlockSpec((1, width, triple), lambda s: (s, 0, 0))]
        + [pl.BlockSpec((1, width, hidden), lambda s: (s, 0, 0))] * 3
        + [pl.BlockSpec(block, lambda s: (0, jnp.maximum(s - EARLY, 0), 0))],
        out_shape=[jax.ShapeDtypeStruct((segments, width, triple), BF16)]
        + [jax.ShapeDtypeStruct((segments, width, hidden), BF16)] * 3
        + [jax.ShapeDtypeStruct((sources, (segments - EARLY) * RANK_ROWS, width), BF16)],
        compiler_params=pltpu.CompilerParams(vmem_limit_bytes=60 << 20),
        cost_estimate=pl.CostEstimate(
            flops=6 * sources * lines * width * triple,
            bytes_accessed=6 * sources * lines * width + 5 * segments * width * triple,
            transcendentals=0,
        ),
    )(rows, *grads, own_acts, peer_acts, own, peer)


def both_cores_kernel(own_ref, *refs):
    out_ref = refs[-1]
    hidden = refs[0].shape[-1]

    @pl.when(pl.program_id(0) < SEGMENTS)
    def _():
        for kind, peer_ref in enumerate(refs[:-1]):
            here = slice(kind * hidden, (kind + 1) * hidden)
            total = own_ref[0, :, here].astype(F32) + peer_ref[0].astype(F32)
            out_ref[0, :, here] = total.astype(BF16)

    @pl.when(pl.program_id(0) >= SEGMENTS)
    def _():
        out_ref[...] = jnp.zeros_like(out_ref)


def both_cores(own, peers, slots):
    segments, width, triple = own.shape
    rows = width // 2
    last = segments - 1
    part = pl.BlockSpec((1, rows, triple), lambda s, r: (jnp.minimum(s, last), r, 0))
    thin = pl.BlockSpec((1, rows, triple // 3), lambda s, r: (jnp.minimum(s, last), r, 0))
    return pl.pallas_call(
        both_cores_kernel,
        grid=(slots, 2),
        in_specs=[part] + [thin] * 3,
        out_specs=pl.BlockSpec((1, rows, triple), lambda s, r: (s, r, 0)),
        out_shape=jax.ShapeDtypeStruct((slots, width, triple), BF16),
        cost_estimate=pl.CostEstimate(
            flops=slots * width * triple, bytes_accessed=6 * slots * width * triple, transcendentals=0
        ),
    )(own, *peers)


def first_grads_kernel(normed_ref, query_ref, attended_ref, branch_ref, out_ref):
    width = branch_ref.shape[1]
    out_ref[:, :width] = contract(attended_ref[...], branch_ref[...], NN).astype(BF16)
    out_ref[:, width:] = contract(normed_ref[...], query_ref[...], ((0,), (1,))).astype(BF16)


def last_grads_kernel(normed_ref, kv_ref, extra_ref, _, out_ref):
    columns = kv_ref.shape[0]
    out_ref[:, :columns] = contract(normed_ref[...], kv_ref[...], ((0,), (1,))).astype(BF16)
    out_ref[:, columns : columns + MORE] = jnp.transpose(extra_ref[...]).astype(BF16)
    out_ref[:, columns + MORE :] = jnp.zeros((out_ref.shape[0], MORE), BF16)


def first_grads(normed, grad_query, attended, branch, every):
    tok, model = normed.shape
    width = attended.shape[0]
    half = width // LANES
    return pl.pallas_call(
        first_grads_kernel,
        grid=(model // LANES,),
        in_specs=[
            pl.BlockSpec((tok, LANES), lambda i: (0, i)),
            pl.BlockSpec((width, tok), lambda i: (0, 0)),
            pl.BlockSpec((LANES, tok), lambda i: (i % half, 0)),
            pl.BlockSpec((tok, width), lambda i: (0, i // half)),
        ],
        out_specs=pl.BlockSpec((LANES, 2 * width), lambda i: (i, 0)),
        out_shape=jax.ShapeDtypeStruct((model, every), BF16),
        cost_estimate=pl.CostEstimate(
            flops=4 * tok * model * width, bytes_accessed=4 * model * width, transcendentals=0
        ),
    )(normed, grad_query, attended, branch)


def last_grads(normed, grad_kv, extra, parts):
    tok, model = normed.shape
    columns = grad_kv.shape[0]
    every = parts.shape[1]
    size = columns + 2 * MORE
    rows = 2 * LANES
    return pl.pallas_call(
        last_grads_kernel,
        grid=(model // rows,),
        in_specs=[
            pl.BlockSpec((tok, rows), lambda i: (0, i)),
            pl.BlockSpec((columns, tok), lambda i: (0, 0)),
            pl.BlockSpec((MORE, rows), lambda i: (0, i)),
            pl.BlockSpec(memory_space=pl.ANY),
        ],
        out_specs=pl.BlockSpec((rows, size), lambda i: (i, (every - size) // size)),
        out_shape=jax.ShapeDtypeStruct(parts.shape, BF16),
        input_output_aliases={3: 0},
        cost_estimate=pl.CostEstimate(
            flops=2 * tok * model * columns, bytes_accessed=2 * model * size, transcendentals=0
        ),
    )(normed, grad_kv, extra, parts)


def unpack_kernel(
    devices, in_ref, query_ref, key_ref, clip_ref,
    wo_ref, wq_ref, wk_ref, wv_ref, gain1_ref, gain2_ref, cq_ref, ck_ref, peak_ref, sq_ref, sk_ref,
):
    at = 0
    group = cq_ref.shape[1] // ck_ref.shape[1]
    heads = cq_ref.shape[1] // HD
    start = 2 * (wo_ref.shape[1] + wk_ref.shape[1])

    @pl.when(pl.program_id(0) == 0)
    def _():
        lines = in_ref[:devices, start : start + MORE].astype(F32)
        high, low = (lines[:, 2 : 2 + heads], lines[:, 2 + heads : 2 + 2 * heads])
        peak = jnp.max(high + low, axis=0, keepdims=True)
        clip = clip_ref[...]
        scale = jnp.sqrt(clip / jnp.maximum(peak, clip))
        peak_ref[...] = peak
        each = lax.broadcasted_iota(jnp.int32, sq_ref.shape, 1) // HD
        of_key = lax.broadcasted_iota(jnp.int32, sk_ref.shape, 1) // HD
        query_scale, key_scale = (jnp.zeros(sq_ref.shape, F32), jnp.zeros(sk_ref.shape, F32))
        for h in range(heads):
            query_scale = jnp.where(each == h, scale[:, h : h + 1], query_scale)
        for g in range(heads // group):
            least = jnp.min(scale[:, g * group : (g + 1) * group], axis=1, keepdims=True)
            key_scale = jnp.where(of_key == g, least, key_scale)
        sq_ref[...] = query_scale
        sk_ref[...] = key_scale

    for target in (wo_ref, wq_ref, wk_ref, wv_ref):
        size = target.shape[1]
        target[...] = in_ref[:, at : at + size].astype(F32)
        at += size
    lines = jnp.transpose(in_ref[:, at : at + MORE].astype(F32))
    here = pl.ds(pl.multiple_of(pl.program_id(0) * LANES, LANES), LANES)
    gain1_ref[here] = lines[0]
    gain2_ref[here] = lines[1]
    cq_ref[...] = (query_ref[...].astype(F32) * sq_ref[...]).astype(BF16)
    ck_ref[...] = (key_ref[...].astype(F32) * sk_ref[...]).astype(BF16)


def unpack(summed, w_query, w_key, clip_limit, devices):
    total, every = summed.shape
    width, narrow = (w_query.shape[1], w_key.shape[1])
    steps = total // LANES
    wide = pl.BlockSpec((LANES, width), lambda i: (i, 0))
    thin = pl.BlockSpec((LANES, narrow), lambda i: (i, 0))
    heads = width // HD
    line = pl.BlockSpec((1, heads), lambda i: (0, 0))
    return pl.pallas_call(
        functools.partial(unpack_kernel, devices),
        grid=(steps,),
        in_specs=[
            pl.BlockSpec((LANES, every), lambda i: (i, 0)),
            wide,
            thin,
            line,
        ],
        out_specs=[
            pl.BlockSpec((LANES, width), lambda i: (i % (steps // 2), i // (steps // 2))),
            wide,
            thin,
            thin,
            pl.BlockSpec((total,), lambda i: (0,)),
            pl.BlockSpec((total,), lambda i: (0,)),
            wide,
            thin,
            line,
        ],
        scratch_shapes=[pltpu.VMEM((1, width), F32), pltpu.VMEM((1, narrow), F32)],
        out_shape=[
            jax.ShapeDtypeStruct((total // 2, 2 * width), F32),
            jax.ShapeDtypeStruct((total, width), F32),
            jax.ShapeDtypeStruct((total, narrow), F32),
            jax.ShapeDtypeStruct((total, narrow), F32),
            jax.ShapeDtypeStruct((total,), F32),
            jax.ShapeDtypeStruct((total,), F32),
            jax.ShapeDtypeStruct((total, width), BF16),
            jax.ShapeDtypeStruct((total, narrow), BF16),
            jax.ShapeDtypeStruct((1, heads), F32),
        ],
        compiler_params=pltpu.CompilerParams(vmem_limit_bytes=60 << 20),
        cost_estimate=pl.CostEstimate(
            flops=total * every, bytes_accessed=8 * total * every, transcendentals=0
        ),
    )(summed, w_query, w_key, clip_limit.reshape(1, heads))


def rms_scale(values):
    return lax.rsqrt(jnp.mean(values * values, axis=-1, keepdims=True) + EPS)


def norm_back(grad_normed, hidden, inverse, gain):
    weighted = grad_normed * gain
    grad_gain = jnp.sum(grad_normed * hidden * inverse, axis=0)
    grad_hidden = inverse * weighted - hidden * inverse**3 * jnp.mean(
        weighted * hidden, axis=-1, keepdims=True
    )
    return (grad_hidden, grad_gain)


def shards(
    tokens,
    out_grad,
    norm1_gain,
    norm2_gain,
    w_query,
    w_key,
    w_value,
    w_out,
    w_gate,
    w_up,
    w_down,
    route_ids,
    route_logits,
    seq_ids,
    piece_ids,
    clip_limit,
):
    tok_dev, model_width = tokens.shape
    dp_size = lax.axis_size("dp")
    tensor_size = lax.axis_size("tensor")
    core = lax.axis_index("tensor")
    local_heads = w_query.shape[1] // HD
    local_kv = w_key.shape[1] // HD
    group = local_heads // local_kv
    plane_groups = [list(range(at, at + PLANE)) for at in range(0, dp_size, PLANE)]
    column_groups = [list(range(at, dp_size, PLANE)) for at in range(PLANE)]


    picks = route_ids.T
    logits = route_logits.T
    gate_exp = jnp.exp(logits - jnp.max(logits, axis=0, keepdims=True))
    gates = gate_exp / jnp.sum(gate_exp, axis=0, keepdims=True)
    number = jnp.arange(PLANE * SEGMENTS, dtype=jnp.int32)
    number = number % SEGMENTS * PLANE + number // SEGMENTS
    same = picks[None] == number[:, None, None]
    member = jnp.any(same, axis=1)
    gate_of = jnp.sum(jnp.where(same, gates[None], 0.0), axis=1)
    place = jnp.arange(tok_dev, dtype=jnp.int32)
    before = (place[:, None] < place[None, :]).astype(BF16)
    rank = contract(member.astype(BF16), before, NN)
    rank = jnp.where(member, rank, -1.0)
    wanted = (tensor_size * jnp.arange(RANK_ROWS, dtype=jnp.int32) + core).astype(F32)
    chosen = rank[:, None, :] == wanted[None, :, None]
    pick = chosen.astype(BF16).reshape(-1, tok_dev)
    gated = jnp.where(chosen, gate_of[:, None, :], 0.0)
    gated = gated.reshape(-1, tok_dev)

    def in_plane(rows):
        rows = rows.reshape(PLANE, -1, model_width)
        return lax.all_to_all(rows, "dp", 0, 0, tiled=True, axis_index_groups=plane_groups)

    def grads_for(first, last):
        shape = (PLANE, SEGMENTS * RANK_ROWS, -1)
        part = pick.reshape(shape)[:, first * RANK_ROWS : last * RANK_ROWS].reshape(-1, tok_dev)
        gate = gated.reshape(shape)[:, first * RANK_ROWS : last * RANK_ROWS].reshape(-1, tok_dev)
        return dispatch(part, out_grad, gate)

    grads_early = in_plane(grads_for(0, EARLY))
    grads_late = grads_for(EARLY, SEGMENTS)

    cosine, sine = rope_tables(tok_dev, dp_size)
    x_float = tokens.astype(F32)
    side = jnp.concatenate(
        [(seq_ids + 1)[None], piece_ids[None], jnp.zeros((AUX - 2, tok_dev), jnp.int32)]
    ).astype(BF16)
    normed1, inverse1, query, block = project(
        tokens, norm1_gain[None], w_query, w_key, w_value, cosine, sine, side
    )
    blocks = tuple(passed_along(block, hop) for hop in range(HOPS, 0, -1)) + (block,)
    blocks, grads_early, grads_late = lax.optimization_barrier((blocks, grads_early, grads_late))
    packed_w = pack_weights(w_gate[0], w_up[0], w_down[0])
    own = lax.all_gather(packed_w, "dp", axis=0, axis_index_groups=column_groups)
    grad_rows = (grads_early, in_plane(grads_late))
    attended, log_total, peaks = attend(query, blocks, group)
    attn_part = contract(attended, w_out, TN)
    hidden1 = x_float + (attn_part + swapped(attn_part))
    inverse2 = rms_scale(hidden1)
    normed2 = (hidden1 * inverse2 * norm2_gain).astype(BF16)

    rows_out = dispatch(pick, normed2)
    rows_out = after(rows_out, grad_rows[1])
    own = after(own, rows_out)
    peer = swapped(own)
    rows_in = in_plane(rows_out)
    out_early = in_plane(expert_first(rows_in, own, peer))
    back, own_acts, peer_acts = expert_back(rows_in, grad_rows, own, peer)

    def combined(weights, rows):
        part = combine(weights, rows)
        return part.astype(F32) + swapped(part).astype(F32)

    sum_own, *sum_peer, out_late = expert_sums(rows_in, grad_rows, own_acts, peer_acts, own, peer)
    sums = both_cores(sum_own, [swapped(part) for part in sum_peer], dp_size // PLANE)
    back = in_plane(after(back, out_early))
    out_late = in_plane(after(out_late, back))
    grad_normed2 = combined(pick, after(back, sums))
    sums = lax.psum_scatter(
        sums, "dp", scatter_dimension=0, tiled=True, axis_index_groups=column_groups
    )

    grad_top = out_grad.astype(F32)
    grad_from_norm2, grad_gain2 = norm_back(grad_normed2, hidden1, inverse2, norm2_gain)
    grad_hidden1 = grad_top + grad_from_norm2
    grad_branch = grad_hidden1.astype(BF16)
    grad_attended = contract(w_out, grad_branch, NT).astype(BF16)
    grad_query_pre, *grad_blocks = attend_back(
        query, grad_attended, log_total, cosine, sine, blocks, group
    )
    every = 2 * w_query.shape[1] + 2 * w_key.shape[1] + 2 * MORE
    parts = first_grads(normed1, grad_query_pre, attended, grad_branch, every)
    returned = [
        passed_along(grad_blocks[number], -hop) for number, hop in enumerate(range(HOPS, 0, -1))
    ]
    returned = after(returned, parts)
    kv_total = grad_blocks[-1]
    for part in returned:
        kv_total = kv_total + part.astype(F32)
    kv_rows = local_kv * HD
    grad_key_pre = rotate(kv_total[:kv_rows], cosine, -sine).astype(BF16)
    grad_value = kv_total[kv_rows:].astype(BF16)

    grad_norm1_part = (
        contract(grad_query_pre, w_query, ((0,), (1,)))
        + contract(grad_key_pre, w_key, ((0,), (1,)))
        + contract(grad_value, w_value, ((0,), (1,)))
    ).astype(BF16)

    grad_normed1 = grad_norm1_part.astype(F32) + swapped(grad_norm1_part).astype(F32)
    grad_from_norm1, grad_gain1 = norm_back(grad_normed1, x_float, inverse1, norm1_gain)
    input_grad = grad_hidden1 + grad_from_norm1
    peak = jnp.max(peaks, axis=1)
    peak_high = peak.astype(BF16).astype(F32)
    peak_pair = jnp.concatenate([peak_high, peak - peak_high])
    places = jnp.arange(model_width)[None] == lax.axis_index("dp")
    peak_rows = jnp.where(places, peak_pair[:, None], 0.0)
    extra = jnp.concatenate([grad_gain1[None], grad_gain2[None], peak_rows])
    extra = jnp.pad(extra, ((0, MORE - len(extra)), (0, 0)))
    parts = last_grads(normed1, jnp.concatenate([grad_key_pre, grad_value]), extra, parts)
    parts, sums, out_early, out_late = lax.optimization_barrier((parts, sums, out_early, out_late))
    summed = lax.psum(parts, "dp")
    expert_out = jnp.concatenate([out_early, out_late], axis=1)
    output = (hidden1 + combined(gated.astype(BF16), expert_out)).astype(BF16)
    grad_gate, grad_up, grad_down = jnp.split(sums[0].astype(F32), 3, axis=1)
    grad_down = grad_down.T
    grad_wo, grad_wq, grad_wk, grad_wv, sum1, sum2, clipped_query, clipped_key, head_peaks = unpack(
        summed, w_query, w_key, clip_limit, dp_size
    )
    return (
        output,
        input_grad,
        grad_wq,
        grad_wk,
        grad_wv,
        grad_wo,
        sum1,
        sum2,
        grad_gate[None],
        grad_up[None],
        grad_down[None],
        clipped_query,
        clipped_key,
        head_peaks.reshape(-1),
    )


def solution(mesh):
    in_specs = (
        P("dp", None),
        P("dp", None),
        P(),
        P(),
        P(None, "tensor"),
        P(None, "tensor"),
        P(None, "tensor"),
        P("tensor", None),
        P("dp", None, "tensor"),
        P("dp", None, "tensor"),
        P("dp", "tensor", None),
        P("dp", None),
        P("dp", None),
        P("dp"),
        P("dp"),
        P("tensor"),
    )
    out_specs = (
        P("dp", None),
        P("dp", None),
        P(None, "tensor"),
        P(None, "tensor"),
        P(None, "tensor"),
        P("tensor", None),
        P(),
        P(),
        P("dp", None, "tensor"),
        P("dp", None, "tensor"),
        P("dp", "tensor", None),
        P(None, "tensor"),
        P(None, "tensor"),
        P("tensor"),
    )
    return jax.shard_map(shards, mesh=mesh, in_specs=in_specs, out_specs=out_specs, check_vma=False)
```

```python
import functools
import math

import jax
import jax.numpy as jnp
import numpy as np
from jax import lax
from jax.experimental import pallas as pl
from jax.experimental.pallas import tpu as pltpu
from jax.sharding import PartitionSpec as P

HD = 64
TOP = 8
CAP = 64
HOPS = 4
RANK_ROWS = 32
PLANE = 16
SEGMENTS = 3
EARLY = 1
AUX = 16
LANES = 256
MORE = 128

EPS = 1e-06
ROPE_BASE = 10000.0
NEG_FILL = -1e30
BF16 = jnp.bfloat16
F32 = jnp.float32


def contract(left, right, dims):
    return lax.dot_general(left, right, (dims, ((), ())), preferred_element_type=F32)


NN = ((1,), (0,))
NT = ((1,), (1,))
TN = ((0,), (0,))


def swapped(array):
    return lax.ppermute(array, "tensor", [(0, 1), (1, 0)])


def after(array, other):
    return lax.optimization_barrier((array, other))[0]


def passed_along(value, steps):
    count = lax.axis_size("dp")
    first, last = (max(0, -steps), min(count, count - steps))
    return lax.ppermute(value, "dp", [(s, s + steps) for s in range(first, last)])


def rope_tables(count, dp_size):
    freq = np.exp(np.arange(HD // 2) * (-2.0 * math.log(ROPE_BASE) / HD))
    base = np.arange(dp_size)[:, None] * count * freq[None, :]
    local = freq[:, None] * np.arange(count)[None, :]
    index = lax.axis_index("dp")
    cos_base = jnp.asarray(np.cos(base), F32)[index][:, None]
    sin_base = jnp.asarray(np.sin(base), F32)[index][:, None]
    cos_local, sin_local = (jnp.asarray(np.cos(local), F32), jnp.asarray(np.sin(local), F32))
    return (
        cos_base * cos_local - sin_base * sin_local,
        sin_base * cos_local + cos_base * sin_local,
    )


def rotate(values, cosine, sine):
    half = HD // 2
    heads = values.reshape(-1, HD, values.shape[-1])
    first, second = (heads[:, :half], heads[:, half:])
    turned = jnp.concatenate(
        [first * cosine - second * sine, second * cosine + first * sine], axis=1
    )
    return turned.reshape(values.shape)


def fill_bias(blocks, bias):
    tok = bias.shape[1]
    rows = blocks[-1].shape[0] - AUX
    own = blocks[-1][rows:, :].astype(F32)
    seq_q, piece_q = (own[0:1, :], own[1:2, :])
    for number, block in enumerate(blocks):
        side = jnp.transpose(block[rows:, :].astype(F32))
        keep = side[:, 0:1] == seq_q
        if number == len(blocks) - 1:
            at_key = lax.broadcasted_iota(jnp.int32, (tok, tok), 0)
            at_query = lax.broadcasted_iota(jnp.int32, (tok, tok), 1)
            piece = (side[:, 1:2] == piece_q) & (piece_q > 0.0)
            keep = keep & ((at_key <= at_query) | piece)
        bias[number * tok : (number + 1) * tok, :] = jnp.where(keep, 0.0, NEG_FILL)


def all_keys(blocks, start):
    return jnp.concatenate([block[pl.ds(start, HD), :] for block in blocks], axis=1)


def attend_kernel(group, q_ref, k4, k3, k2, k1, k0, out_ref, log_ref, peak_ref, bias):
    blocks = (k4, k3, k2, k1, k0)
    fill_bias(blocks, bias)
    kv_rows = (k0.shape[0] - AUX) // 2

    def one_group(g, _):
        at = pl.multiple_of(g * HD, HD)
        keys = all_keys(blocks, at)
        values = all_keys(blocks, kv_rows + at)
        for j in range(group):
            head = g * group + j
            here = pl.ds(pl.multiple_of(head * HD, HD), HD)
            scores = contract(keys, q_ref[here, :], TN) + bias[...]
            peak = jnp.max(scores, axis=0, keepdims=True)
            weight = jnp.exp(scores - peak)
            total = jnp.sum(weight, axis=0, keepdims=True)
            mixed = contract(values, weight.astype(BF16), NN) * (1.0 / total)
            out_ref[here, :] = mixed.astype(BF16)
            log_ref[pl.ds(head, 1), :] = peak + jnp.log(total)
            peak_ref[pl.ds(head, 1), :] = peak
        return 0

    lax.fori_loop(0, kv_rows // HD, one_group, 0)


def attend(q, blocks, group):
    rows, tok = q.shape
    heads = rows // HD
    return pl.pallas_call(
        functools.partial(attend_kernel, group),
        out_shape=(
            jax.ShapeDtypeStruct((rows, tok), BF16),
            jax.ShapeDtypeStruct((heads, tok), F32),
            jax.ShapeDtypeStruct((heads, tok), F32),
        ),
        scratch_shapes=[pltpu.VMEM((len(blocks) * tok, tok), F32)],
        compiler_params=pltpu.CompilerParams(vmem_limit_bytes=48 << 20),
        cost_estimate=pl.CostEstimate(
            flops=4 * rows * tok * tok * len(blocks),
            bytes_accessed=4 * rows * tok + 2 * len(blocks) * 528 * tok,
            transcendentals=heads * tok * tok * len(blocks),
        ),
    )(q, *blocks)


def attend_back_kernel(
    group, q_ref, g_ref, log_ref, cos_ref, sin_ref, k4, k3, k2, k1, k0,
    dq_ref, d4, d3, d2, d1, d0, bias,
):
    blocks = (k4, k3, k2, k1, k0)
    grads = (d4, d3, d2, d1, d0)
    fill_bias(blocks, bias)
    kv_rows = (k0.shape[0] - AUX) // 2
    tok = bias.shape[1]
    half = HD // 2

    def one_group(g, _):
        at = pl.multiple_of(g * HD, HD)
        keys = all_keys(blocks, at)
        values = all_keys(blocks, kv_rows + at)
        key_sum = value_sum = None
        for j in range(group):
            head = g * group + j
            start = pl.multiple_of(head * HD, HD)
            query, grad = (q_ref[pl.ds(start, HD), :], g_ref[pl.ds(start, HD), :])
            scores = contract(keys, query, TN) + bias[...]
            probs = jnp.exp(scores - log_ref[pl.ds(head, 1), :])
            grad_probs = contract(values, grad, TN)
            delta = jnp.sum(probs * grad_probs, axis=0, keepdims=True)
            grad_scores = (probs * (grad_probs - delta)).astype(BF16)
            key_part = contract(query, grad_scores, NT)
            value_part = contract(grad, probs.astype(BF16), NT)
            key_sum = key_part if key_sum is None else key_sum + key_part
            value_sum = value_part if value_sum is None else value_sum + value_part
            turned = contract(keys, grad_scores, NN) * (HD**-0.5)
            first, second = (turned[:half], turned[half:])
            cosine, sine = (cos_ref[...], sin_ref[...])
            dq_ref[pl.ds(start, half), :] = (first * cosine + second * sine).astype(BF16)
            dq_ref[pl.ds(start + half, half), :] = (second * cosine - first * sine).astype(BF16)
        for number, grad_ref in enumerate(grads):
            piece = slice(number * tok, (number + 1) * tok)
            grad_ref[pl.ds(at, HD), :] = key_sum[:, piece].astype(grad_ref.dtype)
            grad_ref[pl.ds(kv_rows + at, HD), :] = value_sum[:, piece].astype(grad_ref.dtype)
        return 0

    lax.fori_loop(0, kv_rows // HD, one_group, 0)


def attend_back(q, grad, log_total, cosine, sine, blocks, group):
    rows, tok = q.shape
    kv = blocks[0].shape[0] - AUX
    return pl.pallas_call(
        functools.partial(attend_back_kernel, group),
        out_shape=(
            jax.ShapeDtypeStruct((rows, tok), BF16),
            *(jax.ShapeDtypeStruct((kv, tok), BF16) for _ in blocks[1:]),
            jax.ShapeDtypeStruct((kv, tok), F32),
        ),
        scratch_shapes=[pltpu.VMEM((len(blocks) * tok, tok), F32)],
        compiler_params=pltpu.CompilerParams(vmem_limit_bytes=48 << 20),
        cost_estimate=pl.CostEstimate(
            flops=500 * rows * tok * tok * len(blocks),
            bytes_accessed=6 * rows * tok + 4 * len(blocks) * 528 * tok,
            transcendentals=rows // HD * tok * tok * len(blocks),
        ),
    )(q, grad, log_total, cosine, sine, *blocks)


def dispatch_kernel(pick_ref, rows_ref, *refs):
    rows = contract(pick_ref[...], rows_ref[...], NN)
    for gate_ref in refs[:-1]:
        rows = rows * jnp.sum(gate_ref[...], axis=1, keepdims=True)
    refs[-1][...] = rows.astype(BF16)


def dispatch(pick, rows, *gates):
    slots, tok = pick.shape
    width = rows.shape[1]
    return pl.pallas_call(
        dispatch_kernel,
        grid=(slots // LANES,),
        in_specs=[
            pl.BlockSpec((LANES, tok), lambda i: (i, 0)),
            pl.BlockSpec((tok, width), lambda i: (0, 0)),
        ]
        + [pl.BlockSpec((LANES, tok), lambda i: (i, 0))] * len(gates),
        out_specs=pl.BlockSpec((LANES, width), lambda i: (i, 0)),
        out_shape=jax.ShapeDtypeStruct((slots, width), BF16),
        cost_estimate=pl.CostEstimate(
            flops=2 * slots * tok * width, bytes_accessed=2 * slots * (width + tok), transcendentals=0
        ),
    )(pick, rows, *gates)


def combine_kernel(weight_ref, rows_ref, out_ref):
    rows = rows_ref[...].reshape(weight_ref.shape[0], -1)
    out_ref[...] = contract(weight_ref[...], rows, TN).astype(BF16)


def combine(weights, rows):
    sources, lines, width = rows.shape
    slots, tok = weights.shape
    part = 512
    return pl.pallas_call(
        combine_kernel,
        grid=(width // part,),
        in_specs=[
            pl.BlockSpec((slots, tok), lambda i: (0, 0)),
            pl.BlockSpec((sources, lines, part), lambda i: (0, 0, i)),
        ],
        out_specs=pl.BlockSpec((tok, part), lambda i: (0, i)),
        out_shape=jax.ShapeDtypeStruct((tok, width), BF16),
        cost_estimate=pl.CostEstimate(
            flops=2 * slots * tok * width, bytes_accessed=2 * slots * (width + tok), transcendentals=0
        ),
    )(weights, rows)


def project_kernel(
    x_ref, gain_ref, wq_ref, wk_ref, wv_ref, cos_ref, sin_ref, side_ref,
    normed_ref, inverse_ref, q_ref, block_ref,
):
    x = x_ref[...].astype(F32)
    inverse = lax.rsqrt(jnp.mean(x * x, axis=-1, keepdims=True) + EPS)
    inverse_ref[...] = inverse
    normed_ref[...] = (x * inverse * gain_ref[...]).astype(BF16)
    kv = wk_ref.shape[1]
    step, half = (2 * HD, HD // 2)
    block_ref[2 * kv :, :] = side_ref[...]

    def columns(weight_ref, c):
        lanes = pl.ds(pl.multiple_of(c * step, step), step)
        return contract(weight_ref[:, lanes], normed_ref[...], ((0,), (1,)))

    def rotated(weight_ref, out_ref, scale):
        def one(c, _):
            both = columns(weight_ref, c)
            cosine, sine = (cos_ref[...] * scale, sin_ref[...] * scale)
            for head in range(2):
                first, second = (both[head * HD : head * HD + half], both[head * HD + half : (head + 1) * HD])
                at = pl.multiple_of(c * step + head * HD, HD)
                out_ref[pl.ds(at, half), :] = (first * cosine - second * sine).astype(BF16)
                out_ref[pl.ds(at + half, half), :] = (second * cosine + first * sine).astype(BF16)
            return 0

        lax.fori_loop(0, weight_ref.shape[1] // step, one, 0)

    def one_value(c, _):
        at = pl.multiple_of(kv + c * step, step)
        block_ref[pl.ds(at, step), :] = columns(wv_ref, c).astype(BF16)
        return 0

    rotated(wk_ref, block_ref, 1.0)
    lax.fori_loop(0, kv // step, one_value, 0)
    rotated(wq_ref, q_ref, HD**-0.5)


def project(tokens, gain, w_query, w_key, w_value, cosine, sine, side):
    tok, model = tokens.shape
    width, kv = (w_query.shape[1], w_key.shape[1])
    return pl.pallas_call(
        project_kernel,
        out_shape=(
            jax.ShapeDtypeStruct((tok, model), BF16),
            jax.ShapeDtypeStruct((tok, 1), F32),
            jax.ShapeDtypeStruct((width, tok), BF16),
            jax.ShapeDtypeStruct((2 * kv + AUX, tok), BF16),
        ),
        compiler_params=pltpu.CompilerParams(vmem_limit_bytes=40 << 20),
        cost_estimate=pl.CostEstimate(
            flops=2 * tok * model * (width + 2 * kv),
            bytes_accessed=2 * model * (width + 2 * kv + 3 * tok),
            transcendentals=0,
        ),
    )(tokens, gain, w_query, w_key, w_value, cosine, sine, side)


def pack_weights_kernel(gate_ref, up_ref, down_ref, out_ref):
    hidden = gate_ref.shape[1]
    out_ref[:, :hidden] = gate_ref[...]
    out_ref[:, hidden : 2 * hidden] = up_ref[...]
    out_ref[:, 2 * hidden :] = jnp.transpose(down_ref[...].astype(F32)).astype(BF16)


def pack_weights(gate, up, down):
    width, hidden = gate.shape
    rows = width // 2
    thin = pl.BlockSpec((rows, hidden), lambda i: (i, 0))
    return pl.pallas_call(
        pack_weights_kernel,
        grid=(2,),
        in_specs=[thin, thin, pl.BlockSpec((hidden, rows), lambda i: (0, i))],
        out_specs=pl.BlockSpec((rows, 3 * hidden), lambda i: (i, 0)),
        out_shape=jax.ShapeDtypeStruct((width, 3 * hidden), BF16),
        cost_estimate=pl.CostEstimate(
            flops=width * hidden, bytes_accessed=12 * width * hidden, transcendentals=0
        ),
    )(gate, up, down)


def expert_first_kernel(x_ref, own_ref, peer_ref, out_ref):
    width = x_ref.shape[-1]
    rows = x_ref[...].reshape(-1, width)
    hidden = own_ref.shape[-1] // 3
    out = None
    for weights in (own_ref, peer_ref):
        both = contract(rows, weights[0, :, : 2 * hidden], NN)
        gate_act, up_act = (both[:, :hidden], both[:, hidden:])
        inner = gate_act * (1.0 / (1.0 + jnp.exp(-gate_act))) * up_act
        part = contract(inner.astype(BF16), weights[0, :, 2 * hidden :], NT)
        out = part if out is None else out + part
    out_ref[...] = out.astype(BF16).reshape(out_ref.shape)


def expert_first(rows, own, peer):
    sources, _, width = rows.shape
    triple = own.shape[-1]
    step = sources // 2
    part = pl.BlockSpec((step, RANK_ROWS, width), lambda s, j: (j, s, 0))
    weight = pl.BlockSpec((1, width, triple), lambda s, j: (s, 0, 0))
    return pl.pallas_call(
        expert_first_kernel,
        grid=(EARLY, 2),
        in_specs=[part, weight, weight],
        out_specs=part,
        out_shape=jax.ShapeDtypeStruct((sources, EARLY * RANK_ROWS, width), BF16),
        compiler_params=pltpu.CompilerParams(vmem_limit_bytes=56 << 20),
        cost_estimate=pl.CostEstimate(
            flops=4 * sources * EARLY * RANK_ROWS * width * triple,
            bytes_accessed=4 * sources * EARLY * RANK_ROWS * width + 4 * EARLY * width * triple,
            transcendentals=sources * EARLY * RANK_ROWS * triple * 2 // 3,
        ),
    )(rows, own, peer)


def of_segment(early_ref, late_ref, sources=slice(None), lanes=slice(None)):
    early, late = (ref[sources, :, lanes] for ref in (early_ref, late_ref))
    chosen = jnp.where(pl.program_id(0) < EARLY, early, late)
    return chosen.reshape(-1, chosen.shape[-1])


def expert_kernel(x_ref, g1_ref, g2_ref, own_ref, peer_ref, dx_ref, own_acts, peer_acts):
    hidden = own_ref.shape[-1] // 3
    sources = x_ref.shape[0] // 2
    count = sources * RANK_ROWS

    def one_half(half, _):
        here = pl.ds(half * sources, sources)
        there = pl.ds(pl.multiple_of(half * count, count), count)
        rows = x_ref[here].reshape(count, -1)
        grads = of_segment(g1_ref, g2_ref, here)
        back = None
        for weights, acts in ((own_ref, own_acts), (peer_ref, peer_acts)):
            both = contract(rows, weights[0, :, : 2 * hidden], NN)
            grad_inner = contract(grads, weights[0, :, 2 * hidden :], NN)
            gate_act, up_act = (both[:, :hidden], both[:, hidden:])
            sigmoid = 1.0 / (1.0 + jnp.exp(-gate_act))
            silu = gate_act * sigmoid
            dgate = grad_inner * up_act * (sigmoid * (1.0 + gate_act * (1.0 - sigmoid)))
            acts[0, there, :hidden] = dgate.astype(BF16)
            acts[0, there, hidden : 2 * hidden] = (grad_inner * silu).astype(BF16)
            acts[0, there, 2 * hidden :] = (silu * up_act).astype(BF16)
            part = contract(acts[0, there, : 2 * hidden], weights[0, :, : 2 * hidden], NT)
            back = part if back is None else back + part
        dx_ref[here] = back.astype(BF16).reshape(sources, RANK_ROWS, -1)
        return 0

    lax.fori_loop(0, 2, one_half, 0)


def segment_specs(block):
    return [
        pl.BlockSpec(block, lambda s: (0, s, 0)),
        pl.BlockSpec(block, lambda s: (0, jnp.minimum(s, EARLY - 1), 0)),
        pl.BlockSpec(block, lambda s: (0, jnp.maximum(s - EARLY, 0), 0)),
    ]


def expert_back(rows, grads, own, peer):
    sources, lines, width = rows.shape
    segments, triple = (lines // RANK_ROWS, own.shape[-1])
    count = sources * RANK_ROWS
    specs = segment_specs((sources, RANK_ROWS, width))
    wide = specs[0]
    weight = pl.BlockSpec((1, width, triple), lambda s: (s, 0, 0))
    act = pl.BlockSpec((1, count, triple), lambda s: (s, 0, 0))
    return pl.pallas_call(
        expert_kernel,
        grid=(segments,),
        in_specs=[*specs, weight, weight],
        out_specs=[wide, act, act],
        out_shape=[
            jax.ShapeDtypeStruct(rows.shape, BF16),
            jax.ShapeDtypeStruct((segments, count, triple), BF16),
            jax.ShapeDtypeStruct((segments, count, triple), BF16),
        ],
        compiler_params=pltpu.CompilerParams(vmem_limit_bytes=56 << 20),
        cost_estimate=pl.CostEstimate(
            flops=7 * sources * lines * width * triple,
            bytes_accessed=6 * sources * lines * width + 4 * segments * width * triple,
            transcendentals=2 * sources * lines * triple // 3,
        ),
    )(rows, *grads, own, peer)


def expert_sums_kernel(x_ref, g1_ref, g2_ref, own_acts, peer_acts, own_ref, peer_ref, sum_own, *outs):
    width = x_ref.shape[-1]
    hidden = own_ref.shape[-1]
    late_ref = outs[3]
    chunk = width // 3

    def one_chunk(c, _):
        lanes = pl.ds(pl.multiple_of(c * chunk, chunk), chunk)
        rows = x_ref[:, :, lanes].reshape(-1, chunk)
        grads = of_segment(g1_ref, g2_ref, slice(None), lanes)
        for side, acts in enumerate((own_acts, peer_acts)):
            first = contract(rows, acts[0, :, : 2 * hidden], TN).astype(BF16)
            second = contract(grads, acts[0, :, 2 * hidden :], TN).astype(BF16)
            if side == 0:
                sum_own[0, lanes, : 2 * hidden] = first
                sum_own[0, lanes, 2 * hidden :] = second
            else:
                outs[0][0, lanes, :] = first[:, :hidden]
                outs[1][0, lanes, :] = first[:, hidden:]
                outs[2][0, lanes, :] = second
        return 0

    lax.fori_loop(0, 3, one_chunk, 0)
    sources = x_ref.shape[0] // 2
    count = sources * RANK_ROWS

    def one_half(half, _):
        there = pl.ds(pl.multiple_of(half * count, count), count)
        out = contract(own_acts[0, there, 2 * hidden :], own_ref[0], NT)
        out = out + contract(peer_acts[0, there, 2 * hidden :], peer_ref[0], NT)
        late_ref[pl.ds(half * sources, sources)] = out.astype(BF16).reshape(sources, RANK_ROWS, -1)
        return 0

    @pl.when(pl.program_id(0) >= EARLY)
    def _():
        lax.fori_loop(0, 2, one_half, 0)


def expert_sums(rows, grads, own_acts, peer_acts, own, peer):
    sources, lines, width = rows.shape
    segments, triple = (lines // RANK_ROWS, own.shape[-1])
    hidden = triple // 3
    count = sources * RANK_ROWS
    block = (sources, RANK_ROWS, width)
    down = pl.BlockSpec((1, width, hidden), lambda s: (s, 0, 2))
    act = pl.BlockSpec((1, count, triple), lambda s: (s, 0, 0))
    return pl.pallas_call(
        expert_sums_kernel,
        grid=(segments,),
        in_specs=[*segment_specs(block), act, act, down, down],
        out_specs=[pl.BlockSpec((1, width, triple), lambda s: (s, 0, 0))]
        + [pl.BlockSpec((1, width, hidden), lambda s: (s, 0, 0))] * 3
        + [pl.BlockSpec(block, lambda s: (0, jnp.maximum(s - EARLY, 0), 0))],
        out_shape=[jax.ShapeDtypeStruct((segments, width, triple), BF16)]
        + [jax.ShapeDtypeStruct((segments, width, hidden), BF16)] * 3
        + [jax.ShapeDtypeStruct((sources, (segments - EARLY) * RANK_ROWS, width), BF16)],
        compiler_params=pltpu.CompilerParams(vmem_limit_bytes=60 << 20),
        cost_estimate=pl.CostEstimate(
            flops=6 * sources * lines * width * triple,
            bytes_accessed=6 * sources * lines * width + 5 * segments * width * triple,
            transcendentals=0,
        ),
    )(rows, *grads, own_acts, peer_acts, own, peer)


def both_cores_kernel(own_ref, *refs):
    out_ref = refs[-1]
    hidden = refs[0].shape[-1]

    @pl.when(pl.program_id(0) < SEGMENTS)
    def _():
        for kind, peer_ref in enumerate(refs[:-1]):
            here = slice(kind * hidden, (kind + 1) * hidden)
            total = own_ref[0, :, here].astype(F32) + peer_ref[0].astype(F32)
            out_ref[0, :, here] = total.astype(BF16)

    @pl.when(pl.program_id(0) >= SEGMENTS)
    def _():
        out_ref[...] = jnp.zeros_like(out_ref)


def both_cores(own, peers, slots):
    segments, width, triple = own.shape
    rows = width // 2
    last = segments - 1
    part = pl.BlockSpec((1, rows, triple), lambda s, r: (jnp.minimum(s, last), r, 0))
    thin = pl.BlockSpec((1, rows, triple // 3), lambda s, r: (jnp.minimum(s, last), r, 0))
    return pl.pallas_call(
        both_cores_kernel,
        grid=(slots, 2),
        in_specs=[part] + [thin] * 3,
        out_specs=pl.BlockSpec((1, rows, triple), lambda s, r: (s, r, 0)),
        out_shape=jax.ShapeDtypeStruct((slots, width, triple), BF16),
        cost_estimate=pl.CostEstimate(
            flops=slots * width * triple, bytes_accessed=6 * slots * width * triple, transcendentals=0
        ),
    )(own, *peers)


def first_grads_kernel(normed_ref, query_ref, attended_ref, branch_ref, out_ref):
    width = branch_ref.shape[1]
    out_ref[:, :width] = contract(attended_ref[...], branch_ref[...], NN).astype(BF16)
    out_ref[:, width:] = contract(normed_ref[...], query_ref[...], ((0,), (1,))).astype(BF16)


def last_grads_kernel(normed_ref, kv_ref, extra_ref, _, out_ref):
    columns = kv_ref.shape[0]
    out_ref[:, :columns] = contract(normed_ref[...], kv_ref[...], ((0,), (1,))).astype(BF16)
    out_ref[:, columns : columns + MORE] = jnp.transpose(extra_ref[...]).astype(BF16)
    out_ref[:, columns + MORE :] = jnp.zeros((out_ref.shape[0], MORE), BF16)


def first_grads(normed, grad_query, attended, branch, every):
    tok, model = normed.shape
    width = attended.shape[0]
    half = width // LANES
    return pl.pallas_call(
        first_grads_kernel,
        grid=(model // LANES,),
        in_specs=[
            pl.BlockSpec((tok, LANES), lambda i: (0, i)),
            pl.BlockSpec((width, tok), lambda i: (0, 0)),
            pl.BlockSpec((LANES, tok), lambda i: (i % half, 0)),
            pl.BlockSpec((tok, width), lambda i: (0, i // half)),
        ],
        out_specs=pl.BlockSpec((LANES, 2 * width), lambda i: (i, 0)),
        out_shape=jax.ShapeDtypeStruct((model, every), BF16),
        cost_estimate=pl.CostEstimate(
            flops=4 * tok * model * width, bytes_accessed=4 * model * width, transcendentals=0
        ),
    )(normed, grad_query, attended, branch)


def last_grads(normed, grad_kv, extra, parts):
    tok, model = normed.shape
    columns = grad_kv.shape[0]
    every = parts.shape[1]
    size = columns + 2 * MORE
    rows = 2 * LANES
    return pl.pallas_call(
        last_grads_kernel,
        grid=(model // rows,),
        in_specs=[
            pl.BlockSpec((tok, rows), lambda i: (0, i)),
            pl.BlockSpec((columns, tok), lambda i: (0, 0)),
            pl.BlockSpec((MORE, rows), lambda i: (0, i)),
            pl.BlockSpec(memory_space=pl.ANY),
        ],
        out_specs=pl.BlockSpec((rows, size), lambda i: (i, (every - size) // size)),
        out_shape=jax.ShapeDtypeStruct(parts.shape, BF16),
        input_output_aliases={3: 0},
        cost_estimate=pl.CostEstimate(
            flops=2 * tok * model * columns, bytes_accessed=2 * model * size, transcendentals=0
        ),
    )(normed, grad_kv, extra, parts)


def unpack_kernel(
    devices, in_ref, query_ref, key_ref, clip_ref,
    wo_ref, wq_ref, wk_ref, wv_ref, gain1_ref, gain2_ref, cq_ref, ck_ref, peak_ref, sq_ref, sk_ref,
):
    at = 0
    group = cq_ref.shape[1] // ck_ref.shape[1]
    heads = cq_ref.shape[1] // HD
    start = 2 * (wo_ref.shape[1] + wk_ref.shape[1])

    @pl.when(pl.program_id(0) == 0)
    def _():
        lines = in_ref[:devices, start : start + MORE].astype(F32)
        high, low = (lines[:, 2 : 2 + heads], lines[:, 2 + heads : 2 + 2 * heads])
        peak = jnp.max(high + low, axis=0, keepdims=True)
        clip = clip_ref[...]
        scale = jnp.sqrt(clip / jnp.maximum(peak, clip))
        peak_ref[...] = peak
        each = lax.broadcasted_iota(jnp.int32, sq_ref.shape, 1) // HD
        of_key = lax.broadcasted_iota(jnp.int32, sk_ref.shape, 1) // HD
        query_scale, key_scale = (jnp.zeros(sq_ref.shape, F32), jnp.zeros(sk_ref.shape, F32))
        for h in range(heads):
            query_scale = jnp.where(each == h, scale[:, h : h + 1], query_scale)
        for g in range(heads // group):
            least = jnp.min(scale[:, g * group : (g + 1) * group], axis=1, keepdims=True)
            key_scale = jnp.where(of_key == g, least, key_scale)
        sq_ref[...] = query_scale
        sk_ref[...] = key_scale

    for target in (wo_ref, wq_ref, wk_ref, wv_ref):
        size = target.shape[1]
        target[...] = in_ref[:, at : at + size].astype(F32)
        at += size
    lines = jnp.transpose(in_ref[:, at : at + MORE].astype(F32))
    here = pl.ds(pl.multiple_of(pl.program_id(0) * LANES, LANES), LANES)
    gain1_ref[here] = lines[0]
    gain2_ref[here] = lines[1]
    cq_ref[...] = (query_ref[...].astype(F32) * sq_ref[...]).astype(BF16)
    ck_ref[...] = (key_ref[...].astype(F32) * sk_ref[...]).astype(BF16)


def unpack(summed, w_query, w_key, clip_limit, devices):
    total, every = summed.shape
    width, narrow = (w_query.shape[1], w_key.shape[1])
    steps = total // LANES
    wide = pl.BlockSpec((LANES, width), lambda i: (i, 0))
    thin = pl.BlockSpec((LANES, narrow), lambda i: (i, 0))
    heads = width // HD
    line = pl.BlockSpec((1, heads), lambda i: (0, 0))
    return pl.pallas_call(
        functools.partial(unpack_kernel, devices),
        grid=(steps,),
        in_specs=[
            pl.BlockSpec((LANES, every), lambda i: (i, 0)),
            wide,
            thin,
            line,
        ],
        out_specs=[
            pl.BlockSpec((LANES, width), lambda i: (i % (steps // 2), i // (steps // 2))),
            wide,
            thin,
            thin,
            pl.BlockSpec((total,), lambda i: (0,)),
            pl.BlockSpec((total,), lambda i: (0,)),
            wide,
            thin,
            line,
        ],
        scratch_shapes=[pltpu.VMEM((1, width), F32), pltpu.VMEM((1, narrow), F32)],
        out_shape=[
            jax.ShapeDtypeStruct((total // 2, 2 * width), F32),
            jax.ShapeDtypeStruct((total, width), F32),
            jax.ShapeDtypeStruct((total, narrow), F32),
            jax.ShapeDtypeStruct((total, narrow), F32),
            jax.ShapeDtypeStruct((total,), F32),
            jax.ShapeDtypeStruct((total,), F32),
            jax.ShapeDtypeStruct((total, width), BF16),
            jax.ShapeDtypeStruct((total, narrow), BF16),
            jax.ShapeDtypeStruct((1, heads), F32),
        ],
        compiler_params=pltpu.CompilerParams(vmem_limit_bytes=60 << 20),
        cost_estimate=pl.CostEstimate(
            flops=total * every, bytes_accessed=8 * total * every, transcendentals=0
        ),
    )(summed, w_query, w_key, clip_limit.reshape(1, heads))


def rms_scale(values):
    return lax.rsqrt(jnp.mean(values * values, axis=-1, keepdims=True) + EPS)


def norm_back(grad_normed, hidden, inverse, gain):
    weighted = grad_normed * gain
    grad_gain = jnp.sum(grad_normed * hidden * inverse, axis=0)
    grad_hidden = inverse * weighted - hidden * inverse**3 * jnp.mean(
        weighted * hidden, axis=-1, keepdims=True
    )
    return (grad_hidden, grad_gain)


def shards(
    tokens,
    out_grad,
    norm1_gain,
    norm2_gain,
    w_query,
    w_key,
    w_value,
    w_out,
    w_gate,
    w_up,
    w_down,
    route_ids,
    route_logits,
    seq_ids,
    piece_ids,
    clip_limit,
):
    tok_dev, model_width = tokens.shape
    dp_size = lax.axis_size("dp")
    tensor_size = lax.axis_size("tensor")
    core = lax.axis_index("tensor")
    local_heads = w_query.shape[1] // HD
    local_kv = w_key.shape[1] // HD
    group = local_heads // local_kv
    plane_groups = [list(range(at, at + PLANE)) for at in range(0, dp_size, PLANE)]
    column_groups = [list(range(at, dp_size, PLANE)) for at in range(PLANE)]


    picks = route_ids.T
    logits = route_logits.T
    gate_exp = jnp.exp(logits - jnp.max(logits, axis=0, keepdims=True))
    gates = gate_exp / jnp.sum(gate_exp, axis=0, keepdims=True)
    number = jnp.arange(PLANE * SEGMENTS, dtype=jnp.int32)
    number = number % SEGMENTS * PLANE + number // SEGMENTS
    same = picks[None] == number[:, None, None]
    member = jnp.any(same, axis=1)
    gate_of = jnp.sum(jnp.where(same, gates[None], 0.0), axis=1)
    place = jnp.arange(tok_dev, dtype=jnp.int32)
    before = (place[:, None] < place[None, :]).astype(BF16)
    rank = contract(member.astype(BF16), before, NN)
    rank = jnp.where(member, rank, -1.0)
    wanted = (tensor_size * jnp.arange(RANK_ROWS, dtype=jnp.int32) + core).astype(F32)
    chosen = rank[:, None, :] == wanted[None, :, None]
    pick = chosen.astype(BF16).reshape(-1, tok_dev)
    gated = jnp.where(chosen, gate_of[:, None, :], 0.0)
    gated = gated.reshape(-1, tok_dev)

    def in_plane(rows):
        rows = rows.reshape(PLANE, -1, model_width)
        return lax.all_to_all(rows, "dp", 0, 0, tiled=True, axis_index_groups=plane_groups)

    def grads_for(first, last):
        shape = (PLANE, SEGMENTS * RANK_ROWS, -1)
        part = pick.reshape(shape)[:, first * RANK_ROWS : last * RANK_ROWS].reshape(-1, tok_dev)
        gate = gated.reshape(shape)[:, first * RANK_ROWS : last * RANK_ROWS].reshape(-1, tok_dev)
        return dispatch(part, out_grad, gate)

    grads_early = in_plane(grads_for(0, EARLY))
    grads_late = grads_for(EARLY, SEGMENTS)

    cosine, sine = rope_tables(tok_dev, dp_size)
    x_float = tokens.astype(F32)
    side = jnp.concatenate(
        [(seq_ids + 1)[None], piece_ids[None], jnp.zeros((AUX - 2, tok_dev), jnp.int32)]
    ).astype(BF16)
    normed1, inverse1, query, block = project(
        tokens, norm1_gain[None], w_query, w_key, w_value, cosine, sine, side
    )
    blocks = tuple(passed_along(block, hop) for hop in range(HOPS, 0, -1)) + (block,)
    blocks, grads_early, grads_late = lax.optimization_barrier((blocks, grads_early, grads_late))
    packed_w = pack_weights(w_gate[0], w_up[0], w_down[0])
    own = lax.all_gather(packed_w, "dp", axis=0, axis_index_groups=column_groups)
    grad_rows = (grads_early, in_plane(grads_late))
    attended, log_total, peaks = attend(query, blocks, group)
    attn_part = contract(attended, w_out, TN)
    hidden1 = x_float + (attn_part + swapped(attn_part))
    inverse2 = rms_scale(hidden1)
    normed2 = (hidden1 * inverse2 * norm2_gain).astype(BF16)

    rows_out = dispatch(pick, normed2)
    rows_out = after(rows_out, grad_rows[1])
    own = after(own, rows_out)
    peer = swapped(own)
    rows_in = in_plane(rows_out)
    out_early = in_plane(expert_first(rows_in, own, peer))
    back, own_acts, peer_acts = expert_back(rows_in, grad_rows, own, peer)

    def combined(weights, rows):
        part = combine(weights, rows)
        return part.astype(F32) + swapped(part).astype(F32)

    sum_own, *sum_peer, out_late = expert_sums(rows_in, grad_rows, own_acts, peer_acts, own, peer)
    sums = both_cores(sum_own, [swapped(part) for part in sum_peer], dp_size // PLANE)
    back = in_plane(after(back, out_early))
    out_late = in_plane(after(out_late, back))
    grad_normed2 = combined(pick, after(back, sums))
    sums = lax.psum_scatter(
        sums, "dp", scatter_dimension=0, tiled=True, axis_index_groups=column_groups
    )

    grad_top = out_grad.astype(F32)
    grad_from_norm2, grad_gain2 = norm_back(grad_normed2, hidden1, inverse2, norm2_gain)
    grad_hidden1 = grad_top + grad_from_norm2
    grad_branch = grad_hidden1.astype(BF16)
    grad_attended = contract(w_out, grad_branch, NT).astype(BF16)
    grad_query_pre, *grad_blocks = attend_back(
        query, grad_attended, log_total, cosine, sine, blocks, group
    )
    every = 2 * w_query.shape[1] + 2 * w_key.shape[1] + 2 * MORE
    parts = first_grads(normed1, grad_query_pre, attended, grad_branch, every)
    returned = [
        passed_along(grad_blocks[number], -hop) for number, hop in enumerate(range(HOPS, 0, -1))
    ]
    returned = after(returned, parts)
    kv_total = grad_blocks[-1]
    for part in returned:
        kv_total = kv_total + part.astype(F32)
    kv_rows = local_kv * HD
    grad_key_pre = rotate(kv_total[:kv_rows], cosine, -sine).astype(BF16)
    grad_value = kv_total[kv_rows:].astype(BF16)

    grad_norm1_part = (
        contract(grad_query_pre, w_query, ((0,), (1,)))
        + contract(grad_key_pre, w_key, ((0,), (1,)))
        + contract(grad_value, w_value, ((0,), (1,)))
    ).astype(BF16)

    grad_normed1 = grad_norm1_part.astype(F32) + swapped(grad_norm1_part).astype(F32)
    grad_from_norm1, grad_gain1 = norm_back(grad_normed1, x_float, inverse1, norm1_gain)
    input_grad = grad_hidden1 + grad_from_norm1
    peak = jnp.max(peaks, axis=1)
    peak_high = peak.astype(BF16).astype(F32)
    peak_pair = jnp.concatenate([peak_high, peak - peak_high])
    places = jnp.arange(model_width)[None] == lax.axis_index("dp")
    peak_rows = jnp.where(places, peak_pair[:, None], 0.0)
    extra = jnp.concatenate([grad_gain1[None], grad_gain2[None], peak_rows])
    extra = jnp.pad(extra, ((0, MORE - len(extra)), (0, 0)))
    parts = last_grads(normed1, jnp.concatenate([grad_key_pre, grad_value]), extra, parts)
    parts, sums, out_early, out_late = lax.optimization_barrier((parts, sums, out_early, out_late))
    summed = lax.psum(parts, "dp")
    expert_out = jnp.concatenate([out_early, out_late], axis=1)
    output = (hidden1 + combined(gated.astype(BF16), expert_out)).astype(BF16)
    grad_gate, grad_up, grad_down = jnp.split(sums[0].astype(F32), 3, axis=1)
    grad_down = grad_down.T
    grad_wo, grad_wq, grad_wk, grad_wv, sum1, sum2, clipped_query, clipped_key, head_peaks = unpack(
        summed, w_query, w_key, clip_limit, dp_size
    )
    return (
        output,
        input_grad,
        grad_wq,
        grad_wk,
        grad_wv,
        grad_wo,
        sum1,
        sum2,
        grad_gate[None],
        grad_up[None],
        grad_down[None],
        clipped_query,
        clipped_key,
        head_peaks.reshape(-1),
    )


def solution(mesh):
    in_specs = (
        P("dp", None),
        P("dp", None),
        P(),
        P(),
        P(None, "tensor"),
        P(None, "tensor"),
        P(None, "tensor"),
        P("tensor", None),
        P("dp", None, "tensor"),
        P("dp", None, "tensor"),
        P("dp", "tensor", None),
        P("dp", None),
        P("dp", None),
        P("dp"),
        P("dp"),
        P("tensor"),
    )
    out_specs = (
        P("dp", None),
        P("dp", None),
        P(None, "tensor"),
        P(None, "tensor"),
        P(None, "tensor"),
        P("tensor", None),
        P(),
        P(),
        P("dp", None, "tensor"),
        P("dp", None, "tensor"),
        P("dp", "tensor", None),
        P(None, "tensor"),
        P(None, "tensor"),
        P("tensor"),
    )
    return jax.shard_map(shards, mesh=mesh, in_specs=in_specs, out_specs=out_specs, check_vma=False)
```
